32 devices in a mesh: dp: 8 (over y, x, core), tensor: 4 (over z).
Axes of the slice: x: 2, y: 2, z: 4, core: 2. Of those that a mesh axis runs over, the one named last changes fastest.
Arguments:
- tokens: bfloat16 [8192, 1024], P('dp', 'tensor'), may hold values from -6 to 6
- doc_lengths: int32 [8, 6], P('dp'), may hold values from 1 to 512, 1024 in all within a row
- grad_out: bfloat16 [8192, 1024], P('dp', 'tensor'), may hold values from -6 to 6
- norm_gains: float32 [4, 1024], replicated, may hold values from 0.1 to 1.9
- head_gains: float32 [2, 64], replicated, may hold values from 0.1 to 1.9
- conv_in: bfloat16 [1024, 3, 1024], P(None, None, 'tensor'), may hold values from -0.1875 to 0.1875
- conv_kernel: float32 [3, 1024], P(None, 'tensor'), may hold values from -3 to 3
- conv_out: bfloat16 [1024, 1024], P('tensor'), may hold values from -0.1875 to 0.1875
- query_w: bfloat16 [1024, 1024], P(None, 'tensor'), may hold values from -0.1875 to 0.1875
- kv_w: bfloat16 [1024, 2, 512], P(None, None, 'tensor'), may hold values from -0.1875 to 0.1875
- out_w: bfloat16 [1024, 1024], P('tensor'), may hold values from -1.75 to 1.75
- gate_up: bfloat16 [2, 1024, 2, 4608], P(None, 'dp', None, 'tensor'), may hold values from -0.1875 to 0.1875
- down: bfloat16 [2, 4608, 1024], P(None, 'tensor', 'dp'), may hold values from -0.09375 to 0.09375
Outputs:
- output: bfloat16 [8192, 1024], P('dp', 'tensor')
- grad_tokens: float32 [8192, 1024], P('dp', 'tensor')
- grad_norm_gains: float32 [4, 1024], replicated
- grad_head_gains: float32 [2, 64], replicated
- grad_conv_in: float32 [1024, 3, 1024], P('dp', None, 'tensor')
- grad_conv_kernel: float32 [3, 1024], replicated
- grad_conv_out: float32 [1024, 1024], P('tensor', 'dp')
- grad_query_w: float32 [1024, 1024], P('dp', 'tensor')
- grad_kv_w: float32 [1024, 2, 512], P('dp', None, 'tensor')
- grad_out_w: float32 [1024, 1024], P('tensor', 'dp')
- grad_gate_up: float32 [2, 1024, 2, 4608], P(None, 'dp', None, 'tensor')
- grad_down: float32 [2, 4608, 1024], P(None, 'tensor', 'dp')
The draws below stay inside these ranges and needn't reach their ends.
Inputs may be any that keep to these rules, and one draw needn't show every extreme that they name: `doc_lengths`: in each row the 6 document lengths sum to 1024, and the longest is 512.
All inputs are finite; a program needn't handle non-finite values.
Results may differ from the reference program's by a relative error of at most 0.024.
Values may be sent and summed in bfloat16 or wider, within the bound.
A program may use at most 192 MiB of HBM per device.

```python
import math
import jax
import jax.numpy as jnp
import numpy as np
from jax import lax

D = 1024
FF = 4608
HEADS = 16
KV_HEADS = 8
HEAD_DIM = 64
KERNEL = 3
DOCS = 6
SEQ_LEN = 1024
ROWS = 8
TOKENS = 8192
MOST_DOC = 512


def levels(rng, extent, pieces, least, largest):
    def one(dim, blocks):
        heights = jax.random.uniform(jax.random.fold_in(jax.random.fold_in(rng, 6), dim), (blocks,), jnp.float32, least / len(pieces), largest / len(pieces))
        return jnp.repeat(jnp.exp(heights), extent[dim] // blocks).reshape((-1,) + (1,) * (len(extent) - dim - 1))

    loudness = one(*pieces[0])
    for cut in pieces[1:]:
        loudness = loudness * one(*cut)
    return loudness


def profile(number_of, total, most, lean):
    portions = [(1 << 20) // math.isqrt(grade ** lean) + 1 for grade in range(2, number_of + 1)]
    spare, holding = total - most - (number_of - 1), [1] * (number_of - 1)
    while spare > 0:
        free = [i for i in range(number_of - 1) if holding[i] < most]
        whole, left = sum([portions[i] for i in free]), spare
        for i in free:
            extra = min(most - holding[i], max(1, left * portions[i] // whole), spare)
            holding[i] = holding[i] + extra
            spare = spare - extra
    return np.array([most] + holding)


def uneven(own_key, amount, total, limit, skew):
    if amount == 2:
        one = jax.random.randint(own_key, (), max(1, total - limit), min(limit, total - 1) + 1)
        return jnp.stack([one, total - one])
    lengths = jnp.asarray(profile(amount, total, limit, skew), jnp.int32)
    couples = (amount - 1) // 2
    source_of, sink = lengths[1:1 + 2 * couples:2], lengths[2:2 + 2 * couples:2]
    slack = jnp.minimum(source_of - 1, limit - sink)
    moved = jax.random.randint(jax.random.fold_in(own_key, 1), (couples,), 0, 1 << 20) % (slack + 1)
    lengths = lengths.at[1:1 + 2 * couples:2].set(source_of - moved).at[2:2 + 2 * couples:2].set(sink + moved)
    return lengths[jax.random.permutation(jax.random.fold_in(own_key, 2), amount)]


def bell_draw(stream_key, shape, spread, bound, shards=(), kind=jnp.bfloat16):
    factor_of = levels(stream_key, shape, shards, -0.22, 0.18) if shards else 1.0
    drawn = jax.random.normal(stream_key, shape, jnp.float32) * spread * factor_of
    return jnp.minimum(jnp.maximum(drawn, -bound), bound).astype(kind)


def setup_inputs(seed: int = 0) -> dict:
    key_list = jax.random.split(jax.random.key(seed), 14)
    return {
        "tokens": bell_draw(key_list[0], (TOKENS, D), 1.0, 6.0, ((0, 8), (1, 4))),
        "doc_lengths": jax.vmap(lambda own: uneven(own, DOCS, SEQ_LEN, MOST_DOC, 2))(jax.random.split(key_list[1], ROWS)).reshape((ROWS, DOCS)).astype(jnp.int32),
        "grad_out": bell_draw(key_list[2], (TOKENS, D), 1.0, 6.0, ((0, 8), (1, 4))),
        "norm_gains": jnp.clip(1.0 + 0.18 * jax.random.normal(key_list[3], (4, D), jnp.float32), 0.1, 1.9),
        "head_gains": jnp.clip(1.0 + 0.18 * jax.random.normal(key_list[4], (2, HEAD_DIM), jnp.float32), 0.1, 1.9),
        "conv_in": bell_draw(key_list[5], (D, 3, D), D ** -0.5, 0.1875, ((2, 4),)),
        "conv_kernel": bell_draw(key_list[6], (KERNEL, D), 0.6, 3.0, ((1, 4),), jnp.float32),
        "conv_out": bell_draw(key_list[7], (D, D), D ** -0.5, 0.1875, ((0, 4),)),
        "query_w": bell_draw(key_list[8], (D, HEADS * HEAD_DIM), D ** -0.5, 0.1875, ((1, 4),)),
        "kv_w": bell_draw(key_list[9], (D, 2, KV_HEADS * HEAD_DIM), D ** -0.5, 0.1875, ((2, 4),)),
        "out_w": bell_draw(key_list[10], (HEADS * HEAD_DIM, D), (max(1, HEADS * HEAD_DIM * 12 // SEQ_LEN)) ** -0.5, 1.75, ((0, 4),)),
        "gate_up": bell_draw(key_list[11], (2, D, 2, FF), D ** -0.5, 0.1875, ((1, 8), (3, 4))),
        "down": bell_draw(key_list[12], (2, FF, D), FF ** -0.5, 0.09375, ((1, 4), (2, 8))),
    }


epsilon = 1e-05
rope_base = 1000000.0

@jax.custom_vjp
def low(v):
    return lax.optimization_barrier(v.astype(jnp.bfloat16)).astype(jnp.float32)

@jax.custom_vjp
def low_back(v):
    return v

def low_keep(v):
    return (low(v), None)

def low_pass(kept, grad):
    return (grad,)

def back_keep(v):
    return (v, None)

def back_low(kept, grad):
    return (low(grad),)
low.defvjp(low_keep, low_pass)
low_back.defvjp(back_keep, back_low)

def matmul(left, right):
    return jnp.dot(left, right, precision=lax.Precision.HIGHEST, preferred_element_type=jnp.float32)

def rms_norm(values, norm_gain):
    inverse = lax.rsqrt(lax.optimization_barrier(jnp.mean(values * values, axis=-1, keepdims=True)) + epsilon)
    return values * inverse * norm_gain

def doc_layout(lengths_row, length):
    doc_ends = jnp.cumsum(lengths_row).astype(jnp.int32)
    places = jnp.arange(length, dtype=jnp.int32)
    passed = places[:, None] >= doc_ends[None, :]
    segment = lax.optimization_barrier(jnp.sum(passed.astype(jnp.int32), axis=1)).astype(jnp.int32)
    doc_start = lax.optimization_barrier(jnp.max(jnp.where(passed, doc_ends[None, :], 0), axis=1)).astype(jnp.int32)
    return (segment, places - doc_start)

def rope_tables(position, head_dim):
    half_dim = head_dim // 2
    inverse = rope_base ** (-2.0 * jnp.arange(half_dim, dtype=jnp.float32) / head_dim)
    angles = position.astype(jnp.float32)[:, None] * inverse[None, :]
    return (jnp.cos(angles)[:, None, :], jnp.sin(angles)[:, None, :])

def rotate(values, tables):
    cosine, sine = tables
    half_dim = values.shape[-1] // 2
    first_half, second_half = (values[..., :half_dim], values[..., half_dim:])
    return jnp.concatenate([first_half * cosine - second_half * sine, second_half * cosine + first_half * sine], axis=-1)

def shift_down(values, offset):
    filler = jnp.zeros((offset,) + values.shape[1:], values.dtype)
    return jnp.concatenate([filler, values[:values.shape[0] - offset]], axis=0)

def same_document(segment, offset):
    places = jnp.arange(segment.shape[0], dtype=jnp.int32)
    return (segment == shift_down(segment, offset)) & (places >= offset)

def conv_mixer(stream, norm_gain, conv_in, conv_kernel, conv_out, segment):
    length, width = stream.shape
    normed = low(rms_norm(stream, norm_gain))
    projected = low_back(matmul(normed, conv_in.reshape(width, -1))).reshape(length, 3, width)
    gated = projected[:, 0] * projected[:, 2]
    summed = conv_kernel[0] * gated
    for offset in range(1, conv_kernel.shape[0]):
        summed = summed + conv_kernel[offset] * jnp.where(same_document(segment, offset)[:, None], shift_down(gated, offset), 0.0)
    mixed_low = low(projected[:, 1] * summed)
    return low_back(matmul(mixed_low, conv_out))

def feed_forward(stream, norm_gain, gate_up_w, down_w):
    length, width = stream.shape
    normed = low(rms_norm(stream, norm_gain))
    hidden = low_back(matmul(normed, gate_up_w.reshape(width, -1))).reshape(length, 2, -1)
    active = low(jax.nn.silu(hidden[:, 0]) * hidden[:, 1])
    return low_back(matmul(active, down_w))

def attention(query, keys, values, segment):
    length, heads, head_dim = query.shape
    kv_count = keys.shape[1]
    groups = heads // kv_count
    block_rows = min(length, 512)
    key_places = jnp.arange(length, dtype=jnp.int32)
    score_scale = head_dim ** (-0.5)

    def one_block(block_index):
        block_start = (block_index * block_rows).astype(jnp.int32)
        query_block = lax.dynamic_slice_in_dim(query, block_start, block_rows, 0).reshape(block_rows, kv_count, groups, head_dim)
        segment_block = lax.dynamic_slice_in_dim(segment, block_start, block_rows, 0)
        query_places = block_start + jnp.arange(block_rows, dtype=jnp.int32)
        raw = jnp.einsum('bkgd,skd->kgbs', query_block, keys, precision=lax.Precision.HIGHEST)
        scores = low_back(raw * score_scale)
        allowed = (key_places[None, :] <= query_places[:, None]) & (segment[None, :] == segment_block[:, None])
        scores = jnp.where(allowed, scores, -1e+30)
        top = lax.optimization_barrier(jnp.max(scores, axis=-1, keepdims=True))
        weights = jnp.exp(scores - top)
        probs = weights / lax.optimization_barrier(jnp.sum(weights, axis=-1, keepdims=True))
        attended = jnp.einsum('kgbs,skd->bkgd', low(probs), values, precision=lax.Precision.HIGHEST)
        return attended.reshape(block_rows, heads, head_dim)
    blocks = lax.map(jax.checkpoint(one_block), jnp.arange(length // block_rows, dtype=jnp.int32))
    return blocks.reshape(length, heads, head_dim)

def attention_mixer(stream, norm_gain, head_gains, query_w, kv_w, out_w, segment, tables):
    length, width = stream.shape
    normed = low(rms_norm(stream, norm_gain))
    query_raw = low_back(matmul(normed, query_w)).reshape(length, HEADS, HEAD_DIM)
    pair_raw = low_back(matmul(normed, kv_w.reshape(width, -1))).reshape(length, 2, KV_HEADS, HEAD_DIM)
    query = low(rotate(rms_norm(query_raw, head_gains[0]), tables))
    keys = low(rotate(rms_norm(pair_raw[:, 0], head_gains[1]), tables))
    values = low(pair_raw[:, 1])
    attended = low(low_back(attention(query, keys, values, segment)))
    return low_back(matmul(attended.reshape(length, -1), out_w))

def block_forward(params, stream, segment, tables):
    norm_gains, head_gains, conv_in, conv_kernel, conv_out, query_w, kv_w, out_w, gate_up, down = params
    stream = stream + conv_mixer(stream, norm_gains[0], conv_in, conv_kernel, conv_out, segment)
    stream = stream + feed_forward(stream, norm_gains[1], gate_up[0], down[0])
    stream = stream + attention_mixer(stream, norm_gains[2], head_gains, query_w, kv_w, out_w, segment, tables)
    stream = stream + feed_forward(stream, norm_gains[3], gate_up[1], down[1])
    return stream

def reference(tokens, doc_lengths, grad_out, norm_gains, head_gains, conv_in, conv_kernel, conv_out, query_w, kv_w, out_w, gate_up, down):
    weights = tuple((argument.astype(jnp.float32) for argument in (norm_gains, head_gains, conv_in, conv_kernel, conv_out, query_w, kv_w, out_w, gate_up, down)))
    row_count = doc_lengths.shape[0]
    inputs = tokens.astype(jnp.float32).reshape(row_count, SEQ_LEN, D)
    cotangent = grad_out.astype(jnp.float32).reshape(row_count, SEQ_LEN, D)

    def one_row(running, row_items):
        row_input, row_cotangent, row_lengths = row_items
        segment, position = doc_layout(row_lengths, SEQ_LEN)
        tables = rope_tables(position, HEAD_DIM)

        def forward(params, stream):
            return block_forward(params, stream, segment, tables)
        result, pullback = jax.vjp(forward, weights, row_input)
        grad_params, grad_input = pullback(row_cotangent)
        running = jax.tree.map(jnp.add, running, grad_params)
        return (running, (result.astype(jnp.bfloat16), grad_input))
    initial = jax.tree.map(jnp.zeros_like, weights)
    summed_grads, (outputs, grad_inputs) = lax.scan(one_row, initial, (inputs, cotangent, doc_lengths))
    return (outputs.reshape(TOKENS, D), grad_inputs.reshape(TOKENS, D), summed_grads[0], summed_grads[1], summed_grads[2], summed_grads[3], summed_grads[4], summed_grads[5], summed_grads[6], summed_grads[7], summed_grads[8], summed_grads[9])
```

```python
import jax
import jax.numpy as jnp
from jax import lax
from jax.sharding import Mesh, PartitionSpec as P

epsilon = 1e-05
rope_base = 1000000.0
TP = ("c", "zl")
DP = ("r", "zh")
BF = jnp.bfloat16
F32 = jnp.float32


def doc_layout(lengths_row, length):
    count = lengths_row.shape[0]
    upto = jnp.arange(count)[:, None] >= jnp.arange(count)[None, :]
    doc_ends = jnp.sum(jnp.where(upto, lengths_row[None, :], 0), axis=1)
    places = jnp.arange(length, dtype=jnp.int32)
    passed = places[:, None] >= doc_ends[None, :]
    segment = jnp.sum(passed.astype(jnp.int32), axis=1)
    doc_start = jnp.max(jnp.where(passed, doc_ends[None, :], 0), axis=1)
    return (segment, places - doc_start)


def rope_tables(position, head_dim):
    half_dim = head_dim // 2
    inverse = rope_base ** (-2.0 * jnp.arange(half_dim, dtype=F32) / head_dim)
    angles = position.astype(F32)[:, None] * inverse[None, :]
    return (jnp.cos(angles)[:, None, :], jnp.sin(angles)[:, None, :])


def rotate(values, tables):
    cosine, sine = tables
    half_dim = values.shape[-1] // 2
    first_half, second_half = (values[..., :half_dim], values[..., half_dim:])
    return jnp.concatenate(
        [first_half * cosine - second_half * sine, second_half * cosine + first_half * sine],
        axis=-1,
    )


def rotate_back(gradient, tables):
    cosine, sine = tables
    half_dim = gradient.shape[-1] // 2
    first_half, second_half = (gradient[..., :half_dim], gradient[..., half_dim:])
    return jnp.concatenate(
        [first_half * cosine + second_half * sine, second_half * cosine - first_half * sine],
        axis=-1,
    )


def shift_down(values, offset):
    filler = jnp.zeros((offset,) + values.shape[1:], values.dtype)
    return jnp.concatenate([filler, values[: values.shape[0] - offset]], axis=0)


def shift_up(values, offset):
    filler = jnp.zeros((offset,) + values.shape[1:], values.dtype)
    return jnp.concatenate([values[offset:], filler], axis=0)


def rms_forward(values, norm_gain):
    inverse = lax.rsqrt(jnp.mean(values * values, axis=-1, keepdims=True) + epsilon)
    return (values * inverse * norm_gain, inverse)


def rms_backward(upstream, values, inverse, norm_gain):
    scaled = upstream * norm_gain
    inner = jnp.mean(scaled * values, axis=-1, keepdims=True)
    grad_values = inverse * scaled - values * inverse**3 * inner
    leading = tuple(range(values.ndim - 1))
    grad_gain = jnp.sum(upstream * values * inverse, axis=leading)
    return (grad_values, grad_gain)


def dot(a, b):
    return jnp.dot(a, b, preferred_element_type=F32)


def swap(x):
    return lax.ppermute(x, ("c", "zh"), [(0, 0), (1, 2), (2, 1), (3, 3)])


def gather_rows(block):
    return lax.all_gather(block, TP, axis=0, tiled=True)


def scatter_rows(partial):
    return lax.psum_scatter(partial.astype(BF), TP, scatter_dimension=0, tiled=True).astype(F32)


def gather_dp(shard, axis):
    return lax.all_gather(shard, DP, axis=axis, tiled=True)


def scatter_dp(partial, axis):
    return lax.psum_scatter(partial.astype(BF), DP, scatter_dimension=axis, tiled=True)


def conv_local(normed, conv_in, conv_kernel, same):
    projected = dot(normed, conv_in)
    width = conv_kernel.shape[1]
    gated = projected[:, :width] * projected[:, 2 * width :]
    summed = conv_kernel[0] * gated
    for offset in range(1, conv_kernel.shape[0]):
        summed = summed + conv_kernel[offset] * jnp.where(
            same[offset][:, None], shift_down(gated, offset), 0.0
        )
    mixed = (projected[:, width : 2 * width] * summed).astype(BF)
    return projected, summed, mixed


def ffn_local(normed, w, v):
    hidden = dot(normed, w)
    half = hidden.shape[1] // 2
    active = (jax.nn.silu(hidden[:, :half]) * hidden[:, half:]).astype(BF)
    return hidden, active, dot(active, v)


def local(
    tokens, doc_lengths, grad_out, norm_gains, head_gains, conv_in, conv_kernel, conv_out,
    query_w, kv_w, out_w, gate_up, down,
):
    length = tokens.shape[0]
    head_dim = head_gains.shape[1]
    quarter = lax.axis_index("c") * 2 + lax.axis_index("zl")
    group = 4
    rows = length // group
    segment, position = doc_layout(swap(doc_lengths)[0], length)
    places = jnp.arange(length, dtype=jnp.int32)
    same = [None] + [position >= j for j in range(1, conv_kernel.shape[0])]
    tables = rope_tables(position, head_dim)
    conv_in = swap(conv_in.reshape(conv_in.shape[0], -1))
    conv_kernel = swap(conv_kernel)
    conv_out = swap(conv_out)
    query_w = swap(query_w)
    kv_w = swap(kv_w.reshape(kv_w.shape[0], -1))
    out_w = swap(out_w)
    ws = [gather_dp(swap(gate_up[l].reshape(gate_up.shape[1], -1)), 0) for l in (0, 1)]
    vs = [gather_dp(swap(down[l]), 1) for l in (0, 1)]

    x_full = lax.all_gather(swap(tokens), TP, axis=1, tiled=True)
    up_full = lax.all_gather(swap(grad_out), TP, axis=1, tiled=True)
    my = lambda a: lax.dynamic_slice_in_dim(a, quarter * rows, rows, 0)
    n0 = rms_forward(x_full.astype(F32), norm_gains[0])[0].astype(BF)
    h0 = my(x_full).astype(F32)
    projected, summed, mixed = conv_local(n0, conv_in, conv_kernel, same)
    h1 = h0 + scatter_rows(dot(mixed, conv_out))
    n1 = gather_rows(rms_forward(h1, norm_gains[1])[0].astype(BF))
    hidden0, active0, part = ffn_local(n1, ws[0], vs[0])
    h2 = h1 + scatter_rows(part)
    n2 = gather_rows(rms_forward(h2, norm_gains[2])[0].astype(BF))

    kv_heads = kv_w.shape[1] // 2 // head_dim
    qr = dot(n2, query_w).reshape(length, -1, head_dim)
    pair = dot(n2, kv_w).reshape(length, 2, kv_heads, head_dim)
    qn, qinv = rms_forward(qr, head_gains[0])
    kn, kinv = rms_forward(pair[:, 0], head_gains[1])
    q = rotate(qn, tables).astype(BF)
    k = rotate(kn, tables).astype(BF)
    v = pair[:, 1].astype(BF)
    groups = q.shape[1] // kv_heads
    scale = head_dim ** (-0.5)
    q4 = q.reshape(length, kv_heads, groups, head_dim)
    allowed = (places[None, :] <= places[:, None]) & (segment[None, :] == segment[:, None])
    scores = jnp.einsum("bkgd,skd->kgbs", q4, k, preferred_element_type=F32) * scale
    scores = jnp.where(allowed, scores, -1e30)
    top = jnp.max(scores, axis=-1, keepdims=True)
    weights = jnp.exp(scores - top)
    probs = weights / jnp.sum(weights, axis=-1, keepdims=True)
    probs_low = probs.astype(BF)
    o = jnp.einsum("kgbs,skd->bkgd", probs_low, v, preferred_element_type=F32)
    o = o.reshape(length, -1).astype(BF)
    h3 = h2 + scatter_rows(dot(o, out_w))
    n3 = gather_rows(rms_forward(h3, norm_gains[3])[0].astype(BF))
    hidden1, active1, part = ffn_local(n3, ws[1], vs[1])
    h4 = h3 + scatter_rows(part)
    output = swap(lax.all_to_all(h4.astype(BF), TP, 1, 0, tiled=True))

    def ffn_back(gathered, dh, h, normed, hidden, active, w, vv, gain):
        grad_active = dot(gathered, vv.T)
        grad_down = dot(active.T, gathered)
        half = hidden.shape[1] // 2
        gate, upp = hidden[:, :half], hidden[:, half:]
        s = jax.nn.sigmoid(gate)
        grad_hidden = jnp.concatenate(
            [grad_active * upp * s * (1.0 + gate * (1.0 - s)), grad_active * (gate * s)], axis=1
        ).astype(BF)
        grad_w = dot(normed.T, grad_hidden)
        dn = scatter_rows(dot(grad_hidden, w.T))
        inverse = rms_forward(h, gain)[1]
        term, grad_gain = rms_backward(dn, h, inverse, gain)
        return dh + term, grad_gain, grad_w, grad_down

    dh4 = my(up_full).astype(F32)
    dh3, gain3, gw1, gv1 = ffn_back(up_full, dh4, h3, n3, hidden1, active1, ws[1], vs[1], norm_gains[3])
    dz = gather_rows(dh3.astype(BF))
    grad_out_w = dot(o.T, dz)
    do = dot(dz, out_w.T).astype(BF).reshape(length, kv_heads, groups, head_dim)
    dp = jnp.einsum("bkgd,skd->kgbs", do, v, preferred_element_type=F32)
    inner = jnp.sum(probs * dp, axis=-1, keepdims=True)
    ds = (probs * (dp - inner)).astype(BF)
    dq = jnp.einsum("kgbs,skd->bkgd", ds, k, preferred_element_type=F32) * scale
    dk = jnp.einsum("kgbs,bkgd->skd", ds, q4, preferred_element_type=F32) * scale
    dv = jnp.einsum("kgbs,bkgd->skd", probs_low, do, preferred_element_type=F32)
    dq = dq.reshape(length, -1, head_dim)
    dqr, gq = rms_backward(rotate_back(dq, tables), qr, qinv, head_gains[0])
    dkr, gk = rms_backward(rotate_back(dk, tables), pair[:, 0], kinv, head_gains[1])
    dqr = dqr.astype(BF).reshape(length, -1)
    dpair = jnp.concatenate([dkr.reshape(length, -1), dv.reshape(length, -1)], axis=1).astype(BF)
    gqw = dot(n2.T, dqr)
    gkvw = dot(n2.T, dpair)
    dn2 = scatter_rows(dot(dqr, query_w.T) + dot(dpair, kv_w.T))
    term, gain2 = rms_backward(dn2, h2, rms_forward(h2, norm_gains[2])[1], norm_gains[2])
    dh2 = dh3 + term
    dh1, gain1, gw0, gv0 = ffn_back(
        gather_rows(dh2.astype(BF)), dh2, h1, n1, hidden0, active0, ws[0], vs[0], norm_gains[1]
    )
    dz = gather_rows(dh1.astype(BF))
    gco = dot(mixed.T, dz)
    dy = dot(dz, conv_out.T)
    width = conv_kernel.shape[1]
    gb, gc, gx = (projected[:, i * width : (i + 1) * width] for i in range(3))
    gated = gb * gx
    grad_c = dy * summed
    gs = dy * gc
    gg = conv_kernel[0] * gs
    kernel_rows = [jnp.sum(gs * gated, axis=0)]
    for offset in range(1, conv_kernel.shape[0]):
        masked = jnp.where(same[offset][:, None], gs, 0.0)
        gg = gg + conv_kernel[offset] * shift_up(masked, offset)
        kernel_rows.append(jnp.sum(masked * shift_down(gated, offset), axis=0))
    dprojected = jnp.concatenate([gg * gx, grad_c, gg * gb], axis=1).astype(BF)
    gci = dot(n0.T, dprojected)
    dn0 = scatter_rows(dot(dprojected, conv_in.T))
    term, gain0 = rms_backward(dn0, h0, rms_forward(h0, norm_gains[0])[1], norm_gains[0])
    dh0 = dh1 + term
    grad_tokens = swap(lax.all_to_all(dh0, TP, 1, 0, tiled=True))

    back = lambda g, axis: swap(scatter_dp(g, axis)).astype(F32)
    kernel_full = jnp.zeros((conv_kernel.shape[0], norm_gains.shape[1]), F32)
    kernel_full = lax.dynamic_update_slice_in_dim(
        kernel_full, jnp.stack(kernel_rows), quarter * width, 1
    )
    gains, heads, kernels = lax.psum(
        (jnp.stack([gain0, gain1, gain2, gain3]), jnp.stack([gq, gk]), kernel_full),
        ("r", "c", "zh", "zl"),
    )
    eighth = gate_up.shape[1]
    return (
        output,
        grad_tokens,
        gains,
        heads,
        back(gci, 0).reshape(-1, 3, width),
        kernels,
        back(gco, 1),
        back(gqw, 0),
        back(gkvw, 0).reshape(-1, 2, kv_heads * head_dim),
        back(grad_out_w, 1),
        jnp.stack([back(gw0, 0), back(gw1, 0)]).reshape(2, eighth, 2, -1),
        jnp.stack([back(gv0, 1), back(gv1, 1)]),
    )


def solution(mesh):
    devices = mesh.devices
    dp, tp = devices.shape
    inner = Mesh(devices.reshape(dp // 2, 2, 2, tp // 2), ("r", "c", "zh", "zl"))
    D = ("r", "c")
    T = ("zh", "zl")
    return jax.shard_map(
        local,
        mesh=inner,
        in_specs=(
            P(D, T), P(D, None), P(D, T), P(), P(), P(None, None, T), P(None, T), P(T, None),
            P(None, T), P(None, None, T), P(T, None), P(None, D, None, T), P(None, T, D),
        ),
        out_specs=(
            P(D, T), P(D, T), P(), P(), P(D, None, T), P(), P(T, D), P(D, T), P(D, None, T),
            P(T, D), P(None, D, None, T), P(None, T, D),
        ),
        check_vma=False,
    )
```

```python
import functools
import jax
import jax.numpy as jnp
from jax import lax
from jax.experimental import pallas as pl
from jax.experimental.pallas import tpu as pltpu
from jax.sharding import Mesh, PartitionSpec as P

epsilon = 1e-05
rope_base = 1000000.0
TP = ("c", "zl")
DP = ("r", "zh")
BF = jnp.bfloat16
F32 = jnp.float32
MESH = pl.DeviceIdType.MESH
DMA = pltpu.SemaphoreType.DMA
HBM = pl.BlockSpec(memory_space=pl.ANY)
INV = pl.BlockSpec(memory_space=pltpu.VMEM)
PARTS = 2
LANES = 128


class Group:
    def __init__(self):
        c, z = lax.axis_index("c"), lax.axis_index("zl")
        self.partner, self.twin = {"c": 1 - c}, {"zl": 1 - z}
        self.mine, self.beside = 2 * c + z, 2 * (1 - c) + z
        self.across, self.far = 2 * c + (1 - z), 2 * (1 - c) + (1 - z)
        self.barrier = pltpu.get_barrier_semaphore()

    def greet(self):
        for other in (self.partner, self.twin):
            pl.semaphore_signal(self.barrier, inc=1, device_id=other, device_id_type=MESH)

    def meet(self):
        pl.semaphore_wait(self.barrier, 2)


def at_rows(block, size, start, count):
    return pl.ds(pl.multiple_of(block * size + start, 16), count)


def send(src, dst, sems, index, where):
    return pltpu.make_async_remote_copy(
        src_ref=src, dst_ref=dst, send_sem=sems.at[0, index], recv_sem=sems.at[1, index],
        device_id=where, device_id_type=MESH,
    )


class Gather:
    def __init__(self, group, full, size, near, over, onward):
        self.g, self.full, self.size, self.parts = group, full, size, over.shape[1]
        self.near, self.over, self.onward = near, over, onward
        self.step = size // self.parts

    def view(self, block, part):
        return self.full.at[at_rows(block, self.size, part * self.step, self.step)]

    def link(self, part, block):
        v = self.view(block, part)
        return send(v, v, self.over, part, self.g.twin)

    def close(self, part, block):
        v = self.view(block, part)
        return send(v, v, self.near, part, self.g.partner)

    def pass_on(self, part, block):
        v = self.view(block, part)
        return send(v, v, self.onward, part, self.g.partner)

    def start(self):
        for p in range(self.parts):
            self.link(p, self.g.mine).start()
            self.close(p, self.g.mine).start()

    def wait_beside(self):
        for p in range(self.parts):
            self.close(p, self.g.beside).wait_recv()

    def wait_part(self, p):
        self.link(p, self.g.across).wait_recv()
        self.pass_on(p, self.g.across).start()

    def wait_far(self, p):
        self.pass_on(p, self.g.far).wait_recv()

    def finish(self):
        for p in range(self.parts):
            self.link(p, self.g.mine).wait_send()
            self.close(p, self.g.mine).wait_send()
            self.pass_on(p, self.g.across).wait_send()


class Scatter:
    def __init__(self, group, out_near, in_near, out_over, in_over, near, over, size):
        self.g, self.size, self.parts = group, size, over.shape[1]
        self.out_near, self.in_near, self.out_over, self.in_over = out_near, in_near, out_over, in_over
        self.near, self.over = near, over
        self.step = size // self.parts

    def rows(self, part):
        return pl.ds(part * self.step, self.step)

    def close(self, which, part):
        r = self.rows(part)
        return send(self.out_near.at[which, r], self.in_near.at[which, r], self.near, which * self.parts + part, self.g.partner)

    def link(self, part):
        r = self.rows(part)
        return send(self.out_over.at[r], self.in_over.at[r], self.over, part, self.g.twin)

    def wait_all_sends(self):
        for p in range(self.parts):
            self.close(0, p).wait_send()
            self.close(1, p).wait_send()
            self.link(p).wait_send()


def scatter_scratch(size, width, parts):
    return [
        pltpu.VMEM((2, size, width), BF), pltpu.VMEM((2, size, width), BF), pltpu.VMEM((size, width), BF),
        pltpu.VMEM((size, width), BF), DMA((2, 2 * parts)), DMA((2, parts)),
    ]


def gather_scratch(parts):
    return [DMA((2, parts)), DMA((2, parts)), DMA((2, parts))]


def normalise(h, gain):
    return h * lax.rsqrt(jnp.mean(h * h, axis=-1, keepdims=True) + epsilon) * gain


def mm(a, b):
    return jnp.dot(a, b, preferred_element_type=F32)


def mm_nt(a, b):
    return lax.dot_general(a, b, (((1,), (1,)), ((), ())), preferred_element_type=F32)


def lanes(start, width):
    return pl.ds(pl.multiple_of(start, LANES), width)


def ffn_forward_kernel(
    h_ref, gain_ref, w_hbm, v_hbm, out_ref, n_hbm, u_hbm,
    w, v, nf, u, act, tpart, mine, n_near, n_over, n_on, o_near, i_near, o_over, i_over, s_near, s_over,
    wsem, osem,
):
    g = Group()
    g.greet()
    size, width = h_ref.shape
    hidden = v.shape[0]
    load_w = pltpu.make_async_copy(w_hbm, w, wsem.at[0])
    load_v = pltpu.make_async_copy(v_hbm, v, wsem.at[1])
    load_w.start()
    load_v.start()
    gather = Gather(g, nf, size, n_near, n_over, n_on)
    scatter = Scatter(g, o_near, i_near, o_over, i_over, s_near, s_over, size)
    parts, step = gather.parts, gather.step
    for p in range(parts):
        nf[at_rows(g.mine, size, p * step, step), :] = normalise(
            h_ref[pl.ds(p * step, step), :], gain_ref[...]
        ).astype(BF)
    g.meet()
    gather.start()
    load_w.wait()
    load_v.wait()

    def rows_of(places):
        return jnp.concatenate([nf[r, :] for r, _ in places], axis=0) if len(places) > 1 else nf[places[0][0], :]

    def up(places):
        def body(t, carry):
            x = rows_of(places)
            wt = jnp.concatenate([w[:, lanes(t * LANES, LANES)], w[:, lanes(hidden + t * LANES, LANES)]], axis=1)
            both = mm(x, wt)
            gate, upper = both[:, :LANES], both[:, LANES:]
            a = gate * jax.nn.sigmoid(gate) * upper
            act[:, lanes(t * LANES, LANES)] = a.astype(BF)
            at = 0
            for r, count in places:
                u[r, lanes(t * LANES, LANES)] = gate[at : at + count].astype(BF)
                u[r, lanes(hidden + t * LANES, LANES)] = upper[at : at + count].astype(BF)
                at += count
            return carry

        lax.fori_loop(0, hidden // LANES, body, 0)

    def down(store):
        def body(t, carry):
            cols = lanes(t * 256, 256)
            store(cols, mm(act[...], v[:, cols]))
            return carry

        lax.fori_loop(0, width // 256, body, 0)

    def keep(index, r, count):
        return pltpu.make_async_copy(u.at[r], u_hbm.at[r], osem.at[index])

    whole = lambda block: at_rows(block, size, 0, size)
    up([(whole(g.mine), size)])
    keep(0, whole(g.mine), size).start()

    def put_mine(cols, value):
        mine[:, cols] = value

    down(put_mine)
    gather.wait_beside()
    up([(whole(g.beside), size)])
    keep(1, whole(g.beside), size).start()

    def put_beside(cols, value):
        o_near[1, :, cols] = value.astype(BF)

    down(put_beside)
    for p in range(parts):
        scatter.close(1, p).start()
    for p in range(parts):
        gather.wait_part(p)
        gather.wait_far(p)
        r_across, r_far = at_rows(g.across, size, p * step, step), at_rows(g.far, size, p * step, step)
        up([(r_across, step), (r_far, step)])
        keep(2 + 2 * p, r_across, step).start()
        keep(3 + 2 * p, r_far, step).start()
        here = scatter.rows(p)

        def put(cols, value):
            tpart[:, cols] = value[:step]
            o_near[0, here, cols] = value[step:].astype(BF)

        down(put)
        scatter.close(0, p).start()
        scatter.close(0, p).wait_recv()
        o_over[here, :] = (tpart[...] + i_near[0, here, :].astype(F32)).astype(BF)
        scatter.link(p).start()
    n_out = pltpu.make_async_copy(nf, n_hbm, osem.at[2 + 2 * parts])
    n_out.start()
    for p in range(parts):
        here = scatter.rows(p)
        scatter.close(1, p).wait_recv()
        scatter.link(p).wait_recv()
        out_ref[here, :] = (
            h_ref[here, :] + mine[here, :] + i_near[1, here, :].astype(F32) + i_over[here, :].astype(F32)
        )
    gather.finish()
    scatter.wait_all_sends()
    keep(0, whole(g.mine), size).wait()
    keep(1, whole(g.beside), size).wait()
    for p in range(parts):
        keep(2 + 2 * p, at_rows(g.across, size, p * step, step), step).wait()
        keep(3 + 2 * p, at_rows(g.far, size, p * step, step), step).wait()
    n_out.wait()


def ffn_forward(h, gain, w, v, ident, parts=PARTS):
    size, width = h.shape
    hidden = v.shape[0]
    total = 4 * size
    return pl.pallas_call(
        ffn_forward_kernel,
        out_shape=(
            jax.ShapeDtypeStruct((size, width), F32),
            jax.ShapeDtypeStruct((total, width), BF),
            jax.ShapeDtypeStruct((total, 2 * hidden), BF),
        ),
        in_specs=[INV, INV, HBM, HBM],
        out_specs=(INV, HBM, HBM),
        scratch_shapes=[
            pltpu.VMEM((width, 2 * hidden), BF), pltpu.VMEM((hidden, width), BF), pltpu.VMEM((total, width), BF),
            pltpu.VMEM((total, 2 * hidden), BF), pltpu.VMEM((size, hidden), BF),
            pltpu.VMEM((size // parts, width), F32), pltpu.VMEM((size, width), F32),
            *gather_scratch(parts), *scatter_scratch(size, width, parts), DMA((2,)), DMA((3 + 2 * parts,)),
        ],
        compiler_params=pltpu.CompilerParams(
            collective_id=ident, has_side_effects=True, vmem_limit_bytes=56 * 2**20
        ),
        cost_estimate=pl.CostEstimate(flops=2 * 3 * total * width * hidden, bytes_accessed=2 * 12 * 2**20, transcendentals=0),
        name="ffn_forward",
    )(h, gain, w, v)


def doc_layout(lengths_row, length):
    count = lengths_row.shape[0]
    upto = jnp.arange(count)[:, None] >= jnp.arange(count)[None, :]
    doc_ends = jnp.sum(jnp.where(upto, lengths_row[None, :], 0), axis=1)
    places = jnp.arange(length, dtype=jnp.int32)
    passed = places[:, None] >= doc_ends[None, :]
    segment = jnp.sum(passed.astype(jnp.int32), axis=1)
    doc_start = jnp.max(jnp.where(passed, doc_ends[None, :], 0), axis=1)
    return (segment, places - doc_start)


def rope_tables(position, head_dim):
    half_dim = head_dim // 2
    inverse = rope_base ** (-2.0 * jnp.arange(half_dim, dtype=F32) / head_dim)
    angles = position.astype(F32)[:, None] * inverse[None, :]
    return (jnp.cos(angles)[:, None, :], jnp.sin(angles)[:, None, :])


def rotate(values, tables):
    cosine, sine = tables
    half_dim = values.shape[-1] // 2
    first_half, second_half = (values[..., :half_dim], values[..., half_dim:])
    return jnp.concatenate(
        [first_half * cosine - second_half * sine, second_half * cosine + first_half * sine],
        axis=-1,
    )


def rotate_back(gradient, tables):
    cosine, sine = tables
    half_dim = gradient.shape[-1] // 2
    first_half, second_half = (gradient[..., :half_dim], gradient[..., half_dim:])
    return jnp.concatenate(
        [first_half * cosine + second_half * sine, second_half * cosine - first_half * sine],
        axis=-1,
    )


def shift_down(values, offset):
    filler = jnp.zeros((offset,) + values.shape[1:], values.dtype)
    return jnp.concatenate([filler, values[: values.shape[0] - offset]], axis=0)


def shift_up(values, offset):
    filler = jnp.zeros((offset,) + values.shape[1:], values.dtype)
    return jnp.concatenate([values[offset:], filler], axis=0)


def rms_forward(values, norm_gain):
    inverse = lax.rsqrt(jnp.mean(values * values, axis=-1, keepdims=True) + epsilon)
    return (values * inverse * norm_gain, inverse)


def rms_backward(upstream, values, inverse, norm_gain):
    scaled = upstream * norm_gain
    inner = jnp.mean(scaled * values, axis=-1, keepdims=True)
    grad_values = inverse * scaled - values * inverse**3 * inner
    leading = tuple(range(values.ndim - 1))
    grad_gain = jnp.sum(upstream * values * inverse, axis=leading)
    return (grad_values, grad_gain)


def dot(a, b):
    return jnp.dot(a, b, preferred_element_type=F32)


def swap(x):
    return lax.ppermute(x, ("c", "zh"), [(0, 0), (1, 2), (2, 1), (3, 3)])


def gather_rows(block):
    return lax.all_gather(block, TP, axis=0, tiled=True)


def scatter_rows(partial):
    return lax.psum_scatter(partial.astype(BF), TP, scatter_dimension=0, tiled=True).astype(F32)


def gather_dp(shard, axis):
    return lax.all_gather(shard, DP, axis=axis, tiled=True)


def scatter_dp(partial, axis):
    return lax.psum_scatter(partial.astype(BF), DP, scatter_dimension=axis, tiled=True)


def conv_local(normed, conv_in, conv_kernel, same):
    projected = dot(normed, conv_in)
    width = conv_kernel.shape[1]
    gated = projected[:, :width] * projected[:, 2 * width :]
    summed = conv_kernel[0] * gated
    for offset in range(1, conv_kernel.shape[0]):
        summed = summed + conv_kernel[offset] * jnp.where(
            same[offset][:, None], shift_down(gated, offset), 0.0
        )
    mixed = (projected[:, width : 2 * width] * summed).astype(BF)
    return projected, summed, mixed


def reactivate(hidden):
    hidden = hidden.astype(F32)
    half = hidden.shape[1] // 2
    return hidden, (jax.nn.silu(hidden[:, :half]) * hidden[:, half:]).astype(BF)


def local(
    tokens, doc_lengths, grad_out, norm_gains, head_gains, conv_in, conv_kernel, conv_out,
    query_w, kv_w, out_w, gate_up, down,
):
    length = tokens.shape[0]
    head_dim = head_gains.shape[1]
    quarter = lax.axis_index("c") * 2 + lax.axis_index("zl")
    group = 4
    rows = length // group
    segment, position = doc_layout(swap(doc_lengths)[0], length)
    places = jnp.arange(length, dtype=jnp.int32)
    same = [None] + [position >= j for j in range(1, conv_kernel.shape[0])]
    tables = rope_tables(position, head_dim)
    conv_in = swap(conv_in.reshape(conv_in.shape[0], -1))
    conv_kernel = swap(conv_kernel)
    conv_out = swap(conv_out)
    query_w = swap(query_w)
    kv_w = swap(kv_w.reshape(kv_w.shape[0], -1))
    out_w = swap(out_w)
    ws = [gather_dp(swap(gate_up[l].reshape(gate_up.shape[1], -1)), 0) for l in (0, 1)]
    vs = [gather_dp(swap(down[l]), 1) for l in (0, 1)]

    x_full = lax.all_gather(swap(tokens), TP, axis=1, tiled=True)
    up_full = lax.all_gather(swap(grad_out), TP, axis=1, tiled=True)
    my = lambda a: lax.dynamic_slice_in_dim(a, quarter * rows, rows, 0)
    n0 = rms_forward(x_full.astype(F32), norm_gains[0])[0].astype(BF)
    h0 = my(x_full).astype(F32)
    projected, summed, mixed = conv_local(n0, conv_in, conv_kernel, same)
    h1 = h0 + scatter_rows(dot(mixed, conv_out))
    h2, n1, hidden0 = ffn_forward(h1, norm_gains[1:2], ws[0], vs[0], 1)
    hidden0, active0 = reactivate(hidden0)
    n2 = gather_rows(rms_forward(h2, norm_gains[2])[0].astype(BF))

    kv_heads = kv_w.shape[1] // 2 // head_dim
    qr = dot(n2, query_w).reshape(length, -1, head_dim)
    pair = dot(n2, kv_w).reshape(length, 2, kv_heads, head_dim)
    qn, qinv = rms_forward(qr, head_gains[0])
    kn, kinv = rms_forward(pair[:, 0], head_gains[1])
    q = rotate(qn, tables).astype(BF)
    k = rotate(kn, tables).astype(BF)
    v = pair[:, 1].astype(BF)
    groups = q.shape[1] // kv_heads
    scale = head_dim ** (-0.5)
    q4 = q.reshape(length, kv_heads, groups, head_dim)
    allowed = (places[None, :] <= places[:, None]) & (segment[None, :] == segment[:, None])
    scores = jnp.einsum("bkgd,skd->kgbs", q4, k, preferred_element_type=F32) * scale
    scores = jnp.where(allowed, scores, -1e30)
    top = jnp.max(scores, axis=-1, keepdims=True)
    weights = jnp.exp(scores - top)
    probs = weights / jnp.sum(weights, axis=-1, keepdims=True)
    probs_low = probs.astype(BF)
    o = jnp.einsum("kgbs,skd->bkgd", probs_low, v, preferred_element_type=F32)
    o = o.reshape(length, -1).astype(BF)
    h3 = h2 + scatter_rows(dot(o, out_w))
    h4, n3, hidden1 = ffn_forward(h3, norm_gains[3:4], ws[1], vs[1], 2)
    hidden1, active1 = reactivate(hidden1)
    output = swap(lax.all_to_all(h4.astype(BF), TP, 1, 0, tiled=True))

    def ffn_back(gathered, dh, h, normed, hidden, active, w, vv, gain):
        grad_active = dot(gathered, vv.T)
        grad_down = dot(active.T, gathered)
        half = hidden.shape[1] // 2
        gate, upp = hidden[:, :half], hidden[:, half:]
        s = jax.nn.sigmoid(gate)
        grad_hidden = jnp.concatenate(
            [grad_active * upp * s * (1.0 + gate * (1.0 - s)), grad_active * (gate * s)], axis=1
        ).astype(BF)
        grad_w = dot(normed.T, grad_hidden)
        dn = scatter_rows(dot(grad_hidden, w.T))
        inverse = rms_forward(h, gain)[1]
        term, grad_gain = rms_backward(dn, h, inverse, gain)
        return dh + term, grad_gain, grad_w, grad_down

    dh4 = my(up_full).astype(F32)
    dh3, gain3, gw1, gv1 = ffn_back(up_full, dh4, h3, n3, hidden1, active1, ws[1], vs[1], norm_gains[3])
    dz = gather_rows(dh3.astype(BF))
    grad_out_w = dot(o.T, dz)
    do = dot(dz, out_w.T).astype(BF).reshape(length, kv_heads, groups, head_dim)
    dp = jnp.einsum("bkgd,skd->kgbs", do, v, preferred_element_type=F32)
    inner = jnp.sum(probs * dp, axis=-1, keepdims=True)
    ds = (probs * (dp - inner)).astype(BF)
    dq = jnp.einsum("kgbs,skd->bkgd", ds, k, preferred_element_type=F32) * scale
    dk = jnp.einsum("kgbs,bkgd->skd", ds, q4, preferred_element_type=F32) * scale
    dv = jnp.einsum("kgbs,bkgd->skd", probs_low, do, preferred_element_type=F32)
    dq = dq.reshape(length, -1, head_dim)
    dqr, gq = rms_backward(rotate_back(dq, tables), qr, qinv, head_gains[0])
    dkr, gk = rms_backward(rotate_back(dk, tables), pair[:, 0], kinv, head_gains[1])
    dqr = dqr.astype(BF).reshape(length, -1)
    dpair = jnp.concatenate([dkr.reshape(length, -1), dv.reshape(length, -1)], axis=1).astype(BF)
    gqw = dot(n2.T, dqr)
    gkvw = dot(n2.T, dpair)
    dn2 = scatter_rows(dot(dqr, query_w.T) + dot(dpair, kv_w.T))
    term, gain2 = rms_backward(dn2, h2, rms_forward(h2, norm_gains[2])[1], norm_gains[2])
    dh2 = dh3 + term
    dh1, gain1, gw0, gv0 = ffn_back(
        gather_rows(dh2.astype(BF)), dh2, h1, n1, hidden0, active0, ws[0], vs[0], norm_gains[1]
    )
    dz = gather_rows(dh1.astype(BF))
    gco = dot(mixed.T, dz)
    dy = dot(dz, conv_out.T)
    width = conv_kernel.shape[1]
    gb, gc, gx = (projected[:, i * width : (i + 1) * width] for i in range(3))
    gated = gb * gx
    grad_c = dy * summed
    gs = dy * gc
    gg = conv_kernel[0] * gs
    kernel_rows = [jnp.sum(gs * gated, axis=0)]
    for offset in range(1, conv_kernel.shape[0]):
        masked = jnp.where(same[offset][:, None], gs, 0.0)
        gg = gg + conv_kernel[offset] * shift_up(masked, offset)
        kernel_rows.append(jnp.sum(masked * shift_down(gated, offset), axis=0))
    dprojected = jnp.concatenate([gg * gx, grad_c, gg * gb], axis=1).astype(BF)
    gci = dot(n0.T, dprojected)
    dn0 = scatter_rows(dot(dprojected, conv_in.T))
    term, gain0 = rms_backward(dn0, h0, rms_forward(h0, norm_gains[0])[1], norm_gains[0])
    dh0 = dh1 + term
    grad_tokens = swap(lax.all_to_all(dh0, TP, 1, 0, tiled=True))

    back = lambda g, axis: swap(scatter_dp(g, axis)).astype(F32)
    kernel_full = jnp.zeros((conv_kernel.shape[0], norm_gains.shape[1]), F32)
    kernel_full = lax.dynamic_update_slice_in_dim(
        kernel_full, jnp.stack(kernel_rows), quarter * width, 1
    )
    gains, heads, kernels = lax.psum(
        (jnp.stack([gain0, gain1, gain2, gain3]), jnp.stack([gq, gk]), kernel_full),
        ("r", "c", "zh", "zl"),
    )
    eighth = gate_up.shape[1]
    return (
        output,
        grad_tokens,
        gains,
        heads,
        back(gci, 0).reshape(-1, 3, width),
        kernels,
        back(gco, 1),
        back(gqw, 0),
        back(gkvw, 0).reshape(-1, 2, kv_heads * head_dim),
        back(grad_out_w, 1),
        jnp.stack([back(gw0, 0), back(gw1, 0)]).reshape(2, eighth, 2, -1),
        jnp.stack([back(gv0, 1), back(gv1, 1)]),
    )


def solution(mesh):
    devices = mesh.devices
    dp, tp = devices.shape
    inner = Mesh(devices.reshape(dp // 2, 2, 2, tp // 2), ("r", "c", "zh", "zl"))
    D = ("r", "c")
    T = ("zh", "zl")
    return jax.shard_map(
        local,
        mesh=inner,
        in_specs=(
            P(D, T), P(D, None), P(D, T), P(), P(), P(None, None, T), P(None, T), P(T, None),
            P(None, T), P(None, None, T), P(T, None), P(None, D, None, T), P(None, T, D),
        ),
        out_specs=(
            P(D, T), P(D, T), P(), P(), P(D, None, T), P(), P(T, D), P(D, T), P(D, None, T),
            P(T, D), P(None, D, None, T), P(None, T, D),
        ),
        check_vma=False,
    )
```

```python
import functools
import jax
import jax.numpy as jnp
from jax import lax
from jax.experimental import pallas as pl
from jax.experimental.pallas import tpu as pltpu
from jax.sharding import Mesh, PartitionSpec as P

epsilon = 1e-05
BF = jnp.bfloat16
F32 = jnp.float32
MESH = pl.DeviceIdType.MESH
DMA = pltpu.SemaphoreType.DMA
HBM = pl.BlockSpec(memory_space=pl.ANY)
INV = pl.BlockSpec(memory_space=pltpu.VMEM)
PARTS = 2
LANES = 128


class Group:
    def __init__(self):
        c, z = lax.axis_index("c"), lax.axis_index("zl")
        self.partner, self.twin = {"c": 1 - c}, {"zl": 1 - z}
        self.mine, self.beside = 2 * c + z, 2 * (1 - c) + z
        self.across, self.far = 2 * c + (1 - z), 2 * (1 - c) + (1 - z)
        self.barrier = pltpu.get_barrier_semaphore()

    def greet(self):
        for other in (self.partner, self.twin):
            pl.semaphore_signal(self.barrier, inc=1, device_id=other, device_id_type=MESH)

    def meet(self):
        pl.semaphore_wait(self.barrier, 2)


def at_rows(block, size, start, count):
    return pl.ds(pl.multiple_of(block * size + start, 16), count)


def send(src, dst, sems, index, where):
    return pltpu.make_async_remote_copy(
        src_ref=src, dst_ref=dst, send_sem=sems.at[0, index], recv_sem=sems.at[1, index],
        device_id=where, device_id_type=MESH,
    )


class Gather:
    def __init__(self, group, full, size, near, over, onward):
        self.g, self.full, self.size, self.parts = group, full, size, over.shape[1]
        self.near, self.over, self.onward = near, over, onward
        self.step = size // self.parts

    def view(self, block, part):
        return self.full.at[at_rows(block, self.size, part * self.step, self.step)]

    def link(self, part, block):
        v = self.view(block, part)
        return send(v, v, self.over, part, self.g.twin)

    def close(self, part, block):
        v = self.view(block, part)
        return send(v, v, self.near, part, self.g.partner)

    def pass_on(self, part, block):
        v = self.view(block, part)
        return send(v, v, self.onward, part, self.g.partner)

    def start(self):
        for p in range(self.parts):
            self.link(p, self.g.mine).start()
            self.close(p, self.g.mine).start()

    def wait_beside(self):
        for p in range(self.parts):
            self.close(p, self.g.beside).wait_recv()

    def wait_part(self, p):
        self.link(p, self.g.across).wait_recv()
        self.pass_on(p, self.g.across).start()

    def wait_far(self, p):
        self.pass_on(p, self.g.far).wait_recv()

    def finish(self):
        for p in range(self.parts):
            self.link(p, self.g.mine).wait_send()
            self.close(p, self.g.mine).wait_send()
            self.pass_on(p, self.g.across).wait_send()


class Scatter:
    def __init__(self, group, out_near, in_near, out_over, in_over, near, over, size):
        self.g, self.size, self.parts = group, size, over.shape[1]
        self.out_near, self.in_near, self.out_over, self.in_over = out_near, in_near, out_over, in_over
        self.near, self.over = near, over
        self.step = size // self.parts

    def rows(self, part):
        return pl.ds(part * self.step, self.step)

    def close(self, which, part):
        r = self.rows(part)
        return send(self.out_near.at[which, r], self.in_near.at[which, r], self.near, which * self.parts + part, self.g.partner)

    def link(self, part):
        r = self.rows(part)
        return send(self.out_over.at[r], self.in_over.at[r], self.over, part, self.g.twin)

    def wait_all_sends(self):
        for p in range(self.parts):
            self.close(0, p).wait_send()
            self.close(1, p).wait_send()
            self.link(p).wait_send()


def scatter_scratch(size, width, parts):
    return [
        pltpu.VMEM((2, size, width), BF), pltpu.VMEM((2, size, width), BF), pltpu.VMEM((size, width), BF),
        pltpu.VMEM((size, width), BF), DMA((2, 2 * parts)), DMA((2, parts)),
    ]


def gather_scratch(parts):
    return [DMA((2, parts)), DMA((2, parts)), DMA((2, parts))]


def normalise(h, gain):
    return h * lax.rsqrt(jnp.mean(h * h, axis=-1, keepdims=True) + epsilon) * gain


def mm(a, b):
    return jnp.dot(a, b, preferred_element_type=F32)


def mm_nt(a, b):
    return lax.dot_general(a, b, (((1,), (1,)), ((), ())), preferred_element_type=F32)


def lanes(start, width):
    return pl.ds(pl.multiple_of(start, LANES), width)


def ffn_forward_kernel(
    h_ref, gain_ref, w_hbm, v_hbm, out_ref, n_hbm, u_hbm,
    w, v, nf, u, act, tpart, mine, n_near, n_over, n_on, o_near, i_near, o_over, i_over, s_near, s_over,
    wsem, osem,
):
    g = Group()
    g.greet()
    size, width = h_ref.shape
    hidden = v.shape[0]
    load_w = pltpu.make_async_copy(w_hbm, w, wsem.at[0])
    load_v = pltpu.make_async_copy(v_hbm, v, wsem.at[1])
    load_w.start()
    load_v.start()
    gather = Gather(g, nf, size, n_near, n_over, n_on)
    scatter = Scatter(g, o_near, i_near, o_over, i_over, s_near, s_over, size)
    parts, step = gather.parts, gather.step
    for p in range(parts):
        nf[at_rows(g.mine, size, p * step, step), :] = normalise(
            h_ref[pl.ds(p * step, step), :], gain_ref[...]
        ).astype(BF)
    g.meet()
    gather.start()
    load_w.wait()
    load_v.wait()

    def rows_of(places):
        return jnp.concatenate([nf[r, :] for r, _ in places], axis=0) if len(places) > 1 else nf[places[0][0], :]

    def up(places):
        def body(t, carry):
            x = rows_of(places)
            wt = jnp.concatenate([w[:, lanes(t * LANES, LANES)], w[:, lanes(hidden + t * LANES, LANES)]], axis=1)
            both = mm(x, wt)
            gate, upper = both[:, :LANES], both[:, LANES:]
            a = gate * jax.nn.sigmoid(gate) * upper
            act[:, lanes(t * LANES, LANES)] = a.astype(BF)
            at = 0
            for r, count in places:
                u[r, lanes(t * LANES, LANES)] = gate[at : at + count].astype(BF)
                u[r, lanes(hidden + t * LANES, LANES)] = upper[at : at + count].astype(BF)
                at += count
            return carry

        lax.fori_loop(0, hidden // LANES, body, 0)

    def down(store):
        def body(t, carry):
            cols = lanes(t * 256, 256)
            store(cols, mm(act[...], v[:, cols]))
            return carry

        lax.fori_loop(0, width // 256, body, 0)

    def keep(index, r, count):
        return pltpu.make_async_copy(u.at[r], u_hbm.at[r], osem.at[index])

    whole = lambda block: at_rows(block, size, 0, size)
    up([(whole(g.mine), size)])
    keep(0, whole(g.mine), size).start()

    def put_mine(cols, value):
        mine[:, cols] = value

    down(put_mine)
    gather.wait_beside()
    up([(whole(g.beside), size)])
    keep(1, whole(g.beside), size).start()

    def put_beside(cols, value):
        o_near[1, :, cols] = value.astype(BF)

    down(put_beside)
    for p in range(parts):
        scatter.close(1, p).start()
    for p in range(parts):
        gather.wait_part(p)
        gather.wait_far(p)
        r_across, r_far = at_rows(g.across, size, p * step, step), at_rows(g.far, size, p * step, step)
        up([(r_across, step), (r_far, step)])
        keep(2 + 2 * p, r_across, step).start()
        keep(3 + 2 * p, r_far, step).start()
        here = scatter.rows(p)

        def put(cols, value):
            tpart[:, cols] = value[:step]
            o_near[0, here, cols] = value[step:].astype(BF)

        down(put)
        scatter.close(0, p).start()
        scatter.close(0, p).wait_recv()
        o_over[here, :] = (tpart[...] + i_near[0, here, :].astype(F32)).astype(BF)
        scatter.link(p).start()
    n_out = pltpu.make_async_copy(nf, n_hbm, osem.at[2 + 2 * parts])
    n_out.start()
    for p in range(parts):
        here = scatter.rows(p)
        scatter.close(1, p).wait_recv()
        scatter.link(p).wait_recv()
        out_ref[here, :] = (
            h_ref[here, :] + mine[here, :] + i_near[1, here, :].astype(F32) + i_over[here, :].astype(F32)
        )
    gather.finish()
    scatter.wait_all_sends()
    keep(0, whole(g.mine), size).wait()
    keep(1, whole(g.beside), size).wait()
    for p in range(parts):
        keep(2 + 2 * p, at_rows(g.across, size, p * step, step), step).wait()
        keep(3 + 2 * p, at_rows(g.far, size, p * step, step), step).wait()
    n_out.wait()


def ffn_forward(h, gain, w, v, ident, parts=PARTS):
    size, width = h.shape
    hidden = v.shape[0]
    total = 4 * size
    return pl.pallas_call(
        ffn_forward_kernel,
        out_shape=(
            jax.ShapeDtypeStruct((size, width), F32),
            jax.ShapeDtypeStruct((total, width), BF),
            jax.ShapeDtypeStruct((total, 2 * hidden), BF),
        ),
        in_specs=[INV, INV, HBM, HBM],
        out_specs=(INV, HBM, HBM),
        scratch_shapes=[
            pltpu.VMEM((width, 2 * hidden), BF), pltpu.VMEM((hidden, width), BF), pltpu.VMEM((total, width), BF),
            pltpu.VMEM((total, 2 * hidden), BF), pltpu.VMEM((size, hidden), BF),
            pltpu.VMEM((size // parts, width), F32), pltpu.VMEM((size, width), F32),
            *gather_scratch(parts), *scatter_scratch(size, width, parts), DMA((2,)), DMA((3 + 2 * parts,)),
        ],
        compiler_params=pltpu.CompilerParams(
            collective_id=ident, has_side_effects=True, vmem_limit_bytes=56 * 2**20
        ),
        cost_estimate=pl.CostEstimate(flops=2 * 3 * total * width * hidden, bytes_accessed=2 * 12 * 2**20, transcendentals=0),
        name="ffn_forward",
    )(h, gain, w, v)

def mm_tn(a, b):
    return lax.dot_general(a, b, (((0,), (0,)), ((), ())), preferred_element_type=F32)


def rms_back(dn, h, gain):
    inverse = lax.rsqrt(jnp.mean(h * h, axis=-1, keepdims=True) + epsilon)
    scaled = dn * gain
    inner = jnp.mean(scaled * h, axis=-1, keepdims=True)
    grad_gain = jnp.sum(dn * h * inverse, axis=0, keepdims=True)
    return inverse * scaled - h * (inverse * inverse * inverse * inner), grad_gain


def close_scatter(scatter, mine, dh_ref, h_ref, gain_ref, out_ref, gg_ref):
    gg_ref[...] = jnp.zeros_like(gg_ref)
    for p in range(scatter.parts):
        here = scatter.rows(p)
        scatter.close(1, p).wait_recv()
        scatter.link(p).wait_recv()
        dn = mine[here, :] + scatter.in_near[1, here, :].astype(F32) + scatter.in_over[here, :].astype(F32)
        term, grad_gain = rms_back(dn, h_ref[here, :], gain_ref[...])
        out_ref[here, :] = dh_ref[here, :] + term
        gg_ref[...] += grad_gain


def ffn_backward_kernel(
    known, dh_ref, h_ref, gain_ref, df_hbm, w_hbm, v_hbm, n_hbm, u_hbm, out_ref, gg_ref, gw_hbm, gv_hbm,
    w, v, nf, u, act, df, tpart, mine, gtile, n_near, n_over, n_on, o_near, i_near, o_over, i_over, s_near, s_over,
    wsem, osem,
):
    g = Group()
    g.greet()
    size, width = dh_ref.shape
    hidden = v.shape[0]
    loads = [
        pltpu.make_async_copy(src, dst, wsem.at[i])
        for i, (src, dst) in enumerate([(v_hbm, v), (u_hbm, u), (w_hbm, w), (n_hbm, nf)])
    ]
    if known:
        loads.append(pltpu.make_async_copy(df_hbm, df, wsem.at[4]))
    for load in loads:
        load.start()
    gather = Gather(g, df, size, n_near, n_over, n_on)
    scatter = Scatter(g, o_near, i_near, o_over, i_over, s_near, s_over, size)
    parts, step = gather.parts, gather.step
    if not known:
        df[at_rows(g.mine, size, 0, size), :] = dh_ref[...].astype(BF)
    g.meet()
    if not known:
        gather.start()
    for load in loads:
        load.wait()

    third = hidden // 3

    def cat(ref, places, cols):
        found = [ref[r, cols] for r, _ in places]
        return found[0] if len(found) == 1 else jnp.concatenate(found, axis=0)

    def first(places):
        def body(t, carry):
            cols, more = lanes(t * third, third), lanes(hidden + t * third, third)
            da = mm_nt(cat(df, places, slice(None)), v[cols, :])
            gate, upper = cat(u, places, cols).astype(F32), cat(u, places, more).astype(F32)
            s = jax.nn.sigmoid(gate)
            lit = gate * s
            dgate = (da * upper * s * (1.0 + gate * (1.0 - s))).astype(BF)
            dupper = (da * lit).astype(BF)
            a = (lit * upper).astype(BF)
            at = 0
            for r, count in places:
                u[r, cols] = dgate[at : at + count]
                u[r, more] = dupper[at : at + count]
                act[r, cols] = a[at : at + count]
                at += count
            return carry

        lax.fori_loop(0, 3, body, 0)

    def second(places, store):
        def body(t, carry):
            cols = lanes(t * 256, 256)
            store(cols, mm_nt(cat(u, places, slice(None)), w[cols, :]))
            return carry

        lax.fori_loop(0, width // 256, body, 0)

    whole = lambda block: [(at_rows(block, size, 0, size), size)]

    def put_mine(cols, value):
        mine[:, cols] = value

    def put_beside(cols, value):
        o_near[1, :, cols] = value.astype(BF)

    def own():
        first(whole(g.mine))
        second(whole(g.mine), put_mine)

    def beside():
        first(whole(g.beside))
        second(whole(g.beside), put_beside)
        for p in range(parts):
            scatter.close(1, p).start()

    if not known:
        own()
        gather.wait_beside()
        beside()
    for p in range(parts):
        if not known:
            gather.wait_part(p)
            gather.wait_far(p)
        pair = [(at_rows(b, size, p * step, step), step) for b in (g.across, g.far)]
        first(pair)
        here = scatter.rows(p)

        def put(cols, value):
            tpart[:, cols] = value[:step]
            o_near[0, here, cols] = value[step:].astype(BF)

        second(pair, put)
        scatter.close(0, p).start()
        scatter.close(0, p).wait_recv()
        o_over[here, :] = (tpart[...] + i_near[0, here, :].astype(F32)).astype(BF)
        scatter.link(p).start()
    if known:
        beside()
        own()
    flush = []
    count = 0

    def emit(value, dst):
        nonlocal count
        slot = count % 2
        if count >= 2:
            flush[count - 2].wait()
        gtile[slot, :, : value.shape[1]] = value.astype(BF)
        copy = pltpu.make_async_copy(gtile.at[slot, :, : value.shape[1]], dst, osem.at[slot])
        copy.start()
        flush.append(copy)
        count += 1

    tall = gtile.shape[1]
    for t in range(hidden // tall):
        emit(mm_tn(act[:, t * tall : (t + 1) * tall], df[...]), gv_hbm.at[pl.ds(t * tall, tall), :])
    for t in range(width // tall):
        for k in range(2):
            cols = slice(k * hidden, (k + 1) * hidden)
            emit(mm_tn(nf[:, t * tall : (t + 1) * tall], u[:, cols]), gw_hbm.at[pl.ds(t * tall, tall), cols])
    close_scatter(scatter, mine, dh_ref, h_ref, gain_ref, out_ref, gg_ref)
    if not known:
        gather.finish()
    scatter.wait_all_sends()
    for copy in flush[-2:]:
        copy.wait()


def ffn_backward(dh, h, gain, df, w, v, n, u, ident, parts=PARTS):
    size, width = h.shape
    hidden = v.shape[0]
    total = 4 * size
    known = df is not None
    if not known:
        df = n
    return pl.pallas_call(
        functools.partial(ffn_backward_kernel, known),
        out_shape=(
            jax.ShapeDtypeStruct((size, width), F32),
            jax.ShapeDtypeStruct((1, width), F32),
            jax.ShapeDtypeStruct((width, 2 * hidden), BF),
            jax.ShapeDtypeStruct((hidden, width), BF),
        ),
        in_specs=[INV, INV, INV, HBM, HBM, HBM, HBM, HBM],
        out_specs=(INV, INV, HBM, HBM),
        scratch_shapes=[
            pltpu.VMEM((width, 2 * hidden), BF), pltpu.VMEM((hidden, width), BF), pltpu.VMEM((total, width), BF),
            pltpu.VMEM((total, 2 * hidden), BF), pltpu.VMEM((total, hidden), BF), pltpu.VMEM((total, width), BF),
            pltpu.VMEM((size // parts, width), F32), pltpu.VMEM((size, width), F32),
            pltpu.VMEM((2, 128, hidden), BF),
            *gather_scratch(parts), *scatter_scratch(size, width, parts), DMA((5,)), DMA((2,)),
        ],
        compiler_params=pltpu.CompilerParams(
            collective_id=ident, has_side_effects=True, vmem_limit_bytes=56 * 2**20
        ),
        cost_estimate=pl.CostEstimate(flops=4 * 3 * total * width * hidden, bytes_accessed=2 * 20 * 2**20, transcendentals=0),
        name="ffn_backward",
    )(dh, h, gain, df, w, v, n, u)

MOST_DOC = 512


class Columns(Gather):
    def __init__(self, group, full, near, over, onward):
        super().__init__(group, full, full.shape[0], near, over, onward)
        self.cols = full.shape[1] // 4

    def view(self, block, part):
        return self.full.at[pl.ds(part * self.step, self.step), lanes(block * self.cols, self.cols)]


def cat_rows(ref, places, cols=slice(None)):
    found = [ref[r, cols] for r, _ in places]
    return found[0] if len(found) == 1 else jnp.concatenate(found, axis=0)


def product(src, weight, turned, tile=256):
    def run(places, store):
        width = weight.shape[0] if turned else weight.shape[1]

        def body(t, carry):
            cols = lanes(t * tile, tile)
            x = cat_rows(src, places)
            store(cols, mm_nt(x, weight[cols, :]) if turned else mm(x, weight[:, cols]))
            return carry

        lax.fori_loop(0, width // tile, body, 0)

    return run


def scatter_all(g, scatter, run, mine, tpart):
    size, step = scatter.size, scatter.step
    for p in range(scatter.parts):
        here = scatter.rows(p)

        def put(cols, value):
            tpart[:, cols] = value[:step]
            scatter.out_near[0, here, cols] = value[step:].astype(BF)

        run([(at_rows(b, size, p * step, step), step) for b in (g.across, g.far)], put)
        scatter.close(0, p).start()
        scatter.close(0, p).wait_recv()
        scatter.out_over[here, :] = (tpart[...] + scatter.in_near[0, here, :].astype(F32)).astype(BF)
        scatter.link(p).start()

    def put_beside(cols, value):
        scatter.out_near[1, :, cols] = value.astype(BF)

    run([(at_rows(g.beside, size, 0, size), size)], put_beside)
    for p in range(scatter.parts):
        scatter.close(1, p).start()

    def put_mine(cols, value):
        mine[:, cols] = value

    run([(at_rows(g.mine, size, 0, size), size)], put_mine)


def gather_everything(gather):
    gather.wait_beside()
    for p in range(gather.parts):
        gather.wait_part(p)
    for p in range(gather.parts):
        gather.wait_far(p)


def doc_starts(lengths, places):
    end = jnp.int32(0)
    start = jnp.zeros_like(places)
    for d in range(lengths.shape[1]):
        end = end + lengths[0, d]
        start = jnp.where(places >= end, end, start)
    return start


def start_all(pairs, sems):
    copies = [pltpu.make_async_copy(src, dst, sems.at[i]) for i, (src, dst) in enumerate(pairs)]
    for copy in copies:
        copy.start()
    return copies


def wait_all(copies):
    for copy in copies:
        copy.wait()


def params(ident):
    return pltpu.CompilerParams(collective_id=ident, has_side_effects=True, vmem_limit_bytes=56 * 2**20)


def shaped(shape, dtype):
    return jax.ShapeDtypeStruct(shape, dtype)


SCALARS = pl.BlockSpec(memory_space=pltpu.SMEM)


def conv_taps(gated, within, taps):
    total = gated.shape[0]
    summed = taps[0] * gated
    for j in range(1, len(taps)):
        summed = summed + taps[j] * jnp.where(within >= j, pltpu.roll(gated, j, 0), 0.0)
    return summed


def conv_forward_kernel(
    lengths, x_ref, gain_ref, taps_ref, win_hbm, wout_hbm, out_ref, block_ref, n_hbm, p_hbm,
    win, wout, full, nf, proj, low, mixed, tpart, mine, n_near, n_over, n_on, o_near, i_near, o_over, i_over,
    s_near, s_over, wsem, osem,
):
    g = Group()
    g.greet()
    size, width = out_ref.shape
    total, chans = x_ref.shape[0], wout.shape[0]
    loads = start_all([(win_hbm, win), (wout_hbm, wout)], wsem)
    gather = Columns(g, full, n_near, n_over, n_on)
    scatter = Scatter(g, o_near, i_near, o_over, i_over, s_near, s_over, size)
    full[:, lanes(g.mine * chans, chans)] = x_ref[...]
    g.meet()
    gather.start()
    gather_everything(gather)
    wait_all(loads)

    def project(t, carry):
        rows = at_rows(t, size, 0, size)
        n = normalise(full[rows, :].astype(F32), gain_ref[...]).astype(BF)
        nf[rows, :] = n
        p = mm(n, win[...])
        proj[rows, :] = p
        low[rows, :] = p.astype(BF)
        return carry

    lax.fori_loop(0, total // size, project, 0)
    saves = start_all([(nf, n_hbm), (low, p_hbm)], osem)
    places = lax.broadcasted_iota(jnp.int32, (total, LANES), 0)
    within = places - doc_starts(lengths, places)
    for k in range(chans // LANES):
        b, c, x = (proj[:, pl.ds(i * chans + k * LANES, LANES)] for i in range(3))
        taps = [taps_ref[pl.ds(j, 1), pl.ds(k * LANES, LANES)] for j in range(taps_ref.shape[0])]
        mixed[:, pl.ds(k * LANES, LANES)] = (c * conv_taps(b * x, within, taps)).astype(BF)
    scatter_all(g, scatter, product(mixed, wout, False), mine, tpart)
    own = full[at_rows(g.mine, size, 0, size), :]
    block_ref[...] = own
    for p in range(scatter.parts):
        here = scatter.rows(p)
        scatter.close(1, p).wait_recv()
        scatter.link(p).wait_recv()
        out_ref[here, :] = (
            block_ref[here, :].astype(F32) + mine[here, :] + i_near[1, here, :].astype(F32) + i_over[here, :].astype(F32)
        )
    gather.finish()
    scatter.wait_all_sends()
    wait_all(saves)


def conv_forward(lengths, x, gain, taps, win, wout, ident, parts=PARTS):
    total, chans = x.shape
    width = wout.shape[1]
    size = total // 4
    return pl.pallas_call(
        conv_forward_kernel,
        out_shape=(
            shaped((size, width), F32), shaped((size, width), BF), shaped((total, width), BF), shaped((total, 3 * chans), BF),
        ),
        in_specs=[SCALARS, INV, INV, INV, HBM, HBM],
        out_specs=(INV, INV, HBM, HBM),
        scratch_shapes=[
            pltpu.VMEM((width, 3 * chans), BF), pltpu.VMEM((chans, width), BF), pltpu.VMEM((total, width), BF),
            pltpu.VMEM((total, width), BF), pltpu.VMEM((total, 3 * chans), F32), pltpu.VMEM((total, 3 * chans), BF),
            pltpu.VMEM((total, chans), BF), pltpu.VMEM((size // parts, width), F32), pltpu.VMEM((size, width), F32),
            *gather_scratch(parts), *scatter_scratch(size, width, parts), DMA((2,)), DMA((2,)),
        ],
        compiler_params=params(ident),
        cost_estimate=pl.CostEstimate(flops=2 * 4 * total * width * chans, bytes_accessed=2 * 8 * 2**20, transcendentals=0),
        name="conv_forward",
    )(lengths, x, gain, taps, win, wout)


def conv_backward_kernel(
    lengths, dh_ref, h_ref, gain_ref, taps_ref, win_hbm, wout_hbm, n_hbm, p_hbm, out_ref, gg_ref, gt_ref, gin_hbm, gout_hbm,
    win, wout, nf, low, dz, dy, mixed, dproj, gin, gout, tpart, mine, n_near, n_over, n_on, o_near, i_near, o_over, i_over,
    s_near, s_over, wsem, osem,
):
    g = Group()
    g.greet()
    size, width = dh_ref.shape
    total, chans = 4 * size, wout.shape[0]
    loads = start_all([(wout_hbm, wout), (p_hbm, low), (win_hbm, win), (n_hbm, nf)], wsem)
    gather = Gather(g, dz, size, n_near, n_over, n_on)
    scatter = Scatter(g, o_near, i_near, o_over, i_over, s_near, s_over, size)
    dz[at_rows(g.mine, size, 0, size), :] = dh_ref[...].astype(BF)
    g.meet()
    gather.start()
    wait_all(loads)
    places = lax.broadcasted_iota(jnp.int32, (total, LANES), 0)
    within = places - doc_starts(lengths, places)
    gather_everything(gather)

    def project(t, carry):
        rows = at_rows(t, size, 0, size)
        dy[rows, :] = mm_nt(dz[rows, :], wout[...])
        return carry

    lax.fori_loop(0, total // size, project, 0)
    for k in range(chans // LANES):
        b, c, x = (low[:, pl.ds(i * chans + k * LANES, LANES)].astype(F32) for i in range(3))
        here = pl.ds(k * LANES, LANES)
        taps = [taps_ref[pl.ds(j, 1), here] for j in range(taps_ref.shape[0])]
        gated = b * x
        summed = conv_taps(gated, within, taps)
        d = dy[:, here]
        mixed[:, here] = (c * summed).astype(BF)
        ds = d * c
        dg = taps[0] * ds
        gt_ref[pl.ds(0, 1), here] = jnp.sum(ds * gated, axis=0, keepdims=True)
        for j in range(1, len(taps)):
            masked = jnp.where(within >= j, ds, 0.0)
            dg = dg + taps[j] * pltpu.roll(masked, total - j, 0)
            gt_ref[pl.ds(j, 1), here] = jnp.sum(masked * pltpu.roll(gated, j, 0), axis=0, keepdims=True)
        dproj[:, pl.ds(k * LANES, LANES)] = (dg * x).astype(BF)
        dproj[:, pl.ds(chans + k * LANES, LANES)] = (d * summed).astype(BF)
        dproj[:, pl.ds(2 * chans + k * LANES, LANES)] = (dg * b).astype(BF)
    scatter_all(g, scatter, product(dproj, win, True), mine, tpart)
    gout[...] = mm_tn(mixed[...], dz[...]).astype(BF)
    save = pltpu.make_async_copy(gout, gout_hbm, osem.at[0])
    save.start()
    for t in range(width // 256):
        gin[pl.ds(t * 256, 256), :] = mm_tn(nf[:, pl.ds(t * 256, 256)], dproj[...]).astype(BF)
    more = pltpu.make_async_copy(gin, gin_hbm, osem.at[1])
    more.start()
    close_scatter(scatter, mine, dh_ref, h_ref, gain_ref, out_ref, gg_ref)
    gather.finish()
    scatter.wait_all_sends()
    save.wait()
    more.wait()


def conv_backward(lengths, dh, h, gain, taps, win, wout, n, p, ident, parts=PARTS):
    size, width = dh.shape
    total, chans = 4 * size, wout.shape[0]
    return pl.pallas_call(
        conv_backward_kernel,
        out_shape=(
            shaped((size, width), F32), shaped((1, width), F32), shaped(taps.shape, F32), shaped((width, 3 * chans), BF),
            shaped((chans, width), BF),
        ),
        in_specs=[SCALARS, INV, INV, INV, INV, HBM, HBM, HBM, HBM],
        out_specs=(INV, INV, INV, HBM, HBM),
        scratch_shapes=[
            pltpu.VMEM((width, 3 * chans), BF), pltpu.VMEM((chans, width), BF), pltpu.VMEM((total, width), BF),
            pltpu.VMEM((total, 3 * chans), BF), pltpu.VMEM((total, width), BF), pltpu.VMEM((total, chans), F32),
            pltpu.VMEM((total, chans), BF), pltpu.VMEM((total, 3 * chans), BF), pltpu.VMEM((width, 3 * chans), BF),
            pltpu.VMEM((chans, width), BF), pltpu.VMEM((size // parts, width), F32), pltpu.VMEM((size, width), F32),
            *gather_scratch(parts), *scatter_scratch(size, width, parts), DMA((4,)), DMA((2,)),
        ],
        compiler_params=params(ident),
        cost_estimate=pl.CostEstimate(flops=2 * 8 * total * width * chans, bytes_accessed=2 * 12 * 2**20, transcendentals=0),
        name="conv_backward",
    )(lengths, dh, h, gain, taps, win, wout, n, p)


def head_sums(values, head):
    width = values.shape[1]
    a = lax.broadcasted_iota(jnp.int32, (width, width), 0) // head
    b = lax.broadcasted_iota(jnp.int32, (width, width), 1) // head
    same = jnp.where(a == b, 1.0, 0.0).astype(BF)
    high = values.astype(BF)
    low = (values - high.astype(F32)).astype(BF)
    return mm(high, same) + mm(low, same)


def turn(values, head):
    width = values.shape[1]
    lane = lax.broadcasted_iota(jnp.int32, values.shape, 1)
    return jnp.where(
        lane % head < head // 2, pltpu.roll(values, width - head // 2, 1), pltpu.roll(values, head // 2, 1)
    )


def wide(table, width):
    return jnp.concatenate([table] * (width // table.shape[1]), axis=1)


def norm_turn(raw, gain, cosine, sine, head):
    inverse = lax.rsqrt(head_sums(raw * raw, head) * (1.0 / head) + epsilon)
    v = raw * inverse * gain
    return v * wide(cosine, raw.shape[1]) + turn(v, head) * wide(sine, raw.shape[1])


def norm_turn_back(d, raw, gain, cosine, sine, head):
    d = d * wide(cosine, raw.shape[1]) - turn(d, head) * wide(sine, raw.shape[1])
    inverse = lax.rsqrt(head_sums(raw * raw, head) * (1.0 / head) + epsilon)
    scaled = d * gain
    inner = head_sums(scaled * raw, head) * (1.0 / head)
    grad_gain = jnp.sum(d * raw * inverse, axis=0, keepdims=True)
    return inverse * scaled - raw * (inverse * inverse * inverse * inner), grad_gain


def score_tile(q, k, starts, first_key, first_query, scale):
    raw = mm_nt(k, q) * scale
    key = first_key + lax.broadcasted_iota(jnp.int32, raw.shape, 0)
    query = first_query + lax.broadcasted_iota(jnp.int32, (1, starts.shape[1]), 1)
    copies = raw.shape[1] // starts.shape[1]
    allowed = (key <= wide(query, raw.shape[1])) & (key >= wide(starts, raw.shape[1]))
    return jnp.where(allowed, raw, -1e30)


def softmax_tile(scores):
    top = jnp.max(scores, axis=0, keepdims=True)
    weights = jnp.exp(scores - top)
    return weights / jnp.sum(weights, axis=0, keepdims=True)


def stack_heads(values, head):
    return jnp.concatenate([values[:, i * head : (i + 1) * head] for i in range(values.shape[1] // head)], axis=0)


def attention_tiles(total, tile):
    back = -(-MOST_DOC // tile)
    return [(i * tile, max(0, i - back) * tile, (i + 1) * tile) for i in range(total // tile)]


def attention_forward_kernel(
    head, lengths, h_ref, gain_ref, qgain_ref, kgain_ref, cos_ref, sin_ref, wq_hbm, wkv_hbm, wo_hbm,
    out_ref, n_hbm, raw_hbm, ready_hbm, o_hbm,
    w, wo, nf, raw, low, ready, vt, o, tpart, mine, n_near, n_over, n_on, o_near, i_near, o_over, i_over,
    s_near, s_over, wsem, osem,
):
    g = Group()
    g.greet()
    size, width = h_ref.shape
    total, qw = 4 * size, wo.shape[0]
    kw = (w.shape[1] - qw) // 2
    loads = start_all([(wq_hbm, w.at[:, pl.ds(0, qw)]), (wkv_hbm, w.at[:, pl.ds(qw, 2 * kw)]), (wo_hbm, wo)], wsem)
    gather = Gather(g, nf, size, n_near, n_over, n_on)
    scatter = Scatter(g, o_near, i_near, o_over, i_over, s_near, s_over, size)
    parts, step = gather.parts, gather.step
    nf[at_rows(g.mine, size, 0, size), :] = normalise(h_ref[...], gain_ref[...]).astype(BF)
    g.meet()
    gather.start()
    wait_all(loads)

    def project(block):
        rows = at_rows(block, size, 0, size)
        raw = mm(nf[rows, :], w[...])
        low[rows, :] = raw.astype(BF)
        cosine, sine = cos_ref[rows, :], sin_ref[rows, :]
        ready[rows, pl.ds(0, qw)] = norm_turn(raw[:, :qw], qgain_ref[...], cosine, sine, head).astype(BF)
        ready[rows, pl.ds(qw, kw)] = norm_turn(raw[:, qw : qw + kw], kgain_ref[...], cosine, sine, head).astype(BF)
        ready[rows, pl.ds(qw + kw, kw)] = raw[:, qw + kw :].astype(BF)

    project(g.mine)
    gather.wait_beside()
    project(g.beside)
    for p in range(parts):
        gather.wait_part(p)
    for p in range(parts):
        gather.wait_far(p)

    def rest(i, carry):
        project(jnp.where(i == 0, g.across, g.far))
        return carry

    lax.fori_loop(0, 2, rest, 0)
    saves = start_all([(nf, n_hbm), (low, raw_hbm), (ready, ready_hbm)], osem)
    vt[...] = jnp.transpose(ready[:, pl.ds(qw + kw, kw)].astype(F32)).astype(BF)
    groups = qw // kw
    tile = 256
    scale = head ** (-0.5)
    starts = doc_starts(lengths, lax.broadcasted_iota(jnp.int32, (1, total), 1))
    for first, low_key, high_key in attention_tiles(total, tile):
        keys = pl.ds(low_key, high_key - low_key)
        for kv in range(kw // head):
            q = stack_heads(ready[pl.ds(first, tile), pl.ds(kv * groups * head, groups * head)], head)
            k = ready[keys, pl.ds(qw, kw)][:, kv * head : (kv + 1) * head]
            p = softmax_tile(score_tile(q, k, starts[:, first : first + tile], low_key, first, scale)).astype(BF)
            ot = mm(vt[pl.ds(kv * head, head), keys], p)
            joined = jnp.concatenate([ot[:, i * tile : (i + 1) * tile] for i in range(groups)], axis=0)
            o[pl.ds(first, tile), pl.ds(kv * groups * head, groups * head)] = jnp.transpose(joined).astype(BF)
    save_o = pltpu.make_async_copy(o, o_hbm, osem.at[3])
    save_o.start()
    scatter_all(g, scatter, product(o, wo, False), mine, tpart)
    for p in range(parts):
        here = scatter.rows(p)
        scatter.close(1, p).wait_recv()
        scatter.link(p).wait_recv()
        out_ref[here, :] = (
            h_ref[here, :] + mine[here, :] + i_near[1, here, :].astype(F32) + i_over[here, :].astype(F32)
        )
    gather.finish()
    scatter.wait_all_sends()
    wait_all(saves)
    save_o.wait()


def attention_forward(head, lengths, h, gain, qgain, kgain, cosine, sine, wq, wkv, wo, ident, parts=PARTS):
    size, width = h.shape
    total, qw = 4 * size, wo.shape[0]
    kw = wkv.shape[1] // 2
    every = qw + 2 * kw
    return pl.pallas_call(
        functools.partial(attention_forward_kernel, head),
        out_shape=(
            shaped((size, width), F32), shaped((total, width), BF), shaped((total, every), BF), shaped((total, every), BF),
            shaped((total, qw), BF),
        ),
        in_specs=[SCALARS, INV, INV, INV, INV, INV, INV, HBM, HBM, HBM],
        out_specs=(INV, HBM, HBM, HBM, HBM),
        scratch_shapes=[
            pltpu.VMEM((width, every), BF), pltpu.VMEM((qw, width), BF), pltpu.VMEM((total, width), BF),
            pltpu.VMEM((8, 128), F32), pltpu.VMEM((total, every), BF), pltpu.VMEM((total, every), BF),
            pltpu.VMEM((kw, total), BF), pltpu.VMEM((total, qw), BF),
            pltpu.VMEM((size // parts, width), F32), pltpu.VMEM((size, width), F32),
            *gather_scratch(parts), *scatter_scratch(size, width, parts), DMA((3,)), DMA((4,)),
        ],
        compiler_params=params(ident),
        cost_estimate=pl.CostEstimate(flops=2 * total * width * (every + qw), bytes_accessed=2 * 12 * 2**20, transcendentals=0),
        name="attention_forward",
    )(lengths, h, gain, qgain, kgain, cosine, sine, wq, wkv, wo)


def attention_backward_kernel(
    head, lengths, dh_ref, h_ref, gain_ref, qgain_ref, kgain_ref, cos_ref, sin_ref, wq_hbm, wkv_hbm, wo_hbm,
    n_hbm, raw_hbm, ready_hbm, o_hbm, out_ref, gg_ref, gq_ref, gk_ref, gw_hbm, gwo_hbm,
    w, wo, nf, low, ready, kt, o, dz, do, dq, dkv, dlow, gw, gwo, tpart, mine,
    n_near, n_over, n_on, o_near, i_near, o_over, i_over, s_near, s_over, wsem, osem,
):
    g = Group()
    g.greet()
    size, width = h_ref.shape
    total, qw = 4 * size, wo.shape[0]
    kw = (w.shape[1] - qw) // 2
    loads = start_all(
        [
            (ready_hbm, ready), (wo_hbm, wo), (o_hbm, o), (raw_hbm, low), (wq_hbm, w.at[:, pl.ds(0, qw)]),
            (wkv_hbm, w.at[:, pl.ds(qw, 2 * kw)]), (n_hbm, nf),
        ],
        wsem,
    )
    gather = Gather(g, dz, size, n_near, n_over, n_on)
    scatter = Scatter(g, o_near, i_near, o_over, i_over, s_near, s_over, size)
    dz[at_rows(g.mine, size, 0, size), :] = dh_ref[...].astype(BF)
    g.meet()
    gather.start()
    wait_all(loads)
    kt[...] = jnp.transpose(ready[:, pl.ds(qw, kw)].astype(F32)).astype(BF)
    dkv[...] = jnp.zeros_like(dkv)
    gather_everything(gather)

    def project(t, carry):
        rows = at_rows(t, size, 0, size)
        do[rows, :] = mm_nt(dz[rows, :], wo[...]).astype(BF)
        return carry

    lax.fori_loop(0, total // size, project, 0)
    groups = qw // kw
    tile = 256
    scale = head ** (-0.5)
    starts = doc_starts(lengths, lax.broadcasted_iota(jnp.int32, (1, total), 1))
    for first, low_key, high_key in attention_tiles(total, tile):
        keys = pl.ds(low_key, high_key - low_key)
        for kv in range(kw // head):
            cols = pl.ds(kv * groups * head, groups * head)
            lane = slice(kv * head, (kv + 1) * head)
            q = stack_heads(ready[pl.ds(first, tile), cols], head)
            k, v = ready[keys, pl.ds(qw, kw)][:, lane], ready[keys, pl.ds(qw + kw, kw)][:, lane]
            p = softmax_tile(score_tile(q, k, starts[:, first : first + tile], low_key, first, scale))
            d = stack_heads(do[pl.ds(first, tile), cols], head)
            dp = mm_nt(v, d)
            inner = jnp.sum(p * dp, axis=0, keepdims=True)
            ds = (p * (dp - inner)).astype(BF)
            both = jnp.concatenate([mm(ds, q) * scale, mm(p.astype(BF), d)], axis=1)
            dkv[kv, keys, :] += both
            dqt = mm(kt[pl.ds(kv * head, head), keys], ds) * scale
            joined = jnp.concatenate([dqt[:, i * tile : (i + 1) * tile] for i in range(groups)], axis=0)
            dq[pl.ds(first, tile), cols] = jnp.transpose(joined)
    gq_ref[...] = jnp.zeros_like(gq_ref)
    gk_ref[...] = jnp.zeros_like(gk_ref)

    def finish(t, carry):
        rows = at_rows(t, size, 0, size)
        cosine, sine = cos_ref[rows, :], sin_ref[rows, :]
        d, gq = norm_turn_back(dq[rows, :], low[rows, pl.ds(0, qw)].astype(F32), qgain_ref[...], cosine, sine, head)
        gq_ref[...] += gq
        dlow[rows, pl.ds(0, qw)] = d.astype(BF)
        pairs = [dkv[kv, rows, :] for kv in range(kw // head)]
        dk = jnp.concatenate([x[:, :head] for x in pairs], axis=1)
        dv = jnp.concatenate([x[:, head:] for x in pairs], axis=1)
        d, gk = norm_turn_back(dk, low[rows, pl.ds(qw, kw)].astype(F32), kgain_ref[...], cosine, sine, head)
        gk_ref[...] += gk
        dlow[rows, pl.ds(qw, kw)] = d.astype(BF)
        dlow[rows, pl.ds(qw + kw, kw)] = dv.astype(BF)
        return carry

    lax.fori_loop(0, total // size, finish, 0)
    scatter_all(g, scatter, product(dlow, w, True), mine, tpart)
    gwo[...] = mm_tn(o[...], dz[...]).astype(BF)
    save = pltpu.make_async_copy(gwo, gwo_hbm, osem.at[0])
    save.start()
    for t in range(width // 256):
        gw[pl.ds(t * 256, 256), :] = mm_tn(nf[:, pl.ds(t * 256, 256)], dlow[...]).astype(BF)
    more = pltpu.make_async_copy(gw, gw_hbm, osem.at[1])
    more.start()
    close_scatter(scatter, mine, dh_ref, h_ref, gain_ref, out_ref, gg_ref)
    gather.finish()
    scatter.wait_all_sends()
    save.wait()
    more.wait()


def attention_backward(
    head, lengths, dh, h, gain, qgain, kgain, cosine, sine, wq, wkv, wo, n, raw, ready, o, ident, parts=PARTS
):
    size, width = h.shape
    total, qw = 4 * size, wo.shape[0]
    kw = wkv.shape[1] // 2
    every = qw + 2 * kw
    return pl.pallas_call(
        functools.partial(attention_backward_kernel, head),
        out_shape=(
            shaped((size, width), F32), shaped((1, width), F32), shaped((1, qw), F32), shaped((1, kw), F32),
            shaped((width, every), BF), shaped((qw, width), BF),
        ),
        in_specs=[SCALARS] + [INV] * 7 + [HBM] * 7,
        out_specs=(INV, INV, INV, INV, HBM, HBM),
        scratch_shapes=[
            pltpu.VMEM((width, every), BF), pltpu.VMEM((qw, width), BF), pltpu.VMEM((total, width), BF),
            pltpu.VMEM((total, every), BF), pltpu.VMEM((total, every), BF), pltpu.VMEM((kw, total), BF),
            pltpu.VMEM((total, qw), BF), pltpu.VMEM((total, width), BF), pltpu.VMEM((total, qw), BF),
            pltpu.VMEM((total, qw), F32), pltpu.VMEM((kw // head, total, 2 * head), F32), pltpu.VMEM((total, every), BF),
            pltpu.VMEM((width, every), BF), pltpu.VMEM((qw, width), BF),
            pltpu.VMEM((size // parts, width), F32), pltpu.VMEM((size, width), F32),
            *gather_scratch(parts), *scatter_scratch(size, width, parts), DMA((7,)), DMA((2,)),
        ],
        compiler_params=params(ident),
        cost_estimate=pl.CostEstimate(flops=4 * total * width * (every + qw), bytes_accessed=2 * 20 * 2**20, transcendentals=0),
        name="attention_backward",
    )(lengths, dh, h, gain, qgain, kgain, cosine, sine, wq, wkv, wo, n, raw, ready, o)


rope_base = 1000000.0
TP = ("c", "zl")
DP = ("r", "s", "zh")


def doc_positions(lengths_row, length):
    count = lengths_row.shape[0]
    upto = jnp.arange(count)[:, None] >= jnp.arange(count)[None, :]
    doc_ends = jnp.sum(jnp.where(upto, lengths_row[None, :], 0), axis=1)
    places = jnp.arange(length, dtype=jnp.int32)
    passed = places[:, None] >= doc_ends[None, :]
    return places - jnp.max(jnp.where(passed, doc_ends[None, :], 0), axis=1)


def rope_tables(position, head_dim):
    half_dim = head_dim // 2
    inverse = rope_base ** (-2.0 * jnp.arange(half_dim, dtype=F32) / head_dim)
    angles = position.astype(F32)[:, None] * inverse[None, :]
    cosine, sine = jnp.cos(angles), jnp.sin(angles)
    copies = LANES // head_dim
    return (
        jnp.concatenate([cosine, cosine] * copies, axis=1),
        jnp.concatenate([-sine, sine] * copies, axis=1),
    )


def swap(x):
    return lax.ppermute(x, ("c", "zh"), [(0, 0), (1, 2), (2, 1), (3, 3)])


def gather_dp(shard, axis):
    return lax.all_gather(shard, DP, axis=axis, tiled=True)


def scatter_dp(partial, axis):
    return lax.psum_scatter(partial.astype(BF), DP, scatter_dimension=axis, tiled=True)


def local(
    tokens, doc_lengths, grad_out, norm_gains, head_gains, conv_in, conv_kernel, conv_out,
    query_w, kv_w, out_w, gate_up, down,
):
    length = tokens.shape[0]
    head_dim = head_gains.shape[1]
    quarter = lax.axis_index("c") * 2 + lax.axis_index("zl")
    rows = length // 4
    lengths = swap(doc_lengths)
    cosine, sine = rope_tables(doc_positions(lengths[0], length), head_dim)
    conv_in = swap(conv_in.reshape(conv_in.shape[0], -1))
    conv_kernel = swap(conv_kernel)
    conv_out = swap(conv_out)
    query_w = swap(query_w)
    kv_w = swap(kv_w.reshape(kv_w.shape[0], -1))
    out_w = swap(out_w)
    ws = [gather_dp(swap(gate_up[l].reshape(gate_up.shape[1], -1)), 0) for l in (0, 1)]
    vs = [gather_dp(swap(down[l]), 1) for l in (0, 1)]
    kv_width = kv_w.shape[1] // 2
    qgain = jnp.tile(head_gains[0:1], (1, query_w.shape[1] // head_dim))
    kgain = jnp.tile(head_gains[1:2], (1, kv_width // head_dim))
    gain = [norm_gains[i : i + 1] for i in range(4)]

    up_full = lax.all_gather(swap(grad_out), TP, axis=1, tiled=True)
    h1, x_block, n0, projected = conv_forward(lengths, swap(tokens), gain[0], conv_kernel, conv_in, conv_out, 0)
    h2, n1, hidden0 = ffn_forward(h1, gain[1], ws[0], vs[0], 1)
    h3, n2, raw, ready, attended = attention_forward(
        head_dim, lengths, h2, gain[2], qgain, kgain, cosine, sine, query_w, kv_w, out_w, 2
    )
    h4, n3, hidden1 = ffn_forward(h3, gain[3], ws[1], vs[1], 3)
    output = swap(lax.all_to_all(h4.astype(BF), TP, 1, 0, tiled=True))

    dh4 = lax.dynamic_slice_in_dim(up_full, quarter * rows, rows, 0).astype(F32)
    dh3, gain3, gw1, gv1 = ffn_backward(dh4, h3, gain[3], up_full, ws[1], vs[1], n3, hidden1, 4)
    dh2, gain2, gq, gk, gqkv, gow = attention_backward(
        head_dim, lengths, dh3, h2, gain[2], qgain, kgain, cosine, sine, query_w, kv_w, out_w, n2, raw, ready, attended, 5
    )
    dh1, gain1, gw0, gv0 = ffn_backward(dh2, h1, gain[1], None, ws[0], vs[0], n1, hidden0, 6)
    dh0, gain0, gtaps, gci, gco = conv_backward(
        lengths, dh1, x_block.astype(F32), gain[0], conv_kernel, conv_in, conv_out, n0, projected, 7
    )
    grad_tokens = swap(lax.all_to_all(dh0, TP, 1, 0, tiled=True))

    back = lambda g, axis: swap(scatter_dp(g, axis)).astype(F32)
    kernel_full = jnp.zeros((conv_kernel.shape[0], norm_gains.shape[1]), F32)
    kernel_full = lax.dynamic_update_slice_in_dim(kernel_full, gtaps, quarter * conv_kernel.shape[1], 1)
    head_grads = jnp.stack([jnp.sum(x.reshape(-1, head_dim), axis=0) for x in (gq, gk)])
    gains, heads, kernels = lax.psum(
        (jnp.concatenate([gain0, gain1, gain2, gain3]), head_grads, kernel_full), ("r", "s", "c", "zh", "zl")
    )
    eighth = gate_up.shape[1]
    gqkv = back(gqkv, 0)
    return (
        output,
        grad_tokens,
        gains,
        heads,
        back(gci, 0).reshape(-1, 3, conv_kernel.shape[1]),
        kernels,
        back(gco, 1),
        gqkv[:, : query_w.shape[1]],
        gqkv[:, query_w.shape[1] :].reshape(-1, 2, kv_width),
        back(gow, 1),
        jnp.stack([back(gw0, 0), back(gw1, 0)]).reshape(2, eighth, 2, -1),
        jnp.stack([back(gv0, 1), back(gv1, 1)]),
    )


def solution(mesh):
    devices = mesh.devices
    dp, tp = devices.shape
    inner = Mesh(devices.reshape(dp // 4, 2, 2, 2, tp // 2), ("r", "s", "c", "zh", "zl"))
    D = ("r", "s", "c")
    T = ("zh", "zl")
    return jax.shard_map(
        local,
        mesh=inner,
        in_specs=(
            P(D, T), P(D, None), P(D, T), P(), P(), P(None, None, T), P(None, T), P(T, None),
            P(None, T), P(None, None, T), P(T, None), P(None, D, None, T), P(None, T, D),
        ),
        out_specs=(
            P(D, T), P(D, T), P(), P(), P(D, None, T), P(), P(T, D), P(D, T), P(D, None, T),
            P(T, D), P(None, D, None, T), P(None, T, D),
        ),
        check_vma=False,
    )
```

```python
import functools
import jax
import jax.numpy as jnp
from jax import lax
from jax.experimental import pallas as pl
from jax.experimental.pallas import tpu as pltpu
from jax.sharding import Mesh, PartitionSpec as P

epsilon = 1e-05
BF = jnp.bfloat16
F32 = jnp.float32
MESH = pl.DeviceIdType.MESH
DMA = pltpu.SemaphoreType.DMA
HBM = pl.BlockSpec(memory_space=pl.ANY)
INV = pl.BlockSpec(memory_space=pltpu.VMEM)
PARTS = 2
LANES = 128


class Group:
    def __init__(self, others=()):
        c, z = lax.axis_index("c"), lax.axis_index("zl")
        self.partner, self.twin = {"c": 1 - c}, {"zl": 1 - z}
        self.mine, self.beside = 2 * c + z, 2 * (1 - c) + z
        self.across, self.far = 2 * c + (1 - z), 2 * (1 - c) + (1 - z)
        self.known = [self.partner, self.twin, *others]
        self.barrier = pltpu.get_barrier_semaphore()

    def greet(self):
        for other in self.known:
            pl.semaphore_signal(self.barrier, inc=1, device_id=other, device_id_type=MESH)

    def meet(self):
        pl.semaphore_wait(self.barrier, len(self.known))


def at_rows(block, size, start, count):
    return pl.ds(pl.multiple_of(block * size + start, 16), count)


def send(src, dst, sems, index, where):
    return pltpu.make_async_remote_copy(
        src_ref=src, dst_ref=dst, send_sem=sems.at[0, index], recv_sem=sems.at[1, index],
        device_id=where, device_id_type=MESH,
    )


class Gather:
    def __init__(self, group, full, size, near, over, onward):
        self.g, self.full, self.size, self.parts = group, full, size, over.shape[1]
        self.near, self.over, self.onward = near, over, onward
        self.step = size // self.parts

    def view(self, block, part):
        return self.full.at[at_rows(block, self.size, part * self.step, self.step)]

    def link(self, part, block):
        v = self.view(block, part)
        return send(v, v, self.over, part, self.g.twin)

    def close(self, part, block):
        v = self.view(block, part)
        return send(v, v, self.near, part, self.g.partner)

    def pass_on(self, part, block):
        v = self.view(block, part)
        return send(v, v, self.onward, part, self.g.partner)

    def start(self):
        for p in range(self.parts):
            self.link(p, self.g.mine).start()
            self.close(p, self.g.mine).start()

    def wait_beside(self):
        for p in range(self.parts):
            self.close(p, self.g.beside).wait_recv()

    def wait_part(self, p):
        self.link(p, self.g.across).wait_recv()
        self.pass_on(p, self.g.across).start()

    def wait_far(self, p):
        self.pass_on(p, self.g.far).wait_recv()

    def finish(self):
        for p in range(self.parts):
            self.link(p, self.g.mine).wait_send()
            self.close(p, self.g.mine).wait_send()
            self.pass_on(p, self.g.across).wait_send()


class Scatter:
    def __init__(self, group, out_near, in_near, out_over, in_over, near, over, size):
        self.g, self.size, self.parts = group, size, over.shape[1]
        self.out_near, self.in_near, self.out_over, self.in_over = out_near, in_near, out_over, in_over
        self.near, self.over = near, over
        self.step = size // self.parts

    def rows(self, part):
        return pl.ds(part * self.step, self.step)

    def close(self, which, part):
        r = self.rows(part)
        return send(self.out_near.at[which, r], self.in_near.at[which, r], self.near, which * self.parts + part, self.g.partner)

    def link(self, part):
        r = self.rows(part)
        return send(self.out_over.at[r], self.in_over.at[r], self.over, part, self.g.twin)

    def wait_all_sends(self):
        for p in range(self.parts):
            self.close(0, p).wait_send()
            self.close(1, p).wait_send()
            self.link(p).wait_send()


def scatter_scratch(size, width, parts):
    return [
        pltpu.VMEM((2, size, width), BF), pltpu.VMEM((2, size, width), BF), pltpu.VMEM((size, width), BF),
        pltpu.VMEM((size, width), BF), DMA((2, 2 * parts)), DMA((2, parts)),
    ]


def gather_scratch(parts):
    return [DMA((2, parts)), DMA((2, parts)), DMA((2, parts))]


def normalise(h, gain):
    return h * lax.rsqrt(jnp.mean(h * h, axis=-1, keepdims=True) + epsilon) * gain


def mm(a, b):
    return jnp.dot(a, b, preferred_element_type=F32)


def mm_nt(a, b):
    return lax.dot_general(a, b, (((1,), (1,)), ((), ())), preferred_element_type=F32)


def lanes(start, width):
    return pl.ds(pl.multiple_of(start, LANES), width)


def start_all(pairs, sems):
    copies = [pltpu.make_async_copy(src, dst, sems.at[i]) for i, (src, dst) in enumerate(pairs)]
    for copy in copies:
        copy.start()
    return copies


def wait_all(copies):
    for copy in copies:
        copy.wait()


def params(ident):
    return pltpu.CompilerParams(collective_id=ident, has_side_effects=True, vmem_limit_bytes=56 * 2**20)


def shaped(shape, dtype):
    return jax.ShapeDtypeStruct(shape, dtype)


SCALARS = pl.BlockSpec(memory_space=pltpu.SMEM)


class Place:
    def __init__(self):
        self.y, self.x, self.c, self.zh = (lax.axis_index(a) for a in ("r", "s", "c", "zh"))
        self.across_x, self.across_y = {"s": 1 - self.x}, {"r": 1 - self.y}
        self.partner = {"c": 1 - self.c}
        self.plain = self.c == self.zh

    def over(self, core):
        return {"c": core, "zh": 1 - self.zh}

    def others(self):
        return [self.across_x, self.across_y, self.over(self.c), self.over(1 - self.c)]

    def piece(self, flip_y, flip_x, a):
        y = 1 - self.y if flip_y else self.y
        x = 1 - self.x if flip_x else self.x
        return 4 * y + 2 * x + a


class Fetch:
    steps = 4

    def __init__(self, shard, sources=None):
        rows, cols = shard.shape
        self.ins = [shard]
        self.outs = [jax.ShapeDtypeStruct((8, rows, cols), shard.dtype)]
        self.out_specs = [HBM]
        self.scratch = [DMA((9,)), DMA((8,)), DMA((1,))]

    def bind(self, ins, outs, scratch):
        (self.own,), (self.out,) = ins, outs
        self.sent, self.come, self.sem = scratch
        self.p = Place()

    def copy(self, src, piece, sent, come, where):
        return pltpu.make_async_remote_copy(
            src_ref=src, dst_ref=self.out.at[piece], send_sem=self.sent.at[sent], recv_sem=self.come.at[come],
            device_id=where, device_id_type=MESH,
        )

    def to_plane(self):
        p = self.p
        return self.copy(self.own, p.piece(0, 0, p.c), 0, p.c, p.over(p.zh))

    def to_partner(self):
        p = self.p
        return self.copy(self.own, p.piece(0, 0, p.c), 1, p.c, p.partner)

    def arrived(self, a):
        return self.copy(self.own, self.p.piece(0, 0, a), 0, a, self.p.partner).wait_recv()

    def keep(self):
        return pltpu.make_async_copy(self.own, self.out.at[self.p.piece(0, 0, self.p.c)], self.sem.at[0])

    def to_x(self, a, src):
        return self.copy(src, self.p.piece(0, 0, a), 2 + a, 2 + a, self.p.across_x)

    def to_y(self, a, src):
        return self.copy(src, self.p.piece(0, 0, a), 4 + a, 4 + a, self.p.across_y)

    def spread(self, a, src):
        self.to_x(a, src).start()
        self.to_y(a, src).start()

    def slot(self, a):
        return self.out.at[self.p.piece(0, 0, a)]

    def on_y(self):
        piece = self.p.piece(0, 1, 0)
        return self.copy(self.out.at[piece], piece, 6, 6, self.p.across_y)

    def on_x(self):
        piece = self.p.piece(1, 0, 1)
        return self.copy(self.out.at[piece], piece, 7, 7, self.p.across_x)

    def step(self, k):
        p = self.p
        if k == 0:
            self.to_plane().start()

            @pl.when(p.plain)
            def _():
                self.keep().start()
                self.spread(p.c, self.own)

            @pl.when(jnp.logical_not(p.plain))
            def _():
                self.to_partner().start()

        elif k == 1:

            @pl.when(p.plain)
            def _():
                self.arrived(1 - p.c)
                self.spread(1 - p.c, self.slot(1 - p.c))

            @pl.when(jnp.logical_not(p.plain))
            def _():
                for a in (0, 1):
                    self.arrived(a)
                    self.spread(a, self.slot(a))

        elif k == 2:
            self.to_x(0, self.slot(0)).wait_recv()
            self.on_y().start()
            self.to_y(1, self.slot(1)).wait_recv()
            self.on_x().start()
        else:
            self.to_x(1, self.slot(1)).wait_recv()
            self.to_y(0, self.slot(0)).wait_recv()
            self.on_y().wait()
            self.on_x().wait()
            self.to_plane().wait_send()
            for a in (0, 1):
                self.to_x(a, self.slot(a)).wait_send()
                self.to_y(a, self.slot(a)).wait_send()

            @pl.when(p.plain)
            def _():
                self.keep().wait()

            @pl.when(jnp.logical_not(p.plain))
            def _():
                self.to_partner().wait_send()


class Reduce:
    steps = 4

    def __init__(self, grad, first, rows):
        self.first, self.rows = first, rows
        cols = grad.shape[2]
        self.ins = [grad]
        self.outs = [jax.ShapeDtypeStruct((rows, cols), F32)]
        self.out_specs = [INV]
        self.scratch = [
            pltpu.VMEM((4, rows, cols), BF), pltpu.VMEM((4, rows, cols), BF), pltpu.VMEM((2, rows, cols), BF),
            pltpu.VMEM((2, rows, cols), BF), DMA((9,)), DMA((8,)), DMA((4,)),
        ]

    def bind(self, ins, outs, scratch):
        (self.grad,), (self.out,) = ins, outs
        self.held, self.in1, self.in2, self.in3, self.sent, self.come, self.sem = scratch
        self.p = Place()

    def piece(self, flip_y, flip_x, a):
        return self.grad.at[self.p.piece(flip_y, flip_x, a), pl.ds(self.first, self.rows)]

    def copy(self, src, dst, sent, come, where):
        return pltpu.make_async_remote_copy(
            src_ref=src, dst_ref=dst, send_sem=self.sent.at[sent], recv_sem=self.come.at[come],
            device_id=where, device_id_type=MESH,
        )

    def loads(self):
        kept = [(0, 0, 0), (0, 1, 0), (0, 0, 1), (1, 0, 1)]
        return [pltpu.make_async_copy(self.piece(*k), self.held.at[i], self.sem.at[i]) for i, k in enumerate(kept)]

    def first_hops(self):
        p = self.p
        return [
            self.copy(self.piece(1, 0, 0), self.in1.at[0], 0, 0, p.across_y),
            self.copy(self.piece(1, 1, 0), self.in1.at[1], 1, 1, p.across_y),
            self.copy(self.piece(0, 1, 1), self.in1.at[2], 2, 2, p.across_x),
            self.copy(self.piece(1, 1, 1), self.in1.at[3], 3, 3, p.across_x),
        ]

    def second_hops(self):
        return [
            self.copy(self.held.at[1], self.in2.at[0], 4, 4, self.p.across_x),
            self.copy(self.held.at[3], self.in2.at[1], 5, 5, self.p.across_y),
        ]

    def to_owner(self, a):
        return self.copy(self.held.at[2 * a], self.in3.at[0], 6 + a, 6, self.p.over(a))

    def to_partner(self):
        return self.copy(self.held.at[2 * (1 - self.p.c)], self.in3.at[1], 8, 7, self.p.partner)

    def add(self, i, other):
        self.held[i] = (self.held[i].astype(F32) + other.astype(F32)).astype(BF)

    def step(self, k):
        p = self.p
        if k == 0:
            for hop in [self.first_hops()[i] for i in (1, 3, 0, 2)]:
                hop.start()
            for load in self.loads():
                load.start()
        elif k == 1:
            for load in self.loads():
                load.wait()
            hops, after = self.first_hops(), self.second_hops()
            for i in (1, 3):
                hops[i].wait_recv()
                self.add(i, self.in1[i])
                after[i // 2].start()
            for i in (0, 2):
                hops[i].wait_recv()
                self.add(i, self.in1[i])
        elif k == 2:
            for i, hop in enumerate(self.second_hops()):
                hop.wait_recv()
                self.add(2 * i, self.in2[i])

            @pl.when(p.plain)
            def _():
                self.to_partner().start()

            @pl.when(jnp.logical_not(p.plain))
            def _():
                self.to_owner(0).start()
                self.to_owner(1).start()

        else:
            self.to_owner(0).wait_recv()

            @pl.when(p.plain)
            def _():
                self.out[...] = self.held[2 * p.c].astype(F32) + self.in3[0].astype(F32)
                self.to_partner().wait_send()

            @pl.when(jnp.logical_not(p.plain))
            def _():
                self.to_partner().wait_recv()
                self.out[...] = self.in3[1].astype(F32) + self.in3[0].astype(F32)
                self.to_owner(0).wait_send()
                self.to_owner(1).wait_send()

            for hop in self.first_hops() + self.second_hops():
                hop.wait_send()


class Background:
    def __init__(self, tasks):
        self.tasks = tasks
        self.others = Place().others() if tasks else []

    def step(self, k):
        for task in self.tasks:
            task.step(k)


def hosted(kernel, ident, name, ins, in_specs, outs, out_specs, scratch, tasks, flops, traffic):
    groups = ([], [], [])
    for group, own in zip(groups, (ins, outs, scratch)):
        group.append(len(own))
    ins, in_specs, outs, out_specs, scratch = list(ins), list(in_specs), list(outs), list(out_specs), list(scratch)
    for task in tasks:
        for group, more in zip(groups, (task.ins, task.outs, task.scratch)):
            group.append(len(more))
        ins += task.ins
        in_specs += [HBM] * len(task.ins)
        outs += task.outs
        out_specs += task.out_specs
        scratch += task.scratch

    def split(refs, counts):
        at, found = 0, []
        for count in counts:
            found.append(refs[at : at + count])
            at += count
        return found

    def body(*refs):
        parts = [split(part, group) for part, group in zip(split(refs, [sum(g) for g in groups]), groups)]
        for task, *mine in zip(tasks, *(part[1:] for part in parts)):
            task.bind(*mine)
        kernel(*parts[0][0], *parts[1][0], *parts[2][0], Background(tasks))

    results = pl.pallas_call(
        body,
        out_shape=tuple(outs),
        in_specs=in_specs,
        out_specs=tuple(out_specs),
        scratch_shapes=scratch,
        compiler_params=params(ident),
        cost_estimate=pl.CostEstimate(flops=flops, bytes_accessed=traffic, transcendentals=0),
        name=name,
    )(*ins)
    results = split(list(results), groups[1])
    return results[0], [r[0] for r in results[1:]]


def put_rows(scratch, first, value):
    tall = scratch.shape[1]
    done = 0
    while done < value.shape[0]:
        piece, at = divmod(first + done, tall)
        count = min(tall - at, value.shape[0] - done)
        scratch[piece, pl.ds(at, count), :] = value[done : done + count]
        done += count


def put_columns(scratch, first, value):
    wide_piece = scratch.shape[2]
    for piece in range(scratch.shape[0]):
        scratch[piece, pl.ds(first, value.shape[0]), :] = value[:, piece * wide_piece : (piece + 1) * wide_piece]


def column_loads(pieces, whole):
    each = pieces.shape[2]
    return [(pieces.at[i], whole.at[:, pl.ds(i * each, each)]) for i in range(pieces.shape[0])]


def ffn_forward_kernel(
    h_ref, gain_ref, w_hbm, v_hbm, out_ref, n_hbm, u_hbm,
    w, v, nf, u, act, tpart, mine, n_near, n_over, n_on, o_near, i_near, o_over, i_over, s_near, s_over,
    wsem, osem, bg,
):
    g = Group(bg.others)
    g.greet()
    size, width = h_ref.shape
    hidden = v.shape[0]
    loads = start_all([(w_hbm, w)] + column_loads(v_hbm, v), wsem)
    gather = Gather(g, nf, size, n_near, n_over, n_on)
    scatter = Scatter(g, o_near, i_near, o_over, i_over, s_near, s_over, size)
    parts, step = gather.parts, gather.step
    for p in range(parts):
        nf[at_rows(g.mine, size, p * step, step), :] = normalise(
            h_ref[pl.ds(p * step, step), :], gain_ref[...]
        ).astype(BF)
    g.meet()
    gather.start()
    bg.step(0)
    wait_all(loads)

    def rows_of(places):
        return jnp.concatenate([nf[r, :] for r, _ in places], axis=0) if len(places) > 1 else nf[places[0][0], :]

    def up(places):
        def body(t, carry):
            x = rows_of(places)
            wt = jnp.concatenate([w[:, lanes(t * LANES, LANES)], w[:, lanes(hidden + t * LANES, LANES)]], axis=1)
            both = mm(x, wt)
            gate, upper = both[:, :LANES], both[:, LANES:]
            a = gate * jax.nn.sigmoid(gate) * upper
            act[:, lanes(t * LANES, LANES)] = a.astype(BF)
            at = 0
            for r, count in places:
                u[r, lanes(t * LANES, LANES)] = gate[at : at + count].astype(BF)
                u[r, lanes(hidden + t * LANES, LANES)] = upper[at : at + count].astype(BF)
                at += count
            return carry

        lax.fori_loop(0, hidden // LANES, body, 0)

    def down(store):
        def body(t, carry):
            cols = lanes(t * 256, 256)
            store(cols, mm(act[...], v[:, cols]))
            return carry

        lax.fori_loop(0, width // 256, body, 0)

    def keep(index, r, count):
        return pltpu.make_async_copy(u.at[r], u_hbm.at[r], osem.at[index])

    whole = lambda block: at_rows(block, size, 0, size)
    up([(whole(g.mine), size)])
    keep(0, whole(g.mine), size).start()

    def put_mine(cols, value):
        mine[:, cols] = value

    down(put_mine)
    gather.wait_beside()
    up([(whole(g.beside), size)])
    keep(1, whole(g.beside), size).start()

    def put_beside(cols, value):
        o_near[1, :, cols] = value.astype(BF)

    down(put_beside)
    for p in range(parts):
        scatter.close(1, p).start()
    bg.step(1)
    for p in range(parts):
        gather.wait_part(p)
        gather.wait_far(p)
        r_across, r_far = at_rows(g.across, size, p * step, step), at_rows(g.far, size, p * step, step)
        up([(r_across, step), (r_far, step)])
        keep(2 + 2 * p, r_across, step).start()
        keep(3 + 2 * p, r_far, step).start()
        here = scatter.rows(p)

        def put(cols, value):
            tpart[:, cols] = value[:step]
            o_near[0, here, cols] = value[step:].astype(BF)

        down(put)
        scatter.close(0, p).start()
        scatter.close(0, p).wait_recv()
        o_over[here, :] = (tpart[...] + i_near[0, here, :].astype(F32)).astype(BF)
        scatter.link(p).start()
    n_out = pltpu.make_async_copy(nf, n_hbm, osem.at[2 + 2 * parts])
    n_out.start()
    bg.step(2)
    for p in range(parts):
        here = scatter.rows(p)
        scatter.close(1, p).wait_recv()
        scatter.link(p).wait_recv()
        out_ref[here, :] = (
            h_ref[here, :] + mine[here, :] + i_near[1, here, :].astype(F32) + i_over[here, :].astype(F32)
        )
    gather.finish()
    scatter.wait_all_sends()
    keep(0, whole(g.mine), size).wait()
    keep(1, whole(g.beside), size).wait()
    for p in range(parts):
        keep(2 + 2 * p, at_rows(g.across, size, p * step, step), step).wait()
        keep(3 + 2 * p, at_rows(g.far, size, p * step, step), step).wait()
    n_out.wait()
    bg.step(3)


def ffn_forward(h, gain, w, v, ident, tasks=(), parts=PARTS):
    size, width = h.shape
    hidden = v.shape[1]
    total = 4 * size
    return hosted(
        ffn_forward_kernel, ident, "ffn_forward", [h, gain, w, v], [INV, INV, HBM, HBM],
        [shaped((size, width), F32), shaped((total, width), BF), shaped((total, 2 * hidden), BF)], [INV, HBM, HBM],
        [
            pltpu.VMEM((width, 2 * hidden), BF), pltpu.VMEM((hidden, width), BF), pltpu.VMEM((total, width), BF),
            pltpu.VMEM((total, 2 * hidden), BF), pltpu.VMEM((size, hidden), BF),
            pltpu.VMEM((size // parts, width), F32), pltpu.VMEM((size, width), F32),
            *gather_scratch(parts), *scatter_scratch(size, width, parts), DMA((1 + v.shape[0],)), DMA((3 + 2 * parts,)),
        ],
        tasks, 6 * total * width * hidden, 2**24,
    )


def mm_tn(a, b):
    return lax.dot_general(a, b, (((0,), (0,)), ((), ())), preferred_element_type=F32)


def rms_back(dn, h, gain):
    inverse = lax.rsqrt(jnp.mean(h * h, axis=-1, keepdims=True) + epsilon)
    scaled = dn * gain
    inner = jnp.mean(scaled * h, axis=-1, keepdims=True)
    grad_gain = jnp.sum(dn * h * inverse, axis=0, keepdims=True)
    return inverse * scaled - h * (inverse * inverse * inverse * inner), grad_gain


def close_scatter(scatter, mine, dh_ref, h_ref, gain_ref, out_ref, gg_ref):
    gg_ref[...] = jnp.zeros_like(gg_ref)
    for p in range(scatter.parts):
        here = scatter.rows(p)
        scatter.close(1, p).wait_recv()
        scatter.link(p).wait_recv()
        dn = mine[here, :] + scatter.in_near[1, here, :].astype(F32) + scatter.in_over[here, :].astype(F32)
        term, grad_gain = rms_back(dn, h_ref[here, :], gain_ref[...])
        out_ref[here, :] = dh_ref[here, :] + term
        gg_ref[...] += grad_gain


def ffn_backward_kernel(
    known, dh_ref, h_ref, gain_ref, df_hbm, w_hbm, v_hbm, n_hbm, u_hbm, out_ref, gg_ref, gw_hbm, gv_hbm,
    w, v, nf, u, act, df, tpart, mine, gtile, gv, n_near, n_over, n_on, o_near, i_near, o_over, i_over, s_near, s_over,
    wsem, osem, bg,
):
    g = Group(bg.others)
    g.greet()
    size, width = dh_ref.shape
    hidden = v.shape[0]
    loads = column_loads(v_hbm, v) + [(u_hbm, u), (w_hbm, w), (n_hbm, nf)]
    loads = start_all(loads + [(df_hbm, df)] if known else loads, wsem)
    gather = Gather(g, df, size, n_near, n_over, n_on)
    scatter = Scatter(g, o_near, i_near, o_over, i_over, s_near, s_over, size)
    parts, step = gather.parts, gather.step
    if not known:
        df[at_rows(g.mine, size, 0, size), :] = dh_ref[...].astype(BF)
    g.meet()
    if not known:
        gather.start()
    bg.step(0)
    wait_all(loads)

    third = hidden // 3

    def cat(ref, places, cols):
        found = [ref[r, cols] for r, _ in places]
        return found[0] if len(found) == 1 else jnp.concatenate(found, axis=0)

    def first(places):
        def body(t, carry):
            cols, more = lanes(t * third, third), lanes(hidden + t * third, third)
            da = mm_nt(cat(df, places, slice(None)), v[cols, :])
            gate, upper = cat(u, places, cols).astype(F32), cat(u, places, more).astype(F32)
            s = jax.nn.sigmoid(gate)
            lit = gate * s
            dgate = (da * upper * s * (1.0 + gate * (1.0 - s))).astype(BF)
            dupper = (da * lit).astype(BF)
            a = (lit * upper).astype(BF)
            at = 0
            for r, count in places:
                u[r, cols] = dgate[at : at + count]
                u[r, more] = dupper[at : at + count]
                act[r, cols] = a[at : at + count]
                at += count
            return carry

        lax.fori_loop(0, 3, body, 0)

    def second(places, store):
        def body(t, carry):
            cols = lanes(t * 256, 256)
            store(cols, mm_nt(cat(u, places, slice(None)), w[cols, :]))
            return carry

        lax.fori_loop(0, width // 256, body, 0)

    whole = lambda block: [(at_rows(block, size, 0, size), size)]

    def put_mine(cols, value):
        mine[:, cols] = value

    def put_beside(cols, value):
        o_near[1, :, cols] = value.astype(BF)

    def own():
        first(whole(g.mine))
        second(whole(g.mine), put_mine)

    def beside():
        first(whole(g.beside))
        second(whole(g.beside), put_beside)
        for p in range(parts):
            scatter.close(1, p).start()

    if not known:
        own()
        gather.wait_beside()
        beside()
    for p in range(parts):
        if not known:
            gather.wait_part(p)
            gather.wait_far(p)
        pair = [(at_rows(b, size, p * step, step), step) for b in (g.across, g.far)]
        first(pair)
        here = scatter.rows(p)

        def put(cols, value):
            tpart[:, cols] = value[:step]
            o_near[0, here, cols] = value[step:].astype(BF)

        second(pair, put)
        scatter.close(0, p).start()
        scatter.close(0, p).wait_recv()
        o_over[here, :] = (tpart[...] + i_near[0, here, :].astype(F32)).astype(BF)
        scatter.link(p).start()
    if known:
        beside()
        own()
    flush = []
    count = 0

    def emit(value, dst):
        nonlocal count
        slot = count % 2
        if count >= 2:
            flush[count - 2].wait()
        gtile[slot, :, : value.shape[1]] = value.astype(BF)
        copy = pltpu.make_async_copy(gtile.at[slot, :, : value.shape[1]], dst, osem.at[slot])
        copy.start()
        flush.append(copy)
        count += 1

    tall = gtile.shape[1]
    for t in range(3):
        put_columns(gv, t * third, mm_tn(act[:, t * third : (t + 1) * third], df[...]).astype(BF))
    save = pltpu.make_async_copy(gv, gv_hbm, osem.at[2])
    save.start()
    bg.step(1)
    each = gw_hbm.shape[1]
    for t in range(width // tall):
        piece, at = divmod(t * tall, each)
        for k in range(2):
            cols = slice(k * hidden, (k + 1) * hidden)
            emit(mm_tn(nf[:, t * tall : (t + 1) * tall], u[:, cols]), gw_hbm.at[piece, pl.ds(at, tall), cols])
    bg.step(2)
    close_scatter(scatter, mine, dh_ref, h_ref, gain_ref, out_ref, gg_ref)
    if not known:
        gather.finish()
    scatter.wait_all_sends()
    for copy in flush[-2:]:
        copy.wait()
    save.wait()
    bg.step(3)


def ffn_backward(dh, h, gain, df, w, v, n, u, ident, tasks=(), parts=PARTS):
    size, width = h.shape
    pieces, hidden = v.shape[:2]
    total = 4 * size
    known = df is not None
    if not known:
        df = n
    return hosted(
        functools.partial(ffn_backward_kernel, known), ident, "ffn_backward", [dh, h, gain, df, w, v, n, u],
        [INV, INV, INV] + [HBM] * 5,
        [
            shaped((size, width), F32), shaped((1, width), F32), shaped((pieces, width // pieces, 2 * hidden), BF),
            shaped((pieces, hidden, width // pieces), BF),
        ],
        [INV, INV, HBM, HBM],
        [
            pltpu.VMEM((width, 2 * hidden), BF), pltpu.VMEM((hidden, width), BF), pltpu.VMEM((total, width), BF),
            pltpu.VMEM((total, 2 * hidden), BF), pltpu.VMEM((total, hidden), BF), pltpu.VMEM((total, width), BF),
            pltpu.VMEM((size // parts, width), F32), pltpu.VMEM((size, width), F32),
            pltpu.VMEM((2, 128, hidden), BF), pltpu.VMEM((pieces, hidden, width // pieces), BF),
            *gather_scratch(parts), *scatter_scratch(size, width, parts), DMA((4 + pieces,)), DMA((3,)),
        ],
        tasks, 12 * total * width * hidden, 2**25,
    )


MOST_DOC = 512


class Columns(Gather):
    def __init__(self, group, full, near, over, onward):
        super().__init__(group, full, full.shape[0], near, over, onward)
        self.cols = full.shape[1] // 4

    def view(self, block, part):
        return self.full.at[pl.ds(part * self.step, self.step), lanes(block * self.cols, self.cols)]


def cat_rows(ref, places, cols=slice(None)):
    found = [ref[r, cols] for r, _ in places]
    return found[0] if len(found) == 1 else jnp.concatenate(found, axis=0)


def product(src, weight, turned, tile=256):
    def run(places, store):
        width = weight.shape[0] if turned else weight.shape[1]

        def body(t, carry):
            cols = lanes(t * tile, tile)
            x = cat_rows(src, places)
            store(cols, mm_nt(x, weight[cols, :]) if turned else mm(x, weight[:, cols]))
            return carry

        lax.fori_loop(0, width // tile, body, 0)

    return run


def scatter_all(g, scatter, run, mine, tpart):
    size, step = scatter.size, scatter.step
    for p in range(scatter.parts):
        here = scatter.rows(p)

        def put(cols, value):
            tpart[:, cols] = value[:step]
            scatter.out_near[0, here, cols] = value[step:].astype(BF)

        run([(at_rows(b, size, p * step, step), step) for b in (g.across, g.far)], put)
        scatter.close(0, p).start()
        scatter.close(0, p).wait_recv()
        scatter.out_over[here, :] = (tpart[...] + scatter.in_near[0, here, :].astype(F32)).astype(BF)
        scatter.link(p).start()

    def put_beside(cols, value):
        scatter.out_near[1, :, cols] = value.astype(BF)

    run([(at_rows(g.beside, size, 0, size), size)], put_beside)
    for p in range(scatter.parts):
        scatter.close(1, p).start()

    def put_mine(cols, value):
        mine[:, cols] = value

    run([(at_rows(g.mine, size, 0, size), size)], put_mine)


def gather_everything(gather):
    gather.wait_beside()
    for p in range(gather.parts):
        gather.wait_part(p)
    for p in range(gather.parts):
        gather.wait_far(p)


def doc_starts(lengths, places):
    end = jnp.int32(0)
    start = jnp.zeros_like(places)
    for d in range(lengths.shape[1]):
        end = end + lengths[0, d]
        start = jnp.where(places >= end, end, start)
    return start


def conv_taps(gated, within, taps):
    total = gated.shape[0]
    summed = taps[0] * gated
    for j in range(1, len(taps)):
        summed = summed + taps[j] * jnp.where(within >= j, pltpu.roll(gated, j, 0), 0.0)
    return summed


def conv_forward_kernel(
    lengths, x_ref, gain_ref, taps_ref, win_hbm, wout_hbm, out_ref, block_ref, n_hbm, p_hbm,
    win, wout, full, nf, proj, low, mixed, tpart, mine, n_near, n_over, n_on, o_near, i_near, o_over, i_over,
    s_near, s_over, wsem, osem, bg,
):
    g = Group(bg.others)
    g.greet()
    size, width = out_ref.shape
    total, chans = x_ref.shape[0], wout.shape[0]
    loads = start_all([(win_hbm, win), (wout_hbm, wout)], wsem)
    gather = Columns(g, full, n_near, n_over, n_on)
    scatter = Scatter(g, o_near, i_near, o_over, i_over, s_near, s_over, size)
    full[:, lanes(g.mine * chans, chans)] = x_ref[...]
    g.meet()
    gather.start()
    bg.step(0)
    gather_everything(gather)
    wait_all(loads)

    def project(t, carry):
        rows = at_rows(t, size, 0, size)
        n = normalise(full[rows, :].astype(F32), gain_ref[...]).astype(BF)
        nf[rows, :] = n
        p = mm(n, win[...])
        proj[rows, :] = p
        low[rows, :] = p.astype(BF)
        return carry

    lax.fori_loop(0, total // size, project, 0)
    saves = start_all([(nf, n_hbm), (low, p_hbm)], osem)
    places = lax.broadcasted_iota(jnp.int32, (total, LANES), 0)
    within = places - doc_starts(lengths, places)
    for k in range(chans // LANES):
        b, c, x = (proj[:, pl.ds(i * chans + k * LANES, LANES)] for i in range(3))
        taps = [taps_ref[pl.ds(j, 1), pl.ds(k * LANES, LANES)] for j in range(taps_ref.shape[0])]
        mixed[:, pl.ds(k * LANES, LANES)] = (c * conv_taps(b * x, within, taps)).astype(BF)
    scatter_all(g, scatter, product(mixed, wout, False), mine, tpart)
    bg.step(1)
    own = full[at_rows(g.mine, size, 0, size), :]
    block_ref[...] = own
    for p in range(scatter.parts):
        here = scatter.rows(p)
        scatter.close(1, p).wait_recv()
        scatter.link(p).wait_recv()
        out_ref[here, :] = (
            block_ref[here, :].astype(F32) + mine[here, :] + i_near[1, here, :].astype(F32) + i_over[here, :].astype(F32)
        )
    bg.step(2)
    gather.finish()
    scatter.wait_all_sends()
    wait_all(saves)
    bg.step(3)


def conv_forward(lengths, x, gain, taps, win, wout, ident, tasks=(), parts=PARTS):
    total, chans = x.shape
    width = wout.shape[1]
    size = total // 4
    return hosted(
        conv_forward_kernel, ident, "conv_forward", [lengths, x, gain, taps, win, wout],
        [SCALARS, INV, INV, INV, HBM, HBM],
        [
            shaped((size, width), F32), shaped((size, width), BF), shaped((total, width), BF), shaped((total, 3 * chans), BF),
        ],
        [INV, INV, HBM, HBM],
        [
            pltpu.VMEM((width, 3 * chans), BF), pltpu.VMEM((chans, width), BF), pltpu.VMEM((total, width), BF),
            pltpu.VMEM((total, width), BF), pltpu.VMEM((total, 3 * chans), F32), pltpu.VMEM((total, 3 * chans), BF),
            pltpu.VMEM((total, chans), BF), pltpu.VMEM((size // parts, width), F32), pltpu.VMEM((size, width), F32),
            *gather_scratch(parts), *scatter_scratch(size, width, parts), DMA((2,)), DMA((2,)),
        ],
        tasks, 8 * total * width * chans, 2**24,
    )


def conv_backward_kernel(
    lengths, dh_ref, h_ref, gain_ref, taps_ref, win_hbm, wout_hbm, n_hbm, p_hbm, out_ref, gg_ref, gt_ref, gin_hbm, gout_hbm,
    win, wout, nf, low, dz, dy, mixed, dproj, gin, gout, tpart, mine, n_near, n_over, n_on, o_near, i_near, o_over, i_over,
    s_near, s_over, wsem, osem, bg,
):
    g = Group(bg.others)
    g.greet()
    size, width = dh_ref.shape
    total, chans = 4 * size, wout.shape[0]
    loads = start_all([(wout_hbm, wout), (p_hbm, low), (win_hbm, win), (n_hbm, nf)], wsem)
    gather = Gather(g, dz, size, n_near, n_over, n_on)
    scatter = Scatter(g, o_near, i_near, o_over, i_over, s_near, s_over, size)
    dz[at_rows(g.mine, size, 0, size), :] = dh_ref[...].astype(BF)
    g.meet()
    gather.start()
    bg.step(0)
    wait_all(loads)
    places = lax.broadcasted_iota(jnp.int32, (total, LANES), 0)
    within = places - doc_starts(lengths, places)
    gather_everything(gather)

    def project(t, carry):
        rows = at_rows(t, size, 0, size)
        dy[rows, :] = mm_nt(dz[rows, :], wout[...])
        return carry

    lax.fori_loop(0, total // size, project, 0)
    for k in range(chans // LANES):
        b, c, x = (low[:, pl.ds(i * chans + k * LANES, LANES)].astype(F32) for i in range(3))
        here = pl.ds(k * LANES, LANES)
        taps = [taps_ref[pl.ds(j, 1), here] for j in range(taps_ref.shape[0])]
        gated = b * x
        summed = conv_taps(gated, within, taps)
        d = dy[:, here]
        mixed[:, here] = (c * summed).astype(BF)
        ds = d * c
        dg = taps[0] * ds
        gt_ref[pl.ds(0, 1), here] = jnp.sum(ds * gated, axis=0, keepdims=True)
        for j in range(1, len(taps)):
            masked = jnp.where(within >= j, ds, 0.0)
            dg = dg + taps[j] * pltpu.roll(masked, total - j, 0)
            gt_ref[pl.ds(j, 1), here] = jnp.sum(masked * pltpu.roll(gated, j, 0), axis=0, keepdims=True)
        dproj[:, pl.ds(k * LANES, LANES)] = (dg * x).astype(BF)
        dproj[:, pl.ds(chans + k * LANES, LANES)] = (d * summed).astype(BF)
        dproj[:, pl.ds(2 * chans + k * LANES, LANES)] = (dg * b).astype(BF)
    scatter_all(g, scatter, product(dproj, win, True), mine, tpart)
    put_columns(gout, 0, mm_tn(mixed[...], dz[...]).astype(BF))
    save = pltpu.make_async_copy(gout, gout_hbm, osem.at[0])
    save.start()
    for t in range(width // 256):
        put_rows(gin, t * 256, mm_tn(nf[:, pl.ds(t * 256, 256)], dproj[...]).astype(BF))
    more = pltpu.make_async_copy(gin, gin_hbm, osem.at[1])
    more.start()
    bg.step(1)
    close_scatter(scatter, mine, dh_ref, h_ref, gain_ref, out_ref, gg_ref)
    gather.finish()
    scatter.wait_all_sends()
    save.wait()
    more.wait()
    bg.step(2)
    bg.step(3)


def conv_backward(lengths, dh, h, gain, taps, win, wout, n, p, pieces, ident, tasks=(), parts=PARTS):
    size, width = dh.shape
    total, chans = 4 * size, wout.shape[0]
    each = width // pieces
    return hosted(
        conv_backward_kernel, ident, "conv_backward", [lengths, dh, h, gain, taps, win, wout, n, p],
        [SCALARS, INV, INV, INV, INV, HBM, HBM, HBM, HBM],
        [
            shaped((size, width), F32), shaped((1, width), F32), shaped(taps.shape, F32),
            shaped((pieces, each, 3 * chans), BF), shaped((pieces, chans, each), BF),
        ],
        [INV, INV, INV, HBM, HBM],
        [
            pltpu.VMEM((width, 3 * chans), BF), pltpu.VMEM((chans, width), BF), pltpu.VMEM((total, width), BF),
            pltpu.VMEM((total, 3 * chans), BF), pltpu.VMEM((total, width), BF), pltpu.VMEM((total, chans), F32),
            pltpu.VMEM((total, chans), BF), pltpu.VMEM((total, 3 * chans), BF), pltpu.VMEM((pieces, each, 3 * chans), BF),
            pltpu.VMEM((pieces, chans, each), BF), pltpu.VMEM((size // parts, width), F32), pltpu.VMEM((size, width), F32),
            *gather_scratch(parts), *scatter_scratch(size, width, parts), DMA((4,)), DMA((2,)),
        ],
        tasks, 16 * total * width * chans, 2**24,
    )


def head_sums(values, head):
    width = values.shape[1]
    a = lax.broadcasted_iota(jnp.int32, (width, width), 0) // head
    b = lax.broadcasted_iota(jnp.int32, (width, width), 1) // head
    same = jnp.where(a == b, 1.0, 0.0).astype(BF)
    high = values.astype(BF)
    low = (values - high.astype(F32)).astype(BF)
    return mm(high, same) + mm(low, same)


def turn(values, head):
    width = values.shape[1]
    lane = lax.broadcasted_iota(jnp.int32, values.shape, 1)
    return jnp.where(
        lane % head < head // 2, pltpu.roll(values, width - head // 2, 1), pltpu.roll(values, head // 2, 1)
    )


def wide(table, width):
    return jnp.concatenate([table] * (width // table.shape[1]), axis=1)


def norm_turn(raw, gain, cosine, sine, head):
    inverse = lax.rsqrt(head_sums(raw * raw, head) * (1.0 / head) + epsilon)
    v = raw * inverse * gain
    return v * wide(cosine, raw.shape[1]) + turn(v, head) * wide(sine, raw.shape[1])


def norm_turn_back(d, raw, gain, cosine, sine, head):
    d = d * wide(cosine, raw.shape[1]) - turn(d, head) * wide(sine, raw.shape[1])
    inverse = lax.rsqrt(head_sums(raw * raw, head) * (1.0 / head) + epsilon)
    scaled = d * gain
    inner = head_sums(scaled * raw, head) * (1.0 / head)
    grad_gain = jnp.sum(d * raw * inverse, axis=0, keepdims=True)
    return inverse * scaled - raw * (inverse * inverse * inverse * inner), grad_gain


def score_tile(q, k, starts, first_key, first_query, scale):
    raw = mm_nt(k, q) * scale
    key = first_key + lax.broadcasted_iota(jnp.int32, raw.shape, 0)
    query = first_query + lax.broadcasted_iota(jnp.int32, (1, starts.shape[1]), 1)
    copies = raw.shape[1] // starts.shape[1]
    allowed = (key <= wide(query, raw.shape[1])) & (key >= wide(starts, raw.shape[1]))
    return jnp.where(allowed, raw, -1e30)


def softmax_tile(scores):
    top = jnp.max(scores, axis=0, keepdims=True)
    weights = jnp.exp(scores - top)
    return weights / jnp.sum(weights, axis=0, keepdims=True)


def stack_heads(values, head):
    return jnp.concatenate([values[:, i * head : (i + 1) * head] for i in range(values.shape[1] // head)], axis=0)


def attention_tiles(total, tile):
    back = -(-MOST_DOC // tile)
    return [(i * tile, max(0, i - back) * tile, (i + 1) * tile) for i in range(total // tile)]


def attention_forward_kernel(
    head, lengths, h_ref, gain_ref, qgain_ref, kgain_ref, cos_ref, sin_ref, wq_hbm, wkv_hbm, wo_hbm,
    out_ref, n_hbm, raw_hbm, ready_hbm, o_hbm,
    w, wo, nf, low, ready, vt, o, tpart, mine, n_near, n_over, n_on, o_near, i_near, o_over, i_over,
    s_near, s_over, wsem, osem, bg,
):
    g = Group(bg.others)
    g.greet()
    size, width = h_ref.shape
    total, qw = 4 * size, wo.shape[0]
    kw = (w.shape[1] - qw) // 2
    loads = start_all([(wq_hbm, w.at[:, pl.ds(0, qw)]), (wkv_hbm, w.at[:, pl.ds(qw, 2 * kw)]), (wo_hbm, wo)], wsem)
    gather = Gather(g, nf, size, n_near, n_over, n_on)
    scatter = Scatter(g, o_near, i_near, o_over, i_over, s_near, s_over, size)
    parts, step = gather.parts, gather.step
    nf[at_rows(g.mine, size, 0, size), :] = normalise(h_ref[...], gain_ref[...]).astype(BF)
    g.meet()
    gather.start()
    bg.step(0)
    wait_all(loads)

    def project(block):
        rows = at_rows(block, size, 0, size)
        raw = mm(nf[rows, :], w[...])
        low[rows, :] = raw.astype(BF)
        cosine, sine = cos_ref[rows, :], sin_ref[rows, :]
        ready[rows, pl.ds(0, qw)] = norm_turn(raw[:, :qw], qgain_ref[...], cosine, sine, head).astype(BF)
        ready[rows, pl.ds(qw, kw)] = norm_turn(raw[:, qw : qw + kw], kgain_ref[...], cosine, sine, head).astype(BF)
        ready[rows, pl.ds(qw + kw, kw)] = raw[:, qw + kw :].astype(BF)

    project(g.mine)
    gather.wait_beside()
    project(g.beside)
    for p in range(parts):
        gather.wait_part(p)
    for p in range(parts):
        gather.wait_far(p)

    def rest(i, carry):
        project(jnp.where(i == 0, g.across, g.far))
        return carry

    lax.fori_loop(0, 2, rest, 0)
    bg.step(1)
    saves = start_all([(nf, n_hbm), (low, raw_hbm), (ready, ready_hbm)], osem)
    vt[...] = jnp.transpose(ready[:, pl.ds(qw + kw, kw)].astype(F32)).astype(BF)
    groups = qw // kw
    tile = 256
    scale = head ** (-0.5)
    starts = doc_starts(lengths, lax.broadcasted_iota(jnp.int32, (1, total), 1))
    for first, low_key, high_key in attention_tiles(total, tile):
        keys = pl.ds(low_key, high_key - low_key)
        for kv in range(kw // head):
            q = stack_heads(ready[pl.ds(first, tile), pl.ds(kv * groups * head, groups * head)], head)
            k = ready[keys, pl.ds(qw, kw)][:, kv * head : (kv + 1) * head]
            p = softmax_tile(score_tile(q, k, starts[:, first : first + tile], low_key, first, scale)).astype(BF)
            ot = mm(vt[pl.ds(kv * head, head), keys], p)
            joined = jnp.concatenate([ot[:, i * tile : (i + 1) * tile] for i in range(groups)], axis=0)
            o[pl.ds(first, tile), pl.ds(kv * groups * head, groups * head)] = jnp.transpose(joined).astype(BF)
    bg.step(2)
    save_o = pltpu.make_async_copy(o, o_hbm, osem.at[3])
    save_o.start()
    scatter_all(g, scatter, product(o, wo, False), mine, tpart)
    for p in range(parts):
        here = scatter.rows(p)
        scatter.close(1, p).wait_recv()
        scatter.link(p).wait_recv()
        out_ref[here, :] = (
            h_ref[here, :] + mine[here, :] + i_near[1, here, :].astype(F32) + i_over[here, :].astype(F32)
        )
    gather.finish()
    scatter.wait_all_sends()
    wait_all(saves)
    save_o.wait()
    bg.step(3)


def attention_forward(head, lengths, h, gain, qgain, kgain, cosine, sine, wq, wkv, wo, ident, tasks=(), parts=PARTS):
    size, width = h.shape
    total, qw = 4 * size, wo.shape[0]
    kw = wkv.shape[1] // 2
    every = qw + 2 * kw
    return hosted(
        functools.partial(attention_forward_kernel, head), ident, "attention_forward",
        [lengths, h, gain, qgain, kgain, cosine, sine, wq, wkv, wo], [SCALARS] + [INV] * 6 + [HBM] * 3,
        [
            shaped((size, width), F32), shaped((total, width), BF), shaped((total, every), BF), shaped((total, every), BF),
            shaped((total, qw), BF),
        ],
        [INV] + [HBM] * 4,
        [
            pltpu.VMEM((width, every), BF), pltpu.VMEM((qw, width), BF), pltpu.VMEM((total, width), BF),
            pltpu.VMEM((total, every), BF), pltpu.VMEM((total, every), BF),
            pltpu.VMEM((kw, total), BF), pltpu.VMEM((total, qw), BF),
            pltpu.VMEM((size // parts, width), F32), pltpu.VMEM((size, width), F32),
            *gather_scratch(parts), *scatter_scratch(size, width, parts), DMA((3,)), DMA((4,)),
        ],
        tasks, 2 * total * width * (every + qw), 2**24,
    )


def attention_backward_kernel(
    head, lengths, dh_ref, h_ref, gain_ref, qgain_ref, kgain_ref, cos_ref, sin_ref, wq_hbm, wkv_hbm, wo_hbm,
    n_hbm, raw_hbm, ready_hbm, o_hbm, out_ref, gg_ref, gq_ref, gk_ref, gw_hbm, gwo_hbm,
    w, wo, nf, low, ready, kt, o, dz, do, dq, dkv, dlow, gw, gwo, tpart, mine,
    n_near, n_over, n_on, o_near, i_near, o_over, i_over, s_near, s_over, wsem, osem, bg,
):
    g = Group(bg.others)
    g.greet()
    size, width = h_ref.shape
    total, qw = 4 * size, wo.shape[0]
    kw = (w.shape[1] - qw) // 2
    loads = start_all(
        [
            (ready_hbm, ready), (wo_hbm, wo), (o_hbm, o), (raw_hbm, low), (wq_hbm, w.at[:, pl.ds(0, qw)]),
            (wkv_hbm, w.at[:, pl.ds(qw, 2 * kw)]), (n_hbm, nf),
        ],
        wsem,
    )
    gather = Gather(g, dz, size, n_near, n_over, n_on)
    scatter = Scatter(g, o_near, i_near, o_over, i_over, s_near, s_over, size)
    dz[at_rows(g.mine, size, 0, size), :] = dh_ref[...].astype(BF)
    g.meet()
    gather.start()
    bg.step(0)
    wait_all(loads)
    kt[...] = jnp.transpose(ready[:, pl.ds(qw, kw)].astype(F32)).astype(BF)
    dkv[...] = jnp.zeros_like(dkv)
    gather_everything(gather)

    def project(t, carry):
        rows = at_rows(t, size, 0, size)
        do[rows, :] = mm_nt(dz[rows, :], wo[...]).astype(BF)
        return carry

    lax.fori_loop(0, total // size, project, 0)
    groups = qw // kw
    tile = 256
    scale = head ** (-0.5)
    starts = doc_starts(lengths, lax.broadcasted_iota(jnp.int32, (1, total), 1))
    for first, low_key, high_key in attention_tiles(total, tile):
        keys = pl.ds(low_key, high_key - low_key)
        for kv in range(kw // head):
            cols = pl.ds(kv * groups * head, groups * head)
            lane = slice(kv * head, (kv + 1) * head)
            q = stack_heads(ready[pl.ds(first, tile), cols], head)
            k, v = ready[keys, pl.ds(qw, kw)][:, lane], ready[keys, pl.ds(qw + kw, kw)][:, lane]
            p = softmax_tile(score_tile(q, k, starts[:, first : first + tile], low_key, first, scale))
            d = stack_heads(do[pl.ds(first, tile), cols], head)
            dp = mm_nt(v, d)
            inner = jnp.sum(p * dp, axis=0, keepdims=True)
            ds = (p * (dp - inner)).astype(BF)
            both = jnp.concatenate([mm(ds, q) * scale, mm(p.astype(BF), d)], axis=1)
            dkv[kv, keys, :] += both
            dqt = mm(kt[pl.ds(kv * head, head), keys], ds) * scale
            joined = jnp.concatenate([dqt[:, i * tile : (i + 1) * tile] for i in range(groups)], axis=0)
            dq[pl.ds(first, tile), cols] = jnp.transpose(joined)
    bg.step(1)
    gq_ref[...] = jnp.zeros_like(gq_ref)
    gk_ref[...] = jnp.zeros_like(gk_ref)

    def finish(t, carry):
        rows = at_rows(t, size, 0, size)
        cosine, sine = cos_ref[rows, :], sin_ref[rows, :]
        d, gq = norm_turn_back(dq[rows, :], low[rows, pl.ds(0, qw)].astype(F32), qgain_ref[...], cosine, sine, head)
        gq_ref[...] += gq
        dlow[rows, pl.ds(0, qw)] = d.astype(BF)
        pairs = [dkv[kv, rows, :] for kv in range(kw // head)]
        dk = jnp.concatenate([x[:, :head] for x in pairs], axis=1)
        dv = jnp.concatenate([x[:, head:] for x in pairs], axis=1)
        d, gk = norm_turn_back(dk, low[rows, pl.ds(qw, kw)].astype(F32), kgain_ref[...], cosine, sine, head)
        gk_ref[...] += gk
        dlow[rows, pl.ds(qw, kw)] = d.astype(BF)
        dlow[rows, pl.ds(qw + kw, kw)] = dv.astype(BF)
        return carry

    lax.fori_loop(0, total // size, finish, 0)
    scatter_all(g, scatter, product(dlow, w, True), mine, tpart)
    put_columns(gwo, 0, mm_tn(o[...], dz[...]).astype(BF))
    save = pltpu.make_async_copy(gwo, gwo_hbm, osem.at[0])
    save.start()
    for t in range(width // 256):
        put_rows(gw, t * 256, mm_tn(nf[:, pl.ds(t * 256, 256)], dlow[...]).astype(BF))
    more = pltpu.make_async_copy(gw, gw_hbm, osem.at[1])
    more.start()
    bg.step(2)
    close_scatter(scatter, mine, dh_ref, h_ref, gain_ref, out_ref, gg_ref)
    gather.finish()
    scatter.wait_all_sends()
    save.wait()
    more.wait()
    bg.step(3)


def attention_backward(
    head, lengths, dh, h, gain, qgain, kgain, cosine, sine, wq, wkv, wo, n, raw, ready, o, pieces, ident, tasks=(),
    parts=PARTS,
):
    size, width = h.shape
    total, qw = 4 * size, wo.shape[0]
    kw = wkv.shape[1] // 2
    every = qw + 2 * kw
    each = width // pieces
    return hosted(
        functools.partial(attention_backward_kernel, head), ident, "attention_backward",
        [lengths, dh, h, gain, qgain, kgain, cosine, sine, wq, wkv, wo, n, raw, ready, o], [SCALARS] + [INV] * 7 + [HBM] * 7,
        [
            shaped((size, width), F32), shaped((1, width), F32), shaped((1, qw), F32), shaped((1, kw), F32),
            shaped((pieces, each, every), BF), shaped((pieces, qw, each), BF),
        ],
        [INV, INV, INV, INV, HBM, HBM],
        [
            pltpu.VMEM((width, every), BF), pltpu.VMEM((qw, width), BF), pltpu.VMEM((total, width), BF),
            pltpu.VMEM((total, every), BF), pltpu.VMEM((total, every), BF), pltpu.VMEM((kw, total), BF),
            pltpu.VMEM((total, qw), BF), pltpu.VMEM((total, width), BF), pltpu.VMEM((total, qw), BF),
            pltpu.VMEM((total, qw), F32), pltpu.VMEM((kw // head, total, 2 * head), F32), pltpu.VMEM((total, every), BF),
            pltpu.VMEM((pieces, each, every), BF), pltpu.VMEM((pieces, qw, each), BF),
            pltpu.VMEM((size // parts, width), F32), pltpu.VMEM((size, width), F32),
            *gather_scratch(parts), *scatter_scratch(size, width, parts), DMA((7,)), DMA((2,)),
        ],
        tasks, 4 * total * width * (every + qw), 2**25,
    )


def tail_kernel(token_ref, done_ref, bg):
    g = Group(bg.others)
    g.greet()
    g.meet()
    done_ref[...] = token_ref[...]
    for k in range(4):
        bg.step(k)


def tail(token, ident, tasks):
    return hosted(
        tail_kernel, ident, "tail", [token], [INV], [shaped(token.shape, token.dtype)], [INV], [], tasks, 0, 2**22
    )


rope_base = 1000000.0
TP = ("c", "zl")
DP = ("r", "s", "zh")


def doc_positions(lengths_row, length):
    count = lengths_row.shape[0]
    upto = jnp.arange(count)[:, None] >= jnp.arange(count)[None, :]
    doc_ends = jnp.sum(jnp.where(upto, lengths_row[None, :], 0), axis=1)
    places = jnp.arange(length, dtype=jnp.int32)
    passed = places[:, None] >= doc_ends[None, :]
    return places - jnp.max(jnp.where(passed, doc_ends[None, :], 0), axis=1)


def rope_tables(position, head_dim):
    half_dim = head_dim // 2
    inverse = rope_base ** (-2.0 * jnp.arange(half_dim, dtype=F32) / head_dim)
    angles = position.astype(F32)[:, None] * inverse[None, :]
    cosine, sine = jnp.cos(angles), jnp.sin(angles)
    copies = LANES // head_dim
    return (
        jnp.concatenate([cosine, cosine] * copies, axis=1),
        jnp.concatenate([-sine, sine] * copies, axis=1),
    )


def swap(x):
    return lax.ppermute(x, ("c", "zh"), [(0, 0), (1, 2), (2, 1), (3, 3)])


def gather_dp(shard, axis):
    return lax.all_gather(swap(shard), DP, axis=axis, tiled=True)


def scatter_dp(partial, axis):
    return swap(lax.psum_scatter(partial, DP, scatter_dimension=axis, tiled=True)).astype(F32)


def local(
    planes, tokens, doc_lengths, grad_out, norm_gains, head_gains, conv_in, conv_kernel, conv_out,
    query_w, kv_w, out_w, gate_up, down,
):
    length = tokens.shape[0]
    head_dim = head_gains.shape[1]
    quarter = lax.axis_index("c") * 2 + lax.axis_index("zl")
    rows = length // 4
    lengths = swap(doc_lengths)
    cosine, sine = rope_tables(doc_positions(lengths[0], length), head_dim)
    conv_in = swap(conv_in.reshape(conv_in.shape[0], -1))
    conv_kernel = swap(conv_kernel)
    conv_out = swap(conv_out)
    query_w = swap(query_w)
    kv_w = swap(kv_w.reshape(kv_w.shape[0], -1))
    out_w = swap(out_w)
    own_w = [gate_up[l].reshape(gate_up.shape[1], -1) for l in (0, 1)]
    own_v = [down[l] for l in (0, 1)]
    pieces = 8 if planes else 1
    kv_width = kv_w.shape[1] // 2
    qgain = jnp.tile(head_gains[0:1], (1, query_w.shape[1] // head_dim))
    kgain = jnp.tile(head_gains[1:2], (1, kv_width // head_dim))
    gain = [norm_gains[i : i + 1] for i in range(4)]
    ws, vs = [None, None], [None, None]

    def take_w(l, pieces_of):
        ws[l] = pieces_of.reshape(-1, pieces_of.shape[-1])

    if not planes:
        for l in (0, 1):
            take_w(l, gather_dp(own_w[l], 0))
            vs[l] = gather_dp(own_v[l], 1)[None]

    up_full = lax.all_gather(swap(grad_out), TP, axis=1, tiled=True)
    (h1, x_block, n0, projected), got = conv_forward(
        lengths, swap(tokens), gain[0], conv_kernel, conv_in, conv_out, 0, list(([Fetch(own_w[0]), Fetch(own_v[0])] if planes else ()))
    )
    if planes:
        take_w(0, got[0])
        vs[0] = got[1]
    (h2, n1, hidden0), got = ffn_forward(h1, gain[1], ws[0], vs[0], 1, list(([Fetch(own_v[1])] if planes else ())))
    if planes:
        vs[1] = got[0]
    (h3, n2, raw, ready, attended), got = attention_forward(
        head_dim, lengths, h2, gain[2], qgain, kgain, cosine, sine, query_w, kv_w, out_w, 2, list(([Fetch(own_w[1])] if planes else ()))
    )
    if planes:
        take_w(1, got[0])
    (h4, n3, hidden1), _ = ffn_forward(h3, gain[3], ws[1], vs[1], 3)
    output = swap(lax.all_to_all(h4.astype(BF), TP, 1, 0, tiled=True))

    def halves(grad):
        half = grad.shape[1] // 2
        return [Reduce(grad, 0, half), Reduce(grad, half, half)]

    def whole(grad):
        return [Reduce(grad, 0, grad.shape[1])]

    dh4 = lax.dynamic_slice_in_dim(up_full, quarter * rows, rows, 0).astype(F32)
    (dh3, gain3, gw1, gv1), _ = ffn_backward(dh4, h3, gain[3], up_full, ws[1], vs[1], n3, hidden1, 4)
    (dh2, gain2, gq, gk, gqkv, gow), sums_w1 = attention_backward(
        head_dim, lengths, dh3, h2, gain[2], qgain, kgain, cosine, sine, query_w, kv_w, out_w, n2, raw, ready, attended,
        pieces, 5, list((halves(gw1) if planes else ())),
    )
    (dh1, gain1, gw0, gv0), sums_v1 = ffn_backward(
        dh2, h1, gain[1], None, ws[0], vs[0], n1, hidden0, 6, list((whole(gv1) + whole(gqkv) + whole(gow) if planes else ()))
    )
    (dh0, gain0, gtaps, gci, gco), sums_w0 = conv_backward(
        lengths, dh1, x_block.astype(F32), gain[0], conv_kernel, conv_in, conv_out, n0, projected, pieces, 7,
        list((halves(gw0) if planes else ())),
    )
    grad_tokens = swap(lax.all_to_all(dh0, TP, 1, 0, tiled=True))
    if planes:
        _, (gv0, gci, gco) = tail(gain0, 8, whole(gv0) + whole(gci) + whole(gco))
        gv1, gqkv, gow = sums_v1
        gw0, gw1 = (jnp.concatenate(sums, axis=0) for sums in (sums_w0, sums_w1))
    else:
        gw0, gw1, gci, gqkv = (scatter_dp(g[0], 0) for g in (gw0, gw1, gci, gqkv))
        gv0, gv1, gco, gow = (scatter_dp(g[0], 1) for g in (gv0, gv1, gco, gow))
    kernel_full = jnp.zeros((conv_kernel.shape[0], norm_gains.shape[1]), F32)
    kernel_full = lax.dynamic_update_slice_in_dim(kernel_full, gtaps, quarter * conv_kernel.shape[1], 1)
    head_grads = jnp.stack([jnp.sum(x.reshape(-1, head_dim), axis=0) for x in (gq, gk)])
    gains, heads, kernels = lax.psum(
        (jnp.concatenate([gain0, gain1, gain2, gain3]), head_grads, kernel_full), ("r", "s", "c", "zh", "zl")
    )
    return (
        output,
        grad_tokens,
        gains,
        heads,
        gci.reshape(-1, 3, conv_kernel.shape[1]),
        kernels,
        gco,
        gqkv[:, : query_w.shape[1]],
        gqkv[:, query_w.shape[1] :].reshape(-1, 2, kv_width),
        gow,
        jnp.stack([gw0, gw1]).reshape(2, gate_up.shape[1], 2, -1),
        jnp.stack([gv0, gv1]),
    )


def solution(mesh):
    devices = mesh.devices
    dp, tp = devices.shape
    inner = Mesh(devices.reshape(dp // 4, 2, 2, 2, tp // 2), ("r", "s", "c", "zh", "zl"))
    D = ("r", "s", "c")
    T = ("zh", "zl")
    return jax.shard_map(
        functools.partial(local, dp == 8),
        mesh=inner,
        in_specs=(
            P(D, T), P(D, None), P(D, T), P(), P(), P(None, None, T), P(None, T), P(T, None),
            P(None, T), P(None, None, T), P(T, None), P(None, D, None, T), P(None, T, D),
        ),
        out_specs=(
            P(D, T), P(D, T), P(), P(), P(D, None, T), P(), P(T, D), P(D, T), P(D, None, T),
            P(T, D), P(None, D, None, T), P(None, T, D),
        ),
        check_vma=False,
    )
```

```python
import functools
import jax
import jax.numpy as jnp
from jax import lax
from jax.experimental import pallas as pl
from jax.experimental.pallas import tpu as pltpu
from jax.sharding import Mesh, PartitionSpec as P

epsilon = 1e-05
BF = jnp.bfloat16
F32 = jnp.float32
MESH = pl.DeviceIdType.MESH
DMA = pltpu.SemaphoreType.DMA
HBM = pl.BlockSpec(memory_space=pl.ANY)
INV = pl.BlockSpec(memory_space=pltpu.VMEM)
PARTS = 2
LANES = 128


class Group:
    def __init__(self, others=(), calls=True):
        c, z = lax.axis_index("c"), lax.axis_index("zl")
        self.partner, self.twin = {"c": 1 - c}, {"zl": 1 - z}
        self.mine, self.beside = 2 * c + z, 2 * (1 - c) + z
        self.across, self.far = 2 * c + (1 - z), 2 * (1 - c) + (1 - z)
        self.known = [self.partner, self.twin, *others]
        self.c, self.z = c, z
        self.barrier = pltpu.get_barrier_semaphore() if calls else None

    def greet(self):
        for other in self.known:
            pl.semaphore_signal(self.barrier, inc=1, device_id=other, device_id_type=MESH)

    def meet(self):
        pl.semaphore_wait(self.barrier, len(self.known))


def at_rows(block, size, start, count):
    return pl.ds(pl.multiple_of(block * size + start, 16), count)


def send(src, dst, sems, index, where):
    return pltpu.make_async_remote_copy(
        src_ref=src, dst_ref=dst, send_sem=sems.at[0, index], recv_sem=sems.at[1, index],
        device_id=where, device_id_type=MESH,
    )


class Gather:
    def __init__(self, group, full, size, near, over, onward):
        self.g, self.full, self.size, self.parts = group, full, size, over.shape[1]
        self.near, self.over, self.onward = near, over, onward
        self.step = size // self.parts

    def view(self, block, part):
        return self.full.at[at_rows(block, self.size, part * self.step, self.step)]

    def link(self, part, block):
        v = self.view(block, part)
        return send(v, v, self.over, part, self.g.twin)

    def close(self, part, block):
        v = self.view(block, part)
        return send(v, v, self.near, part, self.g.partner)

    def pass_on(self, part, block):
        v = self.view(block, part)
        return send(v, v, self.onward, part, self.g.partner)

    def start(self):
        for p in range(self.parts):
            self.link(p, self.g.mine).start()
            self.close(p, self.g.mine).start()

    def wait_beside(self):
        for p in range(self.parts):
            self.close(p, self.g.beside).wait_recv()

    def wait_part(self, p):
        self.link(p, self.g.across).wait_recv()
        self.pass_on(p, self.g.across).start()

    def wait_far(self, p):
        self.pass_on(p, self.g.far).wait_recv()

    def finish(self):
        for p in range(self.parts):
            self.link(p, self.g.mine).wait_send()
            self.close(p, self.g.mine).wait_send()
            self.pass_on(p, self.g.across).wait_send()


class Scatter:
    def __init__(self, group, out_near, in_near, out_over, in_over, near, over, size):
        self.g, self.size, self.parts = group, size, over.shape[1]
        self.out_near, self.in_near, self.out_over, self.in_over = out_near, in_near, out_over, in_over
        self.near, self.over = near, over
        self.step = size // self.parts

    def rows(self, part):
        return pl.ds(part * self.step, self.step)

    def close(self, which, part):
        r = self.rows(part)
        return send(self.out_near.at[which, r], self.in_near.at[which, r], self.near, which * self.parts + part, self.g.partner)

    def link(self, part):
        r = self.rows(part)
        return send(self.out_over.at[r], self.in_over.at[r], self.over, part, self.g.twin)

    def wait_all_sends(self):
        for p in range(self.parts):
            self.close(0, p).wait_send()
            self.close(1, p).wait_send()
            self.link(p).wait_send()


def scatter_scratch(size, width, parts):
    return [
        pltpu.VMEM((2, size, width), BF), pltpu.VMEM((2, size, width), BF), pltpu.VMEM((size, width), BF),
        pltpu.VMEM((size, width), BF), DMA((2, 2 * parts)), DMA((2, parts)),
    ]


def gather_scratch(parts):
    return [DMA((2, parts)), DMA((2, parts)), DMA((2, parts))]


def normalise(h, gain):
    return h * lax.rsqrt(jnp.mean(h * h, axis=-1, keepdims=True) + epsilon) * gain


def mm(a, b):
    return jnp.dot(a, b, preferred_element_type=F32)


def mm_nt(a, b):
    return lax.dot_general(a, b, (((1,), (1,)), ((), ())), preferred_element_type=F32)


def lanes(start, width):
    return pl.ds(pl.multiple_of(start, LANES), width)


def start_all(pairs, sems):
    copies = [pltpu.make_async_copy(src, dst, sems.at[i]) for i, (src, dst) in enumerate(pairs)]
    for copy in copies:
        copy.start()
    return copies


def wait_all(copies):
    for copy in copies:
        copy.wait()


def params(ident):
    return pltpu.CompilerParams(collective_id=ident, has_side_effects=True, vmem_limit_bytes=56 * 2**20)


def shaped(shape, dtype):
    return jax.ShapeDtypeStruct(shape, dtype)


class Place:
    def __init__(self):
        self.y, self.x, self.c, self.zh = (lax.axis_index(a) for a in ("r", "s", "c", "zh"))
        self.across_x, self.across_y = {"s": 1 - self.x}, {"r": 1 - self.y}
        self.partner = {"c": 1 - self.c}
        self.plain = self.c == self.zh

    def over(self, core):
        return {"c": core, "zh": 1 - self.zh}

    def swapped(self):
        return self.over(self.zh)

    PLANES = ("x", "y")
    ENDS = ("end", "swap")
    COLUMN = ("end", "swap", "z core", "z end", "z swap")

    def called(self, name):
        z = 1 - lax.axis_index("zl")
        other, far = 1 - self.c, 1 - self.zh
        return {
            "x": self.across_x, "y": self.across_y, "end": self.over(self.c), "swap": self.over(other),
            "z core": {"c": other, "zl": z}, "z end": {"zh": far, "zl": z}, "z swap": {"c": other, "zh": far, "zl": z},
        }[name]

    def piece(self, flip_y, flip_x, a):
        y = 1 - self.y if flip_y else self.y
        x = 1 - self.x if flip_x else self.x
        return 4 * y + 2 * x + a


class Fetch:
    def __init__(self, shard, at):
        rows, cols = shard.shape
        self.at = at
        self.ins = [shard]
        self.outs = [jax.ShapeDtypeStruct((8, rows, cols), shard.dtype)]
        self.out_specs = [HBM]
        self.scratch = [DMA((9,)), DMA((8,)), DMA((1,))]

    def bind(self, ins, outs, scratch):
        (self.own,), (self.out,) = ins, outs
        self.sent, self.come, self.sem = scratch
        self.p = Place()

    def copy(self, src, piece, sent, come, where):
        return pltpu.make_async_remote_copy(
            src_ref=src, dst_ref=self.out.at[piece], send_sem=self.sent.at[sent], recv_sem=self.come.at[come],
            device_id=where, device_id_type=MESH,
        )

    def to_plane(self):
        p = self.p
        return self.copy(self.own, p.piece(0, 0, p.c), 0, p.c, p.over(p.zh))

    def to_partner(self):
        p = self.p
        return self.copy(self.own, p.piece(0, 0, p.c), 1, p.c, p.partner)

    def arrived(self, a):
        return self.copy(self.own, self.p.piece(0, 0, a), 0, a, self.p.partner).wait_recv()

    def keep(self):
        return pltpu.make_async_copy(self.own, self.out.at[self.p.piece(0, 0, self.p.c)], self.sem.at[0])

    def to_x(self, a, src):
        return self.copy(src, self.p.piece(0, 0, a), 2 + a, 2 + a, self.p.across_x)

    def to_y(self, a, src):
        return self.copy(src, self.p.piece(0, 0, a), 4 + a, 4 + a, self.p.across_y)

    def spread(self, a, src):
        self.to_x(a, src).start()
        self.to_y(a, src).start()

    def slot(self, a):
        return self.out.at[self.p.piece(0, 0, a)]

    def on_y(self):
        piece = self.p.piece(0, 1, 0)
        return self.copy(self.out.at[piece], piece, 6, 6, self.p.across_y)

    def on_x(self):
        piece = self.p.piece(1, 0, 1)
        return self.copy(self.out.at[piece], piece, 7, 7, self.p.across_x)

    def greets(self):
        return Place.PLANES + Place.ENDS

    def step(self, k):
        p = self.p
        if k == 0:

            @pl.when(p.plain)
            def _():
                self.keep().start()
                self.spread(p.c, self.own)

            @pl.when(jnp.logical_not(p.plain))
            def _():
                self.to_partner().start()

        elif k == 1:
            self.to_plane().start()

            @pl.when(p.plain)
            def _():
                self.arrived(1 - p.c)
                self.spread(1 - p.c, self.slot(1 - p.c))

        elif k == 2:

            @pl.when(jnp.logical_not(p.plain))
            def _():
                for a in (0, 1):
                    self.arrived(a)
                    self.spread(a, self.slot(a))

        elif k == 3:
            self.to_x(0, self.slot(0)).wait_recv()
            self.on_y().start()
            self.to_y(1, self.slot(1)).wait_recv()
            self.on_x().start()
        else:
            self.to_x(1, self.slot(1)).wait_recv()
            self.to_y(0, self.slot(0)).wait_recv()
            self.on_y().wait()
            self.on_x().wait()
            self.to_plane().wait_send()
            for a in (0, 1):
                self.to_x(a, self.slot(a)).wait_send()
                self.to_y(a, self.slot(a)).wait_send()

            @pl.when(p.plain)
            def _():
                self.keep().wait()

            @pl.when(jnp.logical_not(p.plain))
            def _():
                self.to_partner().wait_send()


class Take(Fetch):
    def __init__(self, whole, at, inside=None):
        rows, cols = whole.shape
        self.at, self.each = at, rows // 8
        self.ins = [whole]
        self.outs = [] if inside else [jax.ShapeDtypeStruct((rows, cols), whole.dtype)]
        self.out_specs = [] if inside else [HBM]
        self.scratch = [DMA((9,)), DMA((8,)), DMA((1,))]

    def bind(self, ins, outs, scratch):
        (self.own,) = ins
        self.whole = outs[0] if outs else None
        self.sent, self.come, self.sem = scratch
        self.p = Place()

    def rows(self, piece):
        return pl.ds(pl.multiple_of(piece * self.each, 16), self.each)

    def copy(self, src, piece, sent, come, where):
        return pltpu.make_async_remote_copy(
            src_ref=self.own.at[self.rows(piece)] if src is None else src, dst_ref=self.whole.at[self.rows(piece)],
            send_sem=self.sent.at[sent], recv_sem=self.come.at[come], device_id=where, device_id_type=MESH,
        )

    def to_plane(self):
        p = self.p
        return self.copy(None, p.piece(0, 0, p.c), 0, p.c, p.over(p.zh))

    def arrived(self, a):
        return self.copy(None, self.p.piece(0, 0, a), 0, a, self.p.partner).wait_recv()

    def keep(self):
        return pltpu.make_async_copy(self.own, self.whole, self.sem.at[0])

    def slot(self, a):
        return self.whole.at[self.rows(self.p.piece(0, 0, a))]

    def on_y(self):
        piece = self.p.piece(0, 1, 0)
        return self.copy(self.whole.at[self.rows(piece)], piece, 6, 6, self.p.across_y)

    def on_x(self):
        piece = self.p.piece(1, 0, 1)
        return self.copy(self.whole.at[self.rows(piece)], piece, 7, 7, self.p.across_x)

    def step(self, k):
        p = self.p
        if k == 0:

            @pl.when(p.plain)
            def _():
                self.keep().start()

        elif k == 1:
            self.to_plane().start()
        elif k == 2:

            @pl.when(jnp.logical_not(p.plain))
            def _():
                for a in (0, 1):
                    self.arrived(a)
                    self.spread(a, self.slot(a))

        elif k == 3:

            @pl.when(jnp.logical_not(p.plain))
            def _():
                self.to_x(0, self.slot(0)).wait_recv()
                self.on_y().start()
                self.to_y(1, self.slot(1)).wait_recv()
                self.on_x().start()

        else:
            self.to_plane().wait_send()

            @pl.when(p.plain)
            def _():
                self.keep().wait()

            @pl.when(jnp.logical_not(p.plain))
            def _():
                self.to_x(1, self.slot(1)).wait_recv()
                self.to_y(0, self.slot(0)).wait_recv()
                self.on_y().wait()
                self.on_x().wait()
                for a in (0, 1):
                    self.to_x(a, self.slot(a)).wait_send()
                    self.to_y(a, self.slot(a)).wait_send()


class Exchange:
    def __init__(self, src, dst, there, sems, sem, index=0):
        self.p = Place()
        self.src, self.dst, self.there, self.sems, self.sem, self.index = src, dst, there, sems, sem, index

    def stay(self):
        return pltpu.make_async_copy(self.src, self.dst, self.sem.at[self.index])

    def leave(self):
        return send(self.src, self.there, self.sems, self.index, self.p.swapped())

    def come(self):
        return send(self.src, self.dst, self.sems, self.index, self.p.swapped())

    def both(self, stay, leave):
        pl.when(self.p.plain)(stay)
        pl.when(jnp.logical_not(self.p.plain))(leave)

    def start(self):
        self.both(lambda: self.stay().start(), lambda: self.leave().start())

    def arrive(self):
        self.both(lambda: self.stay().wait(), lambda: self.come().wait_recv())

    def finish(self):
        pl.when(jnp.logical_not(self.p.plain))(lambda: self.leave().wait_send())


class Spread:
    def __init__(self, block, at, parts=2):
        rows, cols = block.shape
        self.at, self.parts = at, parts
        self.ins = [block]
        self.outs = [jax.ShapeDtypeStruct((rows, 4 * cols), block.dtype)]
        self.out_specs = [HBM]
        self.scratch = [*gather_scratch(parts), DMA((2, 1)), DMA((1,))]

    def bind(self, ins, outs, scratch):
        (self.block,), (self.full,) = ins, outs
        near, over, onward, sems, sem = scratch
        self.p, self.g = Place(), Group(calls=False)
        self.gather = Columns(self.g, self.full, near, over, onward)
        cols = self.block.shape[1]
        mine, there = (self.full.at[:, lanes(b * cols, cols)] for b in (self.g.mine, self.g.beside))
        self.exchange = Exchange(self.block, mine, there, sems, sem)

    def greets(self):
        return Place.ENDS

    def step(self, k):
        if k == 0:
            self.exchange.start()
        elif k == 1:
            self.exchange.arrive()
            self.gather.start()
        elif k == 2:
            for p in range(self.parts):
                self.gather.wait_part(p)
        elif k == 4:
            self.gather.wait_beside()
            for p in range(self.parts):
                self.gather.wait_far(p)
            self.gather.finish()
            self.exchange.finish()


class Deliver:
    def __init__(self, block, at):
        rows, width = block.shape
        self.at = at
        self.ins = [block]
        self.outs = [jax.ShapeDtypeStruct((4 * rows, width // 4), BF)]
        self.out_specs = [HBM]
        self.scratch = [pltpu.VMEM((rows, width), BF), DMA((4,)), DMA((4,)), DMA((2,))]
        if block.dtype != BF:
            self.scratch.append(pltpu.VMEM((rows, width), block.dtype))

    def bind(self, ins, outs, scratch):
        (self.block,), (self.out,) = ins, outs
        self.low, self.sent, self.come, self.sem = scratch[:4]
        self.wide = scratch[4] if len(scratch) > 4 else self.low
        self.p, self.g = Place(), Group(calls=False)

    def greets(self):
        return Place.COLUMN

    def load(self):
        return pltpu.make_async_copy(self.block, self.wide, self.sem.at[0])

    def parts(self):
        rows, width = self.low.shape
        cols = width // 4
        dst = self.out.at[at_rows(self.g.mine, rows, 0, rows)]
        for f in range(4):
            half, z = divmod(f, 2)
            here = (self.p.c == self.p.zh) & (self.p.zh == half) & (self.g.z == z)
            src = self.low.at[:, pl.ds(f * cols, cols)]
            where = {"c": self.p.zh, "zh": jnp.int32(half), "zl": jnp.int32(z)}
            yield here, pltpu.make_async_copy(src, dst, self.sem.at[1]), pltpu.make_async_remote_copy(
                src_ref=src, dst_ref=dst, send_sem=self.sent.at[f], recv_sem=self.come.at[self.g.mine],
                device_id=where, device_id_type=MESH,
            )

    def step(self, k):
        if k == 0:
            self.load().start()
        elif k == 1:
            self.load().wait()
            if self.wide is not self.low:
                self.low[...] = self.wide[...].astype(BF)
            for here, stay, leave in self.parts():
                pl.when(here)(lambda stay=stay: stay.start())
                pl.when(jnp.logical_not(here))(lambda leave=leave: leave.start())
        elif k == 4:
            rows, width = self.low.shape
            for here, stay, leave in self.parts():
                pl.when(here)(lambda stay=stay: stay.wait())
                pl.when(jnp.logical_not(here))(lambda leave=leave: leave.wait_send())
            for b in range(4):
                core, z = divmod(b, 2)
                here = (self.p.c == self.p.zh) & (self.p.c == core) & (self.g.z == z)
                come = pltpu.make_async_remote_copy(
                    src_ref=self.low.at[:, pl.ds(0, width // 4)], dst_ref=self.out.at[pl.ds(b * rows, rows)],
                    send_sem=self.sent.at[0], recv_sem=self.come.at[b], device_id=self.p.partner, device_id_type=MESH,
                )
                pl.when(jnp.logical_not(here))(lambda come=come: come.wait_recv())


class Total:
    def __init__(self, pieces, at, count, axes):
        self.at, self.count, self.axes = at, count, axes
        self.ins = pieces
        self.in_specs = [INV] * len(pieces)
        width = pieces[0].shape[1]
        self.outs = [jax.ShapeDtypeStruct((8, width), F32)]
        self.out_specs = [INV]
        self.scratch = [
            pltpu.VMEM((len(self.axes), 8, width), F32), pltpu.VMEM((len(self.axes), 8, width), F32),
            DMA((2, len(self.axes))),
        ]

    def bind(self, ins, outs, scratch):
        self.pieces, (self.out,) = ins, outs
        self.sum, self.other, self.sems = scratch
        self.p, self.g = Place(), Group(calls=False)

    def greets(self):
        return ("x",) + Place.ENDS + (("y",) if "r" in self.axes else ())

    def hop(self, i):
        axis = self.axes[i]
        return send(self.sum.at[i], self.other.at[i], self.sems, i, {axis: 1 - lax.axis_index(axis)})

    def step(self, k):
        if k == 0:
            gains, taps, heads = self.pieces[:4], self.pieces[4], self.pieces[5:]
            self.sum[0] = jnp.zeros(self.sum.shape[1:], F32)
            for i, gain in enumerate(gains):
                self.sum[0, pl.ds(i, 1), :] = gain[...]
            cols = taps.shape[1]
            self.sum[0, pl.ds(4, self.count), lanes(self.g.mine * cols, cols)] = taps[pl.ds(0, self.count), :]
            done = 0
            for head in heads:
                self.sum[0, pl.ds(7, 1), pl.ds(done, head.shape[1])] = head[...]
                done += head.shape[1]
            self.hop(0).start()
        elif k < 5:
            last = len(self.axes) if k == 4 else k
            for i in range(k - 1, last):
                self.hop(i).wait()
                value = self.sum[i] + self.other[i]
                if i + 1 < len(self.axes):
                    self.sum[i + 1] = value
                    self.hop(i + 1).start()
                else:
                    self.out[...] = value


class Reduce:
    def __init__(self, grad, first, rows, at, last=True):
        self.first, self.rows, self.at, self.last = first, rows, at, last
        cols = grad.shape[2]
        self.ins = [grad]
        self.outs = [shaped((rows, cols), F32) if last else shaped((2, rows, cols), BF)]
        self.out_specs = [INV]
        self.scratch = [
            pltpu.VMEM((4, rows, cols), BF), pltpu.VMEM((4, rows, cols), BF), pltpu.VMEM((2, rows, cols), BF),
            DMA((9,)), DMA((8,)), DMA((4,)),
        ]
        if last:
            self.scratch.append(pltpu.VMEM((2, rows, cols), BF))

    def bind(self, ins, outs, scratch):
        (self.grad,), (self.out,) = ins, outs
        self.held, self.in1, self.in2, self.sent, self.come, self.sem = scratch[:6]
        self.in3 = scratch[6] if self.last else None
        self.p = Place()

    def greets(self):
        return Place.PLANES + (Place.ENDS if self.last else ())

    def fin(self, a):
        return self.held.at[2 * a]

    def piece(self, flip_y, flip_x, a):
        return self.grad.at[self.p.piece(flip_y, flip_x, a), pl.ds(self.first, self.rows)]

    def copy(self, src, dst, sent, come, where):
        return pltpu.make_async_remote_copy(
            src_ref=src, dst_ref=dst, send_sem=self.sent.at[sent], recv_sem=self.come.at[come],
            device_id=where, device_id_type=MESH,
        )

    def loads(self):
        kept = [(0, 0, 0), (0, 1, 0), (0, 0, 1), (1, 0, 1)]
        return [pltpu.make_async_copy(self.piece(*k), self.held.at[i], self.sem.at[i]) for i, k in enumerate(kept)]

    def first_hops(self):
        p = self.p
        return [
            self.copy(self.piece(1, 0, 0), self.in1.at[0], 0, 0, p.across_y),
            self.copy(self.piece(1, 1, 0), self.in1.at[1], 1, 1, p.across_y),
            self.copy(self.piece(0, 1, 1), self.in1.at[2], 2, 2, p.across_x),
            self.copy(self.piece(1, 1, 1), self.in1.at[3], 3, 3, p.across_x),
        ]

    def second_hops(self):
        return [
            self.copy(self.held.at[1], self.in2.at[0], 4, 4, self.p.across_x),
            self.copy(self.held.at[3], self.in2.at[1], 5, 5, self.p.across_y),
        ]

    def to_owner(self, a):
        return self.copy(self.fin(a), self.in3.at[0], 6 + a, 6, self.p.over(a))

    def to_partner(self):
        return self.copy(self.fin(1 - self.p.c), self.in3.at[1], 8, 7, self.p.partner)

    def add(self, i, other):
        self.held[i] = (self.held[i].astype(F32) + other.astype(F32)).astype(BF)

    def step(self, k):
        p = self.p
        if k == 0:
            for hop in [self.first_hops()[i] for i in (1, 3, 0, 2)]:
                hop.start()
            for load in self.loads():
                load.start()
        elif k == 1:
            for load in self.loads():
                load.wait()
            hops, after = self.first_hops(), self.second_hops()
            for i in (1, 3):
                hops[i].wait_recv()
                self.add(i, self.in1[i])
                after[i // 2].start()
            for i in (0, 2):
                hops[i].wait_recv()
                self.add(i, self.in1[i])
        elif k == 2:
            for i, hop in enumerate(self.second_hops()):
                hop.wait_recv()
                if self.last:
                    self.add(2 * i, self.in2[i])
                else:
                    self.out[i] = (self.held[2 * i].astype(F32) + self.in2[i].astype(F32)).astype(BF)
            if self.last:
                self.settle()
        elif k == 4:
            if self.last:
                self.close()
            for hop in self.first_hops() + self.second_hops():
                hop.wait_send()

    def settle(self):
        @pl.when(self.p.plain)
        def _():
            self.to_partner().start()

        @pl.when(jnp.logical_not(self.p.plain))
        def _():
            self.to_owner(0).start()
            self.to_owner(1).start()

    def close(self):
        p = self.p
        self.to_owner(0).wait_recv()

        @pl.when(p.plain)
        def _():
            self.out[...] = self.own(p.c).astype(F32) + self.in3[0].astype(F32)
            self.to_partner().wait_send()

        @pl.when(jnp.logical_not(p.plain))
        def _():
            self.to_partner().wait_recv()
            self.out[...] = self.in3[1].astype(F32) + self.in3[0].astype(F32)
            self.to_owner(0).wait_send()
            self.to_owner(1).wait_send()

    def own(self, a):
        return self.held[2 * a]


class Settle(Reduce):
    def __init__(self, sums, at):
        _, rows, cols = sums.shape
        self.at = at
        self.ins = [sums]
        self.outs = [shaped((rows, cols), F32)]
        self.out_specs = [INV]
        self.scratch = [pltpu.VMEM((rows, cols), BF), pltpu.VMEM((2, rows, cols), BF), DMA((9,)), DMA((8,)), DMA((1,))]

    def bind(self, ins, outs, scratch):
        (self.sums,), (self.out,) = ins, outs
        self.kept, self.in3, self.sent, self.come, self.sem = scratch
        self.p = Place()

    def greets(self):
        return Place.ENDS

    def fin(self, a):
        return self.sums.at[a]

    def own(self, a):
        return self.kept[...]

    def load(self):
        return pltpu.make_async_copy(self.sums.at[self.p.c], self.kept, self.sem.at[0])

    def step(self, k):
        if k == 0:
            self.load().start()
            self.settle()
        elif k == 4:
            self.load().wait()
            self.close()


class Background:
    def __init__(self, tasks, greets):
        self.tasks, self.done, names = tasks, [], list(greets)
        for task in tasks:
            names += [name for name in task.greets() if name not in names]
        place = Place()
        self.others = [place.called(name) for name in names]

    def step(self, k):
        for i in range(4):
            for task in self.tasks:
                if i < len(task.at) and task.at[i] == k:
                    task.step(i)

    def finish(self, tasks=None):
        for task in self.tasks if tasks is None else tasks:
            if task not in self.done:
                task.step(4)
                self.done.append(task)


def hosted(kernel, ident, name, ins, in_specs, outs, out_specs, scratch, tasks, flops, traffic, greets=()):
    groups = ([], [], [])
    for group, own in zip(groups, (ins, outs, scratch)):
        group.append(len(own))
    ins, in_specs, outs, out_specs, scratch = list(ins), list(in_specs), list(outs), list(out_specs), list(scratch)
    for task in tasks:
        for group, more in zip(groups, (task.ins, task.outs, task.scratch)):
            group.append(len(more))
        ins += task.ins
        in_specs += getattr(task, "in_specs", [HBM] * len(task.ins))
        outs += task.outs
        out_specs += task.out_specs
        scratch += task.scratch

    def split(refs, counts):
        at, found = 0, []
        for count in counts:
            found.append(refs[at : at + count])
            at += count
        return found

    def body(*refs):
        parts = [split(part, group) for part, group in zip(split(refs, [sum(g) for g in groups]), groups)]
        for task, *mine in zip(tasks, *(part[1:] for part in parts)):
            task.bind(*mine)
        kernel(*parts[0][0], *parts[1][0], *parts[2][0], Background(tasks, greets))

    results = pl.pallas_call(
        body,
        out_shape=tuple(outs),
        in_specs=in_specs,
        out_specs=tuple(out_specs),
        scratch_shapes=scratch,
        compiler_params=params(ident),
        cost_estimate=pl.CostEstimate(flops=flops, bytes_accessed=traffic, transcendentals=0),
        name=name,
    )(*ins)
    results = split(list(results), groups[1])
    return results[0], [r[0] for r in results[1:] if r]


def put_rows(scratch, first, value):
    tall = scratch.shape[1]
    done = 0
    while done < value.shape[0]:
        piece, at = divmod(first + done, tall)
        count = min(tall - at, value.shape[0] - done)
        scratch[piece, pl.ds(at, count), :] = value[done : done + count]
        done += count


def put_columns(scratch, first, value):
    wide_piece = scratch.shape[2]
    for piece in range(scratch.shape[0]):
        scratch[piece, pl.ds(first, value.shape[0]), :] = value[:, piece * wide_piece : (piece + 1) * wide_piece]


def column_loads(pieces, whole):
    each = pieces.shape[2]
    return [(pieces.at[i], whole.at[:, pl.ds(i * each, each)]) for i in range(pieces.shape[0])]


def ffn_forward_kernel(
    h_ref, gain_ref, w_hbm, v_hbm, out_ref, n_hbm, u_hbm,
    w, v, nf, u, act, tpart, mine, n_near, n_over, n_on, o_near, i_near, o_over, i_over, s_near, s_over,
    wsem, osem, bg,
):
    g = Group(bg.others)
    g.greet()
    size, width = h_ref.shape
    hidden = v.shape[0]
    loads = start_all([(w_hbm, w)] + column_loads(v_hbm, v), wsem)
    gather = Gather(g, nf, size, n_near, n_over, n_on)
    scatter = Scatter(g, o_near, i_near, o_over, i_over, s_near, s_over, size)
    parts, step = gather.parts, gather.step
    for p in range(parts):
        nf[at_rows(g.mine, size, p * step, step), :] = normalise(
            h_ref[pl.ds(p * step, step), :], gain_ref[...]
        ).astype(BF)
    g.meet()
    gather.start()
    bg.step(0)
    wait_all(loads)

    def rows_of(places):
        return jnp.concatenate([nf[r, :] for r, _ in places], axis=0) if len(places) > 1 else nf[places[0][0], :]

    def up(places):
        def body(t, carry):
            x = rows_of(places)
            wt = jnp.concatenate([w[:, lanes(t * LANES, LANES)], w[:, lanes(hidden + t * LANES, LANES)]], axis=1)
            both = mm(x, wt)
            gate, upper = both[:, :LANES], both[:, LANES:]
            a = gate * jax.nn.sigmoid(gate) * upper
            act[:, lanes(t * LANES, LANES)] = a.astype(BF)
            at = 0
            for r, count in places:
                u[r, lanes(t * LANES, LANES)] = gate[at : at + count].astype(BF)
                u[r, lanes(hidden + t * LANES, LANES)] = upper[at : at + count].astype(BF)
                at += count
            return carry

        lax.fori_loop(0, hidden // LANES, body, 0)

    def down(store):
        def body(t, carry):
            cols = lanes(t * 256, 256)
            store(cols, mm(act[...], v[:, cols]))
            return carry

        lax.fori_loop(0, width // 256, body, 0)

    def keep(index, r, count):
        return pltpu.make_async_copy(u.at[r], u_hbm.at[r], osem.at[index])

    whole = lambda block: at_rows(block, size, 0, size)
    up([(whole(g.mine), size)])
    keep(0, whole(g.mine), size).start()

    def put_mine(cols, value):
        mine[:, cols] = value

    down(put_mine)
    gather.wait_beside()
    up([(whole(g.beside), size)])
    keep(1, whole(g.beside), size).start()

    def put_beside(cols, value):
        o_near[1, :, cols] = value.astype(BF)

    down(put_beside)
    for p in range(parts):
        scatter.close(1, p).start()
    bg.step(1)
    for p in range(parts):
        gather.wait_part(p)
        gather.wait_far(p)
        r_across, r_far = at_rows(g.across, size, p * step, step), at_rows(g.far, size, p * step, step)
        up([(r_across, step), (r_far, step)])
        keep(2 + 2 * p, r_across, step).start()
        keep(3 + 2 * p, r_far, step).start()
        here = scatter.rows(p)

        def put(cols, value):
            tpart[:, cols] = value[:step]
            o_near[0, here, cols] = value[step:].astype(BF)

        down(put)
        scatter.close(0, p).start()
        scatter.close(0, p).wait_recv()
        o_over[here, :] = (tpart[...] + i_near[0, here, :].astype(F32)).astype(BF)
        scatter.link(p).start()
    n_out = pltpu.make_async_copy(nf, n_hbm, osem.at[2 + 2 * parts])
    n_out.start()
    bg.step(2)
    for p in range(parts):
        here = scatter.rows(p)
        scatter.close(1, p).wait_recv()
        scatter.link(p).wait_recv()
        out_ref[here, :] = (
            h_ref[here, :] + mine[here, :] + i_near[1, here, :].astype(F32) + i_over[here, :].astype(F32)
        )
    gather.finish()
    scatter.wait_all_sends()
    keep(0, whole(g.mine), size).wait()
    keep(1, whole(g.beside), size).wait()
    for p in range(parts):
        keep(2 + 2 * p, at_rows(g.across, size, p * step, step), step).wait()
        keep(3 + 2 * p, at_rows(g.far, size, p * step, step), step).wait()
    n_out.wait()
    bg.finish()


def ffn_forward(h, gain, w, v, ident, tasks=(), parts=PARTS):
    size, width = h.shape
    hidden = v.shape[1]
    total = 4 * size
    return hosted(
        ffn_forward_kernel, ident, "ffn_forward", [h, gain, w, v], [INV, INV, HBM, HBM],
        [shaped((size, width), F32), shaped((total, width), BF), shaped((total, 2 * hidden), BF)], [INV, HBM, HBM],
        [
            pltpu.VMEM((width, 2 * hidden), BF), pltpu.VMEM((hidden, width), BF), pltpu.VMEM((total, width), BF),
            pltpu.VMEM((total, 2 * hidden), BF), pltpu.VMEM((size, hidden), BF),
            pltpu.VMEM((size // parts, width), F32), pltpu.VMEM((size, width), F32),
            *gather_scratch(parts), *scatter_scratch(size, width, parts), DMA((1 + v.shape[0],)), DMA((3 + 2 * parts,)),
        ],
        tasks, 6 * total * width * hidden, 2**24,
    )


def mm_tn(a, b):
    return lax.dot_general(a, b, (((0,), (0,)), ((), ())), preferred_element_type=F32)


def rms_back(dn, h, gain):
    inverse = lax.rsqrt(jnp.mean(h * h, axis=-1, keepdims=True) + epsilon)
    scaled = dn * gain
    inner = jnp.mean(scaled * h, axis=-1, keepdims=True)
    grad_gain = jnp.sum(dn * h * inverse, axis=0, keepdims=True)
    return inverse * scaled - h * (inverse * inverse * inverse * inner), grad_gain


def close_scatter(scatter, mine, dh_ref, h_ref, gain_ref, out_ref, gg_ref):
    gg_ref[...] = jnp.zeros_like(gg_ref)
    for p in range(scatter.parts):
        here = scatter.rows(p)
        scatter.close(1, p).wait_recv()
        scatter.link(p).wait_recv()
        dn = mine[here, :] + scatter.in_near[1, here, :].astype(F32) + scatter.in_over[here, :].astype(F32)
        term, grad_gain = rms_back(dn, h_ref[here, :], gain_ref[...])
        out_ref[here, :] = dh_ref[here, :] + term
        gg_ref[...] += grad_gain


def ffn_backward_kernel(
    known, dh_ref, h_ref, gain_ref, df_hbm, w_hbm, v_hbm, n_hbm, u_hbm, out_ref, gg_ref, gw_hbm, gv_hbm,
    w, v, nf, u, act, df, tpart, mine, gtile, gv, n_near, n_over, n_on, o_near, i_near, o_over, i_over, s_near, s_over,
    wsem, osem, bg,
):
    g = Group(bg.others)
    g.greet()
    size, width = dh_ref.shape
    hidden = v.shape[0]
    loads = column_loads(v_hbm, v) + [(u_hbm, u), (w_hbm, w), (n_hbm, nf)]
    loads = start_all(loads + [(df_hbm, df)] if known else loads, wsem)
    gather = Gather(g, df, size, n_near, n_over, n_on)
    scatter = Scatter(g, o_near, i_near, o_over, i_over, s_near, s_over, size)
    parts, step = gather.parts, gather.step
    if not known:
        df[at_rows(g.mine, size, 0, size), :] = dh_ref[...].astype(BF)
    g.meet()
    if not known:
        gather.start()
    bg.step(0)
    wait_all(loads)

    third = hidden // 3

    def cat(ref, places, cols):
        found = [ref[r, cols] for r, _ in places]
        return found[0] if len(found) == 1 else jnp.concatenate(found, axis=0)

    def first(places):
        def body(t, carry):
            cols, more = lanes(t * third, third), lanes(hidden + t * third, third)
            da = mm_nt(cat(df, places, slice(None)), v[cols, :])
            gate, upper = cat(u, places, cols).astype(F32), cat(u, places, more).astype(F32)
            s = jax.nn.sigmoid(gate)
            lit = gate * s
            dgate = (da * upper * s * (1.0 + gate * (1.0 - s))).astype(BF)
            dupper = (da * lit).astype(BF)
            a = (lit * upper).astype(BF)
            at = 0
            for r, count in places:
                u[r, cols] = dgate[at : at + count]
                u[r, more] = dupper[at : at + count]
                act[r, cols] = a[at : at + count]
                at += count
            return carry

        lax.fori_loop(0, 3, body, 0)

    def second(places, store):
        def body(t, carry):
            cols = lanes(t * 256, 256)
            store(cols, mm_nt(cat(u, places, slice(None)), w[cols, :]))
            return carry

        lax.fori_loop(0, width // 256, body, 0)

    whole = lambda block: [(at_rows(block, size, 0, size), size)]

    def put_mine(cols, value):
        mine[:, cols] = value

    def put_beside(cols, value):
        o_near[1, :, cols] = value.astype(BF)

    def own():
        first(whole(g.mine))
        second(whole(g.mine), put_mine)

    def beside():
        first(whole(g.beside))
        second(whole(g.beside), put_beside)
        for p in range(parts):
            scatter.close(1, p).start()

    if not known:
        own()
        gather.wait_beside()
        beside()
    bg.step(1)
    for p in range(parts):
        if not known:
            gather.wait_part(p)
            gather.wait_far(p)
        pair = [(at_rows(b, size, p * step, step), step) for b in (g.across, g.far)]
        first(pair)
        here = scatter.rows(p)

        def put(cols, value):
            tpart[:, cols] = value[:step]
            o_near[0, here, cols] = value[step:].astype(BF)

        second(pair, put)
        scatter.close(0, p).start()
        scatter.close(0, p).wait_recv()
        o_over[here, :] = (tpart[...] + i_near[0, here, :].astype(F32)).astype(BF)
        scatter.link(p).start()
    bg.step(2)
    if known:
        beside()
        own()
    flush = []
    count = 0

    def emit(value, dst):
        nonlocal count
        slot = count % 2
        if count >= 2:
            flush[count - 2].wait()
        gtile[slot, :, : value.shape[1]] = value.astype(BF)
        copy = pltpu.make_async_copy(gtile.at[slot, :, : value.shape[1]], dst, osem.at[slot])
        copy.start()
        flush.append(copy)
        count += 1

    tall = gtile.shape[1]
    for t in range(3):
        put_columns(gv, t * third, mm_tn(act[:, t * third : (t + 1) * third], df[...]).astype(BF))
    save = pltpu.make_async_copy(gv, gv_hbm, osem.at[2])
    save.start()
    bg.step(3)
    each = gw_hbm.shape[1]
    for t in range(width // tall):
        piece, at = divmod(t * tall, each)
        for k in range(2):
            cols = slice(k * hidden, (k + 1) * hidden)
            emit(mm_tn(nf[:, t * tall : (t + 1) * tall], u[:, cols]), gw_hbm.at[piece, pl.ds(at, tall), cols])
    bg.step(4)
    close_scatter(scatter, mine, dh_ref, h_ref, gain_ref, out_ref, gg_ref)
    if not known:
        gather.finish()
    scatter.wait_all_sends()
    for copy in flush[-2:]:
        copy.wait()
    save.wait()
    bg.finish()


def ffn_backward(dh, h, gain, df, w, v, n, u, ident, tasks=(), parts=PARTS):
    size, width = h.shape
    pieces, hidden = v.shape[:2]
    total = 4 * size
    known = df is not None
    if not known:
        df = n
    return hosted(
        functools.partial(ffn_backward_kernel, known), ident, "ffn_backward", [dh, h, gain, df, w, v, n, u],
        [INV, INV, INV] + [HBM] * 5,
        [
            shaped((size, width), F32), shaped((1, width), F32), shaped((pieces, width // pieces, 2 * hidden), BF),
            shaped((pieces, hidden, width // pieces), BF),
        ],
        [INV, INV, HBM, HBM],
        [
            pltpu.VMEM((width, 2 * hidden), BF), pltpu.VMEM((hidden, width), BF), pltpu.VMEM((total, width), BF),
            pltpu.VMEM((total, 2 * hidden), BF), pltpu.VMEM((total, hidden), BF), pltpu.VMEM((total, width), BF),
            pltpu.VMEM((size // parts, width), F32), pltpu.VMEM((size, width), F32),
            pltpu.VMEM((2, 128, hidden), BF), pltpu.VMEM((pieces, hidden, width // pieces), BF),
            *gather_scratch(parts), *scatter_scratch(size, width, parts), DMA((4 + pieces,)), DMA((3,)),
        ],
        tasks, 12 * total * width * hidden, 2**25,
    )


MOST_DOC = 512


class Columns(Gather):
    def __init__(self, group, full, near, over, onward):
        super().__init__(group, full, full.shape[0], near, over, onward)
        self.cols = full.shape[1] // 4

    def view(self, block, part):
        return self.full.at[pl.ds(part * self.step, self.step), lanes(block * self.cols, self.cols)]


def cat_rows(ref, places, cols=slice(None)):
    found = [ref[r, cols] for r, _ in places]
    return found[0] if len(found) == 1 else jnp.concatenate(found, axis=0)


def product(src, weight, turned, tile=256):
    def run(places, store):
        width = weight.shape[0] if turned else weight.shape[1]

        def body(t, carry):
            cols = lanes(t * tile, tile)
            x = cat_rows(src, places)
            store(cols, mm_nt(x, weight[cols, :]) if turned else mm(x, weight[:, cols]))
            return carry

        lax.fori_loop(0, width // tile, body, 0)

    return run


def scatter_all(g, scatter, run, mine, tpart):
    size, step = scatter.size, scatter.step
    for p in range(scatter.parts):
        here = scatter.rows(p)

        def put(cols, value):
            tpart[:, cols] = value[:step]
            scatter.out_near[0, here, cols] = value[step:].astype(BF)

        run([(at_rows(b, size, p * step, step), step) for b in (g.across, g.far)], put)
        scatter.close(0, p).start()
        scatter.close(0, p).wait_recv()
        scatter.out_over[here, :] = (tpart[...] + scatter.in_near[0, here, :].astype(F32)).astype(BF)
        scatter.link(p).start()

    def put_beside(cols, value):
        scatter.out_near[1, :, cols] = value.astype(BF)

    run([(at_rows(g.beside, size, 0, size), size)], put_beside)
    for p in range(scatter.parts):
        scatter.close(1, p).start()

    def put_mine(cols, value):
        mine[:, cols] = value

    run([(at_rows(g.mine, size, 0, size), size)], put_mine)


def gather_everything(gather):
    gather.wait_beside()
    for p in range(gather.parts):
        gather.wait_part(p)
    for p in range(gather.parts):
        gather.wait_far(p)


def doc_starts(docs, lengths, places):
    row = lengths[pl.ds(0, 1), :]
    end = jnp.zeros((1, 1), F32)
    start = jnp.zeros_like(places)
    for d in range(docs):
        end = end + row[:, d : d + 1]
        start = jnp.where(places >= end.astype(jnp.int32), end.astype(jnp.int32), start)
    return start


def conv_taps(gated, within, taps):
    total = gated.shape[0]
    summed = taps[0] * gated
    for j in range(1, len(taps)):
        summed = summed + taps[j] * jnp.where(within >= j, pltpu.roll(gated, j, 0), 0.0)
    return summed


def conv_forward_kernel(
    docs, count, inside, lens_ref, x_hbm, gain_ref, taps_ref, win_hbm, wout_hbm,
    out_ref, block_ref, n_hbm, p_hbm, lengths, taps_out, win_out, wout_out,
    win, wout, full, nf, proj, low, mixed, tpart, mine, n_near, n_over, n_on, o_near, i_near, o_over, i_over,
    s_near, s_over, wsem, osem, xsem, xlocal, bg,
):
    g = Group(bg.others)
    g.greet()
    size, width = out_ref.shape
    total, chans = x_hbm.shape[0], wout.shape[0]
    loads = []
    if inside:
        bg.tasks[0].whole, bg.tasks[1].whole = win, wout
    else:
        loads = start_all([(win_hbm, win), (wout_hbm, wout)], wsem)
    gather = Columns(g, full, n_near, n_over, n_on)
    scatter = Scatter(g, o_near, i_near, o_over, i_over, s_near, s_over, size)
    parts = gather.parts
    blocks = [
        Exchange(
            x_hbm.at[pl.ds(p * gather.step, gather.step)],
            *(full.at[pl.ds(p * gather.step, gather.step), lanes(b * chans, chans)] for b in (g.mine, g.beside)),
            xsem, xlocal, p,
        )
        for p in range(parts)
    ]
    small = [Exchange(lens_ref, lengths, lengths, xsem, xlocal, parts), Exchange(taps_ref, taps_out, taps_out, xsem, xlocal, parts + 1)]
    g.meet()
    for block in blocks + small:
        block.start()
    bg.step(0)
    for p in range(parts):
        blocks[p].arrive()
        gather.link(p, g.mine).start()
        gather.close(p, g.mine).start()
    gather.wait_beside()
    bg.step(1)
    for p in range(parts):
        gather.wait_part(p)
    for p in range(parts):
        gather.wait_far(p)
    for block in small:
        block.arrive()
    bg.step(2)
    if inside:
        bg.finish(bg.tasks[:2])
    wait_all(loads)

    def project(t, carry):
        rows = at_rows(t, size, 0, size)
        n = normalise(full[rows, :].astype(F32), gain_ref[...]).astype(BF)
        nf[rows, :] = n
        p = mm(n, win[...])
        proj[rows, :] = p
        low[rows, :] = p.astype(BF)
        return carry

    lax.fori_loop(0, total // size, project, 0)
    saves = start_all([(nf, n_hbm), (low, p_hbm), (win, win_out), (wout, wout_out)], osem)
    places = lax.broadcasted_iota(jnp.int32, (total, LANES), 0)
    within = places - doc_starts(docs, lengths, places)
    for k in range(chans // LANES):
        b, c, x = (proj[:, pl.ds(i * chans + k * LANES, LANES)] for i in range(3))
        taps = [taps_out[pl.ds(j, 1), pl.ds(k * LANES, LANES)] for j in range(count)]
        mixed[:, pl.ds(k * LANES, LANES)] = (c * conv_taps(b * x, within, taps)).astype(BF)
    scatter_all(g, scatter, product(mixed, wout, False), mine, tpart)
    bg.step(3)
    block_ref[...] = full[at_rows(g.mine, size, 0, size), :]
    for p in range(scatter.parts):
        here = scatter.rows(p)
        scatter.close(1, p).wait_recv()
        scatter.link(p).wait_recv()
        out_ref[here, :] = (
            block_ref[here, :].astype(F32) + mine[here, :] + i_near[1, here, :].astype(F32) + i_over[here, :].astype(F32)
        )
    for block in blocks + small:
        block.finish()
    gather.finish()
    scatter.wait_all_sends()
    wait_all(saves)
    bg.finish()


def conv_forward(docs, count, lens, x, gain, taps, win, wout, inside, ident, tasks=(), parts=PARTS, cuts=4):
    total, chans = x.shape
    width = wout.shape[1]
    size = total // 4
    return hosted(
        functools.partial(conv_forward_kernel, docs, count, inside), ident, "conv_forward",
        [lens, x, gain, taps, win, wout], [INV, HBM, INV, INV, HBM, HBM],
        [
            shaped((size, width), F32), shaped((size, width), BF), shaped((total, width), BF), shaped((total, 3 * chans), BF),
            shaped(lens.shape, F32), shaped(taps.shape, F32), shaped(win.shape, BF), shaped(wout.shape, BF),
        ],
        [INV, INV, HBM, HBM, INV, INV, HBM, HBM],
        [
            pltpu.VMEM((width, 3 * chans), BF), pltpu.VMEM((chans, width), BF), pltpu.VMEM((total, width), BF),
            pltpu.VMEM((total, width), BF), pltpu.VMEM((total, 3 * chans), F32), pltpu.VMEM((total, 3 * chans), BF),
            pltpu.VMEM((total, chans), BF), pltpu.VMEM((size // parts, width), F32), pltpu.VMEM((size, width), F32),
            *gather_scratch(cuts), *scatter_scratch(size, width, parts), DMA((2,)), DMA((4,)),
            DMA((2, cuts + 2)), DMA((cuts + 2,)),
        ],
        tasks, 8 * total * width * chans, 2**24, ("swap",),
    )


def conv_backward_kernel(
    docs, count, lengths, dh_ref, h_ref, gain_ref, taps_ref, win_hbm, wout_hbm, n_hbm, p_hbm, out_ref, gg_ref, gt_ref, gin_hbm, gout_hbm,
    win, wout, nf, low, dz, dy, mixed, dproj, gin, gout, tpart, mine, n_near, n_over, n_on, o_near, i_near, o_over, i_over,
    s_near, s_over, wsem, osem, bg,
):
    g = Group(bg.others)
    g.greet()
    size, width = dh_ref.shape
    total, chans = 4 * size, wout.shape[0]
    loads = start_all([(wout_hbm, wout), (p_hbm, low), (win_hbm, win), (n_hbm, nf)], wsem)
    gather = Gather(g, dz, size, n_near, n_over, n_on)
    scatter = Scatter(g, o_near, i_near, o_over, i_over, s_near, s_over, size)
    dz[at_rows(g.mine, size, 0, size), :] = dh_ref[...].astype(BF)
    g.meet()
    gather.start()
    bg.step(0)
    wait_all(loads)
    places = lax.broadcasted_iota(jnp.int32, (total, LANES), 0)
    within = places - doc_starts(docs, lengths, places)
    gather_everything(gather)
    bg.step(1)

    def project(t, carry):
        rows = at_rows(t, size, 0, size)
        dy[rows, :] = mm_nt(dz[rows, :], wout[...])
        return carry

    lax.fori_loop(0, total // size, project, 0)
    for k in range(chans // LANES):
        b, c, x = (low[:, pl.ds(i * chans + k * LANES, LANES)].astype(F32) for i in range(3))
        here = pl.ds(k * LANES, LANES)
        taps = [taps_ref[pl.ds(j, 1), here] for j in range(count)]
        gated = b * x
        summed = conv_taps(gated, within, taps)
        d = dy[:, here]
        mixed[:, here] = (c * summed).astype(BF)
        ds = d * c
        dg = taps[0] * ds
        gt_ref[pl.ds(0, 1), here] = jnp.sum(ds * gated, axis=0, keepdims=True)
        for j in range(1, len(taps)):
            masked = jnp.where(within >= j, ds, 0.0)
            dg = dg + taps[j] * pltpu.roll(masked, total - j, 0)
            gt_ref[pl.ds(j, 1), here] = jnp.sum(masked * pltpu.roll(gated, j, 0), axis=0, keepdims=True)
        dproj[:, pl.ds(k * LANES, LANES)] = (dg * x).astype(BF)
        dproj[:, pl.ds(chans + k * LANES, LANES)] = (d * summed).astype(BF)
        dproj[:, pl.ds(2 * chans + k * LANES, LANES)] = (dg * b).astype(BF)
    bg.step(2)
    scatter_all(g, scatter, product(dproj, win, True), mine, tpart)
    bg.step(3)
    put_columns(gout, 0, mm_tn(mixed[...], dz[...]).astype(BF))
    save = pltpu.make_async_copy(gout, gout_hbm, osem.at[0])
    save.start()
    for t in range(width // 256):
        put_rows(gin, t * 256, mm_tn(nf[:, pl.ds(t * 256, 256)], dproj[...]).astype(BF))
    more = pltpu.make_async_copy(gin, gin_hbm, osem.at[1])
    more.start()
    bg.step(4)
    close_scatter(scatter, mine, dh_ref, h_ref, gain_ref, out_ref, gg_ref)
    gather.finish()
    scatter.wait_all_sends()
    save.wait()
    more.wait()
    bg.step(5)
    bg.finish()


def conv_backward(docs, count, lengths, dh, h, gain, taps, win, wout, n, p, pieces, ident, tasks=(), parts=PARTS):
    size, width = dh.shape
    total, chans = 4 * size, wout.shape[0]
    each = width // pieces
    return hosted(
        functools.partial(conv_backward_kernel, docs, count), ident, "conv_backward",
        [lengths, dh, h, gain, taps, win, wout, n, p],
        [INV, INV, INV, INV, INV, HBM, HBM, HBM, HBM],
        [
            shaped((size, width), F32), shaped((1, width), F32), shaped(taps.shape, F32),
            shaped((pieces, each, 3 * chans), BF), shaped((pieces, chans, each), BF),
        ],
        [INV, INV, INV, HBM, HBM],
        [
            pltpu.VMEM((width, 3 * chans), BF), pltpu.VMEM((chans, width), BF), pltpu.VMEM((total, width), BF),
            pltpu.VMEM((total, 3 * chans), BF), pltpu.VMEM((total, width), BF), pltpu.VMEM((total, chans), F32),
            pltpu.VMEM((total, chans), BF), pltpu.VMEM((total, 3 * chans), BF), pltpu.VMEM((pieces, each, 3 * chans), BF),
            pltpu.VMEM((pieces, chans, each), BF), pltpu.VMEM((size // parts, width), F32), pltpu.VMEM((size, width), F32),
            *gather_scratch(parts), *scatter_scratch(size, width, parts), DMA((4,)), DMA((2,)),
        ],
        tasks, 16 * total * width * chans, 2**24,
    )


def head_sums(values, head):
    width = values.shape[1]
    a = lax.broadcasted_iota(jnp.int32, (width, width), 0) // head
    b = lax.broadcasted_iota(jnp.int32, (width, width), 1) // head
    same = jnp.where(a == b, 1.0, 0.0).astype(BF)
    high = values.astype(BF)
    low = (values - high.astype(F32)).astype(BF)
    return mm(high, same) + mm(low, same)


def turn(values, head):
    width = values.shape[1]
    lane = lax.broadcasted_iota(jnp.int32, values.shape, 1)
    return jnp.where(
        lane % head < head // 2, pltpu.roll(values, width - head // 2, 1), pltpu.roll(values, head // 2, 1)
    )


def wide(table, width):
    return jnp.concatenate([table] * (width // table.shape[1]), axis=1)


def norm_turn(raw, gain, cosine, sine, head):
    inverse = lax.rsqrt(head_sums(raw * raw, head) * (1.0 / head) + epsilon)
    v = raw * inverse * gain
    return v * wide(cosine, raw.shape[1]) + turn(v, head) * wide(sine, raw.shape[1])


def norm_turn_back(d, raw, gain, cosine, sine, head):
    d = d * wide(cosine, raw.shape[1]) - turn(d, head) * wide(sine, raw.shape[1])
    inverse = lax.rsqrt(head_sums(raw * raw, head) * (1.0 / head) + epsilon)
    scaled = d * gain
    inner = head_sums(scaled * raw, head) * (1.0 / head)
    grad_gain = jnp.sum(d * raw * inverse, axis=0, keepdims=True)
    return inverse * scaled - raw * (inverse * inverse * inverse * inner), grad_gain


def score_tile(q, k, starts, first_key, first_query, scale):
    raw = mm_nt(k, q) * scale
    key = first_key + lax.broadcasted_iota(jnp.int32, raw.shape, 0)
    query = first_query + lax.broadcasted_iota(jnp.int32, (1, starts.shape[1]), 1)
    copies = raw.shape[1] // starts.shape[1]
    allowed = (key <= wide(query, raw.shape[1])) & (key >= wide(starts, raw.shape[1]))
    return jnp.where(allowed, raw, -1e30)


def softmax_tile(scores):
    top = jnp.max(scores, axis=0, keepdims=True)
    weights = jnp.exp(scores - top)
    return weights / jnp.sum(weights, axis=0, keepdims=True)


def stack_heads(values, head):
    return jnp.concatenate([values[:, i * head : (i + 1) * head] for i in range(values.shape[1] // head)], axis=0)


def attention_tiles(total, tile):
    back = -(-MOST_DOC // tile)
    return [(i * tile, max(0, i - back) * tile, (i + 1) * tile) for i in range(total // tile)]


def attention_forward_kernel(
    head, docs, lengths, h_ref, gain_ref, qgain_ref, kgain_ref, cos_ref, sin_ref, wq_hbm, wkv_hbm, wo_hbm,
    out_ref, n_hbm, raw_hbm, ready_hbm, o_hbm,
    w, wo, nf, low, ready, vt, o, tpart, mine, n_near, n_over, n_on, o_near, i_near, o_over, i_over,
    s_near, s_over, wsem, osem, bg,
):
    g = Group(bg.others)
    g.greet()
    size, width = h_ref.shape
    total, qw = 4 * size, wo.shape[0]
    kw = (w.shape[1] - qw) // 2
    loads = start_all([(wq_hbm, w.at[:, pl.ds(0, qw)]), (wkv_hbm, w.at[:, pl.ds(qw, 2 * kw)]), (wo_hbm, wo)], wsem)
    gather = Gather(g, nf, size, n_near, n_over, n_on)
    scatter = Scatter(g, o_near, i_near, o_over, i_over, s_near, s_over, size)
    parts, step = gather.parts, gather.step
    nf[at_rows(g.mine, size, 0, size), :] = normalise(h_ref[...], gain_ref[...]).astype(BF)
    g.meet()
    gather.start()
    bg.step(0)
    wait_all(loads)

    def project(block):
        rows = at_rows(block, size, 0, size)
        raw = mm(nf[rows, :], w[...])
        low[rows, :] = raw.astype(BF)
        cosine, sine = cos_ref[rows, :], sin_ref[rows, :]
        ready[rows, pl.ds(0, qw)] = norm_turn(raw[:, :qw], qgain_ref[...], cosine, sine, head).astype(BF)
        ready[rows, pl.ds(qw, kw)] = norm_turn(raw[:, qw : qw + kw], kgain_ref[...], cosine, sine, head).astype(BF)
        ready[rows, pl.ds(qw + kw, kw)] = raw[:, qw + kw :].astype(BF)

    project(g.mine)
    gather.wait_beside()
    project(g.beside)
    for p in range(parts):
        gather.wait_part(p)
    for p in range(parts):
        gather.wait_far(p)

    def rest(i, carry):
        project(jnp.where(i == 0, g.across, g.far))
        return carry

    lax.fori_loop(0, 2, rest, 0)
    bg.step(1)
    saves = start_all([(nf, n_hbm), (low, raw_hbm), (ready, ready_hbm)], osem)
    vt[...] = jnp.transpose(ready[:, pl.ds(qw + kw, kw)].astype(F32)).astype(BF)
    groups = qw // kw
    tile = 256
    scale = head ** (-0.5)
    starts = doc_starts(docs, lengths, lax.broadcasted_iota(jnp.int32, (1, total), 1))
    for first, low_key, high_key in attention_tiles(total, tile):
        keys = pl.ds(low_key, high_key - low_key)
        for kv in range(kw // head):
            q = stack_heads(ready[pl.ds(first, tile), pl.ds(kv * groups * head, groups * head)], head)
            k = ready[keys, pl.ds(qw, kw)][:, kv * head : (kv + 1) * head]
            p = softmax_tile(score_tile(q, k, starts[:, first : first + tile], low_key, first, scale)).astype(BF)
            ot = mm(vt[pl.ds(kv * head, head), keys], p)
            joined = jnp.concatenate([ot[:, i * tile : (i + 1) * tile] for i in range(groups)], axis=0)
            o[pl.ds(first, tile), pl.ds(kv * groups * head, groups * head)] = jnp.transpose(joined).astype(BF)
        if first == tile:
            bg.step(2)
    bg.step(3)
    save_o = pltpu.make_async_copy(o, o_hbm, osem.at[3])
    save_o.start()
    scatter_all(g, scatter, product(o, wo, False), mine, tpart)
    bg.step(4)
    for p in range(parts):
        here = scatter.rows(p)
        scatter.close(1, p).wait_recv()
        scatter.link(p).wait_recv()
        out_ref[here, :] = (
            h_ref[here, :] + mine[here, :] + i_near[1, here, :].astype(F32) + i_over[here, :].astype(F32)
        )
    gather.finish()
    scatter.wait_all_sends()
    wait_all(saves)
    save_o.wait()
    bg.finish()


def attention_forward(head, docs, lengths, h, gain, qgain, kgain, cosine, sine, wq, wkv, wo, ident, tasks=(), parts=PARTS):
    size, width = h.shape
    total, qw = 4 * size, wo.shape[0]
    kw = wkv.shape[1] // 2
    every = qw + 2 * kw
    return hosted(
        functools.partial(attention_forward_kernel, head, docs), ident, "attention_forward",
        [lengths, h, gain, qgain, kgain, cosine, sine, wq, wkv, wo], [INV] * 7 + [HBM] * 3,
        [
            shaped((size, width), F32), shaped((total, width), BF), shaped((total, every), BF), shaped((total, every), BF),
            shaped((total, qw), BF),
        ],
        [INV] + [HBM] * 4,
        [
            pltpu.VMEM((width, every), BF), pltpu.VMEM((qw, width), BF), pltpu.VMEM((total, width), BF),
            pltpu.VMEM((total, every), BF), pltpu.VMEM((total, every), BF),
            pltpu.VMEM((kw, total), BF), pltpu.VMEM((total, qw), BF),
            pltpu.VMEM((size // parts, width), F32), pltpu.VMEM((size, width), F32),
            *gather_scratch(parts), *scatter_scratch(size, width, parts), DMA((3,)), DMA((4,)),
        ],
        tasks, 2 * total * width * (every + qw), 2**24,
    )


def attention_backward_kernel(
    head, docs, lengths, dh_ref, h_ref, gain_ref, qgain_ref, kgain_ref, cos_ref, sin_ref, wq_hbm, wkv_hbm, wo_hbm,
    n_hbm, raw_hbm, ready_hbm, o_hbm, out_ref, gg_ref, gq_ref, gk_ref, gw_hbm, gwo_hbm,
    w, wo, nf, low, ready, kt, o, dz, do, dq, dkv, dlow, gw, gwo, tpart, mine,
    n_near, n_over, n_on, o_near, i_near, o_over, i_over, s_near, s_over, wsem, osem, bg,
):
    g = Group(bg.others)
    g.greet()
    size, width = h_ref.shape
    total, qw = 4 * size, wo.shape[0]
    kw = (w.shape[1] - qw) // 2
    loads = start_all(
        [
            (ready_hbm, ready), (wo_hbm, wo), (o_hbm, o), (raw_hbm, low), (wq_hbm, w.at[:, pl.ds(0, qw)]),
            (wkv_hbm, w.at[:, pl.ds(qw, 2 * kw)]), (n_hbm, nf),
        ],
        wsem,
    )
    gather = Gather(g, dz, size, n_near, n_over, n_on)
    scatter = Scatter(g, o_near, i_near, o_over, i_over, s_near, s_over, size)
    dz[at_rows(g.mine, size, 0, size), :] = dh_ref[...].astype(BF)
    g.meet()
    gather.start()
    bg.step(0)
    wait_all(loads)
    kt[...] = jnp.transpose(ready[:, pl.ds(qw, kw)].astype(F32)).astype(BF)
    dkv[...] = jnp.zeros_like(dkv)
    gather_everything(gather)

    def project(t, carry):
        rows = at_rows(t, size, 0, size)
        do[rows, :] = mm_nt(dz[rows, :], wo[...]).astype(BF)
        return carry

    bg.step(1)

    lax.fori_loop(0, total // size, project, 0)
    groups = qw // kw
    tile = 256
    scale = head ** (-0.5)
    starts = doc_starts(docs, lengths, lax.broadcasted_iota(jnp.int32, (1, total), 1))
    for first, low_key, high_key in attention_tiles(total, tile):
        keys = pl.ds(low_key, high_key - low_key)
        for kv in range(kw // head):
            cols = pl.ds(kv * groups * head, groups * head)
            lane = slice(kv * head, (kv + 1) * head)
            q = stack_heads(ready[pl.ds(first, tile), cols], head)
            k, v = ready[keys, pl.ds(qw, kw)][:, lane], ready[keys, pl.ds(qw + kw, kw)][:, lane]
            p = softmax_tile(score_tile(q, k, starts[:, first : first + tile], low_key, first, scale))
            d = stack_heads(do[pl.ds(first, tile), cols], head)
            dp = mm_nt(v, d)
            inner = jnp.sum(p * dp, axis=0, keepdims=True)
            ds = (p * (dp - inner)).astype(BF)
            both = jnp.concatenate([mm(ds, q) * scale, mm(p.astype(BF), d)], axis=1)
            dkv[kv, keys, :] += both
            dqt = mm(kt[pl.ds(kv * head, head), keys], ds) * scale
            joined = jnp.concatenate([dqt[:, i * tile : (i + 1) * tile] for i in range(groups)], axis=0)
            dq[pl.ds(first, tile), cols] = jnp.transpose(joined)
        if first == tile:
            bg.step(2)
        if first == 2 * tile:
            bg.step(3)
    bg.step(4)
    gq_ref[...] = jnp.zeros_like(gq_ref)
    gk_ref[...] = jnp.zeros_like(gk_ref)

    def finish(t, carry):
        rows = at_rows(t, size, 0, size)
        cosine, sine = cos_ref[rows, :], sin_ref[rows, :]
        d, gq = norm_turn_back(dq[rows, :], low[rows, pl.ds(0, qw)].astype(F32), qgain_ref[...], cosine, sine, head)
        gq_ref[...] += gq
        dlow[rows, pl.ds(0, qw)] = d.astype(BF)
        pairs = [dkv[kv, rows, :] for kv in range(kw // head)]
        dk = jnp.concatenate([x[:, :head] for x in pairs], axis=1)
        dv = jnp.concatenate([x[:, head:] for x in pairs], axis=1)
        d, gk = norm_turn_back(dk, low[rows, pl.ds(qw, kw)].astype(F32), kgain_ref[...], cosine, sine, head)
        gk_ref[...] += gk
        dlow[rows, pl.ds(qw, kw)] = d.astype(BF)
        dlow[rows, pl.ds(qw + kw, kw)] = dv.astype(BF)
        return carry

    lax.fori_loop(0, total // size, finish, 0)
    scatter_all(g, scatter, product(dlow, w, True), mine, tpart)
    put_columns(gwo, 0, mm_tn(o[...], dz[...]).astype(BF))
    save = pltpu.make_async_copy(gwo, gwo_hbm, osem.at[0])
    save.start()
    for t in range(width // 256):
        put_rows(gw, t * 256, mm_tn(nf[:, pl.ds(t * 256, 256)], dlow[...]).astype(BF))
    more = pltpu.make_async_copy(gw, gw_hbm, osem.at[1])
    more.start()
    bg.step(5)
    close_scatter(scatter, mine, dh_ref, h_ref, gain_ref, out_ref, gg_ref)
    gather.finish()
    scatter.wait_all_sends()
    save.wait()
    more.wait()
    bg.finish()


def attention_backward(
    head, docs, lengths, dh, h, gain, qgain, kgain, cosine, sine, wq, wkv, wo, n, raw, ready, o, pieces, ident, tasks=(),
    parts=PARTS,
):
    size, width = h.shape
    total, qw = 4 * size, wo.shape[0]
    kw = wkv.shape[1] // 2
    every = qw + 2 * kw
    each = width // pieces
    return hosted(
        functools.partial(attention_backward_kernel, head, docs), ident, "attention_backward",
        [lengths, dh, h, gain, qgain, kgain, cosine, sine, wq, wkv, wo, n, raw, ready, o], [INV] * 8 + [HBM] * 7,
        [
            shaped((size, width), F32), shaped((1, width), F32), shaped((1, qw), F32), shaped((1, kw), F32),
            shaped((pieces, each, every), BF), shaped((pieces, qw, each), BF),
        ],
        [INV, INV, INV, INV, HBM, HBM],
        [
            pltpu.VMEM((width, every), BF), pltpu.VMEM((qw, width), BF), pltpu.VMEM((total, width), BF),
            pltpu.VMEM((total, every), BF), pltpu.VMEM((total, every), BF), pltpu.VMEM((kw, total), BF),
            pltpu.VMEM((total, qw), BF), pltpu.VMEM((total, width), BF), pltpu.VMEM((total, qw), BF),
            pltpu.VMEM((total, qw), F32), pltpu.VMEM((kw // head, total, 2 * head), F32), pltpu.VMEM((total, every), BF),
            pltpu.VMEM((pieces, each, every), BF), pltpu.VMEM((pieces, qw, each), BF),
            pltpu.VMEM((size // parts, width), F32), pltpu.VMEM((size, width), F32),
            *gather_scratch(parts), *scatter_scratch(size, width, parts), DMA((7,)), DMA((2,)),
        ],
        tasks, 4 * total * width * (every + qw), 2**25,
    )


def tail_kernel(bg):
    g = Group(bg.others)
    g.greet()
    g.meet()
    for k in range(4):
        bg.step(k)
    bg.finish()


def tail(ident, tasks):
    return hosted(tail_kernel, ident, "tail", [], [], [], [], [], tasks, 0, 2**22)[1]


rope_base = 1000000.0
TP = ("c", "zl")
DP = ("r", "s", "zh")


def doc_positions(lengths_row, length):
    count = lengths_row.shape[0]
    upto = jnp.arange(count)[:, None] >= jnp.arange(count)[None, :]
    doc_ends = jnp.sum(jnp.where(upto, lengths_row[None, :], 0), axis=1)
    places = jnp.arange(length, dtype=jnp.int32)
    passed = places[:, None] >= doc_ends[None, :]
    return places - jnp.max(jnp.where(passed, doc_ends[None, :], 0), axis=1)


def rope_tables(position, head_dim):
    half_dim = head_dim // 2
    inverse = rope_base ** (-2.0 * jnp.arange(half_dim, dtype=F32) / head_dim)
    angles = position.astype(F32)[:, None] * inverse[None, :]
    cosine, sine = jnp.cos(angles), jnp.sin(angles)
    copies = LANES // head_dim
    return (
        jnp.concatenate([cosine, cosine] * copies, axis=1),
        jnp.concatenate([-sine, sine] * copies, axis=1),
    )


def swap(x):
    return lax.ppermute(x, ("c", "zh"), [(0, 0), (1, 2), (2, 1), (3, 3)])


def gather_dp(shard, axis):
    return lax.all_gather(swap(shard), DP, axis=axis, tiled=True)


def scatter_dp(partial, axis):
    return swap(lax.psum_scatter(partial, DP, scatter_dimension=axis, tiled=True)).astype(F32)


def local(
    planes, tokens, doc_lengths, grad_out, norm_gains, head_gains, conv_in, conv_kernel, conv_out,
    query_w, kv_w, out_w, gate_up, down,
):
    length = tokens.shape[0]
    head_dim = head_gains.shape[1]
    docs, count = doc_lengths.shape[1], conv_kernel.shape[0]
    conv_in = conv_in.reshape(conv_in.shape[0], -1)
    kv_w = kv_w.reshape(kv_w.shape[0], -1)
    own_w = [gate_up[l].reshape(gate_up.shape[1], -1) for l in (0, 1)]
    own_v = [down[l] for l in (0, 1)]
    pieces = 8 if planes else 1
    kv_width = kv_w.shape[1] // 2
    qgain = jnp.tile(head_gains[0:1], (1, query_w.shape[1] // head_dim))
    kgain = jnp.tile(head_gains[1:2], (1, kv_width // head_dim))
    gain = [norm_gains[i : i + 1] for i in range(4)]
    lens = jnp.pad(doc_lengths.astype(F32), ((0, 7), (0, LANES - docs)))
    taps = jnp.pad(conv_kernel, ((0, 8 - count), (0, 0)))
    rows_of = lambda got: got.reshape(-1, got.shape[-1])
    if planes:
        first = [Take(conv_in, (0, 0, 1, 2), True), Take(conv_out, (0, 0, 1, 2), True)]
        first += [Fetch(own_w[0], (0, 1, 3, 3)), Fetch(own_v[0], (0, 1, 3, 3))]
        second = [Take(x, (0, 0, 1, 2)) for x in (query_w, kv_w, out_w)] + [Fetch(own_v[1], (0, 1, 2, 2))]
        third = [Fetch(own_w[1], (0, 1, 3, 3)), Spread(grad_out, (1, 2, 3))]
    else:
        first, second, third = [], [], [Spread(grad_out, (1, 2, 3))]
        conv_in, conv_out, query_w, kv_w, out_w = map(swap, (conv_in, conv_out, query_w, kv_w, out_w))
        w0, w1 = (gather_dp(w, 0) for w in own_w)
        v0, v1 = (gather_dp(v, 1)[None] for v in own_v)

    (h1, x_block, n0, projected, lens, taps, conv_in, conv_out), got = conv_forward(
        docs, count, lens, tokens, gain[0], taps, conv_in, conv_out, planes, 0, first
    )
    if planes:
        w0, v0 = rows_of(got[0]), got[1]
    (h2, n1, hidden0), got = ffn_forward(h1, gain[1], w0, v0, 1, second)
    if planes:
        query_w, kv_w, out_w, v1 = got
    cosine, sine = rope_tables(doc_positions(lens[0, :docs].astype(jnp.int32), length), head_dim)
    (h3, n2, raw, ready, attended), got = attention_forward(
        head_dim, docs, lens, h2, gain[2], qgain, kgain, cosine, sine, query_w, kv_w, out_w, 2, third
    )
    if planes:
        w1 = rows_of(got[0])
    up_full = got[-1]
    (h4, n3, hidden1), _ = ffn_forward(h3, gain[3], w1, v1, 3)

    def halves(grad, *at):
        half = grad.shape[1] // 2
        return [Reduce(grad, i * half, half, at[i], False) for i in (0, 1)] if planes else []

    def whole(grad, at, last=False):
        return [Reduce(grad, 0, grad.shape[1], at, last)] if planes else []

    def settled(sums):
        return [Settle(x, (0,)) for x in sums]

    quarter = lax.axis_index("c") * 2 + lax.axis_index("zl")
    dh4 = lax.dynamic_slice_in_dim(up_full, quarter * h4.shape[0], h4.shape[0], 0).astype(F32)
    (dh3, gain3, gw1, gv1), (output,) = ffn_backward(
        dh4, h3, gain[3], up_full, w1, v1, n3, hidden1, 4, [Deliver(h4, (0, 2))]
    )
    (dh2, gain2, gq, gk, gqkv, gow), sums = attention_backward(
        head_dim, docs, lens, dh3, h2, gain[2], qgain, kgain, cosine, sine, query_w, kv_w, out_w, n2, raw, ready, attended,
        pieces, 5, halves(gw1, (0, 1, 4), (0, 3, 5)),
    )
    (dh1, gain1, gw0, gv0), got = ffn_backward(
        dh2, h1, gain[1], None, w0, v0, n1, hidden0, 6,
        settled(sums) + whole(gv1, (0, 1, 2)) + whole(gqkv, (0, 2, 3)) + whole(gow, (0, 2, 3)),
    )
    sums_w1, sums = got[:2], got[2:]
    (dh0, gain0, gtaps, gci, gco), got = conv_backward(
        docs, count, lens, dh1, x_block.astype(F32), gain[0], taps, conv_in, conv_out, n0, projected, pieces, 7,
        settled(sums) + halves(gw0, (0, 1, 3), (0, 3, 5)),
    )
    others, sums = got[:3], got[3:]
    grads, totals, *got = tail(
        8,
        [Deliver(dh0, (0, 0)), Total([gain0, gain1, gain2, gain3, gtaps, gq, gk], (0, 1, 2, 3), count, ("c", "zl", "s", *(("r",) if planes else ()), "zh"))]
        + settled(sums) + whole(gv0, (0, 1, 2), True) + whole(gci, (0, 1, 2), True) + whole(gco, (0, 1, 2), True),
    )
    if planes:
        gw1 = jnp.concatenate(sums_w1, axis=0)
        gv1, gqkv, gow = others
        gw0 = jnp.concatenate(got[:2], axis=0)
        gv0, gci, gco = got[2:]
    else:
        totals = lax.psum(totals, "r")
        gw0, gw1, gci, gqkv = (scatter_dp(g[0], 0) for g in (gw0, gw1, gci, gqkv))
        gv0, gv1, gco, gow = (scatter_dp(g[0], 1) for g in (gv0, gv1, gco, gow))
    heads = totals[7, : gq.shape[1] + gk.shape[1]].reshape(-1, head_dim)
    split = gq.shape[1] // head_dim
    return (
        output,
        grads.astype(F32),
        totals[:4],
        jnp.stack([jnp.sum(heads[:split], axis=0), jnp.sum(heads[split:], axis=0)]),
        gci.reshape(-1, 3, conv_kernel.shape[1]),
        totals[4 : 4 + count],
        gco,
        gqkv[:, : query_w.shape[1]],
        gqkv[:, query_w.shape[1] :].reshape(-1, 2, kv_width),
        gow,
        jnp.stack([gw0, gw1]).reshape(2, gate_up.shape[1], 2, -1),
        jnp.stack([gv0, gv1]),
    )


def solution(mesh):
    devices = mesh.devices
    dp, tp = devices.shape
    inner = Mesh(devices.reshape(dp // 4, 2, 2, 2, tp // 2), ("r", "s", "c", "zh", "zl"))
    D = ("r", "s", "c")
    T = ("zh", "zl")
    return jax.shard_map(
        functools.partial(local, dp == 8),
        mesh=inner,
        in_specs=(
            P(D, T), P(D, None), P(D, T), P(), P(), P(None, None, T), P(None, T), P(T, None),
            P(None, T), P(None, None, T), P(T, None), P(None, D, None, T), P(None, T, D),
        ),
        out_specs=(
            P(D, T), P(D, T), P(), P(), P(D, None, T), P(), P(T, D), P(D, T), P(D, None, T),
            P(T, D), P(None, D, None, T), P(None, T, D),
        ),
        check_vma=False,
    )
```

```python
import functools
import jax
import jax.numpy as jnp
from jax import lax
from jax.experimental import pallas as pl
from jax.experimental.pallas import tpu as pltpu
from jax.sharding import Mesh, PartitionSpec as P

epsilon = 1e-05
BF = jnp.bfloat16
F32 = jnp.float32
MESH = pl.DeviceIdType.MESH
DMA = pltpu.SemaphoreType.DMA
HBM = pl.BlockSpec(memory_space=pl.ANY)
INV = pl.BlockSpec(memory_space=pltpu.VMEM)
PARTS = 2
LANES = 128


class Group:
    def __init__(self, others=(), calls=True):
        c, z = lax.axis_index("c"), lax.axis_index("zl")
        self.partner, self.twin = {"c": 1 - c}, {"zl": 1 - z}
        self.mine, self.beside = 2 * c + z, 2 * (1 - c) + z
        self.across, self.far = 2 * c + (1 - z), 2 * (1 - c) + (1 - z)
        self.known = [self.partner, self.twin, *others]
        self.c, self.z = c, z
        self.barrier = pltpu.get_barrier_semaphore() if calls else None

    def greet(self):
        for other in self.known:
            pl.semaphore_signal(self.barrier, inc=1, device_id=other, device_id_type=MESH)

    def meet(self):
        pl.semaphore_wait(self.barrier, len(self.known))


def at_rows(block, size, start, count):
    return pl.ds(pl.multiple_of(block * size + start, 16), count)


def send(src, dst, sems, index, where):
    return pltpu.make_async_remote_copy(
        src_ref=src, dst_ref=dst, send_sem=sems.at[0, index], recv_sem=sems.at[1, index],
        device_id=where, device_id_type=MESH,
    )


class Gather:
    def __init__(self, group, full, size, near, over, onward):
        self.g, self.full, self.size, self.parts = group, full, size, over.shape[1]
        self.near, self.over, self.onward = near, over, onward
        self.step = size // self.parts

    def view(self, block, part):
        return self.full.at[at_rows(block, self.size, part * self.step, self.step)]

    def link(self, part, block):
        v = self.view(block, part)
        return send(v, v, self.over, part, self.g.twin)

    def close(self, part, block):
        v = self.view(block, part)
        return send(v, v, self.near, part, self.g.partner)

    def pass_on(self, part, block):
        v = self.view(block, part)
        return send(v, v, self.onward, part, self.g.partner)

    def start(self):
        for p in range(self.parts):
            self.link(p, self.g.mine).start()
            self.close(p, self.g.mine).start()

    def wait_beside(self):
        for p in range(self.parts):
            self.close(p, self.g.beside).wait_recv()

    def wait_part(self, p):
        self.link(p, self.g.across).wait_recv()
        self.pass_on(p, self.g.across).start()

    def wait_far(self, p):
        self.pass_on(p, self.g.far).wait_recv()

    def finish(self):
        for p in range(self.parts):
            self.link(p, self.g.mine).wait_send()
            self.close(p, self.g.mine).wait_send()
            self.pass_on(p, self.g.across).wait_send()


class Scatter:
    def __init__(self, group, out_near, in_near, out_over, in_over, near, over, size):
        self.g, self.size, self.parts = group, size, over.shape[1]
        self.out_near, self.in_near, self.out_over, self.in_over = out_near, in_near, out_over, in_over
        self.near, self.over = near, over
        self.step = size // self.parts

    def rows(self, part):
        return pl.ds(part * self.step, self.step)

    def close(self, which, part):
        r = self.rows(part)
        return send(self.out_near.at[which, r], self.in_near.at[which, r], self.near, which * self.parts + part, self.g.partner)

    def link(self, part):
        r = self.rows(part)
        return send(self.out_over.at[r], self.in_over.at[r], self.over, part, self.g.twin)

    def wait_all_sends(self):
        for p in range(self.parts):
            self.close(0, p).wait_send()
            self.close(1, p).wait_send()
            self.link(p).wait_send()


def scatter_scratch(size, width, parts):
    return [
        pltpu.VMEM((2, size, width), BF), pltpu.VMEM((2, size, width), BF), pltpu.VMEM((size, width), BF),
        pltpu.VMEM((size, width), BF), DMA((2, 2 * parts)), DMA((2, parts)),
    ]


def gather_scratch(parts):
    return [DMA((2, parts)), DMA((2, parts)), DMA((2, parts))]


def normalise(h, gain):
    return h * lax.rsqrt(jnp.mean(h * h, axis=-1, keepdims=True) + epsilon) * gain


def mm(a, b):
    return jnp.dot(a, b, preferred_element_type=F32)


def mm_nt(a, b):
    return lax.dot_general(a, b, (((1,), (1,)), ((), ())), preferred_element_type=F32)


def lanes(start, width):
    return pl.ds(pl.multiple_of(start, LANES), width)


def start_all(pairs, sems):
    copies = [pltpu.make_async_copy(src, dst, sems.at[i]) for i, (src, dst) in enumerate(pairs)]
    for copy in copies:
        copy.start()
    return copies


def wait_all(copies):
    for copy in copies:
        copy.wait()


def params(ident):
    return pltpu.CompilerParams(collective_id=ident, has_side_effects=True, vmem_limit_bytes=56 * 2**20)


def shaped(shape, dtype):
    return jax.ShapeDtypeStruct(shape, dtype)


END = 99


class Place:
    def __init__(self):
        self.y, self.x, self.c, self.zh = (lax.axis_index(a) for a in ("r", "s", "c", "zh"))
        self.across_x, self.across_y = {"s": 1 - self.x}, {"r": 1 - self.y}
        self.partner = {"c": 1 - self.c}
        self.plain = self.c == self.zh
        self.outer = lax.axis_index("zl") == self.zh

    def over(self, core):
        return {"c": core, "zh": 1 - self.zh}

    def swapped(self):
        return self.over(self.zh)

    PLANES = ("x", "y")
    ENDS = ("end", "swap")
    COLUMN = ("end", "swap", "z core", "z end", "z swap")

    def called(self, name):
        z = 1 - lax.axis_index("zl")
        other, far = 1 - self.c, 1 - self.zh
        return {
            "x": self.across_x, "y": self.across_y, "end": self.over(self.c), "swap": self.over(other),
            "z core": {"c": other, "zl": z}, "z end": {"zh": far, "zl": z}, "z swap": {"c": other, "zh": far, "zl": z},
        }[name]

    def piece(self, flip_y, flip_x, a):
        y = 1 - self.y if flip_y else self.y
        x = 1 - self.x if flip_x else self.x
        return 4 * y + 2 * x + a


class Fetch:
    def __init__(self, shard, at, cuts=1, stage=0):
        rows, cols = shard.shape[-2:]
        self.at, self.cuts, self.stage, self.step_rows = at, cuts, stage, rows // cuts
        self.ins = [shard]
        self.outs = [jax.ShapeDtypeStruct((8, rows, cols), shard.dtype)]
        self.out_specs = [HBM]
        self.in_place = stage == 2
        self.semaphores()
        if not self.in_place:
            self.scratch.append(pltpu.VMEM((rows, cols), BF))

    def semaphores(self):
        self.scratch = [DMA((9 * self.cuts,)), DMA((8 * self.cuts,)), DMA((2,))]

    def bind(self, ins, outs, scratch):
        (self.own,), (self.out,) = ins, outs
        self.sent, self.come, self.sem = scratch[:3]
        self.bounce = scratch[3] if len(scratch) > 3 else None
        self.p = Place()

    def greets(self):
        return Place.PLANES if self.stage == 2 else Place.PLANES + Place.ENDS

    def part(self, ref, q):
        return ref.at[pl.ds(q * self.step_rows, self.step_rows)]

    def given(self, q):
        return self.part(self.own, q)

    def slot(self, piece, q):
        return self.part(self.out.at[piece], q)

    def home(self, a, q):
        return self.slot(self.p.piece(0, 0, a), q)

    def copy(self, src, dst, q, sent, come, where):
        return pltpu.make_async_remote_copy(
            src_ref=src, dst_ref=dst, send_sem=self.sent.at[9 * q + sent], recv_sem=self.come.at[8 * q + come],
            device_id=where, device_id_type=MESH,
        )

    def to_plane(self, q):
        p = self.p
        return self.copy(self.given(q), self.home(p.c, q), q, 0, p.c, p.over(p.zh))

    def to_partner(self, q):
        p = self.p
        return self.copy(self.given(q), self.home(p.c, q), q, 1, p.c, p.partner)

    def arrived(self, a, q):
        self.copy(self.given(q), self.home(a, q), q, 0, a, self.p.partner).wait_recv()

    def keep(self):
        slot = self.out.at[self.p.piece(0, 0, self.p.c)]
        return [
            pltpu.make_async_copy(self.own, self.bounce, self.sem.at[0]),
            pltpu.make_async_copy(self.bounce, slot, self.sem.at[1]),
        ]

    def kept(self):
        self.keep()[0].start()

    def land(self):
        copies = self.keep()
        for i, copy in enumerate(copies):
            if i:
                copy.start()
            copy.wait()

    def to_x(self, a, q, src=None):
        dst = self.slot(self.p.piece(0, 0, a), q)
        return self.copy(dst if src is None else src, dst, q, 2 + a, 2 + a, self.p.across_x)

    def to_y(self, a, q, src=None):
        dst = self.slot(self.p.piece(0, 0, a), q)
        return self.copy(dst if src is None else src, dst, q, 4 + a, 4 + a, self.p.across_y)

    def spread(self, a, q, src):
        self.to_x(a, q, src).start()
        self.to_y(a, q, src).start()

    def on_y(self, q):
        there = self.slot(self.p.piece(0, 1, 0), q)
        return self.copy(there, there, q, 6, 6, self.p.across_y)

    def on_x(self, q):
        there = self.slot(self.p.piece(1, 0, 1), q)
        return self.copy(there, there, q, 7, 7, self.p.across_x)

    def forward(self, q):
        self.to_x(0, q).wait_recv()
        self.on_y(q).start()
        self.to_y(1, q).wait_recv()
        self.on_x(q).start()

    def plain(self, run):
        pl.when(self.p.plain)(run)

    def other(self, run):
        pl.when(jnp.logical_not(self.p.plain))(run)

    def step(self, k):
        p, every = self.p, range(self.cuts)

        def own():
            for q in every:
                self.spread(p.c, q, self.given(q))

        def partner():
            for q in every:
                self.to_partner(q).start()

        def second():
            for q in every:
                self.arrived(1 - p.c, q)
                self.spread(1 - p.c, q, self.home(1 - p.c, q))

        def planes():
            for q in every:
                for a in (0, 1):
                    self.spread(a, q, self.home(a, q))

        def there(q):
            for a in (0, 1):
                self.arrived(a, q)
                self.spread(a, q, self.home(a, q))

        if self.stage == 2:
            if k == 0:
                self.other(planes)
            elif k == 1:
                self.other(lambda: [self.forward(q) for q in every] and None)
            elif k == END:
                self.other(self.close)
        elif k == 0:
            self.plain(self.kept)
            self.other(partner)
            self.plain(own)
            self.plain(second)
        elif k == END:
            for q in every:
                self.to_plane(q).wait_send()
            if self.stage:
                self.plain(self.close)
                self.other(lambda: [self.arrived(a, q) for q in every for a in (0, 1)] and None)
            else:
                self.close()
            self.plain(self.land)
            self.other(lambda: [self.to_partner(q).wait_send() for q in every] and None)
        elif k in (1, 2):
            self.leave(k == 1)
        elif k == 3:
            self.plain(lambda: [self.forward(q) for q in every] and None)
        elif not self.stage:
            q = k - 4
            if q < self.cuts:
                self.other(functools.partial(there, q))
            if q:
                self.other(lambda: self.forward(q - 1))

    def leave(self, outer):
        @pl.when(self.p.outer if outer else jnp.logical_not(self.p.outer))
        def _():
            for q in range(self.cuts):
                self.to_plane(q).start()

    def close(self):
        for q in range(self.cuts):
            self.to_x(1, q).wait_recv()
            self.to_y(0, q).wait_recv()
            self.on_y(q).wait()
            self.on_x(q).wait()
            for a in (0, 1):
                self.to_x(a, q).wait_send()
                self.to_y(a, q).wait_send()


class Take(Fetch):
    def __init__(self, whole, at, inside=False):
        rows, cols = whole.shape
        self.at, self.each, self.cuts, self.stage = at, rows // 8, 1, 0
        self.ins = [whole]
        self.outs = [] if inside else [jax.ShapeDtypeStruct((rows, cols), whole.dtype)]
        self.out_specs = [] if inside else [HBM]
        self.in_place = False
        self.semaphores()
        if not inside:
            self.scratch.append(pltpu.VMEM((rows, cols), BF))

    def bind(self, ins, outs, scratch):
        (self.own,) = ins
        self.whole = outs[0] if outs else None
        self.sent, self.come, self.sem = scratch[:3]
        self.bounce = scratch[3] if len(scratch) > 3 else None
        self.p = Place()

    def rows(self, piece):
        return pl.ds(pl.multiple_of(piece * self.each, 16), self.each)

    def given(self, q):
        return self.own.at[self.rows(self.p.piece(0, 0, self.p.c))]

    def slot(self, piece, q):
        return self.whole.at[self.rows(piece)]

    def keep(self):
        if self.bounce is None:
            return [pltpu.make_async_copy(self.own, self.whole, self.sem.at[0])]
        return [
            pltpu.make_async_copy(self.own, self.bounce, self.sem.at[0]),
            pltpu.make_async_copy(self.bounce, self.whole, self.sem.at[1]),
        ]

    def step(self, k):
        def there():
            for a in (0, 1):
                self.arrived(a, 0)
                self.spread(a, 0, self.home(a, 0))

        def last():
            self.close()

        if k == 0:
            self.plain(self.kept)
        elif k in (1, 2):
            self.leave(k == 1)
        elif k == 3:
            self.other(there)
        elif k == 4:
            self.other(lambda: self.forward(0))
        elif k == END:
            self.to_plane(0).wait_send()
            self.plain(self.land)
            self.other(last)


class Exchange:
    def __init__(self, src, dst, there, sems, sem, index=0):
        self.p = Place()
        self.src, self.dst, self.there, self.sems, self.sem, self.index = src, dst, there, sems, sem, index

    def stay(self):
        return pltpu.make_async_copy(self.src, self.dst, self.sem.at[self.index])

    def leave(self):
        return send(self.src, self.there, self.sems, self.index, self.p.swapped())

    def come(self):
        return send(self.src, self.dst, self.sems, self.index, self.p.swapped())

    def both(self, stay, leave):
        pl.when(self.p.plain)(stay)
        pl.when(jnp.logical_not(self.p.plain))(leave)

    def start(self):
        self.both(lambda: self.stay().start(), lambda: self.leave().start())

    def arrive(self):
        self.both(lambda: self.stay().wait(), lambda: self.come().wait_recv())

    def finish(self):
        pl.when(jnp.logical_not(self.p.plain))(lambda: self.leave().wait_send())


class Spread:
    def __init__(self, block, at, parts=2):
        rows, cols = block.shape
        self.at, self.parts = at, parts
        self.ins = [block]
        self.outs = [jax.ShapeDtypeStruct((rows, 4 * cols), block.dtype)]
        self.out_specs = [HBM]
        self.scratch = [*gather_scratch(parts), DMA((2, 1)), DMA((1,))]

    def bind(self, ins, outs, scratch):
        (self.block,), (self.full,) = ins, outs
        near, over, onward, sems, sem = scratch
        self.p, self.g = Place(), Group(calls=False)
        self.gather = Columns(self.g, self.full, near, over, onward)
        cols = self.block.shape[1]
        mine, there = (self.full.at[:, lanes(b * cols, cols)] for b in (self.g.mine, self.g.beside))
        self.exchange = Exchange(self.block, mine, there, sems, sem)

    def greets(self):
        return Place.ENDS

    def step(self, k):
        if k == 0:
            self.exchange.start()
        elif k == 1:
            self.exchange.arrive()
            self.gather.start()
        elif k == 2:
            for p in range(self.parts):
                self.gather.wait_part(p)
        elif k == END:
            self.gather.wait_beside()
            for p in range(self.parts):
                self.gather.wait_far(p)
            self.gather.finish()
            self.exchange.finish()


class Deliver:
    def __init__(self, block, at):
        rows, width = block.shape
        self.at = at
        self.ins = [block]
        self.outs = [jax.ShapeDtypeStruct((4 * rows, width // 4), BF)]
        self.out_specs = [HBM]
        self.scratch = [pltpu.VMEM((rows, width), BF), DMA((4,)), DMA((4,)), DMA((2,))]
        if block.dtype != BF:
            self.scratch.append(pltpu.VMEM((rows, width), block.dtype))

    def bind(self, ins, outs, scratch):
        (self.block,), (self.out,) = ins, outs
        self.low, self.sent, self.come, self.sem = scratch[:4]
        self.wide = scratch[4] if len(scratch) > 4 else self.low
        self.p, self.g = Place(), Group(calls=False)

    def greets(self):
        return Place.COLUMN

    def load(self):
        return pltpu.make_async_copy(self.block, self.wide, self.sem.at[0])

    def parts(self):
        rows, width = self.low.shape
        cols = width // 4
        dst = self.out.at[at_rows(self.g.mine, rows, 0, rows)]
        for f in range(4):
            half, z = divmod(f, 2)
            here = (self.p.c == self.p.zh) & (self.p.zh == half) & (self.g.z == z)
            src = self.low.at[:, pl.ds(f * cols, cols)]
            where = {"c": self.p.zh, "zh": jnp.int32(half), "zl": jnp.int32(z)}
            yield here, pltpu.make_async_copy(src, dst, self.sem.at[1]), pltpu.make_async_remote_copy(
                src_ref=src, dst_ref=dst, send_sem=self.sent.at[f], recv_sem=self.come.at[self.g.mine],
                device_id=where, device_id_type=MESH,
            )

    def step(self, k):
        if k == 0:
            self.load().start()
        elif k == 1:
            self.load().wait()
            if self.wide is not self.low:
                self.low[...] = self.wide[...].astype(BF)
            for here, stay, leave in self.parts():
                pl.when(here)(lambda stay=stay: stay.start())
                pl.when(jnp.logical_not(here))(lambda leave=leave: leave.start())
        elif k == END:
            rows, width = self.low.shape
            for here, stay, leave in self.parts():
                pl.when(here)(lambda stay=stay: stay.wait())
                pl.when(jnp.logical_not(here))(lambda leave=leave: leave.wait_send())
            for b in range(4):
                core, z = divmod(b, 2)
                here = (self.p.c == self.p.zh) & (self.p.c == core) & (self.g.z == z)
                come = pltpu.make_async_remote_copy(
                    src_ref=self.low.at[:, pl.ds(0, width // 4)], dst_ref=self.out.at[pl.ds(b * rows, rows)],
                    send_sem=self.sent.at[0], recv_sem=self.come.at[b], device_id=self.p.partner, device_id_type=MESH,
                )
                pl.when(jnp.logical_not(here))(lambda come=come: come.wait_recv())


class Total:
    def __init__(self, pieces, at, count, axes):
        self.at, self.count, self.axes = at, count, axes
        self.ins = pieces
        self.in_specs = [INV] * len(pieces)
        width = pieces[0].shape[1]
        self.outs = [jax.ShapeDtypeStruct((8, width), F32)]
        self.out_specs = [INV]
        self.scratch = [
            pltpu.VMEM((len(self.axes), 8, width), F32), pltpu.VMEM((len(self.axes), 8, width), F32),
            DMA((2, len(self.axes))),
        ]

    def bind(self, ins, outs, scratch):
        self.pieces, (self.out,) = ins, outs
        self.sum, self.other, self.sems = scratch
        self.p, self.g = Place(), Group(calls=False)

    def greets(self):
        return ("x",) + Place.ENDS + (("y",) if "r" in self.axes else ())

    def hop(self, i):
        axis = self.axes[i]
        return send(self.sum.at[i], self.other.at[i], self.sems, i, {axis: 1 - lax.axis_index(axis)})

    def step(self, k):
        if k == 0:
            gains, taps, heads = self.pieces[:4], self.pieces[4], self.pieces[5:]
            self.sum[0] = jnp.zeros(self.sum.shape[1:], F32)
            for i, gain in enumerate(gains):
                self.sum[0, pl.ds(i, 1), :] = gain[...]
            cols = taps.shape[1]
            self.sum[0, pl.ds(4, self.count), lanes(self.g.mine * cols, cols)] = taps[pl.ds(0, self.count), :]
            done = 0
            for head in heads:
                self.sum[0, pl.ds(7, 1), pl.ds(done, head.shape[1])] = head[...]
                done += head.shape[1]
            self.hop(0).start()
        else:
            k = min(k, 4)
            last = len(self.axes) if k == 4 else k
            for i in range(k - 1, last):
                self.hop(i).wait()
                value = self.sum[i] + self.other[i]
                if i + 1 < len(self.axes):
                    self.sum[i + 1] = value
                    self.hop(i + 1).start()
                else:
                    self.out[...] = value


class Reduce:
    def __init__(self, grad, first, rows, at, last=True):
        self.first, self.rows, self.at, self.last = first, rows, at, last
        cols = grad.shape[2]
        self.ins = [grad]
        self.outs = [shaped((rows, cols), F32) if last else shaped((2, rows, cols), BF)]
        self.out_specs = [INV]
        self.scratch = [
            pltpu.VMEM((4, rows, cols), BF), pltpu.VMEM((4, rows, cols), BF), pltpu.VMEM((2, rows, cols), BF),
            DMA((9,)), DMA((8,)), DMA((4,)),
        ]
        if last:
            self.scratch.append(pltpu.VMEM((2, rows, cols), BF))

    def bind(self, ins, outs, scratch):
        (self.grad,), (self.out,) = ins, outs
        self.held, self.in1, self.in2, self.sent, self.come, self.sem = scratch[:6]
        self.in3 = scratch[6] if self.last else None
        self.p = Place()

    def greets(self):
        return Place.PLANES + (Place.ENDS if self.last else ())

    def fin(self, a):
        return self.held.at[2 * a]

    def piece(self, flip_y, flip_x, a):
        return self.grad.at[self.p.piece(flip_y, flip_x, a), pl.ds(self.first, self.rows)]

    def copy(self, src, dst, sent, come, where):
        return pltpu.make_async_remote_copy(
            src_ref=src, dst_ref=dst, send_sem=self.sent.at[sent], recv_sem=self.come.at[come],
            device_id=where, device_id_type=MESH,
        )

    def loads(self):
        kept = [(0, 0, 0), (0, 1, 0), (0, 0, 1), (1, 0, 1)]
        return [pltpu.make_async_copy(self.piece(*k), self.held.at[i], self.sem.at[i]) for i, k in enumerate(kept)]

    def first_hops(self):
        p = self.p
        return [
            self.copy(self.piece(1, 0, 0), self.in1.at[0], 0, 0, p.across_y),
            self.copy(self.piece(1, 1, 0), self.in1.at[1], 1, 1, p.across_y),
            self.copy(self.piece(0, 1, 1), self.in1.at[2], 2, 2, p.across_x),
            self.copy(self.piece(1, 1, 1), self.in1.at[3], 3, 3, p.across_x),
        ]

    def second_hops(self):
        return [
            self.copy(self.held.at[1], self.in2.at[0], 4, 4, self.p.across_x),
            self.copy(self.held.at[3], self.in2.at[1], 5, 5, self.p.across_y),
        ]

    def to_owner(self, a):
        return self.copy(self.fin(a), self.in3.at[0], 6 + a, 6, self.p.over(a))

    def to_partner(self):
        return self.copy(self.fin(1 - self.p.c), self.in3.at[1], 8, 7, self.p.partner)

    def add(self, i, other):
        self.held[i] = (self.held[i].astype(F32) + other.astype(F32)).astype(BF)

    def step(self, k):
        p = self.p
        if k == 0:
            for hop in [self.first_hops()[i] for i in (1, 3, 0, 2)]:
                hop.start()
            for load in self.loads():
                load.start()
        elif k == 1:
            for load in self.loads():
                load.wait()
            hops, after = self.first_hops(), self.second_hops()
            for i in (1, 3):
                hops[i].wait_recv()
                self.add(i, self.in1[i])
                after[i // 2].start()
            for i in (0, 2):
                hops[i].wait_recv()
                self.add(i, self.in1[i])
        elif k == 2:
            for i, hop in enumerate(self.second_hops()):
                hop.wait_recv()
                if self.last:
                    self.add(2 * i, self.in2[i])
                else:
                    self.out[i] = (self.held[2 * i].astype(F32) + self.in2[i].astype(F32)).astype(BF)
            if self.last:
                self.settle()
                self.settle(False)
        elif k == END:
            if self.last:
                self.close()
            for hop in self.first_hops() + self.second_hops():
                hop.wait_send()

    def settle(self, outer=True):
        if outer:

            @pl.when(self.p.plain)
            def _():
                self.to_partner().start()

        now = self.p.outer if outer else jnp.logical_not(self.p.outer)

        @pl.when(now & jnp.logical_not(self.p.plain))
        def _():
            self.to_owner(0).start()
            self.to_owner(1).start()

    def close(self):
        p = self.p
        self.to_owner(0).wait_recv()

        @pl.when(p.plain)
        def _():
            self.out[...] = self.own(p.c).astype(F32) + self.in3[0].astype(F32)
            self.to_partner().wait_send()

        @pl.when(jnp.logical_not(p.plain))
        def _():
            self.to_partner().wait_recv()
            self.out[...] = self.in3[1].astype(F32) + self.in3[0].astype(F32)
            self.to_owner(0).wait_send()
            self.to_owner(1).wait_send()

    def own(self, a):
        return self.held[2 * a]


class Settle(Reduce):
    def __init__(self, sums, at):
        _, rows, cols = sums.shape
        self.at = at
        self.ins = [sums]
        self.outs = [shaped((rows, cols), F32)]
        self.out_specs = [INV]
        self.scratch = [pltpu.VMEM((rows, cols), BF), pltpu.VMEM((2, rows, cols), BF), DMA((9,)), DMA((8,)), DMA((1,))]

    def bind(self, ins, outs, scratch):
        (self.sums,), (self.out,) = ins, outs
        self.kept, self.in3, self.sent, self.come, self.sem = scratch
        self.p = Place()

    def greets(self):
        return Place.ENDS

    def fin(self, a):
        return self.sums.at[a]

    def own(self, a):
        return self.kept[...]

    def load(self):
        return pltpu.make_async_copy(self.sums.at[self.p.c], self.kept, self.sem.at[0])

    def step(self, k):
        if k == 0:
            self.load().start()
            self.settle()
        elif k == 1:
            self.settle(False)
        elif k == END:
            self.load().wait()
            self.close()


class Background:
    def __init__(self, tasks, greets):
        self.tasks, self.done, names = tasks, [], list(greets)
        for task in tasks:
            names += [name for name in task.greets() if name not in names]
        place = Place()
        self.others = [place.called(name) for name in names]

    def step(self, k):
        for i in range(max([len(task.at) for task in self.tasks], default=0)):
            for task in self.tasks:
                if i < len(task.at) and task.at[i] == k:
                    task.step(i)

    def finish(self, tasks=None):
        for task in self.tasks if tasks is None else tasks:
            if task not in self.done:
                task.step(END)
                self.done.append(task)


def hosted(kernel, ident, name, ins, in_specs, outs, out_specs, scratch, tasks, flops, traffic, greets=()):
    groups = ([], [], [])
    for group, own in zip(groups, (ins, outs, scratch)):
        group.append(len(own))
    ins, in_specs, outs, out_specs, scratch = list(ins), list(in_specs), list(outs), list(out_specs), list(scratch)
    for task in tasks:
        for group, more in zip(groups, (task.ins, task.outs, task.scratch)):
            group.append(len(more))
        ins += task.ins
        in_specs += getattr(task, "in_specs", [HBM] * len(task.ins))
        outs += task.outs
        out_specs += task.out_specs
        scratch += task.scratch

    def split(refs, counts):
        at, found = 0, []
        for count in counts:
            found.append(refs[at : at + count])
            at += count
        return found

    def body(*refs):
        parts = [split(part, group) for part, group in zip(split(refs, [sum(g) for g in groups]), groups)]
        for task, *mine in zip(tasks, *(part[1:] for part in parts)):
            task.bind(*mine)
        kernel(*parts[0][0], *parts[1][0], *parts[2][0], Background(tasks, greets))

    aliases, at_in, at_out = {}, groups[0][0], groups[1][0]
    for task in tasks:
        if getattr(task, "in_place", False):
            aliases[at_in] = at_out
        at_in += len(task.ins)
        at_out += len(task.outs)
    results = pl.pallas_call(
        body,
        out_shape=tuple(outs),
        in_specs=in_specs,
        out_specs=tuple(out_specs),
        scratch_shapes=scratch,
        input_output_aliases=aliases,
        compiler_params=params(ident),
        cost_estimate=pl.CostEstimate(flops=flops, bytes_accessed=traffic, transcendentals=0),
        name=name,
    )(*ins)
    results = split(list(results), groups[1])
    return results[0], [r[0] for r in results[1:] if r]


def put_rows(scratch, first, value):
    tall = scratch.shape[1]
    done = 0
    while done < value.shape[0]:
        piece, at = divmod(first + done, tall)
        count = min(tall - at, value.shape[0] - done)
        scratch[piece, pl.ds(at, count), :] = value[done : done + count]
        done += count


def put_columns(scratch, first, value):
    wide_piece = scratch.shape[2]
    for piece in range(scratch.shape[0]):
        scratch[piece, pl.ds(first, value.shape[0]), :] = value[:, piece * wide_piece : (piece + 1) * wide_piece]


def column_loads(pieces, whole):
    each = pieces.shape[2]
    return [(pieces.at[i], whole.at[:, pl.ds(i * each, each)]) for i in range(pieces.shape[0])]


def ffn_forward_kernel(
    h_ref, gain_ref, w_hbm, v_hbm, out_ref, n_hbm, u_hbm,
    w, v, nf, u, act, tpart, mine, n_near, n_over, n_on, o_near, i_near, o_over, i_over, s_near, s_over,
    wsem, osem, bg,
):
    g = Group(bg.others)
    g.greet()
    size, width = h_ref.shape
    hidden = v.shape[0]
    loads = start_all([(w_hbm, w)] + column_loads(v_hbm, v), wsem)
    gather = Gather(g, nf, size, n_near, n_over, n_on)
    scatter = Scatter(g, o_near, i_near, o_over, i_over, s_near, s_over, size)
    parts, step = gather.parts, gather.step
    for p in range(parts):
        nf[at_rows(g.mine, size, p * step, step), :] = normalise(
            h_ref[pl.ds(p * step, step), :], gain_ref[...]
        ).astype(BF)
    g.meet()
    gather.start()
    bg.step(0)
    wait_all(loads)

    def rows_of(places):
        return jnp.concatenate([nf[r, :] for r, _ in places], axis=0) if len(places) > 1 else nf[places[0][0], :]

    def up(places):
        def body(t, carry):
            x = rows_of(places)
            wt = jnp.concatenate([w[:, lanes(t * LANES, LANES)], w[:, lanes(hidden + t * LANES, LANES)]], axis=1)
            both = mm(x, wt)
            gate, upper = both[:, :LANES], both[:, LANES:]
            a = gate * jax.nn.sigmoid(gate) * upper
            act[:, lanes(t * LANES, LANES)] = a.astype(BF)
            at = 0
            for r, count in places:
                u[r, lanes(t * LANES, LANES)] = gate[at : at + count].astype(BF)
                u[r, lanes(hidden + t * LANES, LANES)] = upper[at : at + count].astype(BF)
                at += count
            return carry

        lax.fori_loop(0, hidden // LANES, body, 0)

    def down(store):
        def body(t, carry):
            cols = lanes(t * 256, 256)
            store(cols, mm(act[...], v[:, cols]))
            return carry

        lax.fori_loop(0, width // 256, body, 0)

    def keep(index, r, count):
        return pltpu.make_async_copy(u.at[r], u_hbm.at[r], osem.at[index])

    whole = lambda block: at_rows(block, size, 0, size)
    up([(whole(g.mine), size)])
    keep(0, whole(g.mine), size).start()

    def put_mine(cols, value):
        mine[:, cols] = value

    down(put_mine)
    gather.wait_beside()
    up([(whole(g.beside), size)])
    keep(1, whole(g.beside), size).start()

    def put_beside(cols, value):
        o_near[1, :, cols] = value.astype(BF)

    down(put_beside)
    for p in range(parts):
        scatter.close(1, p).start()
    bg.step(1)
    for p in range(parts):
        gather.wait_part(p)
        gather.wait_far(p)
        r_across, r_far = at_rows(g.across, size, p * step, step), at_rows(g.far, size, p * step, step)
        up([(r_across, step), (r_far, step)])
        keep(2 + 2 * p, r_across, step).start()
        keep(3 + 2 * p, r_far, step).start()
        here = scatter.rows(p)

        def put(cols, value):
            tpart[:, cols] = value[:step]
            o_near[0, here, cols] = value[step:].astype(BF)

        down(put)
        scatter.close(0, p).start()
        scatter.close(0, p).wait_recv()
        o_over[here, :] = (tpart[...] + i_near[0, here, :].astype(F32)).astype(BF)
        scatter.link(p).start()
        bg.step(10 + p)
    n_out = pltpu.make_async_copy(nf, n_hbm, osem.at[2 + 2 * parts])
    n_out.start()
    bg.step(2)
    for p in range(parts):
        here = scatter.rows(p)
        scatter.close(1, p).wait_recv()
        scatter.link(p).wait_recv()
        out_ref[here, :] = (
            h_ref[here, :] + mine[here, :] + i_near[1, here, :].astype(F32) + i_over[here, :].astype(F32)
        )
    gather.finish()
    scatter.wait_all_sends()
    keep(0, whole(g.mine), size).wait()
    keep(1, whole(g.beside), size).wait()
    for p in range(parts):
        keep(2 + 2 * p, at_rows(g.across, size, p * step, step), step).wait()
        keep(3 + 2 * p, at_rows(g.far, size, p * step, step), step).wait()
    n_out.wait()
    bg.finish()


def ffn_forward(h, gain, w, v, ident, tasks=(), parts=PARTS):
    size, width = h.shape
    hidden = v.shape[1]
    total = 4 * size
    return hosted(
        ffn_forward_kernel, ident, "ffn_forward", [h, gain, w, v], [INV, INV, HBM, HBM],
        [shaped((size, width), F32), shaped((total, width), BF), shaped((total, 2 * hidden), BF)], [INV, HBM, HBM],
        [
            pltpu.VMEM((width, 2 * hidden), BF), pltpu.VMEM((hidden, width), BF), pltpu.VMEM((total, width), BF),
            pltpu.VMEM((total, 2 * hidden), BF), pltpu.VMEM((size, hidden), BF),
            pltpu.VMEM((size // parts, width), F32), pltpu.VMEM((size, width), F32),
            *gather_scratch(parts), *scatter_scratch(size, width, parts), DMA((1 + v.shape[0],)), DMA((3 + 2 * parts,)),
        ],
        tasks, 6 * total * width * hidden, 2**24,
    )


def mm_tn(a, b):
    return lax.dot_general(a, b, (((0,), (0,)), ((), ())), preferred_element_type=F32)


def rms_back(dn, h, gain):
    inverse = lax.rsqrt(jnp.mean(h * h, axis=-1, keepdims=True) + epsilon)
    scaled = dn * gain
    inner = jnp.mean(scaled * h, axis=-1, keepdims=True)
    grad_gain = jnp.sum(dn * h * inverse, axis=0, keepdims=True)
    return inverse * scaled - h * (inverse * inverse * inverse * inner), grad_gain


def close_scatter(scatter, mine, dh_ref, h_ref, gain_ref, out_ref, gg_ref):
    gg_ref[...] = jnp.zeros_like(gg_ref)
    for p in range(scatter.parts):
        here = scatter.rows(p)
        scatter.close(1, p).wait_recv()
        scatter.link(p).wait_recv()
        dn = mine[here, :] + scatter.in_near[1, here, :].astype(F32) + scatter.in_over[here, :].astype(F32)
        term, grad_gain = rms_back(dn, h_ref[here, :], gain_ref[...])
        out_ref[here, :] = dh_ref[here, :] + term
        gg_ref[...] += grad_gain


def ffn_backward_kernel(
    known, dh_ref, h_ref, gain_ref, df_hbm, w_hbm, v_hbm, n_hbm, u_hbm, out_ref, gg_ref, gw_hbm, gv_hbm,
    w, v, nf, u, act, df, tpart, mine, gtile, gv, n_near, n_over, n_on, o_near, i_near, o_over, i_over, s_near, s_over,
    wsem, osem, bg,
):
    g = Group(bg.others)
    g.greet()
    size, width = dh_ref.shape
    hidden = v.shape[0]
    loads = column_loads(v_hbm, v) + [(u_hbm, u), (w_hbm, w), (n_hbm, nf)]
    loads = start_all(loads + [(df_hbm, df)] if known else loads, wsem)
    gather = Gather(g, df, size, n_near, n_over, n_on)
    scatter = Scatter(g, o_near, i_near, o_over, i_over, s_near, s_over, size)
    parts, step = gather.parts, gather.step
    if not known:
        df[at_rows(g.mine, size, 0, size), :] = dh_ref[...].astype(BF)
    g.meet()
    if not known:
        gather.start()
    bg.step(0)
    wait_all(loads)

    third = hidden // 3

    def cat(ref, places, cols):
        found = [ref[r, cols] for r, _ in places]
        return found[0] if len(found) == 1 else jnp.concatenate(found, axis=0)

    def first(places):
        def body(t, carry):
            cols, more = lanes(t * third, third), lanes(hidden + t * third, third)
            da = mm_nt(cat(df, places, slice(None)), v[cols, :])
            gate, upper = cat(u, places, cols).astype(F32), cat(u, places, more).astype(F32)
            s = jax.nn.sigmoid(gate)
            lit = gate * s
            dgate = (da * upper * s * (1.0 + gate * (1.0 - s))).astype(BF)
            dupper = (da * lit).astype(BF)
            a = (lit * upper).astype(BF)
            at = 0
            for r, count in places:
                u[r, cols] = dgate[at : at + count]
                u[r, more] = dupper[at : at + count]
                act[r, cols] = a[at : at + count]
                at += count
            return carry

        lax.fori_loop(0, 3, body, 0)

    def second(places, store):
        def body(t, carry):
            cols = lanes(t * 256, 256)
            store(cols, mm_nt(cat(u, places, slice(None)), w[cols, :]))
            return carry

        lax.fori_loop(0, width // 256, body, 0)

    whole = lambda block: [(at_rows(block, size, 0, size), size)]

    def put_mine(cols, value):
        mine[:, cols] = value

    def put_beside(cols, value):
        o_near[1, :, cols] = value.astype(BF)

    def own():
        first(whole(g.mine))
        second(whole(g.mine), put_mine)

    def beside():
        first(whole(g.beside))
        second(whole(g.beside), put_beside)
        for p in range(parts):
            scatter.close(1, p).start()

    if not known:
        own()
        gather.wait_beside()
        beside()
    bg.step(1)
    for p in range(parts):
        if not known:
            gather.wait_part(p)
            gather.wait_far(p)
        pair = [(at_rows(b, size, p * step, step), step) for b in (g.across, g.far)]
        first(pair)
        here = scatter.rows(p)

        def put(cols, value):
            tpart[:, cols] = value[:step]
            o_near[0, here, cols] = value[step:].astype(BF)

        second(pair, put)
        scatter.close(0, p).start()
        scatter.close(0, p).wait_recv()
        o_over[here, :] = (tpart[...] + i_near[0, here, :].astype(F32)).astype(BF)
        scatter.link(p).start()
    bg.step(2)
    if known:
        beside()
        own()
    flush = []
    count = 0

    def emit(value, dst):
        nonlocal count
        slot = count % 2
        if count >= 2:
            flush[count - 2].wait()
        gtile[slot, :, : value.shape[1]] = value.astype(BF)
        copy = pltpu.make_async_copy(gtile.at[slot, :, : value.shape[1]], dst, osem.at[slot])
        copy.start()
        flush.append(copy)
        count += 1

    tall = gtile.shape[1]
    for t in range(3):
        put_columns(gv, t * third, mm_tn(act[:, t * third : (t + 1) * third], df[...]).astype(BF))
    save = pltpu.make_async_copy(gv, gv_hbm, osem.at[2])
    save.start()
    bg.step(3)
    each = gw_hbm.shape[1]
    for t in range(width // tall):
        piece, at = divmod(t * tall, each)
        for k in range(2):
            cols = slice(k * hidden, (k + 1) * hidden)
            emit(mm_tn(nf[:, t * tall : (t + 1) * tall], u[:, cols]), gw_hbm.at[piece, pl.ds(at, tall), cols])
    bg.step(4)
    close_scatter(scatter, mine, dh_ref, h_ref, gain_ref, out_ref, gg_ref)
    if not known:
        gather.finish()
    scatter.wait_all_sends()
    for copy in flush[-2:]:
        copy.wait()
    save.wait()
    bg.finish()


def ffn_backward(dh, h, gain, df, w, v, n, u, ident, tasks=(), parts=PARTS):
    size, width = h.shape
    pieces, hidden = v.shape[:2]
    total = 4 * size
    known = df is not None
    if not known:
        df = n
    return hosted(
        functools.partial(ffn_backward_kernel, known), ident, "ffn_backward", [dh, h, gain, df, w, v, n, u],
        [INV, INV, INV] + [HBM] * 5,
        [
            shaped((size, width), F32), shaped((1, width), F32), shaped((pieces, width // pieces, 2 * hidden), BF),
            shaped((pieces, hidden, width // pieces), BF),
        ],
        [INV, INV, HBM, HBM],
        [
            pltpu.VMEM((width, 2 * hidden), BF), pltpu.VMEM((hidden, width), BF), pltpu.VMEM((total, width), BF),
            pltpu.VMEM((total, 2 * hidden), BF), pltpu.VMEM((total, hidden), BF), pltpu.VMEM((total, width), BF),
            pltpu.VMEM((size // parts, width), F32), pltpu.VMEM((size, width), F32),
            pltpu.VMEM((2, 128, hidden), BF), pltpu.VMEM((pieces, hidden, width // pieces), BF),
            *gather_scratch(parts), *scatter_scratch(size, width, parts), DMA((4 + pieces,)), DMA((3,)),
        ],
        tasks, 12 * total * width * hidden, 2**25,
    )


MOST_DOC = 512


class Columns(Gather):
    def __init__(self, group, full, near, over, onward):
        super().__init__(group, full, full.shape[0], near, over, onward)
        self.cols = full.shape[1] // 4

    def view(self, block, part):
        return self.full.at[pl.ds(part * self.step, self.step), lanes(block * self.cols, self.cols)]


def cat_rows(ref, places, cols=slice(None)):
    found = [ref[r, cols] for r, _ in places]
    return found[0] if len(found) == 1 else jnp.concatenate(found, axis=0)


def product(src, weight, turned, tile=256):
    def run(places, store):
        width = weight.shape[0] if turned else weight.shape[1]

        def body(t, carry):
            cols = lanes(t * tile, tile)
            x = cat_rows(src, places)
            store(cols, mm_nt(x, weight[cols, :]) if turned else mm(x, weight[:, cols]))
            return carry

        lax.fori_loop(0, width // tile, body, 0)

    return run


def scatter_all(g, scatter, run, mine, tpart):
    size, step = scatter.size, scatter.step
    for p in range(scatter.parts):
        here = scatter.rows(p)

        def put(cols, value):
            tpart[:, cols] = value[:step]
            scatter.out_near[0, here, cols] = value[step:].astype(BF)

        run([(at_rows(b, size, p * step, step), step) for b in (g.across, g.far)], put)
        scatter.close(0, p).start()
        scatter.close(0, p).wait_recv()
        scatter.out_over[here, :] = (tpart[...] + scatter.in_near[0, here, :].astype(F32)).astype(BF)
        scatter.link(p).start()

    def put_beside(cols, value):
        scatter.out_near[1, :, cols] = value.astype(BF)

    run([(at_rows(g.beside, size, 0, size), size)], put_beside)
    for p in range(scatter.parts):
        scatter.close(1, p).start()

    def put_mine(cols, value):
        mine[:, cols] = value

    run([(at_rows(g.mine, size, 0, size), size)], put_mine)


def gather_everything(gather):
    gather.wait_beside()
    for p in range(gather.parts):
        gather.wait_part(p)
    for p in range(gather.parts):
        gather.wait_far(p)


def doc_starts(docs, lengths, places):
    row = lengths[pl.ds(0, 1), :]
    end = jnp.zeros((1, 1), F32)
    start = jnp.zeros_like(places)
    for d in range(docs):
        end = end + row[:, d : d + 1]
        start = jnp.where(places >= end.astype(jnp.int32), end.astype(jnp.int32), start)
    return start


def conv_taps(gated, within, taps):
    total = gated.shape[0]
    summed = taps[0] * gated
    for j in range(1, len(taps)):
        summed = summed + taps[j] * jnp.where(within >= j, pltpu.roll(gated, j, 0), 0.0)
    return summed


def conv_forward_kernel(
    docs, count, inside, lens_ref, x_hbm, gain_ref, taps_ref, win_hbm, wout_hbm,
    out_ref, block_ref, n_hbm, p_hbm, lengths, taps_out, win_out, wout_out,
    win, wout, full, nf, proj, low, mixed, tpart, mine, n_near, n_over, n_on, o_near, i_near, o_over, i_over,
    s_near, s_over, wsem, osem, xsem, xlocal, bg,
):
    g = Group(bg.others)
    g.greet()
    size, width = out_ref.shape
    total, chans = x_hbm.shape[0], wout.shape[0]
    loads = []
    if inside:
        bg.tasks[0].whole, bg.tasks[1].whole = win, wout
    else:
        loads = start_all([(win_hbm, win), (wout_hbm, wout)], wsem)
    gather = Columns(g, full, n_near, n_over, n_on)
    scatter = Scatter(g, o_near, i_near, o_over, i_over, s_near, s_over, size)
    parts = gather.parts
    blocks = [
        Exchange(
            x_hbm.at[pl.ds(p * gather.step, gather.step)],
            *(full.at[pl.ds(p * gather.step, gather.step), lanes(b * chans, chans)] for b in (g.mine, g.beside)),
            xsem, xlocal, p,
        )
        for p in range(parts)
    ]
    small = [Exchange(lens_ref, lengths, lengths, xsem, xlocal, parts), Exchange(taps_ref, taps_out, taps_out, xsem, xlocal, parts + 1)]
    g.meet()
    for block in blocks + small:
        block.start()
    bg.step(0)
    for p in range(parts):
        blocks[p].arrive()
        gather.link(p, g.mine).start()
        gather.close(p, g.mine).start()
    bg.step(1)
    gather.wait_beside()
    for p in range(parts):
        gather.wait_part(p)
    for p in range(parts):
        gather.wait_far(p)
    for block in small:
        block.arrive()
    bg.step(2)
    if inside:
        bg.finish(bg.tasks[:2])
    wait_all(loads)

    def project(t, carry):
        rows = at_rows(t, size, 0, size)
        n = normalise(full[rows, :].astype(F32), gain_ref[...]).astype(BF)
        nf[rows, :] = n
        p = mm(n, win[...])
        proj[rows, :] = p
        low[rows, :] = p.astype(BF)
        return carry

    lax.fori_loop(0, total // size, project, 0)
    bg.step(4)
    saves = start_all([(nf, n_hbm), (low, p_hbm), (win, win_out), (wout, wout_out)], osem)
    places = lax.broadcasted_iota(jnp.int32, (total, LANES), 0)
    within = places - doc_starts(docs, lengths, places)
    for k in range(chans // LANES):
        b, c, x = (proj[:, pl.ds(i * chans + k * LANES, LANES)] for i in range(3))
        taps = [taps_out[pl.ds(j, 1), pl.ds(k * LANES, LANES)] for j in range(count)]
        mixed[:, pl.ds(k * LANES, LANES)] = (c * conv_taps(b * x, within, taps)).astype(BF)
    bg.step(5)
    scatter_all(g, scatter, product(mixed, wout, False), mine, tpart)
    bg.step(3)
    block_ref[...] = full[at_rows(g.mine, size, 0, size), :]
    for p in range(scatter.parts):
        here = scatter.rows(p)
        scatter.close(1, p).wait_recv()
        scatter.link(p).wait_recv()
        out_ref[here, :] = (
            block_ref[here, :].astype(F32) + mine[here, :] + i_near[1, here, :].astype(F32) + i_over[here, :].astype(F32)
        )
    for block in blocks + small:
        block.finish()
    gather.finish()
    scatter.wait_all_sends()
    wait_all(saves)
    bg.finish()


def conv_forward(docs, count, lens, x, gain, taps, win, wout, inside, ident, tasks=(), parts=PARTS, cuts=4):
    total, chans = x.shape
    width = wout.shape[1]
    size = total // 4
    return hosted(
        functools.partial(conv_forward_kernel, docs, count, inside), ident, "conv_forward",
        [lens, x, gain, taps, win, wout], [INV, HBM, INV, INV, HBM, HBM],
        [
            shaped((size, width), F32), shaped((size, width), BF), shaped((total, width), BF), shaped((total, 3 * chans), BF),
            shaped(lens.shape, F32), shaped(taps.shape, F32), shaped(win.shape, BF), shaped(wout.shape, BF),
        ],
        [INV, INV, HBM, HBM, INV, INV, HBM, HBM],
        [
            pltpu.VMEM((width, 3 * chans), BF), pltpu.VMEM((chans, width), BF), pltpu.VMEM((total, width), BF),
            pltpu.VMEM((total, width), BF), pltpu.VMEM((total, 3 * chans), F32), pltpu.VMEM((total, 3 * chans), BF),
            pltpu.VMEM((total, chans), BF), pltpu.VMEM((size // parts, width), F32), pltpu.VMEM((size, width), F32),
            *gather_scratch(cuts), *scatter_scratch(size, width, parts), DMA((2,)), DMA((4,)),
            DMA((2, cuts + 2)), DMA((cuts + 2,)),
        ],
        tasks, 8 * total * width * chans, 2**24, ("swap",),
    )


def conv_backward_kernel(
    docs, count, lengths, dh_ref, h_ref, gain_ref, taps_ref, win_hbm, wout_hbm, n_hbm, p_hbm, out_ref, gg_ref, gt_ref, gin_hbm, gout_hbm,
    win, wout, nf, low, dz, dy, mixed, dproj, gin, gout, tpart, mine, n_near, n_over, n_on, o_near, i_near, o_over, i_over,
    s_near, s_over, wsem, osem, bg,
):
    g = Group(bg.others)
    g.greet()
    size, width = dh_ref.shape
    total, chans = 4 * size, wout.shape[0]
    loads = start_all([(wout_hbm, wout), (p_hbm, low), (win_hbm, win), (n_hbm, nf)], wsem)
    gather = Gather(g, dz, size, n_near, n_over, n_on)
    scatter = Scatter(g, o_near, i_near, o_over, i_over, s_near, s_over, size)
    dz[at_rows(g.mine, size, 0, size), :] = dh_ref[...].astype(BF)
    g.meet()
    gather.start()
    bg.step(0)
    wait_all(loads)
    places = lax.broadcasted_iota(jnp.int32, (total, LANES), 0)
    within = places - doc_starts(docs, lengths, places)
    gather_everything(gather)
    bg.step(1)

    def project(t, carry):
        rows = at_rows(t, size, 0, size)
        dy[rows, :] = mm_nt(dz[rows, :], wout[...])
        return carry

    lax.fori_loop(0, total // size, project, 0)
    for k in range(chans // LANES):
        b, c, x = (low[:, pl.ds(i * chans + k * LANES, LANES)].astype(F32) for i in range(3))
        here = pl.ds(k * LANES, LANES)
        taps = [taps_ref[pl.ds(j, 1), here] for j in range(count)]
        gated = b * x
        summed = conv_taps(gated, within, taps)
        d = dy[:, here]
        mixed[:, here] = (c * summed).astype(BF)
        ds = d * c
        dg = taps[0] * ds
        gt_ref[pl.ds(0, 1), here] = jnp.sum(ds * gated, axis=0, keepdims=True)
        for j in range(1, len(taps)):
            masked = jnp.where(within >= j, ds, 0.0)
            dg = dg + taps[j] * pltpu.roll(masked, total - j, 0)
            gt_ref[pl.ds(j, 1), here] = jnp.sum(masked * pltpu.roll(gated, j, 0), axis=0, keepdims=True)
        dproj[:, pl.ds(k * LANES, LANES)] = (dg * x).astype(BF)
        dproj[:, pl.ds(chans + k * LANES, LANES)] = (d * summed).astype(BF)
        dproj[:, pl.ds(2 * chans + k * LANES, LANES)] = (dg * b).astype(BF)
    bg.step(2)
    scatter_all(g, scatter, product(dproj, win, True), mine, tpart)
    bg.step(3)
    put_columns(gout, 0, mm_tn(mixed[...], dz[...]).astype(BF))
    save = pltpu.make_async_copy(gout, gout_hbm, osem.at[0])
    save.start()
    for t in range(width // 256):
        put_rows(gin, t * 256, mm_tn(nf[:, pl.ds(t * 256, 256)], dproj[...]).astype(BF))
    more = pltpu.make_async_copy(gin, gin_hbm, osem.at[1])
    more.start()
    bg.step(4)
    close_scatter(scatter, mine, dh_ref, h_ref, gain_ref, out_ref, gg_ref)
    gather.finish()
    scatter.wait_all_sends()
    save.wait()
    more.wait()
    bg.step(5)
    bg.finish()


def conv_backward(docs, count, lengths, dh, h, gain, taps, win, wout, n, p, pieces, ident, tasks=(), parts=PARTS):
    size, width = dh.shape
    total, chans = 4 * size, wout.shape[0]
    each = width // pieces
    return hosted(
        functools.partial(conv_backward_kernel, docs, count), ident, "conv_backward",
        [lengths, dh, h, gain, taps, win, wout, n, p],
        [INV, INV, INV, INV, INV, HBM, HBM, HBM, HBM],
        [
            shaped((size, width), F32), shaped((1, width), F32), shaped(taps.shape, F32),
            shaped((pieces, each, 3 * chans), BF), shaped((pieces, chans, each), BF),
        ],
        [INV, INV, INV, HBM, HBM],
        [
            pltpu.VMEM((width, 3 * chans), BF), pltpu.VMEM((chans, width), BF), pltpu.VMEM((total, width), BF),
            pltpu.VMEM((total, 3 * chans), BF), pltpu.VMEM((total, width), BF), pltpu.VMEM((total, chans), F32),
            pltpu.VMEM((total, chans), BF), pltpu.VMEM((total, 3 * chans), BF), pltpu.VMEM((pieces, each, 3 * chans), BF),
            pltpu.VMEM((pieces, chans, each), BF), pltpu.VMEM((size // parts, width), F32), pltpu.VMEM((size, width), F32),
            *gather_scratch(parts), *scatter_scratch(size, width, parts), DMA((4,)), DMA((2,)),
        ],
        tasks, 16 * total * width * chans, 2**24,
    )


def head_sums(values, head):
    width = values.shape[1]
    a = lax.broadcasted_iota(jnp.int32, (width, width), 0) // head
    b = lax.broadcasted_iota(jnp.int32, (width, width), 1) // head
    same = jnp.where(a == b, 1.0, 0.0).astype(BF)
    high = values.astype(BF)
    low = (values - high.astype(F32)).astype(BF)
    return mm(high, same) + mm(low, same)


def turn(values, head):
    width = values.shape[1]
    lane = lax.broadcasted_iota(jnp.int32, values.shape, 1)
    return jnp.where(
        lane % head < head // 2, pltpu.roll(values, width - head // 2, 1), pltpu.roll(values, head // 2, 1)
    )


def wide(table, width):
    return jnp.concatenate([table] * (width // table.shape[1]), axis=1)


def norm_turn(raw, gain, cosine, sine, head):
    inverse = lax.rsqrt(head_sums(raw * raw, head) * (1.0 / head) + epsilon)
    v = raw * inverse * gain
    return v * wide(cosine, raw.shape[1]) + turn(v, head) * wide(sine, raw.shape[1])


def norm_turn_back(d, raw, gain, cosine, sine, head):
    d = d * wide(cosine, raw.shape[1]) - turn(d, head) * wide(sine, raw.shape[1])
    inverse = lax.rsqrt(head_sums(raw * raw, head) * (1.0 / head) + epsilon)
    scaled = d * gain
    inner = head_sums(scaled * raw, head) * (1.0 / head)
    grad_gain = jnp.sum(d * raw * inverse, axis=0, keepdims=True)
    return inverse * scaled - raw * (inverse * inverse * inverse * inner), grad_gain


def score_tile(q, k, starts, first_key, first_query, scale):
    raw = mm_nt(k, q) * scale
    key = first_key + lax.broadcasted_iota(jnp.int32, raw.shape, 0)
    query = first_query + lax.broadcasted_iota(jnp.int32, (1, starts.shape[1]), 1)
    copies = raw.shape[1] // starts.shape[1]
    allowed = (key <= wide(query, raw.shape[1])) & (key >= wide(starts, raw.shape[1]))
    return jnp.where(allowed, raw, -1e30)


def softmax_tile(scores):
    top = jnp.max(scores, axis=0, keepdims=True)
    weights = jnp.exp(scores - top)
    return weights / jnp.sum(weights, axis=0, keepdims=True)


def stack_heads(values, head):
    return jnp.concatenate([values[:, i * head : (i + 1) * head] for i in range(values.shape[1] // head)], axis=0)


def attention_tiles(total, tile):
    back = -(-MOST_DOC // tile)
    return [(i * tile, max(0, i - back) * tile, (i + 1) * tile) for i in range(total // tile)]


def attention_forward_kernel(
    head, docs, lengths, h_ref, gain_ref, qgain_ref, kgain_ref, cos_ref, sin_ref, wq_hbm, wkv_hbm, wo_hbm,
    out_ref, n_hbm, raw_hbm, ready_hbm, o_hbm,
    w, wo, nf, low, ready, vt, o, tpart, mine, n_near, n_over, n_on, o_near, i_near, o_over, i_over,
    s_near, s_over, wsem, osem, bg,
):
    g = Group(bg.others)
    g.greet()
    size, width = h_ref.shape
    total, qw = 4 * size, wo.shape[0]
    kw = (w.shape[1] - qw) // 2
    loads = start_all([(wq_hbm, w.at[:, pl.ds(0, qw)]), (wkv_hbm, w.at[:, pl.ds(qw, 2 * kw)]), (wo_hbm, wo)], wsem)
    gather = Gather(g, nf, size, n_near, n_over, n_on)
    scatter = Scatter(g, o_near, i_near, o_over, i_over, s_near, s_over, size)
    parts, step = gather.parts, gather.step
    nf[at_rows(g.mine, size, 0, size), :] = normalise(h_ref[...], gain_ref[...]).astype(BF)
    g.meet()
    gather.start()
    bg.step(0)
    wait_all(loads)

    def project(block):
        rows = at_rows(block, size, 0, size)
        raw = mm(nf[rows, :], w[...])
        low[rows, :] = raw.astype(BF)
        cosine, sine = cos_ref[rows, :], sin_ref[rows, :]
        ready[rows, pl.ds(0, qw)] = norm_turn(raw[:, :qw], qgain_ref[...], cosine, sine, head).astype(BF)
        ready[rows, pl.ds(qw, kw)] = norm_turn(raw[:, qw : qw + kw], kgain_ref[...], cosine, sine, head).astype(BF)
        ready[rows, pl.ds(qw + kw, kw)] = raw[:, qw + kw :].astype(BF)

    project(g.mine)
    gather.wait_beside()
    project(g.beside)
    for p in range(parts):
        gather.wait_part(p)
    for p in range(parts):
        gather.wait_far(p)

    def rest(i, carry):
        project(jnp.where(i == 0, g.across, g.far))
        return carry

    lax.fori_loop(0, 2, rest, 0)
    bg.step(1)
    saves = start_all([(nf, n_hbm), (low, raw_hbm), (ready, ready_hbm)], osem)
    vt[...] = jnp.transpose(ready[:, pl.ds(qw + kw, kw)].astype(F32)).astype(BF)
    groups = qw // kw
    tile = 256
    scale = head ** (-0.5)
    starts = doc_starts(docs, lengths, lax.broadcasted_iota(jnp.int32, (1, total), 1))
    for first, low_key, high_key in attention_tiles(total, tile):
        keys = pl.ds(low_key, high_key - low_key)
        for kv in range(kw // head):
            q = stack_heads(ready[pl.ds(first, tile), pl.ds(kv * groups * head, groups * head)], head)
            k = ready[keys, pl.ds(qw, kw)][:, kv * head : (kv + 1) * head]
            p = softmax_tile(score_tile(q, k, starts[:, first : first + tile], low_key, first, scale)).astype(BF)
            ot = mm(vt[pl.ds(kv * head, head), keys], p)
            joined = jnp.concatenate([ot[:, i * tile : (i + 1) * tile] for i in range(groups)], axis=0)
            o[pl.ds(first, tile), pl.ds(kv * groups * head, groups * head)] = jnp.transpose(joined).astype(BF)
        if first == tile:
            bg.step(2)
    bg.step(3)
    save_o = pltpu.make_async_copy(o, o_hbm, osem.at[3])
    save_o.start()
    scatter_all(g, scatter, product(o, wo, False), mine, tpart)
    bg.step(4)
    for p in range(parts):
        here = scatter.rows(p)
        scatter.close(1, p).wait_recv()
        scatter.link(p).wait_recv()
        out_ref[here, :] = (
            h_ref[here, :] + mine[here, :] + i_near[1, here, :].astype(F32) + i_over[here, :].astype(F32)
        )
    gather.finish()
    scatter.wait_all_sends()
    wait_all(saves)
    save_o.wait()
    bg.finish()


def attention_forward(head, docs, lengths, h, gain, qgain, kgain, cosine, sine, wq, wkv, wo, ident, tasks=(), parts=PARTS):
    size, width = h.shape
    total, qw = 4 * size, wo.shape[0]
    kw = wkv.shape[1] // 2
    every = qw + 2 * kw
    return hosted(
        functools.partial(attention_forward_kernel, head, docs), ident, "attention_forward",
        [lengths, h, gain, qgain, kgain, cosine, sine, wq, wkv, wo], [INV] * 7 + [HBM] * 3,
        [
            shaped((size, width), F32), shaped((total, width), BF), shaped((total, every), BF), shaped((total, every), BF),
            shaped((total, qw), BF),
        ],
        [INV] + [HBM] * 4,
        [
            pltpu.VMEM((width, every), BF), pltpu.VMEM((qw, width), BF), pltpu.VMEM((total, width), BF),
            pltpu.VMEM((total, every), BF), pltpu.VMEM((total, every), BF),
            pltpu.VMEM((kw, total), BF), pltpu.VMEM((total, qw), BF),
            pltpu.VMEM((size // parts, width), F32), pltpu.VMEM((size, width), F32),
            *gather_scratch(parts), *scatter_scratch(size, width, parts), DMA((3,)), DMA((4,)),
        ],
        tasks, 2 * total * width * (every + qw), 2**24,
    )


def attention_backward_kernel(
    head, docs, lengths, dh_ref, h_ref, gain_ref, qgain_ref, kgain_ref, cos_ref, sin_ref, wq_hbm, wkv_hbm, wo_hbm,
    n_hbm, raw_hbm, ready_hbm, o_hbm, out_ref, gg_ref, gq_ref, gk_ref, gw_hbm, gwo_hbm,
    w, wo, nf, low, ready, kt, o, dz, do, dq, dkv, dlow, gw, gwo, tpart, mine,
    n_near, n_over, n_on, o_near, i_near, o_over, i_over, s_near, s_over, wsem, osem, bg,
):
    g = Group(bg.others)
    g.greet()
    size, width = h_ref.shape
    total, qw = 4 * size, wo.shape[0]
    kw = (w.shape[1] - qw) // 2
    loads = start_all(
        [
            (ready_hbm, ready), (wo_hbm, wo), (o_hbm, o), (raw_hbm, low), (wq_hbm, w.at[:, pl.ds(0, qw)]),
            (wkv_hbm, w.at[:, pl.ds(qw, 2 * kw)]), (n_hbm, nf),
        ],
        wsem,
    )
    gather = Gather(g, dz, size, n_near, n_over, n_on)
    scatter = Scatter(g, o_near, i_near, o_over, i_over, s_near, s_over, size)
    dz[at_rows(g.mine, size, 0, size), :] = dh_ref[...].astype(BF)
    g.meet()
    gather.start()
    bg.step(0)
    wait_all(loads)
    kt[...] = jnp.transpose(ready[:, pl.ds(qw, kw)].astype(F32)).astype(BF)
    dkv[...] = jnp.zeros_like(dkv)
    gather_everything(gather)

    def project(t, carry):
        rows = at_rows(t, size, 0, size)
        do[rows, :] = mm_nt(dz[rows, :], wo[...]).astype(BF)
        return carry

    bg.step(1)

    lax.fori_loop(0, total // size, project, 0)
    groups = qw // kw
    tile = 256
    scale = head ** (-0.5)
    starts = doc_starts(docs, lengths, lax.broadcasted_iota(jnp.int32, (1, total), 1))
    for first, low_key, high_key in attention_tiles(total, tile):
        keys = pl.ds(low_key, high_key - low_key)
        for kv in range(kw // head):
            cols = pl.ds(kv * groups * head, groups * head)
            lane = slice(kv * head, (kv + 1) * head)
            q = stack_heads(ready[pl.ds(first, tile), cols], head)
            k, v = ready[keys, pl.ds(qw, kw)][:, lane], ready[keys, pl.ds(qw + kw, kw)][:, lane]
            p = softmax_tile(score_tile(q, k, starts[:, first : first + tile], low_key, first, scale))
            d = stack_heads(do[pl.ds(first, tile), cols], head)
            dp = mm_nt(v, d)
            inner = jnp.sum(p * dp, axis=0, keepdims=True)
            ds = (p * (dp - inner)).astype(BF)
            both = jnp.concatenate([mm(ds, q) * scale, mm(p.astype(BF), d)], axis=1)
            dkv[kv, keys, :] += both
            dqt = mm(kt[pl.ds(kv * head, head), keys], ds) * scale
            joined = jnp.concatenate([dqt[:, i * tile : (i + 1) * tile] for i in range(groups)], axis=0)
            dq[pl.ds(first, tile), cols] = jnp.transpose(joined)
        if first == tile:
            bg.step(2)
        if first == 2 * tile:
            bg.step(3)
    bg.step(4)
    gq_ref[...] = jnp.zeros_like(gq_ref)
    gk_ref[...] = jnp.zeros_like(gk_ref)

    def finish(t, carry):
        rows = at_rows(t, size, 0, size)
        cosine, sine = cos_ref[rows, :], sin_ref[rows, :]
        d, gq = norm_turn_back(dq[rows, :], low[rows, pl.ds(0, qw)].astype(F32), qgain_ref[...], cosine, sine, head)
        gq_ref[...] += gq
        dlow[rows, pl.ds(0, qw)] = d.astype(BF)
        pairs = [dkv[kv, rows, :] for kv in range(kw // head)]
        dk = jnp.concatenate([x[:, :head] for x in pairs], axis=1)
        dv = jnp.concatenate([x[:, head:] for x in pairs], axis=1)
        d, gk = norm_turn_back(dk, low[rows, pl.ds(qw, kw)].astype(F32), kgain_ref[...], cosine, sine, head)
        gk_ref[...] += gk
        dlow[rows, pl.ds(qw, kw)] = d.astype(BF)
        dlow[rows, pl.ds(qw + kw, kw)] = dv.astype(BF)
        return carry

    lax.fori_loop(0, total // size, finish, 0)
    scatter_all(g, scatter, product(dlow, w, True), mine, tpart)
    put_columns(gwo, 0, mm_tn(o[...], dz[...]).astype(BF))
    save = pltpu.make_async_copy(gwo, gwo_hbm, osem.at[0])
    save.start()
    for t in range(width // 256):
        put_rows(gw, t * 256, mm_tn(nf[:, pl.ds(t * 256, 256)], dlow[...]).astype(BF))
    more = pltpu.make_async_copy(gw, gw_hbm, osem.at[1])
    more.start()
    bg.step(5)
    close_scatter(scatter, mine, dh_ref, h_ref, gain_ref, out_ref, gg_ref)
    gather.finish()
    scatter.wait_all_sends()
    save.wait()
    more.wait()
    bg.finish()


def attention_backward(
    head, docs, lengths, dh, h, gain, qgain, kgain, cosine, sine, wq, wkv, wo, n, raw, ready, o, pieces, ident, tasks=(),
    parts=PARTS,
):
    size, width = h.shape
    total, qw = 4 * size, wo.shape[0]
    kw = wkv.shape[1] // 2
    every = qw + 2 * kw
    each = width // pieces
    return hosted(
        functools.partial(attention_backward_kernel, head, docs), ident, "attention_backward",
        [lengths, dh, h, gain, qgain, kgain, cosine, sine, wq, wkv, wo, n, raw, ready, o], [INV] * 8 + [HBM] * 7,
        [
            shaped((size, width), F32), shaped((1, width), F32), shaped((1, qw), F32), shaped((1, kw), F32),
            shaped((pieces, each, every), BF), shaped((pieces, qw, each), BF),
        ],
        [INV, INV, INV, INV, HBM, HBM],
        [
            pltpu.VMEM((width, every), BF), pltpu.VMEM((qw, width), BF), pltpu.VMEM((total, width), BF),
            pltpu.VMEM((total, every), BF), pltpu.VMEM((total, every), BF), pltpu.VMEM((kw, total), BF),
            pltpu.VMEM((total, qw), BF), pltpu.VMEM((total, width), BF), pltpu.VMEM((total, qw), BF),
            pltpu.VMEM((total, qw), F32), pltpu.VMEM((kw // head, total, 2 * head), F32), pltpu.VMEM((total, every), BF),
            pltpu.VMEM((pieces, each, every), BF), pltpu.VMEM((pieces, qw, each), BF),
            pltpu.VMEM((size // parts, width), F32), pltpu.VMEM((size, width), F32),
            *gather_scratch(parts), *scatter_scratch(size, width, parts), DMA((7,)), DMA((2,)),
        ],
        tasks, 4 * total * width * (every + qw), 2**25,
    )


def tail_kernel(bg):
    g = Group(bg.others)
    g.greet()
    g.meet()
    for k in range(4):
        bg.step(k)
    bg.finish()


def tail(ident, tasks):
    return hosted(tail_kernel, ident, "tail", [], [], [], [], [], tasks, 0, 2**22)[1]


rope_base = 1000000.0
TP = ("c", "zl")
DP = ("r", "s", "zh")


def doc_positions(lengths_row, length):
    count = lengths_row.shape[0]
    upto = jnp.arange(count)[:, None] >= jnp.arange(count)[None, :]
    doc_ends = jnp.sum(jnp.where(upto, lengths_row[None, :], 0), axis=1)
    places = jnp.arange(length, dtype=jnp.int32)
    passed = places[:, None] >= doc_ends[None, :]
    return places - jnp.max(jnp.where(passed, doc_ends[None, :], 0), axis=1)


def rope_tables(position, head_dim):
    half_dim = head_dim // 2
    inverse = rope_base ** (-2.0 * jnp.arange(half_dim, dtype=F32) / head_dim)
    angles = position.astype(F32)[:, None] * inverse[None, :]
    cosine, sine = jnp.cos(angles), jnp.sin(angles)
    copies = LANES // head_dim
    return (
        jnp.concatenate([cosine, cosine] * copies, axis=1),
        jnp.concatenate([-sine, sine] * copies, axis=1),
    )


def swap(x):
    return lax.ppermute(x, ("c", "zh"), [(0, 0), (1, 2), (2, 1), (3, 3)])


def gather_dp(shard, axis):
    return lax.all_gather(swap(shard), DP, axis=axis, tiled=True)


def scatter_dp(partial, axis):
    return swap(lax.psum_scatter(partial, DP, scatter_dimension=axis, tiled=True)).astype(F32)


def local(
    planes, tokens, doc_lengths, grad_out, norm_gains, head_gains, conv_in, conv_kernel, conv_out,
    query_w, kv_w, out_w, gate_up, down,
):
    length = tokens.shape[0]
    head_dim = head_gains.shape[1]
    docs, count = doc_lengths.shape[1], conv_kernel.shape[0]
    conv_in = conv_in.reshape(conv_in.shape[0], -1)
    kv_w = kv_w.reshape(kv_w.shape[0], -1)
    own_w = [gate_up[l].reshape(gate_up.shape[1], -1) for l in (0, 1)]
    own_v = [down[l] for l in (0, 1)]
    pieces = 8 if planes else 1
    kv_width = kv_w.shape[1] // 2
    qgain = jnp.tile(head_gains[0:1], (1, query_w.shape[1] // head_dim))
    kgain = jnp.tile(head_gains[1:2], (1, kv_width // head_dim))
    gain = [norm_gains[i : i + 1] for i in range(4)]
    lens = jnp.pad(doc_lengths.astype(F32), ((0, 7), (0, LANES - docs)))
    taps = jnp.pad(conv_kernel, ((0, 8 - count), (0, 0)))
    rows_of = lambda got: got.reshape(-1, got.shape[-1])
    if planes:
        first = [Take(conv_in, (0, 1, 1, 2, 2), True), Take(conv_out, (0, 1, 1, 2, 2), True)]
        first += [Fetch(own_w[0], (0, 1, 1, 2, 4, 5, 3, 3, 3), 4), Fetch(own_v[0], (0, 1, 1, 2, 3, 3, 3), 2)]
        first += [Take(x, (0, 3, 3, 3, 3)) for x in (query_w, kv_w, out_w)]
        second = [Fetch(own_w[1], (0, 0, 0, 2), 1, 1), Fetch(own_v[1], (0, 0, 0, 2), 1, 1)]
    else:
        first, second, third = [], [], []
        conv_in, conv_out, query_w, kv_w, out_w = map(swap, (conv_in, conv_out, query_w, kv_w, out_w))
        w0, w1 = (gather_dp(w, 0) for w in own_w)
        v0, v1 = (gather_dp(v, 1)[None] for v in own_v)

    (h1, x_block, n0, projected, lens, taps, conv_in, conv_out), got = conv_forward(
        docs, count, lens, tokens, gain[0], taps, conv_in, conv_out, planes, 0, first
    )
    if planes:
        w0, v0 = rows_of(got[0]), got[1]
        query_w, kv_w, out_w = got[2:]
    (h2, n1, hidden0), got = ffn_forward(h1, gain[1], w0, v0, 1, second)
    if planes:
        third = [Fetch(got[0], (0, 4), 2, 2), Fetch(got[1], (0, 4), 1, 2)]
    cosine, sine = rope_tables(doc_positions(lens[0, :docs].astype(jnp.int32), length), head_dim)
    (h3, n2, raw, ready, attended), got = attention_forward(
        head_dim, docs, lens, h2, gain[2], qgain, kgain, cosine, sine, query_w, kv_w, out_w, 2, third
    )
    if planes:
        w1, v1 = rows_of(got[0]), got[1]
    (h4, n3, hidden1), (up_full,) = ffn_forward(h3, gain[3], w1, v1, 3, [Spread(grad_out, (0, 1, 2))])

    def halves(grad, *at):
        half = grad.shape[1] // 2
        return [Reduce(grad, i * half, half, at[i], False) for i in (0, 1)] if planes else []

    def whole(grad, at, last=False):
        return [Reduce(grad, 0, grad.shape[1], at, last)] if planes else []

    def settled(sums, at):
        return [Settle(x, at) for x in sums]

    quarter = lax.axis_index("c") * 2 + lax.axis_index("zl")
    dh4 = lax.dynamic_slice_in_dim(up_full, quarter * h4.shape[0], h4.shape[0], 0).astype(F32)
    (dh3, gain3, gw1, gv1), (output,) = ffn_backward(
        dh4, h3, gain[3], up_full, w1, v1, n3, hidden1, 4, [Deliver(h4, (0, 2))]
    )
    (dh2, gain2, gq, gk, gqkv, gow), sums = attention_backward(
        head_dim, docs, lens, dh3, h2, gain[2], qgain, kgain, cosine, sine, query_w, kv_w, out_w, n2, raw, ready, attended,
        pieces, 5, halves(gw1, (0, 1, 4), (0, 3, 5)),
    )
    (dh1, gain1, gw0, gv0), got = ffn_backward(
        dh2, h1, gain[1], None, w0, v0, n1, hidden0, 6,
        settled(sums, (0, 2)) + whole(gv1, (0, 1, 2)) + whole(gqkv, (0, 2, 3)) + whole(gow, (0, 2, 3)),
    )
    sums_w1, sums = got[:2], got[2:]
    (dh0, gain0, gtaps, gci, gco), got = conv_backward(
        docs, count, lens, dh1, x_block.astype(F32), gain[0], taps, conv_in, conv_out, n0, projected, pieces, 7,
        settled(sums, (0, 3)) + halves(gw0, (0, 1, 3), (0, 3, 5)),
    )
    others, sums = got[:3], got[3:]
    grads, totals, *got = tail(
        8,
        [Deliver(dh0, (0, 0)), Total([gain0, gain1, gain2, gain3, gtaps, gq, gk], (0, 1, 2, 3), count, ("c", "zl", "s", *(("r",) if planes else ()), "zh"))]
        + settled(sums, (0, 0)) + whole(gv0, (0, 1, 2), True) + whole(gci, (0, 1, 2), True) + whole(gco, (0, 1, 2), True),
    )
    if planes:
        gw1 = jnp.concatenate(sums_w1, axis=0)
        gv1, gqkv, gow = others
        gw0 = jnp.concatenate(got[:2], axis=0)
        gv0, gci, gco = got[2:]
    else:
        totals = lax.psum(totals, "r")
        gw0, gw1, gci, gqkv = (scatter_dp(g[0], 0) for g in (gw0, gw1, gci, gqkv))
        gv0, gv1, gco, gow = (scatter_dp(g[0], 1) for g in (gv0, gv1, gco, gow))
    heads = totals[7, : gq.shape[1] + gk.shape[1]].reshape(-1, head_dim)
    split = gq.shape[1] // head_dim
    return (
        output,
        grads.astype(F32),
        totals[:4],
        jnp.stack([jnp.sum(heads[:split], axis=0), jnp.sum(heads[split:], axis=0)]),
        gci.reshape(-1, 3, conv_kernel.shape[1]),
        totals[4 : 4 + count],
        gco,
        gqkv[:, : query_w.shape[1]],
        gqkv[:, query_w.shape[1] :].reshape(-1, 2, kv_width),
        gow,
        jnp.stack([gw0, gw1]).reshape(2, gate_up.shape[1], 2, -1),
        jnp.stack([gv0, gv1]),
    )


def solution(mesh):
    devices = mesh.devices
    dp, tp = devices.shape
    inner = Mesh(devices.reshape(dp // 4, 2, 2, 2, tp // 2), ("r", "s", "c", "zh", "zl"))
    D = ("r", "s", "c")
    T = ("zh", "zl")
    return jax.shard_map(
        functools.partial(local, dp == 8),
        mesh=inner,
        in_specs=(
            P(D, T), P(D, None), P(D, T), P(), P(), P(None, None, T), P(None, T), P(T, None),
            P(None, T), P(None, None, T), P(T, None), P(None, D, None, T), P(None, T, D),
        ),
        out_specs=(
            P(D, T), P(D, T), P(), P(), P(D, None, T), P(), P(T, D), P(D, T), P(D, None, T),
            P(T, D), P(None, D, None, T), P(None, T, D),
        ),
        check_vma=False,
    )
```

```python
import functools
import jax
import jax.numpy as jnp
from jax import lax
from jax.experimental import pallas as pl
from jax.experimental.pallas import tpu as pltpu
from jax.sharding import Mesh, PartitionSpec as P

epsilon = 1e-05
BF = jnp.bfloat16
F32 = jnp.float32
MESH = pl.DeviceIdType.MESH
DMA = pltpu.SemaphoreType.DMA
HBM = pl.BlockSpec(memory_space=pl.ANY)
INV = pl.BlockSpec(memory_space=pltpu.VMEM)
PARTS = 2
LANES = 128


class Group:
    def __init__(self, others=(), calls=True):
        c, z = lax.axis_index("c"), lax.axis_index("zl")
        self.partner, self.twin = {"c": 1 - c}, {"zl": 1 - z}
        self.mine, self.beside = 2 * c + z, 2 * (1 - c) + z
        self.across, self.far = 2 * c + (1 - z), 2 * (1 - c) + (1 - z)
        self.known = [self.partner, self.twin, *others]
        self.c, self.z = c, z
        self.barrier = pltpu.get_barrier_semaphore() if calls else None

    def greet(self):
        for other in self.known:
            pl.semaphore_signal(self.barrier, inc=1, device_id=other, device_id_type=MESH)

    def meet(self):
        pl.semaphore_wait(self.barrier, len(self.known))


def at_rows(block, size, start, count):
    return pl.ds(pl.multiple_of(block * size + start, 16), count)


def send(src, dst, sems, index, where):
    return pltpu.make_async_remote_copy(
        src_ref=src, dst_ref=dst, send_sem=sems.at[0, index], recv_sem=sems.at[1, index],
        device_id=where, device_id_type=MESH,
    )


class Gather:
    def __init__(self, group, full, size, near, over, onward):
        self.g, self.full, self.size, self.parts = group, full, size, over.shape[1]
        self.near, self.over, self.onward = near, over, onward
        self.step = size // self.parts

    def view(self, block, part):
        return self.full.at[at_rows(block, self.size, part * self.step, self.step)]

    def link(self, part, block):
        v = self.view(block, part)
        return send(v, v, self.over, part, self.g.twin)

    def close(self, part, block):
        v = self.view(block, part)
        return send(v, v, self.near, part, self.g.partner)

    def pass_on(self, part, block):
        v = self.view(block, part)
        return send(v, v, self.onward, part, self.g.partner)

    def start(self):
        for p in range(self.parts):
            self.link(p, self.g.mine).start()
            self.close(p, self.g.mine).start()

    def wait_beside(self):
        for p in range(self.parts):
            self.close(p, self.g.beside).wait_recv()

    def wait_part(self, p):
        self.link(p, self.g.across).wait_recv()
        self.pass_on(p, self.g.across).start()

    def wait_far(self, p):
        self.pass_on(p, self.g.far).wait_recv()

    def finish(self):
        for p in range(self.parts):
            self.link(p, self.g.mine).wait_send()
            self.close(p, self.g.mine).wait_send()
            self.pass_on(p, self.g.across).wait_send()


class Scatter:
    def __init__(self, group, out_near, in_near, out_over, in_over, near, over, size):
        self.g, self.size, self.parts = group, size, over.shape[1]
        self.out_near, self.in_near, self.out_over, self.in_over = out_near, in_near, out_over, in_over
        self.near, self.over = near, over
        self.step = size // self.parts

    def rows(self, part):
        return pl.ds(part * self.step, self.step)

    def close(self, which, part):
        r = self.rows(part)
        return send(self.out_near.at[which, r], self.in_near.at[which, r], self.near, which * self.parts + part, self.g.partner)

    def link(self, part):
        r = self.rows(part)
        return send(self.out_over.at[r], self.in_over.at[r], self.over, part, self.g.twin)

    def wait_all_sends(self):
        for p in range(self.parts):
            self.close(0, p).wait_send()
            self.close(1, p).wait_send()
            self.link(p).wait_send()


def scatter_scratch(size, width, parts):
    return [
        pltpu.VMEM((2, size, width), BF), pltpu.VMEM((2, size, width), BF), pltpu.VMEM((size, width), BF),
        pltpu.VMEM((size, width), BF), DMA((2, 2 * parts)), DMA((2, parts)),
    ]


def gather_scratch(parts):
    return [DMA((2, parts)), DMA((2, parts)), DMA((2, parts))]


def normalise(h, gain):
    return h * lax.rsqrt(jnp.mean(h * h, axis=-1, keepdims=True) + epsilon) * gain


def mm(a, b):
    return jnp.dot(a, b, preferred_element_type=F32)


def mm_nt(a, b):
    return lax.dot_general(a, b, (((1,), (1,)), ((), ())), preferred_element_type=F32)


def lanes(start, width):
    return pl.ds(pl.multiple_of(start, LANES), width)


def start_all(pairs, sems):
    copies = [pltpu.make_async_copy(src, dst, sems.at[i]) for i, (src, dst) in enumerate(pairs)]
    for copy in copies:
        copy.start()
    return copies


def wait_all(copies):
    for copy in copies:
        copy.wait()


def params(ident):
    return pltpu.CompilerParams(collective_id=ident, has_side_effects=True, vmem_limit_bytes=56 * 2**20)


def shaped(shape, dtype):
    return jax.ShapeDtypeStruct(shape, dtype)


END = 99


class Place:
    def __init__(self):
        self.y, self.x, self.c, self.zh = (lax.axis_index(a) for a in ("r", "s", "c", "zh"))
        self.across_x, self.across_y = {"s": 1 - self.x}, {"r": 1 - self.y}
        self.partner = {"c": 1 - self.c}
        self.plain = self.c == self.zh
        self.outer = lax.axis_index("zl") == self.zh

    def over(self, core):
        return {"c": core, "zh": 1 - self.zh}

    def swapped(self):
        return self.over(self.zh)

    PLANES = ("x", "y")
    ENDS = ("end", "swap")
    COLUMN = ("end", "swap", "z core", "z end", "z swap")

    def called(self, name):
        z = 1 - lax.axis_index("zl")
        other, far = 1 - self.c, 1 - self.zh
        return {
            "x": self.across_x, "y": self.across_y, "end": self.over(self.c), "swap": self.over(other),
            "z core": {"c": other, "zl": z}, "z end": {"zh": far, "zl": z}, "z swap": {"c": other, "zh": far, "zl": z},
        }[name]

    def piece(self, flip_y, flip_x, a):
        y = 1 - self.y if flip_y else self.y
        x = 1 - self.x if flip_x else self.x
        return 4 * y + 2 * x + a


class Fetch:
    def __init__(self, shard, at, cuts=1, stage=0):
        rows, cols = shard.shape[-2:]
        self.at, self.cuts, self.stage, self.step_rows = at, cuts, stage, rows // cuts
        self.ins = [shard]
        self.outs = [jax.ShapeDtypeStruct((8, rows, cols), shard.dtype)]
        self.out_specs = [HBM]
        self.in_place = stage == 2
        self.semaphores()
        if not self.in_place:
            self.scratch.append(pltpu.VMEM((rows, cols), BF))

    def semaphores(self):
        self.scratch = [DMA((9 * self.cuts,)), DMA((8 * self.cuts,)), DMA((2,))]

    def bind(self, ins, outs, scratch):
        (self.own,), (self.out,) = ins, outs
        self.sent, self.come, self.sem = scratch[:3]
        self.bounce = scratch[3] if len(scratch) > 3 else None
        self.p = Place()

    def greets(self):
        return Place.PLANES if self.stage == 2 else Place.PLANES + Place.ENDS

    def part(self, ref, q):
        return ref.at[pl.ds(q * self.step_rows, self.step_rows)]

    def given(self, q):
        return self.part(self.own, q)

    def slot(self, piece, q):
        return self.part(self.out.at[piece], q)

    def home(self, a, q):
        return self.slot(self.p.piece(0, 0, a), q)

    def copy(self, src, dst, q, sent, come, where):
        return pltpu.make_async_remote_copy(
            src_ref=src, dst_ref=dst, send_sem=self.sent.at[9 * q + sent], recv_sem=self.come.at[8 * q + come],
            device_id=where, device_id_type=MESH,
        )

    def to_plane(self, q):
        p = self.p
        return self.copy(self.given(q), self.home(p.c, q), q, 0, p.c, p.over(p.zh))

    def to_partner(self, q):
        p = self.p
        return self.copy(self.given(q), self.home(p.c, q), q, 1, p.c, p.partner)

    def arrived(self, a, q):
        self.copy(self.given(q), self.home(a, q), q, 0, a, self.p.partner).wait_recv()

    def keep(self):
        slot = self.out.at[self.p.piece(0, 0, self.p.c)]
        return [
            pltpu.make_async_copy(self.own, self.bounce, self.sem.at[0]),
            pltpu.make_async_copy(self.bounce, slot, self.sem.at[1]),
        ]

    def kept(self):
        self.keep()[0].start()

    def land(self):
        copies = self.keep()
        for i, copy in enumerate(copies):
            if i:
                copy.start()
            copy.wait()

    def to_x(self, a, q, src=None):
        dst = self.slot(self.p.piece(0, 0, a), q)
        return self.copy(dst if src is None else src, dst, q, 2 + a, 2 + a, self.p.across_x)

    def to_y(self, a, q, src=None):
        dst = self.slot(self.p.piece(0, 0, a), q)
        return self.copy(dst if src is None else src, dst, q, 4 + a, 4 + a, self.p.across_y)

    def spread(self, a, q, src):
        self.to_x(a, q, src).start()
        self.to_y(a, q, src).start()

    def on_y(self, q):
        there = self.slot(self.p.piece(0, 1, 0), q)
        return self.copy(there, there, q, 6, 6, self.p.across_y)

    def on_x(self, q):
        there = self.slot(self.p.piece(1, 0, 1), q)
        return self.copy(there, there, q, 7, 7, self.p.across_x)

    def forward(self, q):
        self.to_x(0, q).wait_recv()
        self.on_y(q).start()
        self.to_y(1, q).wait_recv()
        self.on_x(q).start()

    def plain(self, run):
        pl.when(self.p.plain)(run)

    def other(self, run):
        pl.when(jnp.logical_not(self.p.plain))(run)

    def step(self, k):
        p, every = self.p, range(self.cuts)

        def own():
            for q in every:
                self.spread(p.c, q, self.given(q))

        def partner():
            for q in every:
                self.to_partner(q).start()

        def second():
            for q in every:
                self.arrived(1 - p.c, q)
                self.spread(1 - p.c, q, self.home(1 - p.c, q))

        def planes():
            for q in every:
                for a in (0, 1):
                    self.spread(a, q, self.home(a, q))

        def there(q):
            for a in (0, 1):
                self.arrived(a, q)
                self.spread(a, q, self.home(a, q))

        if self.stage == 2:
            if k == 0:
                self.other(planes)
            elif k == 1:
                self.other(lambda: [self.forward(q) for q in every] and None)
            elif k == END:
                self.other(self.close)
        elif k == 0:
            self.plain(self.kept)
            self.other(partner)
            self.plain(own)
            self.plain(second)
        elif k == END:
            for q in every:
                self.to_plane(q).wait_send()
            if self.stage:
                self.plain(self.close)
                self.other(lambda: [self.arrived(a, q) for q in every for a in (0, 1)] and None)
            else:
                self.close()
            self.plain(self.land)
            self.other(lambda: [self.to_partner(q).wait_send() for q in every] and None)
        elif k in (1, 2):
            self.leave(k == 1)
        elif k == 3:
            self.plain(lambda: [self.forward(q) for q in every] and None)
        elif not self.stage:
            q = k - 4
            if q < self.cuts:
                self.other(functools.partial(there, q))
            if q:
                self.other(lambda: self.forward(q - 1))

    def leave(self, outer):
        @pl.when(self.p.outer if outer else jnp.logical_not(self.p.outer))
        def _():
            for q in range(self.cuts):
                self.to_plane(q).start()

    def close(self):
        for q in range(self.cuts):
            self.to_x(1, q).wait_recv()
            self.to_y(0, q).wait_recv()
            self.on_y(q).wait()
            self.on_x(q).wait()
            for a in (0, 1):
                self.to_x(a, q).wait_send()
                self.to_y(a, q).wait_send()


class Take(Fetch):
    def __init__(self, whole, at, inside=False):
        rows, cols = whole.shape
        self.at, self.each, self.cuts, self.stage = at, rows // 8, 1, 0
        self.ins = [whole]
        self.outs = [] if inside else [jax.ShapeDtypeStruct((rows, cols), whole.dtype)]
        self.out_specs = [] if inside else [HBM]
        self.in_place = False
        self.semaphores()
        if not inside:
            self.scratch.append(pltpu.VMEM((rows, cols), BF))

    def bind(self, ins, outs, scratch):
        (self.own,) = ins
        self.whole = outs[0] if outs else None
        self.sent, self.come, self.sem = scratch[:3]
        self.bounce = scratch[3] if len(scratch) > 3 else None
        self.p = Place()

    def rows(self, piece):
        return pl.ds(pl.multiple_of(piece * self.each, 16), self.each)

    def given(self, q):
        return self.own.at[self.rows(self.p.piece(0, 0, self.p.c))]

    def slot(self, piece, q):
        return self.whole.at[self.rows(piece)]

    def keep(self):
        if self.bounce is None:
            return [pltpu.make_async_copy(self.own, self.whole, self.sem.at[0])]
        return [
            pltpu.make_async_copy(self.own, self.bounce, self.sem.at[0]),
            pltpu.make_async_copy(self.bounce, self.whole, self.sem.at[1]),
        ]

    def step(self, k):
        def there():
            for a in (0, 1):
                self.arrived(a, 0)
                self.spread(a, 0, self.home(a, 0))

        def last():
            self.close()

        if k == 0:
            self.plain(self.kept)
        elif k in (1, 2):
            self.leave(k == 1)
        elif k == 3:
            self.other(there)
        elif k == 4:
            self.other(lambda: self.forward(0))
        elif k == END:
            self.to_plane(0).wait_send()
            self.plain(self.land)
            self.other(last)


class Exchange:
    def __init__(self, src, dst, there, sems, sem, index=0):
        self.p = Place()
        self.src, self.dst, self.there, self.sems, self.sem, self.index = src, dst, there, sems, sem, index

    def stay(self):
        return pltpu.make_async_copy(self.src, self.dst, self.sem.at[self.index])

    def leave(self):
        return send(self.src, self.there, self.sems, self.index, self.p.swapped())

    def come(self):
        return send(self.src, self.dst, self.sems, self.index, self.p.swapped())

    def both(self, stay, leave):
        pl.when(self.p.plain)(stay)
        pl.when(jnp.logical_not(self.p.plain))(leave)

    def start(self):
        self.both(lambda: self.stay().start(), lambda: self.leave().start())

    def arrive(self):
        self.both(lambda: self.stay().wait(), lambda: self.come().wait_recv())

    def finish(self):
        pl.when(jnp.logical_not(self.p.plain))(lambda: self.leave().wait_send())


class Spread:
    def __init__(self, block, at, parts=2):
        rows, cols = block.shape
        self.at, self.parts = at, parts
        self.ins = [block]
        self.outs = [jax.ShapeDtypeStruct((rows, 4 * cols), block.dtype)]
        self.out_specs = [HBM]
        self.scratch = [*gather_scratch(parts), DMA((2, 1)), DMA((1,))]

    def bind(self, ins, outs, scratch):
        (self.block,), (self.full,) = ins, outs
        near, over, onward, sems, sem = scratch
        self.p, self.g = Place(), Group(calls=False)
        self.gather = Columns(self.g, self.full, near, over, onward)
        cols = self.block.shape[1]
        mine, there = (self.full.at[:, lanes(b * cols, cols)] for b in (self.g.mine, self.g.beside))
        self.exchange = Exchange(self.block, mine, there, sems, sem)

    def greets(self):
        return Place.ENDS

    def step(self, k):
        if k == 0:
            self.exchange.start()
        elif k == 1:
            self.exchange.arrive()
            self.gather.start()
        elif k == 2:
            for p in range(self.parts):
                self.gather.wait_part(p)
        elif k == END:
            self.gather.wait_beside()
            for p in range(self.parts):
                self.gather.wait_far(p)
            self.gather.finish()
            self.exchange.finish()


class Deliver:
    def __init__(self, block, at):
        rows, width = block.shape
        self.at = at
        self.ins = [block]
        self.outs = [jax.ShapeDtypeStruct((4 * rows, width // 4), BF)]
        self.out_specs = [HBM]
        self.scratch = [pltpu.VMEM((rows, width), BF), DMA((4,)), DMA((4,)), DMA((2,))]
        if block.dtype != BF:
            self.scratch.append(pltpu.VMEM((rows, width), block.dtype))

    def bind(self, ins, outs, scratch):
        (self.block,), (self.out,) = ins, outs
        self.low, self.sent, self.come, self.sem = scratch[:4]
        self.wide = scratch[4] if len(scratch) > 4 else self.low
        self.p, self.g = Place(), Group(calls=False)

    def greets(self):
        return Place.COLUMN

    def load(self):
        return pltpu.make_async_copy(self.block, self.wide, self.sem.at[0])

    def parts(self):
        rows, width = self.low.shape
        cols = width // 4
        dst = self.out.at[at_rows(self.g.mine, rows, 0, rows)]
        for f in range(4):
            half, z = divmod(f, 2)
            here = (self.p.c == self.p.zh) & (self.p.zh == half) & (self.g.z == z)
            src = self.low.at[:, pl.ds(f * cols, cols)]
            where = {"c": self.p.zh, "zh": jnp.int32(half), "zl": jnp.int32(z)}
            yield here, pltpu.make_async_copy(src, dst, self.sem.at[1]), pltpu.make_async_remote_copy(
                src_ref=src, dst_ref=dst, send_sem=self.sent.at[f], recv_sem=self.come.at[self.g.mine],
                device_id=where, device_id_type=MESH,
            )

    def step(self, k):
        if k == 0:
            self.load().start()
        elif k == 1:
            self.load().wait()
            if self.wide is not self.low:
                self.low[...] = self.wide[...].astype(BF)
            for here, stay, leave in self.parts():
                pl.when(here)(lambda stay=stay: stay.start())
                pl.when(jnp.logical_not(here))(lambda leave=leave: leave.start())
        elif k == END:
            rows, width = self.low.shape
            for here, stay, leave in self.parts():
                pl.when(here)(lambda stay=stay: stay.wait())
                pl.when(jnp.logical_not(here))(lambda leave=leave: leave.wait_send())
            for b in range(4):
                core, z = divmod(b, 2)
                here = (self.p.c == self.p.zh) & (self.p.c == core) & (self.g.z == z)
                come = pltpu.make_async_remote_copy(
                    src_ref=self.low.at[:, pl.ds(0, width // 4)], dst_ref=self.out.at[pl.ds(b * rows, rows)],
                    send_sem=self.sent.at[0], recv_sem=self.come.at[b], device_id=self.p.partner, device_id_type=MESH,
                )
                pl.when(jnp.logical_not(here))(lambda come=come: come.wait_recv())


class Total:
    def __init__(self, pieces, at, count, axes):
        self.at, self.count, self.axes = at, count, axes
        self.ins = pieces
        self.in_specs = [INV] * len(pieces)
        width = pieces[0].shape[1]
        self.outs = [jax.ShapeDtypeStruct((8, width), F32)]
        self.out_specs = [INV]
        self.scratch = [
            pltpu.VMEM((len(self.axes), 8, width), F32), pltpu.VMEM((len(self.axes), 8, width), F32),
            DMA((2, len(self.axes))),
        ]

    def bind(self, ins, outs, scratch):
        self.pieces, (self.out,) = ins, outs
        self.sum, self.other, self.sems = scratch
        self.p, self.g = Place(), Group(calls=False)

    def greets(self):
        return ("x",) + Place.ENDS + (("y",) if "r" in self.axes else ())

    def hop(self, i):
        axis = self.axes[i]
        return send(self.sum.at[i], self.other.at[i], self.sems, i, {axis: 1 - lax.axis_index(axis)})

    def step(self, k):
        if k == 0:
            gains, taps, heads = self.pieces[:4], self.pieces[4], self.pieces[5:]
            self.sum[0] = jnp.zeros(self.sum.shape[1:], F32)
            for i, gain in enumerate(gains):
                self.sum[0, pl.ds(i, 1), :] = gain[...]
            cols = taps.shape[1]
            self.sum[0, pl.ds(4, self.count), lanes(self.g.mine * cols, cols)] = taps[pl.ds(0, self.count), :]
            done = 0
            for head in heads:
                self.sum[0, pl.ds(7, 1), pl.ds(done, head.shape[1])] = head[...]
                done += head.shape[1]
            self.hop(0).start()
        else:
            k = min(k, 4)
            last = len(self.axes) if k == 4 else k
            for i in range(k - 1, last):
                self.hop(i).wait()
                value = self.sum[i] + self.other[i]
                if i + 1 < len(self.axes):
                    self.sum[i + 1] = value
                    self.hop(i + 1).start()
                else:
                    self.out[...] = value


class Reduce:
    def __init__(self, grad, first, rows, at, last=True):
        self.first, self.rows, self.at, self.last = first, rows, at, last
        cols = grad.shape[2]
        self.ins = [grad]
        self.outs = [shaped((rows, cols), F32) if last else shaped((2, rows, cols), BF)]
        self.out_specs = [INV]
        self.scratch = [
            pltpu.VMEM((4, rows, cols), BF), pltpu.VMEM((4, rows, cols), BF), pltpu.VMEM((2, rows, cols), BF),
            DMA((9,)), DMA((8,)), DMA((4,)),
        ]
        if last:
            self.scratch.append(pltpu.VMEM((2, rows, cols), BF))

    def bind(self, ins, outs, scratch):
        (self.grad,), (self.out,) = ins, outs
        self.held, self.in1, self.in2, self.sent, self.come, self.sem = scratch[:6]
        self.in3 = scratch[6] if self.last else None
        self.p = Place()

    def greets(self):
        return Place.PLANES + (Place.ENDS if self.last else ())

    def fin(self, a):
        return self.held.at[2 * a]

    def piece(self, flip_y, flip_x, a):
        return self.grad.at[self.p.piece(flip_y, flip_x, a), pl.ds(self.first, self.rows)]

    def copy(self, src, dst, sent, come, where):
        return pltpu.make_async_remote_copy(
            src_ref=src, dst_ref=dst, send_sem=self.sent.at[sent], recv_sem=self.come.at[come],
            device_id=where, device_id_type=MESH,
        )

    def loads(self):
        kept = [(0, 0, 0), (0, 1, 0), (0, 0, 1), (1, 0, 1)]
        return [pltpu.make_async_copy(self.piece(*k), self.held.at[i], self.sem.at[i]) for i, k in enumerate(kept)]

    def first_hops(self):
        p = self.p
        return [
            self.copy(self.piece(1, 0, 0), self.in1.at[0], 0, 0, p.across_y),
            self.copy(self.piece(1, 1, 0), self.in1.at[1], 1, 1, p.across_y),
            self.copy(self.piece(0, 1, 1), self.in1.at[2], 2, 2, p.across_x),
            self.copy(self.piece(1, 1, 1), self.in1.at[3], 3, 3, p.across_x),
        ]

    def second_hops(self):
        return [
            self.copy(self.held.at[1], self.in2.at[0], 4, 4, self.p.across_x),
            self.copy(self.held.at[3], self.in2.at[1], 5, 5, self.p.across_y),
        ]

    def to_owner(self, a):
        return self.copy(self.fin(a), self.in3.at[0], 6 + a, 6, self.p.over(a))

    def to_partner(self):
        return self.copy(self.fin(1 - self.p.c), self.in3.at[1], 8, 7, self.p.partner)

    def add(self, i, other):
        self.held[i] = (self.held[i].astype(F32) + other.astype(F32)).astype(BF)

    def step(self, k):
        p = self.p
        if k == 0:
            for hop in [self.first_hops()[i] for i in (1, 3, 0, 2)]:
                hop.start()
            for load in self.loads():
                load.start()
        elif k == 1:
            for load in self.loads():
                load.wait()
            hops, after = self.first_hops(), self.second_hops()
            for i in (1, 3):
                hops[i].wait_recv()
                self.add(i, self.in1[i])
                after[i // 2].start()
            for i in (0, 2):
                hops[i].wait_recv()
                self.add(i, self.in1[i])
        elif k == 2:
            for i, hop in enumerate(self.second_hops()):
                hop.wait_recv()
                if self.last:
                    self.add(2 * i, self.in2[i])
                else:
                    self.out[i] = (self.held[2 * i].astype(F32) + self.in2[i].astype(F32)).astype(BF)
            if self.last:
                self.settle()
                self.settle(False)
        elif k == END:
            if self.last:
                self.close()
            for hop in self.first_hops() + self.second_hops():
                hop.wait_send()

    def settle(self, outer=True):
        if outer:

            @pl.when(self.p.plain)
            def _():
                self.to_partner().start()

        now = self.p.outer if outer else jnp.logical_not(self.p.outer)

        @pl.when(now & jnp.logical_not(self.p.plain))
        def _():
            self.to_owner(0).start()
            self.to_owner(1).start()

    def close(self):
        p = self.p
        self.to_owner(0).wait_recv()

        @pl.when(p.plain)
        def _():
            self.out[...] = self.own(p.c).astype(F32) + self.in3[0].astype(F32)
            self.to_partner().wait_send()

        @pl.when(jnp.logical_not(p.plain))
        def _():
            self.to_partner().wait_recv()
            self.out[...] = self.in3[1].astype(F32) + self.in3[0].astype(F32)
            self.to_owner(0).wait_send()
            self.to_owner(1).wait_send()

    def own(self, a):
        return self.held[2 * a]


class Settle(Reduce):
    def __init__(self, sums, at):
        _, rows, cols = sums.shape
        self.at = at
        self.ins = [sums]
        self.outs = [shaped((rows, cols), F32)]
        self.out_specs = [INV]
        self.scratch = [pltpu.VMEM((rows, cols), BF), pltpu.VMEM((2, rows, cols), BF), DMA((9,)), DMA((8,)), DMA((1,))]

    def bind(self, ins, outs, scratch):
        (self.sums,), (self.out,) = ins, outs
        self.kept, self.in3, self.sent, self.come, self.sem = scratch
        self.p = Place()

    def greets(self):
        return Place.ENDS

    def fin(self, a):
        return self.sums.at[a]

    def own(self, a):
        return self.kept[...]

    def load(self):
        return pltpu.make_async_copy(self.sums.at[self.p.c], self.kept, self.sem.at[0])

    def step(self, k):
        if k == 0:
            self.load().start()
            self.settle()
        elif k == 1:
            self.settle(False)
        elif k == END:
            self.load().wait()
            self.close()


class Background:
    def __init__(self, tasks, greets):
        self.tasks, self.done, names = tasks, [], list(greets)
        for task in tasks:
            names += [name for name in task.greets() if name not in names]
        place = Place()
        self.others = [place.called(name) for name in names]

    def step(self, k):
        for i in range(max([len(task.at) for task in self.tasks], default=0)):
            for task in self.tasks:
                if i < len(task.at) and task.at[i] == k:
                    task.step(i)

    def finish(self, tasks=None):
        for task in self.tasks if tasks is None else tasks:
            if task not in self.done:
                task.step(END)
                self.done.append(task)


def hosted(kernel, ident, name, ins, in_specs, outs, out_specs, scratch, tasks, flops, traffic, greets=()):
    groups = ([], [], [])
    for group, own in zip(groups, (ins, outs, scratch)):
        group.append(len(own))
    ins, in_specs, outs, out_specs, scratch = list(ins), list(in_specs), list(outs), list(out_specs), list(scratch)
    for task in tasks:
        for group, more in zip(groups, (task.ins, task.outs, task.scratch)):
            group.append(len(more))
        ins += task.ins
        in_specs += getattr(task, "in_specs", [HBM] * len(task.ins))
        outs += task.outs
        out_specs += task.out_specs
        scratch += task.scratch

    def split(refs, counts):
        at, found = 0, []
        for count in counts:
            found.append(refs[at : at + count])
            at += count
        return found

    def body(*refs):
        parts = [split(part, group) for part, group in zip(split(refs, [sum(g) for g in groups]), groups)]
        for task, *mine in zip(tasks, *(part[1:] for part in parts)):
            task.bind(*mine)
        kernel(*parts[0][0], *parts[1][0], *parts[2][0], Background(tasks, greets))

    aliases, at_in, at_out = {}, groups[0][0], groups[1][0]
    for task in tasks:
        if getattr(task, "in_place", False):
            aliases[at_in] = at_out
        at_in += len(task.ins)
        at_out += len(task.outs)
    results = pl.pallas_call(
        body,
        out_shape=tuple(outs),
        in_specs=in_specs,
        out_specs=tuple(out_specs),
        scratch_shapes=scratch,
        input_output_aliases=aliases,
        compiler_params=params(ident),
        cost_estimate=pl.CostEstimate(flops=flops, bytes_accessed=traffic, transcendentals=0),
        name=name,
    )(*ins)
    results = split(list(results), groups[1])
    return results[0], [r[0] for r in results[1:] if r]


def put_rows(scratch, first, value, cols=slice(None)):
    tall = scratch.shape[1]
    done = 0
    while done < value.shape[0]:
        piece, at = divmod(first + done, tall)
        count = min(tall - at, value.shape[0] - done)
        scratch[piece, pl.ds(at, count), cols] = value[done : done + count]
        done += count


def put_columns(scratch, first, value):
    wide_piece = scratch.shape[2]
    for piece in range(scratch.shape[0]):
        scratch[piece, pl.ds(first, value.shape[0]), :] = value[:, piece * wide_piece : (piece + 1) * wide_piece]


def column_loads(pieces, whole):
    each = pieces.shape[2]
    return [(pieces.at[i], whole.at[:, pl.ds(i * each, each)]) for i in range(pieces.shape[0])]


def ffn_forward_kernel(
    h_ref, gain_ref, w_hbm, v_hbm, out_ref, n_hbm, u_hbm,
    w, v, nf, u, act, tpart, mine, n_near, n_over, n_on, o_near, i_near, o_over, i_over, s_near, s_over,
    wsem, osem, bg,
):
    g = Group(bg.others)
    g.greet()
    size, width = h_ref.shape
    hidden = v.shape[0]
    loads = start_all([(w_hbm, w)] + column_loads(v_hbm, v), wsem)
    gather = Gather(g, nf, size, n_near, n_over, n_on)
    scatter = Scatter(g, o_near, i_near, o_over, i_over, s_near, s_over, size)
    parts, step = gather.parts, gather.step
    for p in range(parts):
        nf[at_rows(g.mine, size, p * step, step), :] = normalise(
            h_ref[pl.ds(p * step, step), :], gain_ref[...]
        ).astype(BF)
    g.meet()
    gather.start()
    bg.step(0)
    wait_all(loads)

    third = hidden // 3

    def rows_of(places):
        return jnp.concatenate([nf[r, :] for r, _ in places], axis=0) if len(places) > 1 else nf[places[0][0], :]

    def up(places):
        def body(t, carry):
            x = rows_of(places)
            cols, more = lanes(t * third, third), lanes(hidden + t * third, third)
            both = mm(x, jnp.concatenate([w[:, cols], w[:, more]], axis=1))
            gate, upper = both[:, :third], both[:, third:]
            a = gate * jax.nn.sigmoid(gate) * upper
            act[:, cols] = a.astype(BF)
            at = 0
            for r, count in places:
                u[r, cols] = gate[at : at + count].astype(BF)
                u[r, more] = upper[at : at + count].astype(BF)
                at += count
            return carry

        lax.fori_loop(0, 3, body, 0)

    def down(store):
        store(slice(None), mm(act[...], v[...]))

    def keep(index, r, count):
        return pltpu.make_async_copy(u.at[r], u_hbm.at[r], osem.at[index])

    whole = lambda block: at_rows(block, size, 0, size)
    up([(whole(g.mine), size)])
    keep(0, whole(g.mine), size).start()

    def put_mine(cols, value):
        mine[:, cols] = value

    down(put_mine)
    gather.wait_beside()
    up([(whole(g.beside), size)])
    keep(1, whole(g.beside), size).start()

    def put_beside(cols, value):
        o_near[1, :, cols] = value.astype(BF)

    down(put_beside)
    for p in range(parts):
        scatter.close(1, p).start()
    bg.step(1)
    for p in range(parts):
        gather.wait_part(p)
        gather.wait_far(p)
        r_across, r_far = at_rows(g.across, size, p * step, step), at_rows(g.far, size, p * step, step)
        up([(r_across, step), (r_far, step)])
        keep(2 + 2 * p, r_across, step).start()
        keep(3 + 2 * p, r_far, step).start()
        here = scatter.rows(p)

        def put(cols, value):
            tpart[:, cols] = value[:step]
            o_near[0, here, cols] = value[step:].astype(BF)

        down(put)
        scatter.close(0, p).start()
        scatter.close(0, p).wait_recv()
        o_over[here, :] = (tpart[...] + i_near[0, here, :].astype(F32)).astype(BF)
        scatter.link(p).start()
        bg.step(10 + p)
    n_out = pltpu.make_async_copy(nf, n_hbm, osem.at[2 + 2 * parts])
    n_out.start()
    bg.step(2)
    for p in range(parts):
        here = scatter.rows(p)
        scatter.close(1, p).wait_recv()
        scatter.link(p).wait_recv()
        out_ref[here, :] = (
            h_ref[here, :] + mine[here, :] + i_near[1, here, :].astype(F32) + i_over[here, :].astype(F32)
        )
    gather.finish()
    scatter.wait_all_sends()
    keep(0, whole(g.mine), size).wait()
    keep(1, whole(g.beside), size).wait()
    for p in range(parts):
        keep(2 + 2 * p, at_rows(g.across, size, p * step, step), step).wait()
        keep(3 + 2 * p, at_rows(g.far, size, p * step, step), step).wait()
    n_out.wait()
    bg.step(6)
    bg.finish()


def ffn_forward(h, gain, w, v, ident, tasks=(), parts=PARTS):
    size, width = h.shape
    hidden = v.shape[1]
    total = 4 * size
    return hosted(
        ffn_forward_kernel, ident, "ffn_forward", [h, gain, w, v], [INV, INV, HBM, HBM],
        [shaped((size, width), F32), shaped((total, width), BF), shaped((total, 2 * hidden), BF)], [INV, HBM, HBM],
        [
            pltpu.VMEM((width, 2 * hidden), BF), pltpu.VMEM((hidden, width), BF), pltpu.VMEM((total, width), BF),
            pltpu.VMEM((total, 2 * hidden), BF), pltpu.VMEM((size, hidden), BF),
            pltpu.VMEM((size // parts, width), F32), pltpu.VMEM((size, width), F32),
            *gather_scratch(parts), *scatter_scratch(size, width, parts), DMA((1 + v.shape[0],)), DMA((3 + 2 * parts,)),
        ],
        tasks, 6 * total * width * hidden, 2**24,
    )


def mm_tn(a, b):
    return lax.dot_general(a, b, (((0,), (0,)), ((), ())), preferred_element_type=F32)


def rms_back(dn, h, gain):
    inverse = lax.rsqrt(jnp.mean(h * h, axis=-1, keepdims=True) + epsilon)
    scaled = dn * gain
    inner = jnp.mean(scaled * h, axis=-1, keepdims=True)
    grad_gain = jnp.sum(dn * h * inverse, axis=0, keepdims=True)
    return inverse * scaled - h * (inverse * inverse * inverse * inner), grad_gain


def close_scatter(scatter, mine, dh_ref, h_ref, gain_ref, out_ref, gg_ref):
    gg_ref[...] = jnp.zeros_like(gg_ref)
    for p in range(scatter.parts):
        here = scatter.rows(p)
        scatter.close(1, p).wait_recv()
        scatter.link(p).wait_recv()
        dn = mine[here, :] + scatter.in_near[1, here, :].astype(F32) + scatter.in_over[here, :].astype(F32)
        term, grad_gain = rms_back(dn, h_ref[here, :], gain_ref[...])
        out_ref[here, :] = dh_ref[here, :].astype(F32) + term
        gg_ref[...] += grad_gain


def ffn_backward_kernel(
    known, dh_ref, h_ref, gain_ref, df_hbm, w_hbm, v_hbm, n_hbm, u_hbm, out_ref, gg_ref, gw_hbm, gv_hbm,
    w, v, nf, u, act, df, tpart, mine, gw, gv, n_near, n_over, n_on, o_near, i_near, o_over, i_over, s_near, s_over,
    wsem, osem, bg,
):
    g = Group(bg.others)
    g.greet()
    size, width = h_ref.shape
    hidden = v.shape[0]
    loads = column_loads(v_hbm, v) + [(u_hbm, u), (w_hbm, w), (n_hbm, nf)]
    loads = start_all(loads + [(df_hbm, df)] if known else loads, wsem)
    gather = Gather(g, df, size, n_near, n_over, n_on)
    scatter = Scatter(g, o_near, i_near, o_over, i_over, s_near, s_over, size)
    parts, step = gather.parts, gather.step
    if not known:
        df[at_rows(g.mine, size, 0, size), :] = dh_ref[...].astype(BF)
    g.meet()
    if not known:
        gather.start()
    bg.step(0)
    wait_all(loads)

    third = hidden // 3

    def cat(ref, places, cols):
        found = [ref[r, cols] for r, _ in places]
        return found[0] if len(found) == 1 else jnp.concatenate(found, axis=0)

    def first(places):
        def body(t, carry):
            cols, more = lanes(t * third, third), lanes(hidden + t * third, third)
            da = mm_nt(cat(df, places, slice(None)), v[cols, :])
            gate, upper = cat(u, places, cols).astype(F32), cat(u, places, more).astype(F32)
            s = jax.nn.sigmoid(gate)
            lit = gate * s
            dgate = (da * upper * s * (1.0 + gate * (1.0 - s))).astype(BF)
            dupper = (da * lit).astype(BF)
            a = (lit * upper).astype(BF)
            at = 0
            for r, count in places:
                u[r, cols] = dgate[at : at + count]
                u[r, more] = dupper[at : at + count]
                act[r, cols] = a[at : at + count]
                at += count
            return carry

        lax.fori_loop(0, 3, body, 0)

    def second(places, store):
        def body(t, carry):
            cols = lanes(t * 512, 512)
            store(cols, mm_nt(cat(u, places, slice(None)), w[cols, :]))
            return carry

        lax.fori_loop(0, width // 512, body, 0)

    whole = lambda block: [(at_rows(block, size, 0, size), size)]

    def put_mine(cols, value):
        mine[:, cols] = value

    def put_beside(cols, value):
        o_near[1, :, cols] = value.astype(BF)

    def own():
        first(whole(g.mine))
        second(whole(g.mine), put_mine)

    def beside():
        first(whole(g.beside))
        second(whole(g.beside), put_beside)
        for p in range(parts):
            scatter.close(1, p).start()

    if not known:
        own()
        gather.wait_beside()
        beside()
    bg.step(1)
    for p in range(parts):
        if not known:
            gather.wait_part(p)
            gather.wait_far(p)
        pair = [(at_rows(b, size, p * step, step), step) for b in (g.across, g.far)]
        first(pair)
        here = scatter.rows(p)

        def put(cols, value):
            tpart[:, cols] = value[:step]
            o_near[0, here, cols] = value[step:].astype(BF)

        second(pair, put)
        scatter.close(0, p).start()
        scatter.close(0, p).wait_recv()
        o_over[here, :] = (tpart[...] + i_near[0, here, :].astype(F32)).astype(BF)
        scatter.link(p).start()
    bg.step(2)
    if known:
        beside()
        own()
    for t in range(3):
        put_columns(gv, t * third, mm_tn(act[:, t * third : (t + 1) * third], df[...]).astype(BF))
    save = pltpu.make_async_copy(gv, gv_hbm, osem.at[2])
    save.start()
    bg.step(3)
    for t in range(width // 512):
        for k in range(2):
            cols = slice(k * hidden, (k + 1) * hidden)
            put_rows(gw, t * 512, mm_tn(nf[:, t * 512 : (t + 1) * 512], u[:, cols]).astype(BF), cols)
    more = pltpu.make_async_copy(gw, gw_hbm, osem.at[0])
    more.start()
    bg.step(4)
    close_scatter(scatter, mine, df.at[at_rows(g.mine, size, 0, size)] if known else dh_ref, h_ref, gain_ref, out_ref, gg_ref)
    if not known:
        gather.finish()
    scatter.wait_all_sends()
    more.wait()
    save.wait()
    bg.step(6)
    bg.finish()


def ffn_backward(dh, h, gain, df, w, v, n, u, ident, tasks=(), parts=PARTS):
    size, width = h.shape
    pieces, hidden = v.shape[:2]
    total = 4 * size
    known = df is not None
    if known:
        dh = gain
    else:
        df = n
    return hosted(
        functools.partial(ffn_backward_kernel, known), ident, "ffn_backward", [dh, h, gain, df, w, v, n, u],
        [INV, INV, INV] + [HBM] * 5,
        [
            shaped((size, width), F32), shaped((1, width), F32), shaped((pieces, width // pieces, 2 * hidden), BF),
            shaped((pieces, hidden, width // pieces), BF),
        ],
        [INV, INV, HBM, HBM],
        [
            pltpu.VMEM((width, 2 * hidden), BF), pltpu.VMEM((hidden, width), BF), pltpu.VMEM((total, width), BF),
            pltpu.VMEM((total, 2 * hidden), BF), pltpu.VMEM((total, hidden), BF), pltpu.VMEM((total, width), BF),
            pltpu.VMEM((size // parts, width), F32), pltpu.VMEM((size, width), F32),
            pltpu.VMEM((pieces, width // pieces, 2 * hidden), BF), pltpu.VMEM((pieces, hidden, width // pieces), BF),
            *gather_scratch(parts), *scatter_scratch(size, width, parts), DMA((4 + pieces,)), DMA((3,)),
        ],
        tasks, 12 * total * width * hidden, 2**25,
    )


MOST_DOC = 512


class Columns(Gather):
    def __init__(self, group, full, near, over, onward):
        super().__init__(group, full, full.shape[0], near, over, onward)
        self.cols = full.shape[1] // 4

    def view(self, block, part):
        return self.full.at[pl.ds(part * self.step, self.step), lanes(block * self.cols, self.cols)]


def cat_rows(ref, places, cols=slice(None)):
    found = [ref[r, cols] for r, _ in places]
    return found[0] if len(found) == 1 else jnp.concatenate(found, axis=0)


def product(src, weight, turned, tile=512):
    def run(places, store):
        width = weight.shape[0] if turned else weight.shape[1]

        def body(t, carry):
            cols = lanes(t * tile, tile)
            x = cat_rows(src, places)
            store(cols, mm_nt(x, weight[cols, :]) if turned else mm(x, weight[:, cols]))
            return carry

        lax.fori_loop(0, width // tile, body, 0)

    return run


def scatter_all(g, scatter, run, mine, tpart):
    size, step = scatter.size, scatter.step
    for p in range(scatter.parts):
        here = scatter.rows(p)

        def put(cols, value):
            tpart[:, cols] = value[:step]
            scatter.out_near[0, here, cols] = value[step:].astype(BF)

        run([(at_rows(b, size, p * step, step), step) for b in (g.across, g.far)], put)
        scatter.close(0, p).start()
        scatter.close(0, p).wait_recv()
        scatter.out_over[here, :] = (tpart[...] + scatter.in_near[0, here, :].astype(F32)).astype(BF)
        scatter.link(p).start()

    def put_beside(cols, value):
        scatter.out_near[1, :, cols] = value.astype(BF)

    run([(at_rows(g.beside, size, 0, size), size)], put_beside)
    for p in range(scatter.parts):
        scatter.close(1, p).start()

    def put_mine(cols, value):
        mine[:, cols] = value

    run([(at_rows(g.mine, size, 0, size), size)], put_mine)


def gather_everything(gather):
    gather.wait_beside()
    for p in range(gather.parts):
        gather.wait_part(p)
    for p in range(gather.parts):
        gather.wait_far(p)


def doc_starts(docs, lengths, places):
    row = lengths[pl.ds(0, 1), :]
    end = jnp.zeros((1, 1), F32)
    start = jnp.zeros_like(places)
    for d in range(docs):
        end = end + row[:, d : d + 1]
        start = jnp.where(places >= end.astype(jnp.int32), end.astype(jnp.int32), start)
    return start


def conv_taps(gated, within, taps):
    total = gated.shape[0]
    summed = taps[0] * gated
    for j in range(1, len(taps)):
        summed = summed + taps[j] * jnp.where(within >= j, pltpu.roll(gated, j, 0), 0.0)
    return summed


def conv_forward_kernel(
    docs, count, inside, lens_ref, x_hbm, gain_ref, taps_ref, win_hbm, wout_hbm,
    out_ref, block_ref, n_hbm, p_hbm, lengths, taps_out, win_out, wout_out,
    win, wout, full, nf, proj, low, mixed, tpart, mine, n_near, n_over, n_on, o_near, i_near, o_over, i_over,
    s_near, s_over, wsem, osem, xsem, xlocal, bg,
):
    g = Group(bg.others)
    g.greet()
    size, width = out_ref.shape
    total, chans = x_hbm.shape[0], wout.shape[0]
    loads = []
    if inside:
        bg.tasks[0].whole, bg.tasks[1].whole = win, wout
    else:
        loads = start_all([(win_hbm, win), (wout_hbm, wout)], wsem)
    gather = Columns(g, full, n_near, n_over, n_on)
    scatter = Scatter(g, o_near, i_near, o_over, i_over, s_near, s_over, size)
    parts = gather.parts
    blocks = [
        Exchange(
            x_hbm.at[pl.ds(p * gather.step, gather.step)],
            *(full.at[pl.ds(p * gather.step, gather.step), lanes(b * chans, chans)] for b in (g.mine, g.beside)),
            xsem, xlocal, p,
        )
        for p in range(parts)
    ]
    small = [Exchange(lens_ref, lengths, lengths, xsem, xlocal, parts), Exchange(taps_ref, taps_out, taps_out, xsem, xlocal, parts + 1)]
    g.meet()
    for block in blocks + small:
        block.start()
    bg.step(0)
    for p in range(parts):
        blocks[p].arrive()
        gather.link(p, g.mine).start()
        gather.close(p, g.mine).start()
    bg.step(1)
    gather.wait_beside()
    for p in range(parts):
        gather.wait_part(p)
    for p in range(parts):
        gather.wait_far(p)
    for block in small:
        block.arrive()
    bg.step(2)
    if inside:
        bg.finish(bg.tasks[:2])
    wait_all(loads)

    def project(t, carry):
        rows = at_rows(t, size, 0, size)
        n = normalise(full[rows, :].astype(F32), gain_ref[...]).astype(BF)
        nf[rows, :] = n
        p = mm(n, win[...])
        proj[rows, :] = p
        low[rows, :] = p.astype(BF)
        return carry

    lax.fori_loop(0, total // size, project, 0)
    bg.step(4)
    saves = start_all([(nf, n_hbm), (low, p_hbm), (win, win_out), (wout, wout_out)], osem)
    places = lax.broadcasted_iota(jnp.int32, (total, LANES), 0)
    within = places - doc_starts(docs, lengths, places)
    for k in range(chans // LANES):
        b, c, x = (proj[:, pl.ds(i * chans + k * LANES, LANES)] for i in range(3))
        taps = [taps_out[pl.ds(j, 1), pl.ds(k * LANES, LANES)] for j in range(count)]
        mixed[:, pl.ds(k * LANES, LANES)] = (c * conv_taps(b * x, within, taps)).astype(BF)
    bg.step(5)
    scatter_all(g, scatter, product(mixed, wout, False), mine, tpart)
    bg.step(3)
    block_ref[...] = full[at_rows(g.mine, size, 0, size), :]
    for p in range(scatter.parts):
        here = scatter.rows(p)
        scatter.close(1, p).wait_recv()
        scatter.link(p).wait_recv()
        out_ref[here, :] = (
            block_ref[here, :].astype(F32) + mine[here, :] + i_near[1, here, :].astype(F32) + i_over[here, :].astype(F32)
        )
    for block in blocks + small:
        block.finish()
    gather.finish()
    scatter.wait_all_sends()
    wait_all(saves)
    bg.step(6)
    bg.finish()


def conv_forward(docs, count, lens, x, gain, taps, win, wout, inside, ident, tasks=(), parts=PARTS, cuts=4):
    total, chans = x.shape
    width = wout.shape[1]
    size = total // 4
    return hosted(
        functools.partial(conv_forward_kernel, docs, count, inside), ident, "conv_forward",
        [lens, x, gain, taps, win, wout], [INV, HBM, INV, INV, HBM, HBM],
        [
            shaped((size, width), F32), shaped((size, width), BF), shaped((total, width), BF), shaped((total, 3 * chans), BF),
            shaped(lens.shape, F32), shaped(taps.shape, F32), shaped(win.shape, BF), shaped(wout.shape, BF),
        ],
        [INV, INV, HBM, HBM, INV, INV, HBM, HBM],
        [
            pltpu.VMEM((width, 3 * chans), BF), pltpu.VMEM((chans, width), BF), pltpu.VMEM((total, width), BF),
            pltpu.VMEM((total, width), BF), pltpu.VMEM((total, 3 * chans), F32), pltpu.VMEM((total, 3 * chans), BF),
            pltpu.VMEM((total, chans), BF), pltpu.VMEM((size // parts, width), F32), pltpu.VMEM((size, width), F32),
            *gather_scratch(cuts), *scatter_scratch(size, width, parts), DMA((2,)), DMA((4,)),
            DMA((2, cuts + 2)), DMA((cuts + 2,)),
        ],
        tasks, 8 * total * width * chans, 2**24, ("swap",),
    )


def conv_backward_kernel(
    docs, count, lengths, dh_ref, h_ref, gain_ref, taps_ref, win_hbm, wout_hbm, n_hbm, p_hbm, out_ref, gg_ref, gt_ref, gin_hbm, gout_hbm,
    win, wout, nf, low, dz, dy, mixed, dproj, gin, gout, tpart, mine, n_near, n_over, n_on, o_near, i_near, o_over, i_over,
    s_near, s_over, wsem, osem, bg,
):
    g = Group(bg.others)
    g.greet()
    size, width = dh_ref.shape
    total, chans = 4 * size, wout.shape[0]
    loads = start_all([(wout_hbm, wout), (p_hbm, low), (win_hbm, win), (n_hbm, nf)], wsem)
    gather = Gather(g, dz, size, n_near, n_over, n_on)
    scatter = Scatter(g, o_near, i_near, o_over, i_over, s_near, s_over, size)
    dz[at_rows(g.mine, size, 0, size), :] = dh_ref[...].astype(BF)
    g.meet()
    gather.start()
    bg.step(0)
    wait_all(loads)
    places = lax.broadcasted_iota(jnp.int32, (total, LANES), 0)
    within = places - doc_starts(docs, lengths, places)
    gather_everything(gather)
    bg.step(1)

    def project(t, carry):
        rows = at_rows(t, size, 0, size)
        dy[rows, :] = mm_nt(dz[rows, :], wout[...])
        return carry

    lax.fori_loop(0, total // size, project, 0)
    for k in range(chans // LANES):
        b, c, x = (low[:, pl.ds(i * chans + k * LANES, LANES)].astype(F32) for i in range(3))
        here = pl.ds(k * LANES, LANES)
        taps = [taps_ref[pl.ds(j, 1), here] for j in range(count)]
        gated = b * x
        summed = conv_taps(gated, within, taps)
        d = dy[:, here]
        mixed[:, here] = (c * summed).astype(BF)
        ds = d * c
        dg = taps[0] * ds
        gt_ref[pl.ds(0, 1), here] = jnp.sum(ds * gated, axis=0, keepdims=True)
        for j in range(1, len(taps)):
            masked = jnp.where(within >= j, ds, 0.0)
            dg = dg + taps[j] * pltpu.roll(masked, total - j, 0)
            gt_ref[pl.ds(j, 1), here] = jnp.sum(masked * pltpu.roll(gated, j, 0), axis=0, keepdims=True)
        dproj[:, pl.ds(k * LANES, LANES)] = (dg * x).astype(BF)
        dproj[:, pl.ds(chans + k * LANES, LANES)] = (d * summed).astype(BF)
        dproj[:, pl.ds(2 * chans + k * LANES, LANES)] = (dg * b).astype(BF)
    bg.step(2)
    scatter_all(g, scatter, product(dproj, win, True), mine, tpart)
    bg.step(3)
    put_columns(gout, 0, mm_tn(mixed[...], dz[...]).astype(BF))
    save = pltpu.make_async_copy(gout, gout_hbm, osem.at[0])
    save.start()
    for t in range(width // 256):
        put_rows(gin, t * 256, mm_tn(nf[:, pl.ds(t * 256, 256)], dproj[...]).astype(BF))
    more = pltpu.make_async_copy(gin, gin_hbm, osem.at[1])
    more.start()
    bg.step(4)
    close_scatter(scatter, mine, dh_ref, h_ref, gain_ref, out_ref, gg_ref)
    gather.finish()
    scatter.wait_all_sends()
    save.wait()
    more.wait()
    bg.step(5)
    bg.step(6)
    bg.finish()


def conv_backward(docs, count, lengths, dh, h, gain, taps, win, wout, n, p, pieces, ident, tasks=(), parts=PARTS):
    size, width = dh.shape
    total, chans = 4 * size, wout.shape[0]
    each = width // pieces
    return hosted(
        functools.partial(conv_backward_kernel, docs, count), ident, "conv_backward",
        [lengths, dh, h, gain, taps, win, wout, n, p],
        [INV, INV, INV, INV, INV, HBM, HBM, HBM, HBM],
        [
            shaped((size, width), F32), shaped((1, width), F32), shaped(taps.shape, F32),
            shaped((pieces, each, 3 * chans), BF), shaped((pieces, chans, each), BF),
        ],
        [INV, INV, INV, HBM, HBM],
        [
            pltpu.VMEM((width, 3 * chans), BF), pltpu.VMEM((chans, width), BF), pltpu.VMEM((total, width), BF),
            pltpu.VMEM((total, 3 * chans), BF), pltpu.VMEM((total, width), BF), pltpu.VMEM((total, chans), F32),
            pltpu.VMEM((total, chans), BF), pltpu.VMEM((total, 3 * chans), BF), pltpu.VMEM((pieces, each, 3 * chans), BF),
            pltpu.VMEM((pieces, chans, each), BF), pltpu.VMEM((size // parts, width), F32), pltpu.VMEM((size, width), F32),
            *gather_scratch(parts), *scatter_scratch(size, width, parts), DMA((4,)), DMA((2,)),
        ],
        tasks, 16 * total * width * chans, 2**24,
    )


def head_sums(values, head):
    width = values.shape[1]
    a = lax.broadcasted_iota(jnp.int32, (width, width), 0) // head
    b = lax.broadcasted_iota(jnp.int32, (width, width), 1) // head
    same = jnp.where(a == b, 1.0, 0.0).astype(BF)
    high = values.astype(BF)
    low = (values - high.astype(F32)).astype(BF)
    return mm(high, same) + mm(low, same)


def turn(values, head):
    width = values.shape[1]
    lane = lax.broadcasted_iota(jnp.int32, values.shape, 1)
    return jnp.where(
        lane % head < head // 2, pltpu.roll(values, width - head // 2, 1), pltpu.roll(values, head // 2, 1)
    )


def wide(table, width):
    return jnp.concatenate([table] * (width // table.shape[1]), axis=1)


def norm_turn(raw, gain, cosine, sine, head):
    inverse = lax.rsqrt(head_sums(raw * raw, head) * (1.0 / head) + epsilon)
    v = raw * inverse * gain
    return v * wide(cosine, raw.shape[1]) + turn(v, head) * wide(sine, raw.shape[1])


def norm_turn_back(d, raw, gain, cosine, sine, head):
    d = d * wide(cosine, raw.shape[1]) - turn(d, head) * wide(sine, raw.shape[1])
    inverse = lax.rsqrt(head_sums(raw * raw, head) * (1.0 / head) + epsilon)
    scaled = d * gain
    inner = head_sums(scaled * raw, head) * (1.0 / head)
    grad_gain = jnp.sum(d * raw * inverse, axis=0, keepdims=True)
    return inverse * scaled - raw * (inverse * inverse * inverse * inner), grad_gain


def score_tile(q, k, starts, first_key, first_query, scale):
    raw = mm_nt(k, q) * scale
    key = first_key + lax.broadcasted_iota(jnp.int32, raw.shape, 0)
    query = first_query + lax.broadcasted_iota(jnp.int32, (1, starts.shape[1]), 1)
    copies = raw.shape[1] // starts.shape[1]
    allowed = (key <= wide(query, raw.shape[1])) & (key >= wide(starts, raw.shape[1]))
    return jnp.where(allowed, raw, -1e30)


def softmax_tile(scores):
    top = jnp.max(scores, axis=0, keepdims=True)
    weights = jnp.exp(scores - top)
    return weights / jnp.sum(weights, axis=0, keepdims=True)


def stack_heads(values, head):
    return jnp.concatenate([values[:, i * head : (i + 1) * head] for i in range(values.shape[1] // head)], axis=0)


def attention_tiles(total, tile):
    back = -(-MOST_DOC // tile)
    return [(i * tile, max(0, i - back) * tile, (i + 1) * tile) for i in range(total // tile)]


def attention_forward_kernel(
    head, docs, lengths, h_ref, gain_ref, qgain_ref, kgain_ref, cos_ref, sin_ref, wq_hbm, wkv_hbm, wo_hbm,
    out_ref, n_hbm, raw_hbm, ready_hbm, o_hbm,
    w, wo, nf, low, ready, vt, o, tpart, mine, n_near, n_over, n_on, o_near, i_near, o_over, i_over,
    s_near, s_over, wsem, osem, bg,
):
    g = Group(bg.others)
    g.greet()
    size, width = h_ref.shape
    total, qw = 4 * size, wo.shape[0]
    kw = (w.shape[1] - qw) // 2
    loads = start_all([(wq_hbm, w.at[:, pl.ds(0, qw)]), (wkv_hbm, w.at[:, pl.ds(qw, 2 * kw)]), (wo_hbm, wo)], wsem)
    gather = Gather(g, nf, size, n_near, n_over, n_on)
    scatter = Scatter(g, o_near, i_near, o_over, i_over, s_near, s_over, size)
    parts, step = gather.parts, gather.step
    nf[at_rows(g.mine, size, 0, size), :] = normalise(h_ref[...], gain_ref[...]).astype(BF)
    g.meet()
    gather.start()
    bg.step(0)
    wait_all(loads)

    def project(block):
        rows = at_rows(block, size, 0, size)
        raw = mm(nf[rows, :], w[...])
        low[rows, :] = raw.astype(BF)
        cosine, sine = cos_ref[rows, :], sin_ref[rows, :]
        ready[rows, pl.ds(0, qw)] = norm_turn(raw[:, :qw], qgain_ref[...], cosine, sine, head).astype(BF)
        ready[rows, pl.ds(qw, kw)] = norm_turn(raw[:, qw : qw + kw], kgain_ref[...], cosine, sine, head).astype(BF)
        ready[rows, pl.ds(qw + kw, kw)] = raw[:, qw + kw :].astype(BF)

    project(g.mine)
    gather.wait_beside()
    project(g.beside)
    for p in range(parts):
        gather.wait_part(p)
    for p in range(parts):
        gather.wait_far(p)

    def rest(i, carry):
        project(jnp.where(i == 0, g.across, g.far))
        return carry

    lax.fori_loop(0, 2, rest, 0)
    bg.step(1)
    saves = start_all([(nf, n_hbm), (low, raw_hbm), (ready, ready_hbm)], osem)
    vt[...] = jnp.transpose(ready[:, pl.ds(qw + kw, kw)].astype(F32)).astype(BF)
    groups = qw // kw
    tile = 256
    scale = head ** (-0.5)
    starts = doc_starts(docs, lengths, lax.broadcasted_iota(jnp.int32, (1, total), 1))
    for first, low_key, high_key in attention_tiles(total, tile):
        keys = pl.ds(low_key, high_key - low_key)
        for kv in range(kw // head):
            q = stack_heads(ready[pl.ds(first, tile), pl.ds(kv * groups * head, groups * head)], head)
            k = ready[keys, pl.ds(qw, kw)][:, kv * head : (kv + 1) * head]
            p = softmax_tile(score_tile(q, k, starts[:, first : first + tile], low_key, first, scale)).astype(BF)
            ot = mm(vt[pl.ds(kv * head, head), keys], p)
            joined = jnp.concatenate([ot[:, i * tile : (i + 1) * tile] for i in range(groups)], axis=0)
            o[pl.ds(first, tile), pl.ds(kv * groups * head, groups * head)] = jnp.transpose(joined).astype(BF)
        if first == tile:
            bg.step(2)
    bg.step(3)
    save_o = pltpu.make_async_copy(o, o_hbm, osem.at[3])
    save_o.start()
    scatter_all(g, scatter, product(o, wo, False), mine, tpart)
    bg.step(4)
    for p in range(parts):
        here = scatter.rows(p)
        scatter.close(1, p).wait_recv()
        scatter.link(p).wait_recv()
        out_ref[here, :] = (
            h_ref[here, :] + mine[here, :] + i_near[1, here, :].astype(F32) + i_over[here, :].astype(F32)
        )
    gather.finish()
    scatter.wait_all_sends()
    wait_all(saves)
    save_o.wait()
    bg.step(6)
    bg.finish()


def attention_forward(head, docs, lengths, h, gain, qgain, kgain, cosine, sine, wq, wkv, wo, ident, tasks=(), parts=PARTS):
    size, width = h.shape
    total, qw = 4 * size, wo.shape[0]
    kw = wkv.shape[1] // 2
    every = qw + 2 * kw
    return hosted(
        functools.partial(attention_forward_kernel, head, docs), ident, "attention_forward",
        [lengths, h, gain, qgain, kgain, cosine, sine, wq, wkv, wo], [INV] * 7 + [HBM] * 3,
        [
            shaped((size, width), F32), shaped((total, width), BF), shaped((total, every), BF), shaped((total, every), BF),
            shaped((total, qw), BF),
        ],
        [INV] + [HBM] * 4,
        [
            pltpu.VMEM((width, every), BF), pltpu.VMEM((qw, width), BF), pltpu.VMEM((total, width), BF),
            pltpu.VMEM((total, every), BF), pltpu.VMEM((total, every), BF),
            pltpu.VMEM((kw, total), BF), pltpu.VMEM((total, qw), BF),
            pltpu.VMEM((size // parts, width), F32), pltpu.VMEM((size, width), F32),
            *gather_scratch(parts), *scatter_scratch(size, width, parts), DMA((3,)), DMA((4,)),
        ],
        tasks, 2 * total * width * (every + qw), 2**24,
    )


def attention_backward_kernel(
    head, docs, lengths, dh_ref, h_ref, gain_ref, qgain_ref, kgain_ref, cos_ref, sin_ref, wq_hbm, wkv_hbm, wo_hbm,
    n_hbm, raw_hbm, ready_hbm, o_hbm, out_ref, gg_ref, gq_ref, gk_ref, gw_hbm, gwo_hbm,
    w, wo, nf, low, ready, kt, o, dz, do, dq, dkv, dlow, gw, gwo, tpart, mine,
    n_near, n_over, n_on, o_near, i_near, o_over, i_over, s_near, s_over, wsem, osem, bg,
):
    g = Group(bg.others)
    g.greet()
    size, width = h_ref.shape
    total, qw = 4 * size, wo.shape[0]
    kw = (w.shape[1] - qw) // 2
    loads = start_all(
        [
            (ready_hbm, ready), (wo_hbm, wo), (o_hbm, o), (raw_hbm, low), (wq_hbm, w.at[:, pl.ds(0, qw)]),
            (wkv_hbm, w.at[:, pl.ds(qw, 2 * kw)]), (n_hbm, nf),
        ],
        wsem,
    )
    gather = Gather(g, dz, size, n_near, n_over, n_on)
    scatter = Scatter(g, o_near, i_near, o_over, i_over, s_near, s_over, size)
    dz[at_rows(g.mine, size, 0, size), :] = dh_ref[...].astype(BF)
    g.meet()
    gather.start()
    bg.step(0)
    wait_all(loads)
    kt[...] = jnp.transpose(ready[:, pl.ds(qw, kw)].astype(F32)).astype(BF)
    dkv[...] = jnp.zeros_like(dkv)
    gather_everything(gather)

    def project(t, carry):
        rows = at_rows(t, size, 0, size)
        do[rows, :] = mm_nt(dz[rows, :], wo[...]).astype(BF)
        return carry

    bg.step(1)

    lax.fori_loop(0, total // size, project, 0)
    groups = qw // kw
    tile = 256
    scale = head ** (-0.5)
    starts = doc_starts(docs, lengths, lax.broadcasted_iota(jnp.int32, (1, total), 1))
    for first, low_key, high_key in attention_tiles(total, tile):
        keys = pl.ds(low_key, high_key - low_key)
        for kv in range(kw // head):
            cols = pl.ds(kv * groups * head, groups * head)
            lane = slice(kv * head, (kv + 1) * head)
            q = stack_heads(ready[pl.ds(first, tile), cols], head)
            k, v = ready[keys, pl.ds(qw, kw)][:, lane], ready[keys, pl.ds(qw + kw, kw)][:, lane]
            p = softmax_tile(score_tile(q, k, starts[:, first : first + tile], low_key, first, scale))
            d = stack_heads(do[pl.ds(first, tile), cols], head)
            dp = mm_nt(v, d)
            inner = jnp.sum(p * dp, axis=0, keepdims=True)
            ds = (p * (dp - inner)).astype(BF)
            both = jnp.concatenate([mm(ds, q) * scale, mm(p.astype(BF), d)], axis=1)
            dkv[kv, keys, :] += both
            dqt = mm(kt[pl.ds(kv * head, head), keys], ds) * scale
            joined = jnp.concatenate([dqt[:, i * tile : (i + 1) * tile] for i in range(groups)], axis=0)
            dq[pl.ds(first, tile), cols] = jnp.transpose(joined)
        if first == tile:
            bg.step(2)
        if first == 2 * tile:
            bg.step(3)
    bg.step(4)
    gq_ref[...] = jnp.zeros_like(gq_ref)
    gk_ref[...] = jnp.zeros_like(gk_ref)

    def finish(t, carry):
        rows = at_rows(t, size, 0, size)
        cosine, sine = cos_ref[rows, :], sin_ref[rows, :]
        d, gq = norm_turn_back(dq[rows, :], low[rows, pl.ds(0, qw)].astype(F32), qgain_ref[...], cosine, sine, head)
        gq_ref[...] += gq
        dlow[rows, pl.ds(0, qw)] = d.astype(BF)
        pairs = [dkv[kv, rows, :] for kv in range(kw // head)]
        dk = jnp.concatenate([x[:, :head] for x in pairs], axis=1)
        dv = jnp.concatenate([x[:, head:] for x in pairs], axis=1)
        d, gk = norm_turn_back(dk, low[rows, pl.ds(qw, kw)].astype(F32), kgain_ref[...], cosine, sine, head)
        gk_ref[...] += gk
        dlow[rows, pl.ds(qw, kw)] = d.astype(BF)
        dlow[rows, pl.ds(qw + kw, kw)] = dv.astype(BF)
        return carry

    lax.fori_loop(0, total // size, finish, 0)
    scatter_all(g, scatter, product(dlow, w, True), mine, tpart)
    put_columns(gwo, 0, mm_tn(o[...], dz[...]).astype(BF))
    save = pltpu.make_async_copy(gwo, gwo_hbm, osem.at[0])
    save.start()
    for t in range(width // 256):
        put_rows(gw, t * 256, mm_tn(nf[:, pl.ds(t * 256, 256)], dlow[...]).astype(BF))
    more = pltpu.make_async_copy(gw, gw_hbm, osem.at[1])
    more.start()
    bg.step(5)
    close_scatter(scatter, mine, dh_ref, h_ref, gain_ref, out_ref, gg_ref)
    gather.finish()
    scatter.wait_all_sends()
    save.wait()
    more.wait()
    bg.step(6)
    bg.finish()


def attention_backward(
    head, docs, lengths, dh, h, gain, qgain, kgain, cosine, sine, wq, wkv, wo, n, raw, ready, o, pieces, ident, tasks=(),
    parts=PARTS,
):
    size, width = h.shape
    total, qw = 4 * size, wo.shape[0]
    kw = wkv.shape[1] // 2
    every = qw + 2 * kw
    each = width // pieces
    return hosted(
        functools.partial(attention_backward_kernel, head, docs), ident, "attention_backward",
        [lengths, dh, h, gain, qgain, kgain, cosine, sine, wq, wkv, wo, n, raw, ready, o], [INV] * 8 + [HBM] * 7,
        [
            shaped((size, width), F32), shaped((1, width), F32), shaped((1, qw), F32), shaped((1, kw), F32),
            shaped((pieces, each, every), BF), shaped((pieces, qw, each), BF),
        ],
        [INV, INV, INV, INV, HBM, HBM],
        [
            pltpu.VMEM((width, every), BF), pltpu.VMEM((qw, width), BF), pltpu.VMEM((total, width), BF),
            pltpu.VMEM((total, every), BF), pltpu.VMEM((total, every), BF), pltpu.VMEM((kw, total), BF),
            pltpu.VMEM((total, qw), BF), pltpu.VMEM((total, width), BF), pltpu.VMEM((total, qw), BF),
            pltpu.VMEM((total, qw), F32), pltpu.VMEM((kw // head, total, 2 * head), F32), pltpu.VMEM((total, every), BF),
            pltpu.VMEM((pieces, each, every), BF), pltpu.VMEM((pieces, qw, each), BF),
            pltpu.VMEM((size // parts, width), F32), pltpu.VMEM((size, width), F32),
            *gather_scratch(parts), *scatter_scratch(size, width, parts), DMA((7,)), DMA((2,)),
        ],
        tasks, 4 * total * width * (every + qw), 2**25,
    )


def tail_kernel(bg):
    g = Group(bg.others)
    g.greet()
    g.meet()
    for k in range(4):
        bg.step(k)
    bg.step(6)
    bg.finish()


def tail(ident, tasks):
    return hosted(tail_kernel, ident, "tail", [], [], [], [], [], tasks, 0, 2**22)[1]


rope_base = 1000000.0
TP = ("c", "zl")
DP = ("r", "s", "zh")


def doc_positions(lengths_row, length):
    count = lengths_row.shape[0]
    upto = jnp.arange(count)[:, None] >= jnp.arange(count)[None, :]
    doc_ends = jnp.sum(jnp.where(upto, lengths_row[None, :], 0), axis=1)
    places = jnp.arange(length, dtype=jnp.int32)
    passed = places[:, None] >= doc_ends[None, :]
    return places - jnp.max(jnp.where(passed, doc_ends[None, :], 0), axis=1)


def rope_tables(position, head_dim):
    half_dim = head_dim // 2
    inverse = rope_base ** (-2.0 * jnp.arange(half_dim, dtype=F32) / head_dim)
    angles = position.astype(F32)[:, None] * inverse[None, :]
    cosine, sine = jnp.cos(angles), jnp.sin(angles)
    copies = LANES // head_dim
    return (
        jnp.concatenate([cosine, cosine] * copies, axis=1),
        jnp.concatenate([-sine, sine] * copies, axis=1),
    )


def swap(x):
    return lax.ppermute(x, ("c", "zh"), [(0, 0), (1, 2), (2, 1), (3, 3)])


def gather_dp(shard, axis):
    return lax.all_gather(swap(shard), DP, axis=axis, tiled=True)


def scatter_dp(partial, axis):
    return swap(lax.psum_scatter(partial, DP, scatter_dimension=axis, tiled=True)).astype(F32)


def local(
    planes, tokens, doc_lengths, grad_out, norm_gains, head_gains, conv_in, conv_kernel, conv_out,
    query_w, kv_w, out_w, gate_up, down,
):
    length = tokens.shape[0]
    head_dim = head_gains.shape[1]
    docs, count = doc_lengths.shape[1], conv_kernel.shape[0]
    conv_in = conv_in.reshape(conv_in.shape[0], -1)
    kv_w = kv_w.reshape(kv_w.shape[0], -1)
    own_w = [gate_up[l].reshape(gate_up.shape[1], -1) for l in (0, 1)]
    own_v = [down[l] for l in (0, 1)]
    pieces = 8 if planes else 1
    kv_width = kv_w.shape[1] // 2
    qgain = jnp.tile(head_gains[0:1], (1, query_w.shape[1] // head_dim))
    kgain = jnp.tile(head_gains[1:2], (1, kv_width // head_dim))
    gain = [norm_gains[i : i + 1] for i in range(4)]
    lens = jnp.pad(doc_lengths.astype(F32), ((0, 7), (0, LANES - docs)))
    taps = jnp.pad(conv_kernel, ((0, 8 - count), (0, 0)))
    rows_of = lambda got: got.reshape(-1, got.shape[-1])
    if planes:
        first = [Take(conv_in, (0, 1, 1, 2, 2), True), Take(conv_out, (0, 1, 1, 2, 2), True)]
        first += [Fetch(own_w[0], (0, 1, 1, 2, 4, 5, 3, 3, 3), 4), Fetch(own_v[0], (0, 1, 1, 2, 3, 3, 3), 2)]
        first += [Take(x, (0, 3, 3, 3, 3)) for x in (query_w, kv_w, out_w)]
        second = [Fetch(own_w[1], (0, 0, 0, 2), 1, 1), Fetch(own_v[1], (0, 0, 0, 2), 1, 1)]
    else:
        first, second, third = [], [], []
        conv_in, conv_out, query_w, kv_w, out_w = map(swap, (conv_in, conv_out, query_w, kv_w, out_w))
        w0, w1 = (gather_dp(w, 0) for w in own_w)
        v0, v1 = (gather_dp(v, 1)[None] for v in own_v)

    (h1, x_block, n0, projected, lens, taps, conv_in, conv_out), got = conv_forward(
        docs, count, lens, tokens, gain[0], taps, conv_in, conv_out, planes, 0, first
    )
    if planes:
        w0, v0 = rows_of(got[0]), got[1]
        query_w, kv_w, out_w = got[2:]
    (h2, n1, hidden0), got = ffn_forward(h1, gain[1], w0, v0, 1, second)
    if planes:
        third = [Fetch(got[0], (0, 4), 2, 2), Fetch(got[1], (0, 4), 1, 2)]
    cosine, sine = rope_tables(doc_positions(lens[0, :docs].astype(jnp.int32), length), head_dim)
    (h3, n2, raw, ready, attended), got = attention_forward(
        head_dim, docs, lens, h2, gain[2], qgain, kgain, cosine, sine, query_w, kv_w, out_w, 2, third
    )
    if planes:
        w1, v1 = rows_of(got[0]), got[1]
    (h4, n3, hidden1), (up_full,) = ffn_forward(h3, gain[3], w1, v1, 3, [Spread(grad_out, (0, 1, 2))])

    def halves(grad, first, second, last=False):
        half = grad.shape[1] // 2
        return [Reduce(grad, 0, half, first, last), Reduce(grad, half, half, second, False)] if planes else []

    def whole(grad, at, last=False):
        return [Reduce(grad, 0, grad.shape[1], at, last)] if planes else []

    def settled(sums, at):
        return [Settle(x, at) for x in sums]

    (dh3, gain3, gw1, gv1), (output,) = ffn_backward(
        None, h3, gain[3], up_full, w1, v1, n3, hidden1, 4, [Deliver(h4, (0, 2))]
    )
    (dh2, gain2, gq, gk, gqkv, gow), sums = attention_backward(
        head_dim, docs, lens, dh3, h2, gain[2], qgain, kgain, cosine, sine, query_w, kv_w, out_w, n2, raw, ready, attended,
        pieces, 5, halves(gw1, (0, 2, 5), (0, 4, 6)),
    )
    (dh1, gain1, gw0, gv0), got = ffn_backward(
        dh2, h1, gain[1], None, w0, v0, n1, hidden0, 6,
        settled(sums, (0, 2)) + whole(gv1, (0, 1, 2)) + whole(gqkv, (0, 2, 3)) + whole(gow, (0, 2, 3)),
    )
    sums_w1, sums = got[:2], got[2:]
    (dh0, gain0, gtaps, gci, gco), got = conv_backward(
        docs, count, lens, dh1, x_block.astype(F32), gain[0], taps, conv_in, conv_out, n0, projected, pieces, 7,
        settled(sums, (0, 3)) + halves(gw0, (0, 1, 4), (0, 3, 6), True),
    )
    others, first_w0, sums = got[:3], got[3:4], got[4:]
    totals, grads, *got = tail(
        8,
        [Total([gain0, gain1, gain2, gain3, gtaps, gq, gk], (0, 1, 2, 3), count, ("zh", "s", *(("r",) if planes else ()), "zl", "c")), Deliver(dh0, (0, 0))]
        + settled(sums, (0, 0)) + whole(gv0, (0, 0, 1), True) + whole(gci, (1, 2, 3), True) + whole(gco, (1, 2, 3), True),
    )
    if planes:
        gw1 = jnp.concatenate(sums_w1, axis=0)
        gv1, gqkv, gow = others
        gw0 = jnp.concatenate([first_w0[0], got[0]], axis=0)
        gv0, gci, gco = got[1:]
    else:
        totals = lax.psum(totals, "r")
        gw0, gw1, gci, gqkv = (scatter_dp(g[0], 0) for g in (gw0, gw1, gci, gqkv))
        gv0, gv1, gco, gow = (scatter_dp(g[0], 1) for g in (gv0, gv1, gco, gow))
    heads = totals[7, : gq.shape[1] + gk.shape[1]].reshape(-1, head_dim)
    split = gq.shape[1] // head_dim
    return (
        output,
        grads.astype(F32),
        totals[:4],
        jnp.stack([jnp.sum(heads[:split], axis=0), jnp.sum(heads[split:], axis=0)]),
        gci.reshape(-1, 3, conv_kernel.shape[1]),
        totals[4 : 4 + count],
        gco,
        gqkv[:, : query_w.shape[1]],
        gqkv[:, query_w.shape[1] :].reshape(-1, 2, kv_width),
        gow,
        jnp.stack([gw0, gw1]).reshape(2, gate_up.shape[1], 2, -1),
        jnp.stack([gv0, gv1]),
    )


def solution(mesh):
    devices = mesh.devices
    dp, tp = devices.shape
    inner = Mesh(devices.reshape(dp // 4, 2, 2, 2, tp // 2), ("r", "s", "c", "zh", "zl"))
    D = ("r", "s", "c")
    T = ("zh", "zl")
    return jax.shard_map(
        functools.partial(local, dp == 8),
        mesh=inner,
        in_specs=(
            P(D, T), P(D, None), P(D, T), P(), P(), P(None, None, T), P(None, T), P(T, None),
            P(None, T), P(None, None, T), P(T, None), P(None, D, None, T), P(None, T, D),
        ),
        out_specs=(
            P(D, T), P(D, T), P(), P(), P(D, None, T), P(), P(T, D), P(D, T), P(D, None, T),
            P(T, D), P(None, D, None, T), P(None, T, D),
        ),
        check_vma=False,
    )
```

```python
import functools
import jax
import jax.numpy as jnp
from jax import lax
from jax.experimental import pallas as pl
from jax.experimental.pallas import tpu as pltpu
from jax.sharding import Mesh, PartitionSpec as P

epsilon = 1e-05
BF = jnp.bfloat16
F32 = jnp.float32
MESH = pl.DeviceIdType.MESH
DMA = pltpu.SemaphoreType.DMA
HBM = pl.BlockSpec(memory_space=pl.ANY)
INV = pl.BlockSpec(memory_space=pltpu.VMEM)
PARTS = 2
LANES = 128


class Group:
    def __init__(self, others=(), calls=True):
        c, z = lax.axis_index("c"), lax.axis_index("zl")
        self.partner, self.twin = {"c": 1 - c}, {"zl": 1 - z}
        self.mine, self.beside = 2 * c + z, 2 * (1 - c) + z
        self.across, self.far = 2 * c + (1 - z), 2 * (1 - c) + (1 - z)
        self.known = [self.partner, self.twin, *others]
        self.c, self.z = c, z
        self.barrier = pltpu.get_barrier_semaphore() if calls else None

    def greet(self):
        for other in self.known:
            pl.semaphore_signal(self.barrier, inc=1, device_id=other, device_id_type=MESH)

    def meet(self):
        pl.semaphore_wait(self.barrier, len(self.known))


def at_rows(block, size, start, count):
    return pl.ds(pl.multiple_of(block * size + start, 16), count)


def send(src, dst, sems, index, where):
    return pltpu.make_async_remote_copy(
        src_ref=src, dst_ref=dst, send_sem=sems.at[0, index], recv_sem=sems.at[1, index],
        device_id=where, device_id_type=MESH,
    )


class Gather:
    def __init__(self, group, full, size, near, over, onward):
        self.g, self.full, self.size, self.parts = group, full, size, over.shape[1]
        self.near, self.over, self.onward = near, over, onward
        self.step = size // self.parts

    def view(self, block, part):
        return self.full.at[at_rows(block, self.size, part * self.step, self.step)]

    def link(self, part, block):
        v = self.view(block, part)
        return send(v, v, self.over, part, self.g.twin)

    def close(self, part, block):
        v = self.view(block, part)
        return send(v, v, self.near, part, self.g.partner)

    def pass_on(self, part, block):
        v = self.view(block, part)
        return send(v, v, self.onward, part, self.g.partner)

    def start(self):
        for p in range(self.parts):
            self.link(p, self.g.mine).start()
            self.close(p, self.g.mine).start()

    def wait_beside(self):
        for p in range(self.parts):
            self.close(p, self.g.beside).wait_recv()

    def wait_part(self, p):
        self.link(p, self.g.across).wait_recv()
        self.pass_on(p, self.g.across).start()

    def wait_far(self, p):
        self.pass_on(p, self.g.far).wait_recv()

    def finish(self):
        for p in range(self.parts):
            self.link(p, self.g.mine).wait_send()
            self.close(p, self.g.mine).wait_send()
            self.pass_on(p, self.g.across).wait_send()


class Scatter:
    def __init__(self, group, out_near, in_near, out_over, in_over, near, over, size):
        self.g, self.size, self.parts = group, size, over.shape[1]
        self.out_near, self.in_near, self.out_over, self.in_over = out_near, in_near, out_over, in_over
        self.near, self.over = near, over
        self.step = size // self.parts

    def rows(self, part):
        return pl.ds(part * self.step, self.step)

    def close(self, which, part):
        r = self.rows(part)
        return send(self.out_near.at[which, r], self.in_near.at[which, r], self.near, which * self.parts + part, self.g.partner)

    def link(self, part):
        r = self.rows(part)
        return send(self.out_over.at[r], self.in_over.at[r], self.over, part, self.g.twin)

    def wait_all_sends(self):
        for p in range(self.parts):
            self.close(0, p).wait_send()
            self.close(1, p).wait_send()
            self.link(p).wait_send()


def scatter_scratch(size, width, parts):
    return [
        pltpu.VMEM((2, size, width), BF), pltpu.VMEM((2, size, width), BF), pltpu.VMEM((size, width), BF),
        pltpu.VMEM((size, width), BF), DMA((2, 2 * parts)), DMA((2, parts)),
    ]


def gather_scratch(parts):
    return [DMA((2, parts)), DMA((2, parts)), DMA((2, parts))]


def normalise(h, gain):
    return h * lax.rsqrt(jnp.mean(h * h, axis=-1, keepdims=True) + epsilon) * gain


def mm(a, b):
    return jnp.dot(a, b, preferred_element_type=F32)


def mm_nt(a, b):
    return lax.dot_general(a, b, (((1,), (1,)), ((), ())), preferred_element_type=F32)


def lanes(start, width):
    return pl.ds(pl.multiple_of(start, LANES), width)


def start_all(pairs, sems):
    copies = [pltpu.make_async_copy(src, dst, sems.at[i]) for i, (src, dst) in enumerate(pairs)]
    for copy in copies:
        copy.start()
    return copies


def wait_all(copies):
    for copy in copies:
        copy.wait()


def params(ident):
    return pltpu.CompilerParams(collective_id=ident, has_side_effects=True, vmem_limit_bytes=56 * 2**20)


def shaped(shape, dtype):
    return jax.ShapeDtypeStruct(shape, dtype)


END = 99


class Place:
    def __init__(self):
        self.y, self.x, self.c, self.zh = (lax.axis_index(a) for a in ("r", "s", "c", "zh"))
        self.across_x, self.across_y = {"s": 1 - self.x}, {"r": 1 - self.y}
        self.partner = {"c": 1 - self.c}
        self.plain = self.c == self.zh
        self.outer = lax.axis_index("zl") == self.zh

    def over(self, core):
        return {"c": core, "zh": 1 - self.zh}

    def swapped(self):
        return self.over(self.zh)

    PLANES = ("x", "y")
    ENDS = ("end", "swap")
    COLUMN = ("end", "swap", "z core", "z end", "z swap")

    def called(self, name):
        z = 1 - lax.axis_index("zl")
        other, far = 1 - self.c, 1 - self.zh
        return {
            "x": self.across_x, "y": self.across_y, "end": self.over(self.c), "swap": self.over(other),
            "z core": {"c": other, "zl": z}, "z end": {"zh": far, "zl": z}, "z swap": {"c": other, "zh": far, "zl": z},
        }[name]

    def piece(self, flip_y, flip_x, a):
        y = 1 - self.y if flip_y else self.y
        x = 1 - self.x if flip_x else self.x
        return 4 * y + 2 * x + a


class Fetch:
    def __init__(self, shard, at, cuts=1, stage=0):
        rows, cols = shard.shape[-2:]
        self.at, self.cuts, self.stage, self.step_rows = at, cuts, stage, rows // cuts
        self.ins = [shard]
        self.outs = [jax.ShapeDtypeStruct((8, rows, cols), shard.dtype)]
        self.out_specs = [HBM]
        self.in_place = stage == 2
        self.semaphores()
        if not self.in_place:
            self.scratch.append(pltpu.VMEM((rows, cols), BF))

    def semaphores(self):
        self.scratch = [DMA((9 * self.cuts,)), DMA((8 * self.cuts,)), DMA((2,))]

    def bind(self, ins, outs, scratch):
        (self.own,), (self.out,) = ins, outs
        self.sent, self.come, self.sem = scratch[:3]
        self.bounce = scratch[3] if len(scratch) > 3 else None
        self.p = Place()

    def greets(self):
        return Place.PLANES if self.stage == 2 else Place.PLANES + Place.ENDS

    def part(self, ref, q):
        return ref.at[pl.ds(q * self.step_rows, self.step_rows)]

    def given(self, q):
        return self.part(self.own, q)

    def slot(self, piece, q):
        return self.part(self.out.at[piece], q)

    def home(self, a, q):
        return self.slot(self.p.piece(0, 0, a), q)

    def copy(self, src, dst, q, sent, come, where):
        return pltpu.make_async_remote_copy(
            src_ref=src, dst_ref=dst, send_sem=self.sent.at[9 * q + sent], recv_sem=self.come.at[8 * q + come],
            device_id=where, device_id_type=MESH,
        )

    def to_plane(self, q):
        p = self.p
        return self.copy(self.given(q), self.home(p.c, q), q, 0, p.c, p.over(p.zh))

    def to_partner(self, q):
        p = self.p
        return self.copy(self.given(q), self.home(p.c, q), q, 1, p.c, p.partner)

    def arrived(self, a, q):
        self.copy(self.given(q), self.home(a, q), q, 0, a, self.p.partner).wait_recv()

    def keep(self):
        slot = self.out.at[self.p.piece(0, 0, self.p.c)]
        return [
            pltpu.make_async_copy(self.own, self.bounce, self.sem.at[0]),
            pltpu.make_async_copy(self.bounce, slot, self.sem.at[1]),
        ]

    def kept(self):
        self.keep()[0].start()

    def land(self):
        copies = self.keep()
        for i, copy in enumerate(copies):
            if i:
                copy.start()
            copy.wait()

    def to_x(self, a, q, src=None):
        dst = self.slot(self.p.piece(0, 0, a), q)
        return self.copy(dst if src is None else src, dst, q, 2 + a, 2 + a, self.p.across_x)

    def to_y(self, a, q, src=None):
        dst = self.slot(self.p.piece(0, 0, a), q)
        return self.copy(dst if src is None else src, dst, q, 4 + a, 4 + a, self.p.across_y)

    def spread(self, a, q, src):
        self.to_x(a, q, src).start()
        self.to_y(a, q, src).start()

    def on_y(self, q):
        there = self.slot(self.p.piece(0, 1, 0), q)
        return self.copy(there, there, q, 6, 6, self.p.across_y)

    def on_x(self, q):
        there = self.slot(self.p.piece(1, 0, 1), q)
        return self.copy(there, there, q, 7, 7, self.p.across_x)

    def forward(self, q):
        self.to_x(0, q).wait_recv()
        self.on_y(q).start()
        self.to_y(1, q).wait_recv()
        self.on_x(q).start()

    def plain(self, run):
        pl.when(self.p.plain)(run)

    def other(self, run):
        pl.when(jnp.logical_not(self.p.plain))(run)

    def step(self, k):
        p, every = self.p, range(self.cuts)

        def own():
            for q in every:
                self.spread(p.c, q, self.given(q))

        def partner():
            for q in every:
                self.to_partner(q).start()

        def second():
            for q in every:
                self.arrived(1 - p.c, q)
                self.spread(1 - p.c, q, self.home(1 - p.c, q))

        def planes():
            for q in every:
                for a in (0, 1):
                    self.spread(a, q, self.home(a, q))

        def there(q):
            for a in (0, 1):
                self.arrived(a, q)
                self.spread(a, q, self.home(a, q))

        if self.stage == 2:
            if k == 0:
                self.other(planes)
            elif k == 1:
                self.other(lambda: [self.forward(q) for q in every] and None)
            elif k == END:
                self.other(self.close)
        elif k == 0:
            self.plain(self.kept)
            self.other(partner)
            self.plain(own)
            self.plain(second)
        elif k == END:
            for q in every:
                self.to_plane(q).wait_send()
            if self.stage:
                self.plain(self.close)
                self.other(lambda: [self.arrived(a, q) for q in every for a in (0, 1)] and None)
            else:
                self.close()
            self.plain(self.land)
            self.other(lambda: [self.to_partner(q).wait_send() for q in every] and None)
        elif k in (1, 2):
            self.leave(k == 1)
        elif k == 3:
            self.plain(lambda: [self.forward(q) for q in every] and None)
        elif not self.stage:
            q = k - 4
            if q < self.cuts:
                self.other(functools.partial(there, q))
            if q:
                self.other(lambda: self.forward(q - 1))

    def leave(self, outer):
        @pl.when(self.p.outer if outer else jnp.logical_not(self.p.outer))
        def _():
            for q in range(self.cuts):
                self.to_plane(q).start()

    def close(self):
        for q in range(self.cuts):
            self.to_x(1, q).wait_recv()
            self.to_y(0, q).wait_recv()
            self.on_y(q).wait()
            self.on_x(q).wait()
            for a in (0, 1):
                self.to_x(a, q).wait_send()
                self.to_y(a, q).wait_send()


class Take(Fetch):
    def __init__(self, whole, at, inside=False):
        rows, cols = whole.shape
        self.at, self.each, self.cuts, self.stage = at, rows // 8, 1, 0
        self.ins = [whole]
        self.outs = [] if inside else [jax.ShapeDtypeStruct((rows, cols), whole.dtype)]
        self.out_specs = [] if inside else [HBM]
        self.in_place = False
        self.semaphores()
        if not inside:
            self.scratch.append(pltpu.VMEM((rows, cols), BF))

    def bind(self, ins, outs, scratch):
        (self.own,) = ins
        self.whole = outs[0] if outs else None
        self.sent, self.come, self.sem = scratch[:3]
        self.bounce = scratch[3] if len(scratch) > 3 else None
        self.p = Place()

    def rows(self, piece):
        return pl.ds(pl.multiple_of(piece * self.each, 16), self.each)

    def given(self, q):
        return self.own.at[self.rows(self.p.piece(0, 0, self.p.c))]

    def slot(self, piece, q):
        return self.whole.at[self.rows(piece)]

    def keep(self):
        if self.bounce is None:
            return [pltpu.make_async_copy(self.own, self.whole, self.sem.at[0])]
        return [
            pltpu.make_async_copy(self.own, self.bounce, self.sem.at[0]),
            pltpu.make_async_copy(self.bounce, self.whole, self.sem.at[1]),
        ]

    def step(self, k):
        def there():
            for a in (0, 1):
                self.arrived(a, 0)
                self.spread(a, 0, self.home(a, 0))

        def last():
            self.close()

        if k == 0:
            self.plain(self.kept)
        elif k in (1, 2):
            self.leave(k == 1)
        elif k == 3:
            self.other(there)
        elif k == 4:
            self.other(lambda: self.forward(0))
        elif k == END:
            self.to_plane(0).wait_send()
            self.plain(self.land)
            self.other(last)


class Exchange:
    def __init__(self, src, dst, there, sems, sem, index=0):
        self.p = Place()
        self.src, self.dst, self.there, self.sems, self.sem, self.index = src, dst, there, sems, sem, index

    def stay(self):
        return pltpu.make_async_copy(self.src, self.dst, self.sem.at[self.index])

    def leave(self):
        return send(self.src, self.there, self.sems, self.index, self.p.swapped())

    def come(self):
        return send(self.src, self.dst, self.sems, self.index, self.p.swapped())

    def both(self, stay, leave):
        pl.when(self.p.plain)(stay)
        pl.when(jnp.logical_not(self.p.plain))(leave)

    def start(self):
        self.both(lambda: self.stay().start(), lambda: self.leave().start())

    def arrive(self):
        self.both(lambda: self.stay().wait(), lambda: self.come().wait_recv())

    def finish(self):
        pl.when(jnp.logical_not(self.p.plain))(lambda: self.leave().wait_send())


class Spread:
    def __init__(self, block, at, parts=2):
        rows, cols = block.shape
        self.at, self.parts = at, parts
        self.ins = [block]
        self.outs = [jax.ShapeDtypeStruct((rows, 4 * cols), block.dtype)]
        self.out_specs = [HBM]
        self.scratch = [*gather_scratch(parts), DMA((2, 1)), DMA((1,))]

    def bind(self, ins, outs, scratch):
        (self.block,), (self.full,) = ins, outs
        near, over, onward, sems, sem = scratch
        self.p, self.g = Place(), Group(calls=False)
        self.gather = Columns(self.g, self.full, near, over, onward)
        cols = self.block.shape[1]
        mine, there = (self.full.at[:, lanes(b * cols, cols)] for b in (self.g.mine, self.g.beside))
        self.exchange = Exchange(self.block, mine, there, sems, sem)

    def greets(self):
        return Place.ENDS

    def step(self, k):
        if k == 0:
            self.exchange.start()
        elif k == 1:
            self.exchange.arrive()
            self.gather.start()
        elif k == 2:
            for p in range(self.parts):
                self.gather.wait_part(p)
        elif k == END:
            self.gather.wait_beside()
            for p in range(self.parts):
                self.gather.wait_far(p)
            self.gather.finish()
            self.exchange.finish()


class Deliver:
    def __init__(self, block, at):
        rows, width = block.shape
        self.at = at
        self.ins = [block]
        self.outs = [jax.ShapeDtypeStruct((4 * rows, width // 4), BF)]
        self.out_specs = [HBM]
        self.scratch = [pltpu.VMEM((rows, width), BF), DMA((4,)), DMA((4,)), DMA((2,))]
        if block.dtype != BF:
            self.scratch.append(pltpu.VMEM((rows, width), block.dtype))

    def bind(self, ins, outs, scratch):
        (self.block,), (self.out,) = ins, outs
        self.low, self.sent, self.come, self.sem = scratch[:4]
        self.wide = scratch[4] if len(scratch) > 4 else self.low
        self.p, self.g = Place(), Group(calls=False)

    def greets(self):
        return Place.COLUMN

    def load(self):
        return pltpu.make_async_copy(self.block, self.wide, self.sem.at[0])

    def parts(self):
        rows, width = self.low.shape
        cols = width // 4
        dst = self.out.at[at_rows(self.g.mine, rows, 0, rows)]
        for f in range(4):
            half, z = divmod(f, 2)
            here = (self.p.c == self.p.zh) & (self.p.zh == half) & (self.g.z == z)
            src = self.low.at[:, pl.ds(f * cols, cols)]
            where = {"c": self.p.zh, "zh": jnp.int32(half), "zl": jnp.int32(z)}
            yield here, pltpu.make_async_copy(src, dst, self.sem.at[1]), pltpu.make_async_remote_copy(
                src_ref=src, dst_ref=dst, send_sem=self.sent.at[f], recv_sem=self.come.at[self.g.mine],
                device_id=where, device_id_type=MESH,
            )

    def step(self, k):
        if k == 0:
            self.load().start()
        elif k == 1:
            self.load().wait()
            if self.wide is not self.low:
                self.low[...] = self.wide[...].astype(BF)
            for here, stay, leave in self.parts():
                pl.when(here)(lambda stay=stay: stay.start())
                pl.when(jnp.logical_not(here))(lambda leave=leave: leave.start())
        elif k == END:
            rows, width = self.low.shape
            for here, stay, leave in self.parts():
                pl.when(here)(lambda stay=stay: stay.wait())
                pl.when(jnp.logical_not(here))(lambda leave=leave: leave.wait_send())
            for b in range(4):
                core, z = divmod(b, 2)
                here = (self.p.c == self.p.zh) & (self.p.c == core) & (self.g.z == z)
                come = pltpu.make_async_remote_copy(
                    src_ref=self.low.at[:, pl.ds(0, width // 4)], dst_ref=self.out.at[pl.ds(b * rows, rows)],
                    send_sem=self.sent.at[0], recv_sem=self.come.at[b], device_id=self.p.partner, device_id_type=MESH,
                )
                pl.when(jnp.logical_not(here))(lambda come=come: come.wait_recv())


class Total:
    def __init__(self, pieces, at, count, axes):
        self.at, self.count, self.axes = at, count, axes
        self.ins = pieces
        self.in_specs = [INV] * len(pieces)
        width = pieces[0].shape[1]
        self.outs = [jax.ShapeDtypeStruct((8, width), F32)]
        self.out_specs = [INV]
        self.scratch = [
            pltpu.VMEM((len(self.axes), 8, width), F32), pltpu.VMEM((len(self.axes), 8, width), F32),
            DMA((2, len(self.axes))),
        ]

    def bind(self, ins, outs, scratch):
        self.pieces, (self.out,) = ins, outs
        self.sum, self.other, self.sems = scratch
        self.p, self.g = Place(), Group(calls=False)

    def greets(self):
        return ("x",) + Place.ENDS + (("y",) if "r" in self.axes else ())

    def hop(self, i):
        axis = self.axes[i]
        return send(self.sum.at[i], self.other.at[i], self.sems, i, {axis: 1 - lax.axis_index(axis)})

    def step(self, k):
        if k == 0:
            gains, taps, heads = self.pieces[:4], self.pieces[4], self.pieces[5:]
            self.sum[0] = jnp.zeros(self.sum.shape[1:], F32)
            for i, gain in enumerate(gains):
                self.sum[0, pl.ds(i, 1), :] = gain[...]
            cols = taps.shape[1]
            self.sum[0, pl.ds(4, self.count), lanes(self.g.mine * cols, cols)] = taps[pl.ds(0, self.count), :]
            done = 0
            for head in heads:
                self.sum[0, pl.ds(7, 1), pl.ds(done, head.shape[1])] = head[...]
                done += head.shape[1]
            self.hop(0).start()
        else:
            k = min(k, 4)
            last = len(self.axes) if k == 4 else k
            for i in range(k - 1, last):
                self.hop(i).wait()
                value = self.sum[i] + self.other[i]
                if i + 1 < len(self.axes):
                    self.sum[i + 1] = value
                    self.hop(i + 1).start()
                else:
                    self.out[...] = value


class Reduce:
    def __init__(self, grad, first, rows, at, last=True):
        self.first, self.rows, self.at, self.last = first, rows, at, last
        cols = grad.shape[2]
        self.ins = [grad]
        self.outs = [shaped((rows, cols), F32) if last else shaped((2, rows, cols), BF)]
        self.out_specs = [INV]
        self.scratch = [
            pltpu.VMEM((4, rows, cols), BF), pltpu.VMEM((4, rows, cols), BF), pltpu.VMEM((2, rows, cols), BF),
            DMA((9,)), DMA((8,)), DMA((4,)),
        ]
        if last:
            self.scratch.append(pltpu.VMEM((2, rows, cols), BF))

    def bind(self, ins, outs, scratch):
        (self.grad,), (self.out,) = ins, outs
        self.held, self.in1, self.in2, self.sent, self.come, self.sem = scratch[:6]
        self.in3 = scratch[6] if self.last else None
        self.p = Place()

    def greets(self):
        return Place.PLANES + (Place.ENDS if self.last else ())

    def fin(self, a):
        return self.held.at[2 * a]

    def piece(self, flip_y, flip_x, a):
        return self.grad.at[self.p.piece(flip_y, flip_x, a), pl.ds(self.first, self.rows)]

    def copy(self, src, dst, sent, come, where):
        return pltpu.make_async_remote_copy(
            src_ref=src, dst_ref=dst, send_sem=self.sent.at[sent], recv_sem=self.come.at[come],
            device_id=where, device_id_type=MESH,
        )

    def loads(self):
        kept = [(0, 0, 0), (0, 1, 0), (0, 0, 1), (1, 0, 1)]
        return [pltpu.make_async_copy(self.piece(*k), self.held.at[i], self.sem.at[i]) for i, k in enumerate(kept)]

    def first_hops(self):
        p = self.p
        return [
            self.copy(self.piece(1, 0, 0), self.in1.at[0], 0, 0, p.across_y),
            self.copy(self.piece(1, 1, 0), self.in1.at[1], 1, 1, p.across_y),
            self.copy(self.piece(0, 1, 1), self.in1.at[2], 2, 2, p.across_x),
            self.copy(self.piece(1, 1, 1), self.in1.at[3], 3, 3, p.across_x),
        ]

    def second_hops(self):
        return [
            self.copy(self.held.at[1], self.in2.at[0], 4, 4, self.p.across_x),
            self.copy(self.held.at[3], self.in2.at[1], 5, 5, self.p.across_y),
        ]

    def to_owner(self, a):
        return self.copy(self.fin(a), self.in3.at[0], 6 + a, 6, self.p.over(a))

    def to_partner(self):
        return self.copy(self.fin(1 - self.p.c), self.in3.at[1], 8, 7, self.p.partner)

    def add(self, i, other):
        self.held[i] = (self.held[i].astype(F32) + other.astype(F32)).astype(BF)

    def step(self, k):
        p = self.p
        if k == 0:
            for hop in [self.first_hops()[i] for i in (1, 3, 0, 2)]:
                hop.start()
            for load in self.loads():
                load.start()
        elif k == 1:
            for load in self.loads():
                load.wait()
            hops, after = self.first_hops(), self.second_hops()
            for i in (1, 3):
                hops[i].wait_recv()
                self.add(i, self.in1[i])
                after[i // 2].start()
            for i in (0, 2):
                hops[i].wait_recv()
                self.add(i, self.in1[i])
        elif k == 2:
            for i, hop in enumerate(self.second_hops()):
                hop.wait_recv()
                if self.last:
                    self.add(2 * i, self.in2[i])
                else:
                    self.out[i] = (self.held[2 * i].astype(F32) + self.in2[i].astype(F32)).astype(BF)
            if self.last:
                self.settle()
                self.settle(False)
        elif k == END:
            if self.last:
                self.close()
            for hop in self.first_hops() + self.second_hops():
                hop.wait_send()

    def settle(self, outer=True):
        if outer:

            @pl.when(self.p.plain)
            def _():
                self.to_partner().start()

        now = self.p.outer if outer else jnp.logical_not(self.p.outer)

        @pl.when(now & jnp.logical_not(self.p.plain))
        def _():
            self.to_owner(0).start()
            self.to_owner(1).start()

    def close(self):
        p = self.p
        self.to_owner(0).wait_recv()

        @pl.when(p.plain)
        def _():
            self.out[...] = self.own(p.c).astype(F32) + self.in3[0].astype(F32)
            self.to_partner().wait_send()

        @pl.when(jnp.logical_not(p.plain))
        def _():
            self.to_partner().wait_recv()
            self.out[...] = self.in3[1].astype(F32) + self.in3[0].astype(F32)
            self.to_owner(0).wait_send()
            self.to_owner(1).wait_send()

    def own(self, a):
        return self.held[2 * a]


class Settle(Reduce):
    def __init__(self, sums, at):
        _, rows, cols = sums.shape
        self.at = at
        self.ins = [sums]
        self.outs = [shaped((rows, cols), F32)]
        self.out_specs = [INV]
        self.scratch = [pltpu.VMEM((rows, cols), BF), pltpu.VMEM((2, rows, cols), BF), DMA((9,)), DMA((8,)), DMA((1,))]

    def bind(self, ins, outs, scratch):
        (self.sums,), (self.out,) = ins, outs
        self.kept, self.in3, self.sent, self.come, self.sem = scratch
        self.p = Place()

    def greets(self):
        return Place.ENDS

    def fin(self, a):
        return self.sums.at[a]

    def own(self, a):
        return self.kept[...]

    def load(self):
        return pltpu.make_async_copy(self.sums.at[self.p.c], self.kept, self.sem.at[0])

    def step(self, k):
        if k == 0:
            self.load().start()
            self.settle()
        elif k == 1:
            self.settle(False)
        elif k == END:
            self.load().wait()
            self.close()


class Background:
    def __init__(self, tasks, greets):
        self.tasks, self.done, names = tasks, [], list(greets)
        for task in tasks:
            names += [name for name in task.greets() if name not in names]
        place = Place()
        self.others = [place.called(name) for name in names]

    def step(self, k):
        for i in range(max([len(task.at) for task in self.tasks], default=0)):
            for task in self.tasks:
                if i < len(task.at) and task.at[i] == k:
                    task.step(i)

    def finish(self, tasks=None):
        for task in self.tasks if tasks is None else tasks:
            if task not in self.done:
                task.step(END)
                self.done.append(task)


def hosted(kernel, ident, name, ins, in_specs, outs, out_specs, scratch, tasks, flops, traffic, greets=()):
    groups = ([], [], [])
    for group, own in zip(groups, (ins, outs, scratch)):
        group.append(len(own))
    ins, in_specs, outs, out_specs, scratch = list(ins), list(in_specs), list(outs), list(out_specs), list(scratch)
    for task in tasks:
        for group, more in zip(groups, (task.ins, task.outs, task.scratch)):
            group.append(len(more))
        ins += task.ins
        in_specs += getattr(task, "in_specs", [HBM] * len(task.ins))
        outs += task.outs
        out_specs += task.out_specs
        scratch += task.scratch

    def split(refs, counts):
        at, found = 0, []
        for count in counts:
            found.append(refs[at : at + count])
            at += count
        return found

    def body(*refs):
        parts = [split(part, group) for part, group in zip(split(refs, [sum(g) for g in groups]), groups)]
        for task, *mine in zip(tasks, *(part[1:] for part in parts)):
            task.bind(*mine)
        kernel(*parts[0][0], *parts[1][0], *parts[2][0], Background(tasks, greets))

    aliases, at_in, at_out = {}, groups[0][0], groups[1][0]
    for task in tasks:
        if getattr(task, "in_place", False):
            aliases[at_in] = at_out
        at_in += len(task.ins)
        at_out += len(task.outs)
    results = pl.pallas_call(
        body,
        out_shape=tuple(outs),
        in_specs=in_specs,
        out_specs=tuple(out_specs),
        scratch_shapes=scratch,
        input_output_aliases=aliases,
        compiler_params=params(ident),
        cost_estimate=pl.CostEstimate(flops=flops, bytes_accessed=traffic, transcendentals=0),
        name=name,
    )(*ins)
    results = split(list(results), groups[1])
    return results[0], [r[0] for r in results[1:] if r]


def put_rows(scratch, first, value, cols=slice(None)):
    tall = scratch.shape[1]
    done = 0
    while done < value.shape[0]:
        piece, at = divmod(first + done, tall)
        count = min(tall - at, value.shape[0] - done)
        scratch[piece, pl.ds(at, count), cols] = value[done : done + count]
        done += count


def put_columns(scratch, first, value):
    wide_piece = scratch.shape[2]
    for piece in range(scratch.shape[0]):
        scratch[piece, pl.ds(first, value.shape[0]), :] = value[:, piece * wide_piece : (piece + 1) * wide_piece]


def column_loads(pieces, whole):
    each = pieces.shape[2]
    return [(pieces.at[i], whole.at[:, pl.ds(i * each, each)]) for i in range(pieces.shape[0])]


def ffn_forward_kernel(
    h_ref, gain_ref, w_hbm, v_hbm, out_ref, n_hbm, u_hbm,
    w, v, nf, u, act, tpart, mine, n_near, n_over, n_on, o_near, i_near, o_over, i_over, s_near, s_over,
    wsem, osem, bg,
):
    g = Group(bg.others)
    g.greet()
    size, width = h_ref.shape
    hidden = v.shape[0]
    loads = start_all([(w_hbm, w)] + column_loads(v_hbm, v), wsem)
    gather = Gather(g, nf, size, n_near, n_over, n_on)
    scatter = Scatter(g, o_near, i_near, o_over, i_over, s_near, s_over, size)
    parts, step = gather.parts, gather.step
    for p in range(parts):
        nf[at_rows(g.mine, size, p * step, step), :] = normalise(
            h_ref[pl.ds(p * step, step), :], gain_ref[...]
        ).astype(BF)
    g.meet()
    gather.start()
    bg.step(0)
    wait_all(loads)

    third = hidden // 3

    def rows_of(places):
        return jnp.concatenate([nf[r, :] for r, _ in places], axis=0) if len(places) > 1 else nf[places[0][0], :]

    def up(places):
        def body(t, carry):
            x = rows_of(places)
            cols, more = lanes(t * third, third), lanes(hidden + t * third, third)
            both = mm(x, jnp.concatenate([w[:, cols], w[:, more]], axis=1))
            gate, upper = both[:, :third], both[:, third:]
            a = gate * jax.nn.sigmoid(gate) * upper
            act[:, cols] = a.astype(BF)
            at = 0
            for r, count in places:
                u[r, cols] = gate[at : at + count].astype(BF)
                u[r, more] = upper[at : at + count].astype(BF)
                at += count
            return carry

        lax.fori_loop(0, 3, body, 0)

    def down(store):
        store(slice(None), mm(act[...], v[...]))

    def keep(index, r, count):
        return pltpu.make_async_copy(u.at[r], u_hbm.at[r], osem.at[index])

    whole = lambda block: at_rows(block, size, 0, size)
    up([(whole(g.mine), size)])
    keep(0, whole(g.mine), size).start()

    def put_mine(cols, value):
        mine[:, cols] = value

    down(put_mine)
    gather.wait_beside()
    up([(whole(g.beside), size)])
    keep(1, whole(g.beside), size).start()

    def put_beside(cols, value):
        o_near[1, :, cols] = value.astype(BF)

    down(put_beside)
    for p in range(parts):
        scatter.close(1, p).start()
    bg.step(1)
    for p in range(parts):
        gather.wait_part(p)
        gather.wait_far(p)
        r_across, r_far = at_rows(g.across, size, p * step, step), at_rows(g.far, size, p * step, step)
        up([(r_across, step), (r_far, step)])
        keep(2 + 2 * p, r_across, step).start()
        keep(3 + 2 * p, r_far, step).start()
        here = scatter.rows(p)

        def put(cols, value):
            tpart[:, cols] = value[:step]
            o_near[0, here, cols] = value[step:].astype(BF)

        down(put)
        scatter.close(0, p).start()
        scatter.close(0, p).wait_recv()
        o_over[here, :] = (tpart[...] + i_near[0, here, :].astype(F32)).astype(BF)
        scatter.link(p).start()
        bg.step(10 + p)
    n_out = pltpu.make_async_copy(nf, n_hbm, osem.at[2 + 2 * parts])
    n_out.start()
    bg.step(2)
    for p in range(parts):
        here = scatter.rows(p)
        scatter.close(1, p).wait_recv()
        scatter.link(p).wait_recv()
        out_ref[here, :] = (
            h_ref[here, :] + mine[here, :] + i_near[1, here, :].astype(F32) + i_over[here, :].astype(F32)
        )
    gather.finish()
    scatter.wait_all_sends()
    keep(0, whole(g.mine), size).wait()
    keep(1, whole(g.beside), size).wait()
    for p in range(parts):
        keep(2 + 2 * p, at_rows(g.across, size, p * step, step), step).wait()
        keep(3 + 2 * p, at_rows(g.far, size, p * step, step), step).wait()
    n_out.wait()
    bg.step(6)
    bg.finish()


def ffn_forward(h, gain, w, v, ident, tasks=(), parts=PARTS):
    size, width = h.shape
    hidden = v.shape[1]
    total = 4 * size
    return hosted(
        ffn_forward_kernel, ident, "ffn_forward", [h, gain, w, v], [INV, INV, HBM, HBM],
        [shaped((size, width), F32), shaped((total, width), BF), shaped((total, 2 * hidden), BF)], [INV, HBM, HBM],
        [
            pltpu.VMEM((width, 2 * hidden), BF), pltpu.VMEM((hidden, width), BF), pltpu.VMEM((total, width), BF),
            pltpu.VMEM((total, 2 * hidden), BF), pltpu.VMEM((size, hidden), BF),
            pltpu.VMEM((size // parts, width), F32), pltpu.VMEM((size, width), F32),
            *gather_scratch(parts), *scatter_scratch(size, width, parts), DMA((1 + v.shape[0],)), DMA((3 + 2 * parts,)),
        ],
        tasks, 6 * total * width * hidden, 2**24,
    )


def mm_tn(a, b):
    return lax.dot_general(a, b, (((0,), (0,)), ((), ())), preferred_element_type=F32)


def rms_back(dn, h, gain):
    inverse = lax.rsqrt(jnp.mean(h * h, axis=-1, keepdims=True) + epsilon)
    scaled = dn * gain
    inner = jnp.mean(scaled * h, axis=-1, keepdims=True)
    grad_gain = jnp.sum(dn * h * inverse, axis=0, keepdims=True)
    return inverse * scaled - h * (inverse * inverse * inverse * inner), grad_gain


def close_scatter(scatter, mine, dh_ref, h_ref, gain_ref, out_ref, gg_ref):
    gg_ref[...] = jnp.zeros_like(gg_ref)
    for p in range(scatter.parts):
        here = scatter.rows(p)
        scatter.close(1, p).wait_recv()
        scatter.link(p).wait_recv()
        dn = mine[here, :] + scatter.in_near[1, here, :].astype(F32) + scatter.in_over[here, :].astype(F32)
        term, grad_gain = rms_back(dn, h_ref[here, :], gain_ref[...])
        out_ref[here, :] = dh_ref[here, :].astype(F32) + term
        gg_ref[...] += grad_gain


def ffn_backward_kernel(
    known, dh_ref, h_ref, gain_ref, df_hbm, w_hbm, v_hbm, n_hbm, u_hbm, out_ref, gg_ref, gw_hbm, gv_hbm,
    w, v, nf, u, act, df, tpart, mine, gw, gv, n_near, n_over, n_on, o_near, i_near, o_over, i_over, s_near, s_over,
    wsem, osem, bg,
):
    g = Group(bg.others)
    g.greet()
    size, width = h_ref.shape
    hidden = v.shape[0]
    loads = column_loads(v_hbm, v) + [(u_hbm, u), (w_hbm, w), (n_hbm, nf)]
    loads = start_all(loads + [(df_hbm, df)] if known else loads, wsem)
    gather = Gather(g, df, size, n_near, n_over, n_on)
    scatter = Scatter(g, o_near, i_near, o_over, i_over, s_near, s_over, size)
    parts, step = gather.parts, gather.step
    if not known:
        df[at_rows(g.mine, size, 0, size), :] = dh_ref[...].astype(BF)
    g.meet()
    if not known:
        gather.start()
    bg.step(0)
    wait_all(loads)

    third = hidden // 3

    def cat(ref, places, cols):
        found = [ref[r, cols] for r, _ in places]
        return found[0] if len(found) == 1 else jnp.concatenate(found, axis=0)

    def first(places):
        def body(t, carry):
            cols, more = lanes(t * third, third), lanes(hidden + t * third, third)
            da = mm_nt(cat(df, places, slice(None)), v[cols, :])
            gate, upper = cat(u, places, cols).astype(F32), cat(u, places, more).astype(F32)
            s = jax.nn.sigmoid(gate)
            lit = gate * s
            dgate = (da * upper * s * (1.0 + gate * (1.0 - s))).astype(BF)
            dupper = (da * lit).astype(BF)
            a = (lit * upper).astype(BF)
            at = 0
            for r, count in places:
                u[r, cols] = dgate[at : at + count]
                u[r, more] = dupper[at : at + count]
                act[r, cols] = a[at : at + count]
                at += count
            return carry

        lax.fori_loop(0, 3, body, 0)

    def second(places, store):
        def body(t, carry):
            cols = lanes(t * 512, 512)
            store(cols, mm_nt(cat(u, places, slice(None)), w[cols, :]))
            return carry

        lax.fori_loop(0, width // 512, body, 0)

    whole = lambda block: [(at_rows(block, size, 0, size), size)]

    def put_mine(cols, value):
        mine[:, cols] = value

    def put_beside(cols, value):
        o_near[1, :, cols] = value.astype(BF)

    def own():
        first(whole(g.mine))
        second(whole(g.mine), put_mine)

    def beside():
        first(whole(g.beside))
        second(whole(g.beside), put_beside)
        for p in range(parts):
            scatter.close(1, p).start()

    if not known:
        own()
        gather.wait_beside()
        beside()
    bg.step(1)
    for p in range(parts):
        if not known:
            gather.wait_part(p)
            gather.wait_far(p)
        pair = [(at_rows(b, size, p * step, step), step) for b in (g.across, g.far)]
        first(pair)
        here = scatter.rows(p)

        def put(cols, value):
            tpart[:, cols] = value[:step]
            o_near[0, here, cols] = value[step:].astype(BF)

        second(pair, put)
        scatter.close(0, p).start()
        scatter.close(0, p).wait_recv()
        o_over[here, :] = (tpart[...] + i_near[0, here, :].astype(F32)).astype(BF)
        scatter.link(p).start()
    bg.step(2)
    if known:
        beside()
        own()
    for t in range(3):
        put_columns(gv, t * third, mm_tn(act[:, t * third : (t + 1) * third], df[...]).astype(BF))
    save = pltpu.make_async_copy(gv, gv_hbm, osem.at[2])
    save.start()
    bg.step(3)
    for t in range(width // 512):
        for k in range(2):
            cols = slice(k * hidden, (k + 1) * hidden)
            put_rows(gw, t * 512, mm_tn(nf[:, t * 512 : (t + 1) * 512], u[:, cols]).astype(BF), cols)
    more = pltpu.make_async_copy(gw, gw_hbm, osem.at[0])
    more.start()
    bg.step(4)
    close_scatter(scatter, mine, df.at[at_rows(g.mine, size, 0, size)] if known else dh_ref, h_ref, gain_ref, out_ref, gg_ref)
    if not known:
        gather.finish()
    scatter.wait_all_sends()
    more.wait()
    save.wait()
    bg.step(6)
    bg.finish()


def ffn_backward(dh, h, gain, df, w, v, n, u, ident, tasks=(), parts=PARTS):
    size, width = h.shape
    pieces, hidden = v.shape[:2]
    total = 4 * size
    known = df is not None
    if known:
        dh = gain
    else:
        df = n
    return hosted(
        functools.partial(ffn_backward_kernel, known), ident, "ffn_backward", [dh, h, gain, df, w, v, n, u],
        [INV, INV, INV] + [HBM] * 5,
        [
            shaped((size, width), F32), shaped((1, width), F32), shaped((pieces, width // pieces, 2 * hidden), BF),
            shaped((pieces, hidden, width // pieces), BF),
        ],
        [INV, INV, HBM, HBM],
        [
            pltpu.VMEM((width, 2 * hidden), BF), pltpu.VMEM((hidden, width), BF), pltpu.VMEM((total, width), BF),
            pltpu.VMEM((total, 2 * hidden), BF), pltpu.VMEM((total, hidden), BF), pltpu.VMEM((total, width), BF),
            pltpu.VMEM((size // parts, width), F32), pltpu.VMEM((size, width), F32),
            pltpu.VMEM((pieces, width // pieces, 2 * hidden), BF), pltpu.VMEM((pieces, hidden, width // pieces), BF),
            *gather_scratch(parts), *scatter_scratch(size, width, parts), DMA((4 + pieces,)), DMA((3,)),
        ],
        tasks, 12 * total * width * hidden, 2**25,
    )


MOST_DOC = 512


class Columns(Gather):
    def __init__(self, group, full, near, over, onward):
        super().__init__(group, full, full.shape[0], near, over, onward)
        self.cols = full.shape[1] // 4

    def view(self, block, part):
        return self.full.at[pl.ds(part * self.step, self.step), lanes(block * self.cols, self.cols)]


def cat_rows(ref, places, cols=slice(None)):
    found = [ref[r, cols] for r, _ in places]
    return found[0] if len(found) == 1 else jnp.concatenate(found, axis=0)


def product(src, weight, turned, tile=512):
    def run(places, store):
        width = weight.shape[0] if turned else weight.shape[1]

        def body(t, carry):
            cols = lanes(t * tile, tile)
            x = cat_rows(src, places)
            store(cols, mm_nt(x, weight[cols, :]) if turned else mm(x, weight[:, cols]))
            return carry

        lax.fori_loop(0, width // tile, body, 0)

    return run


def scatter_all(g, scatter, run, mine, tpart):
    size, step = scatter.size, scatter.step
    for p in range(scatter.parts):
        here = scatter.rows(p)

        def put(cols, value):
            tpart[:, cols] = value[:step]
            scatter.out_near[0, here, cols] = value[step:].astype(BF)

        run([(at_rows(b, size, p * step, step), step) for b in (g.across, g.far)], put)
        scatter.close(0, p).start()
        scatter.close(0, p).wait_recv()
        scatter.out_over[here, :] = (tpart[...] + scatter.in_near[0, here, :].astype(F32)).astype(BF)
        scatter.link(p).start()

    def put_beside(cols, value):
        scatter.out_near[1, :, cols] = value.astype(BF)

    run([(at_rows(g.beside, size, 0, size), size)], put_beside)
    for p in range(scatter.parts):
        scatter.close(1, p).start()

    def put_mine(cols, value):
        mine[:, cols] = value

    run([(at_rows(g.mine, size, 0, size), size)], put_mine)


def gather_everything(gather):
    gather.wait_beside()
    for p in range(gather.parts):
        gather.wait_part(p)
    for p in range(gather.parts):
        gather.wait_far(p)


def doc_starts(docs, lengths, places):
    row = lengths[pl.ds(0, 1), :]
    end = jnp.zeros((1, 1), F32)
    start = jnp.zeros_like(places)
    for d in range(docs):
        end = end + row[:, d : d + 1]
        start = jnp.where(places >= end.astype(jnp.int32), end.astype(jnp.int32), start)
    return start


def conv_taps(gated, within, taps):
    total = gated.shape[0]
    summed = taps[0] * gated
    for j in range(1, len(taps)):
        summed = summed + taps[j] * jnp.where(within >= j, pltpu.roll(gated, j, 0), 0.0)
    return summed


def conv_forward_kernel(
    docs, count, inside, lens_ref, x_hbm, gain_ref, taps_ref, win_hbm, wout_hbm,
    out_ref, block_ref, n_hbm, p_hbm, lengths, taps_out, win_out, wout_out,
    win, wout, full, nf, proj, low, mixed, tpart, mine, n_near, n_over, n_on, o_near, i_near, o_over, i_over,
    s_near, s_over, wsem, osem, xsem, xlocal, bg,
):
    g = Group(bg.others)
    g.greet()
    size, width = out_ref.shape
    total, chans = x_hbm.shape[0], wout.shape[0]
    loads = []
    if inside:
        bg.tasks[0].whole, bg.tasks[1].whole = win, wout
    else:
        loads = start_all([(win_hbm, win), (wout_hbm, wout)], wsem)
    gather = Columns(g, full, n_near, n_over, n_on)
    scatter = Scatter(g, o_near, i_near, o_over, i_over, s_near, s_over, size)
    parts = gather.parts
    blocks = [
        Exchange(
            x_hbm.at[pl.ds(p * gather.step, gather.step)],
            *(full.at[pl.ds(p * gather.step, gather.step), lanes(b * chans, chans)] for b in (g.mine, g.beside)),
            xsem, xlocal, p,
        )
        for p in range(parts)
    ]
    small = [Exchange(lens_ref, lengths, lengths, xsem, xlocal, parts), Exchange(taps_ref, taps_out, taps_out, xsem, xlocal, parts + 1)]
    g.meet()
    for block in blocks + small:
        block.start()
    bg.step(0)
    for p in range(parts):
        blocks[p].arrive()
        gather.link(p, g.mine).start()
        gather.close(p, g.mine).start()
    bg.step(1)
    gather.wait_beside()
    for p in range(parts):
        gather.wait_part(p)
    for p in range(parts):
        gather.wait_far(p)
    for block in small:
        block.arrive()
    bg.step(2)
    if inside:
        bg.finish(bg.tasks[:2])
    wait_all(loads)

    def project(t, carry):
        rows = at_rows(t, size, 0, size)
        n = normalise(full[rows, :].astype(F32), gain_ref[...]).astype(BF)
        nf[rows, :] = n
        p = mm(n, win[...])
        proj[rows, :] = p
        low[rows, :] = p.astype(BF)
        return carry

    lax.fori_loop(0, total // size, project, 0)
    bg.step(4)
    saves = start_all([(nf, n_hbm), (low, p_hbm), (win, win_out), (wout, wout_out)], osem)
    places = lax.broadcasted_iota(jnp.int32, (total, LANES), 0)
    within = places - doc_starts(docs, lengths, places)
    for k in range(chans // LANES):
        b, c, x = (proj[:, pl.ds(i * chans + k * LANES, LANES)] for i in range(3))
        taps = [taps_out[pl.ds(j, 1), pl.ds(k * LANES, LANES)] for j in range(count)]
        mixed[:, pl.ds(k * LANES, LANES)] = (c * conv_taps(b * x, within, taps)).astype(BF)
    bg.step(5)
    scatter_all(g, scatter, product(mixed, wout, False), mine, tpart)
    bg.step(3)
    block_ref[...] = full[at_rows(g.mine, size, 0, size), :]
    for p in range(scatter.parts):
        here = scatter.rows(p)
        scatter.close(1, p).wait_recv()
        scatter.link(p).wait_recv()
        out_ref[here, :] = (
            block_ref[here, :].astype(F32) + mine[here, :] + i_near[1, here, :].astype(F32) + i_over[here, :].astype(F32)
        )
    for block in blocks + small:
        block.finish()
    gather.finish()
    scatter.wait_all_sends()
    wait_all(saves)
    bg.step(6)
    bg.finish()


def conv_forward(docs, count, lens, x, gain, taps, win, wout, inside, ident, tasks=(), parts=PARTS, cuts=4):
    total, chans = x.shape
    width = wout.shape[1]
    size = total // 4
    return hosted(
        functools.partial(conv_forward_kernel, docs, count, inside), ident, "conv_forward",
        [lens, x, gain, taps, win, wout], [INV, HBM, INV, INV, HBM, HBM],
        [
            shaped((size, width), F32), shaped((size, width), BF), shaped((total, width), BF), shaped((total, 3 * chans), BF),
            shaped(lens.shape, F32), shaped(taps.shape, F32), shaped(win.shape, BF), shaped(wout.shape, BF),
        ],
        [INV, INV, HBM, HBM, INV, INV, HBM, HBM],
        [
            pltpu.VMEM((width, 3 * chans), BF), pltpu.VMEM((chans, width), BF), pltpu.VMEM((total, width), BF),
            pltpu.VMEM((total, width), BF), pltpu.VMEM((total, 3 * chans), F32), pltpu.VMEM((total, 3 * chans), BF),
            pltpu.VMEM((total, chans), BF), pltpu.VMEM((size // parts, width), F32), pltpu.VMEM((size, width), F32),
            *gather_scratch(cuts), *scatter_scratch(size, width, parts), DMA((2,)), DMA((4,)),
            DMA((2, cuts + 2)), DMA((cuts + 2,)),
        ],
        tasks, 8 * total * width * chans, 2**24, ("swap",),
    )


def conv_backward_kernel(
    docs, count, lengths, dh_ref, h_ref, gain_ref, taps_ref, win_hbm, wout_hbm, n_hbm, p_hbm, out_ref, gg_ref, gt_ref, gin_hbm, gout_hbm,
    win, wout, nf, low, dz, dy, mixed, dproj, gin, gout, tpart, mine, n_near, n_over, n_on, o_near, i_near, o_over, i_over,
    s_near, s_over, wsem, osem, bg,
):
    g = Group(bg.others)
    g.greet()
    size, width = dh_ref.shape
    total, chans = 4 * size, wout.shape[0]
    loads = start_all([(wout_hbm, wout), (p_hbm, low), (win_hbm, win), (n_hbm, nf)], wsem)
    gather = Gather(g, dz, size, n_near, n_over, n_on)
    scatter = Scatter(g, o_near, i_near, o_over, i_over, s_near, s_over, size)
    dz[at_rows(g.mine, size, 0, size), :] = dh_ref[...].astype(BF)
    g.meet()
    gather.start()
    bg.step(0)
    wait_all(loads)
    places = lax.broadcasted_iota(jnp.int32, (total, LANES), 0)
    within = places - doc_starts(docs, lengths, places)
    gather_everything(gather)
    bg.step(1)

    def project(t, carry):
        rows = at_rows(t, size, 0, size)
        dy[rows, :] = mm_nt(dz[rows, :], wout[...])
        return carry

    lax.fori_loop(0, total // size, project, 0)
    for k in range(chans // LANES):
        b, c, x = (low[:, pl.ds(i * chans + k * LANES, LANES)].astype(F32) for i in range(3))
        here = pl.ds(k * LANES, LANES)
        taps = [taps_ref[pl.ds(j, 1), here] for j in range(count)]
        gated = b * x
        summed = conv_taps(gated, within, taps)
        d = dy[:, here]
        mixed[:, here] = (c * summed).astype(BF)
        ds = d * c
        dg = taps[0] * ds
        gt_ref[pl.ds(0, 1), here] = jnp.sum(ds * gated, axis=0, keepdims=True)
        for j in range(1, len(taps)):
            masked = jnp.where(within >= j, ds, 0.0)
            dg = dg + taps[j] * pltpu.roll(masked, total - j, 0)
            gt_ref[pl.ds(j, 1), here] = jnp.sum(masked * pltpu.roll(gated, j, 0), axis=0, keepdims=True)
        dproj[:, pl.ds(k * LANES, LANES)] = (dg * x).astype(BF)
        dproj[:, pl.ds(chans + k * LANES, LANES)] = (d * summed).astype(BF)
        dproj[:, pl.ds(2 * chans + k * LANES, LANES)] = (dg * b).astype(BF)
    bg.step(2)
    scatter_all(g, scatter, product(dproj, win, True), mine, tpart)
    bg.step(3)
    put_columns(gout, 0, mm_tn(mixed[...], dz[...]).astype(BF))
    save = pltpu.make_async_copy(gout, gout_hbm, osem.at[0])
    save.start()
    for t in range(width // 256):
        put_rows(gin, t * 256, mm_tn(nf[:, pl.ds(t * 256, 256)], dproj[...]).astype(BF))
    more = pltpu.make_async_copy(gin, gin_hbm, osem.at[1])
    more.start()
    bg.step(4)
    close_scatter(scatter, mine, dh_ref, h_ref, gain_ref, out_ref, gg_ref)
    gather.finish()
    scatter.wait_all_sends()
    save.wait()
    more.wait()
    bg.step(5)
    bg.step(6)
    bg.finish()


def conv_backward(docs, count, lengths, dh, h, gain, taps, win, wout, n, p, pieces, ident, tasks=(), parts=PARTS):
    size, width = dh.shape
    total, chans = 4 * size, wout.shape[0]
    each = width // pieces
    return hosted(
        functools.partial(conv_backward_kernel, docs, count), ident, "conv_backward",
        [lengths, dh, h, gain, taps, win, wout, n, p],
        [INV, INV, INV, INV, INV, HBM, HBM, HBM, HBM],
        [
            shaped((size, width), F32), shaped((1, width), F32), shaped(taps.shape, F32),
            shaped((pieces, each, 3 * chans), BF), shaped((pieces, chans, each), BF),
        ],
        [INV, INV, INV, HBM, HBM],
        [
            pltpu.VMEM((width, 3 * chans), BF), pltpu.VMEM((chans, width), BF), pltpu.VMEM((total, width), BF),
            pltpu.VMEM((total, 3 * chans), BF), pltpu.VMEM((total, width), BF), pltpu.VMEM((total, chans), F32),
            pltpu.VMEM((total, chans), BF), pltpu.VMEM((total, 3 * chans), BF), pltpu.VMEM((pieces, each, 3 * chans), BF),
            pltpu.VMEM((pieces, chans, each), BF), pltpu.VMEM((size // parts, width), F32), pltpu.VMEM((size, width), F32),
            *gather_scratch(parts), *scatter_scratch(size, width, parts), DMA((4,)), DMA((2,)),
        ],
        tasks, 16 * total * width * chans, 2**24,
    )


def head_sums(values, head):
    width = values.shape[1]
    a = lax.broadcasted_iota(jnp.int32, (width, width), 0) // head
    b = lax.broadcasted_iota(jnp.int32, (width, width), 1) // head
    same = jnp.where(a == b, 1.0, 0.0).astype(BF)
    high = values.astype(BF)
    low = (values - high.astype(F32)).astype(BF)
    return mm(high, same) + mm(low, same)


def turn(values, head):
    width = values.shape[1]
    lane = lax.broadcasted_iota(jnp.int32, values.shape, 1)
    return jnp.where(
        lane % head < head // 2, pltpu.roll(values, width - head // 2, 1), pltpu.roll(values, head // 2, 1)
    )


def wide(table, width):
    return jnp.concatenate([table] * (width // table.shape[1]), axis=1)


def norm_turn(raw, gain, cosine, sine, head):
    inverse = lax.rsqrt(head_sums(raw * raw, head) * (1.0 / head) + epsilon)
    v = raw * inverse * gain
    return v * wide(cosine, raw.shape[1]) + turn(v, head) * wide(sine, raw.shape[1])


def norm_turn_back(d, raw, gain, cosine, sine, head):
    d = d * wide(cosine, raw.shape[1]) - turn(d, head) * wide(sine, raw.shape[1])
    inverse = lax.rsqrt(head_sums(raw * raw, head) * (1.0 / head) + epsilon)
    scaled = d * gain
    inner = head_sums(scaled * raw, head) * (1.0 / head)
    grad_gain = jnp.sum(d * raw * inverse, axis=0, keepdims=True)
    return inverse * scaled - raw * (inverse * inverse * inverse * inner), grad_gain


def score_tile(q, k, starts, first_key, first_query, scale):
    raw = mm_nt(k, q) * scale
    key = first_key + lax.broadcasted_iota(jnp.int32, raw.shape, 0)
    query = first_query + lax.broadcasted_iota(jnp.int32, (1, starts.shape[1]), 1)
    copies = raw.shape[1] // starts.shape[1]
    allowed = (key <= wide(query, raw.shape[1])) & (key >= wide(starts, raw.shape[1]))
    return jnp.where(allowed, raw, -1e30)


def softmax_tile(scores):
    top = jnp.max(scores, axis=0, keepdims=True)
    weights = jnp.exp(scores - top)
    return weights / jnp.sum(weights, axis=0, keepdims=True)


def stack_heads(values, head):
    return jnp.concatenate([values[:, i * head : (i + 1) * head] for i in range(values.shape[1] // head)], axis=0)


def attention_tiles(total, tile):
    back = -(-MOST_DOC // tile)
    return [(i * tile, max(0, i - back) * tile, (i + 1) * tile) for i in range(total // tile)]


def attention_forward_kernel(
    head, docs, lengths, h_ref, gain_ref, qgain_ref, kgain_ref, speed_ref, wq_hbm, wkv_hbm, wo_hbm,
    out_ref, n_hbm, raw_hbm, ready_hbm, o_hbm, cos_ref, sin_ref,
    w, wo, nf, low, ready, vt, o, tpart, mine, n_near, n_over, n_on, o_near, i_near, o_over, i_over,
    s_near, s_over, wsem, osem, bg,
):
    g = Group(bg.others)
    g.greet()
    size, width = h_ref.shape
    total, qw = 4 * size, wo.shape[0]
    kw = (w.shape[1] - qw) // 2
    loads = start_all([(wq_hbm, w.at[:, pl.ds(0, qw)]), (wkv_hbm, w.at[:, pl.ds(qw, 2 * kw)]), (wo_hbm, wo)], wsem)
    gather = Gather(g, nf, size, n_near, n_over, n_on)
    scatter = Scatter(g, o_near, i_near, o_over, i_over, s_near, s_over, size)
    parts, step = gather.parts, gather.step
    nf[at_rows(g.mine, size, 0, size), :] = normalise(h_ref[...], gain_ref[...]).astype(BF)
    g.meet()
    gather.start()
    bg.step(0)
    places = lax.broadcasted_iota(jnp.int32, (total, LANES), 0)
    angles = (places - doc_starts(docs, lengths, places)).astype(F32) * speed_ref[...]
    lane = lax.broadcasted_iota(jnp.int32, (total, LANES), 1)
    sine = jnp.sin(angles)
    cos_ref[...] = jnp.cos(angles)
    sin_ref[...] = jnp.where(lane % head < head // 2, -sine, sine)
    wait_all(loads)

    def project(block):
        rows = at_rows(block, size, 0, size)
        raw = mm(nf[rows, :], w[...])
        low[rows, :] = raw.astype(BF)
        cosine, sine = cos_ref[rows, :], sin_ref[rows, :]
        ready[rows, pl.ds(0, qw)] = norm_turn(raw[:, :qw], qgain_ref[...], cosine, sine, head).astype(BF)
        ready[rows, pl.ds(qw, kw)] = norm_turn(raw[:, qw : qw + kw], kgain_ref[...], cosine, sine, head).astype(BF)
        ready[rows, pl.ds(qw + kw, kw)] = raw[:, qw + kw :].astype(BF)

    project(g.mine)
    gather.wait_beside()
    project(g.beside)
    for p in range(parts):
        gather.wait_part(p)
    for p in range(parts):
        gather.wait_far(p)

    def rest(i, carry):
        project(jnp.where(i == 0, g.across, g.far))
        return carry

    lax.fori_loop(0, 2, rest, 0)
    bg.step(1)
    saves = start_all([(nf, n_hbm), (low, raw_hbm), (ready, ready_hbm)], osem)
    vt[...] = jnp.transpose(ready[:, pl.ds(qw + kw, kw)].astype(F32)).astype(BF)
    groups = qw // kw
    tile = 256
    scale = head ** (-0.5)
    starts = doc_starts(docs, lengths, lax.broadcasted_iota(jnp.int32, (1, total), 1))
    for first, low_key, high_key in attention_tiles(total, tile):
        keys = pl.ds(low_key, high_key - low_key)
        for kv in range(kw // head):
            q = stack_heads(ready[pl.ds(first, tile), pl.ds(kv * groups * head, groups * head)], head)
            k = ready[keys, pl.ds(qw, kw)][:, kv * head : (kv + 1) * head]
            p = softmax_tile(score_tile(q, k, starts[:, first : first + tile], low_key, first, scale)).astype(BF)
            ot = mm(vt[pl.ds(kv * head, head), keys], p)
            joined = jnp.concatenate([ot[:, i * tile : (i + 1) * tile] for i in range(groups)], axis=0)
            o[pl.ds(first, tile), pl.ds(kv * groups * head, groups * head)] = jnp.transpose(joined).astype(BF)
        if first == tile:
            bg.step(2)
    bg.step(3)
    save_o = pltpu.make_async_copy(o, o_hbm, osem.at[3])
    save_o.start()
    scatter_all(g, scatter, product(o, wo, False), mine, tpart)
    bg.step(4)
    for p in range(parts):
        here = scatter.rows(p)
        scatter.close(1, p).wait_recv()
        scatter.link(p).wait_recv()
        out_ref[here, :] = (
            h_ref[here, :] + mine[here, :] + i_near[1, here, :].astype(F32) + i_over[here, :].astype(F32)
        )
    gather.finish()
    scatter.wait_all_sends()
    wait_all(saves)
    save_o.wait()
    bg.step(6)
    bg.finish()


def attention_forward(head, docs, lengths, h, gain, qgain, kgain, speed, wq, wkv, wo, ident, tasks=(), parts=PARTS):
    size, width = h.shape
    total, qw = 4 * size, wo.shape[0]
    kw = wkv.shape[1] // 2
    every = qw + 2 * kw
    return hosted(
        functools.partial(attention_forward_kernel, head, docs), ident, "attention_forward",
        [lengths, h, gain, qgain, kgain, speed, wq, wkv, wo], [INV] * 6 + [HBM] * 3,
        [
            shaped((size, width), F32), shaped((total, width), BF), shaped((total, every), BF), shaped((total, every), BF),
            shaped((total, qw), BF), shaped((total, LANES), F32), shaped((total, LANES), F32),
        ],
        [INV] + [HBM] * 4 + [INV] * 2,
        [
            pltpu.VMEM((width, every), BF), pltpu.VMEM((qw, width), BF), pltpu.VMEM((total, width), BF),
            pltpu.VMEM((total, every), BF), pltpu.VMEM((total, every), BF),
            pltpu.VMEM((kw, total), BF), pltpu.VMEM((total, qw), BF),
            pltpu.VMEM((size // parts, width), F32), pltpu.VMEM((size, width), F32),
            *gather_scratch(parts), *scatter_scratch(size, width, parts), DMA((3,)), DMA((4,)),
        ],
        tasks, 2 * total * width * (every + qw), 2**24,
    )


def attention_backward_kernel(
    head, docs, lengths, dh_ref, h_ref, gain_ref, qgain_ref, kgain_ref, cos_ref, sin_ref, wq_hbm, wkv_hbm, wo_hbm,
    n_hbm, raw_hbm, ready_hbm, o_hbm, out_ref, gg_ref, gq_ref, gk_ref, gw_hbm, gwo_hbm,
    w, wo, nf, low, ready, kt, o, dz, do, dq, dkv, dlow, gw, gwo, tpart, mine,
    n_near, n_over, n_on, o_near, i_near, o_over, i_over, s_near, s_over, wsem, osem, bg,
):
    g = Group(bg.others)
    g.greet()
    size, width = h_ref.shape
    total, qw = 4 * size, wo.shape[0]
    kw = (w.shape[1] - qw) // 2
    loads = start_all(
        [
            (ready_hbm, ready), (wo_hbm, wo), (o_hbm, o), (raw_hbm, low), (wq_hbm, w.at[:, pl.ds(0, qw)]),
            (wkv_hbm, w.at[:, pl.ds(qw, 2 * kw)]), (n_hbm, nf),
        ],
        wsem,
    )
    gather = Gather(g, dz, size, n_near, n_over, n_on)
    scatter = Scatter(g, o_near, i_near, o_over, i_over, s_near, s_over, size)
    dz[at_rows(g.mine, size, 0, size), :] = dh_ref[...].astype(BF)
    g.meet()
    gather.start()
    bg.step(0)
    wait_all(loads)
    kt[...] = jnp.transpose(ready[:, pl.ds(qw, kw)].astype(F32)).astype(BF)
    dkv[...] = jnp.zeros_like(dkv)
    gather_everything(gather)

    def project(t, carry):
        rows = at_rows(t, size, 0, size)
        do[rows, :] = mm_nt(dz[rows, :], wo[...]).astype(BF)
        return carry

    bg.step(1)

    lax.fori_loop(0, total // size, project, 0)
    groups = qw // kw
    tile = 256
    scale = head ** (-0.5)
    starts = doc_starts(docs, lengths, lax.broadcasted_iota(jnp.int32, (1, total), 1))
    for first, low_key, high_key in attention_tiles(total, tile):
        keys = pl.ds(low_key, high_key - low_key)
        for kv in range(kw // head):
            cols = pl.ds(kv * groups * head, groups * head)
            lane = slice(kv * head, (kv + 1) * head)
            q = stack_heads(ready[pl.ds(first, tile), cols], head)
            k, v = ready[keys, pl.ds(qw, kw)][:, lane], ready[keys, pl.ds(qw + kw, kw)][:, lane]
            p = softmax_tile(score_tile(q, k, starts[:, first : first + tile], low_key, first, scale))
            d = stack_heads(do[pl.ds(first, tile), cols], head)
            dp = mm_nt(v, d)
            inner = jnp.sum(p * dp, axis=0, keepdims=True)
            ds = (p * (dp - inner)).astype(BF)
            both = jnp.concatenate([mm(ds, q) * scale, mm(p.astype(BF), d)], axis=1)
            dkv[kv, keys, :] += both
            dqt = mm(kt[pl.ds(kv * head, head), keys], ds) * scale
            joined = jnp.concatenate([dqt[:, i * tile : (i + 1) * tile] for i in range(groups)], axis=0)
            dq[pl.ds(first, tile), cols] = jnp.transpose(joined)
        if first == tile:
            bg.step(2)
        if first == 2 * tile:
            bg.step(3)
    bg.step(4)
    gq_ref[...] = jnp.zeros_like(gq_ref)
    gk_ref[...] = jnp.zeros_like(gk_ref)

    def finish(t, carry):
        rows = at_rows(t, size, 0, size)
        cosine, sine = cos_ref[rows, :], sin_ref[rows, :]
        d, gq = norm_turn_back(dq[rows, :], low[rows, pl.ds(0, qw)].astype(F32), qgain_ref[...], cosine, sine, head)
        gq_ref[...] += gq
        dlow[rows, pl.ds(0, qw)] = d.astype(BF)
        pairs = [dkv[kv, rows, :] for kv in range(kw // head)]
        dk = jnp.concatenate([x[:, :head] for x in pairs], axis=1)
        dv = jnp.concatenate([x[:, head:] for x in pairs], axis=1)
        d, gk = norm_turn_back(dk, low[rows, pl.ds(qw, kw)].astype(F32), kgain_ref[...], cosine, sine, head)
        gk_ref[...] += gk
        dlow[rows, pl.ds(qw, kw)] = d.astype(BF)
        dlow[rows, pl.ds(qw + kw, kw)] = dv.astype(BF)
        return carry

    lax.fori_loop(0, total // size, finish, 0)
    scatter_all(g, scatter, product(dlow, w, True), mine, tpart)
    put_columns(gwo, 0, mm_tn(o[...], dz[...]).astype(BF))
    save = pltpu.make_async_copy(gwo, gwo_hbm, osem.at[0])
    save.start()
    for t in range(width // 256):
        put_rows(gw, t * 256, mm_tn(nf[:, pl.ds(t * 256, 256)], dlow[...]).astype(BF))
    more = pltpu.make_async_copy(gw, gw_hbm, osem.at[1])
    more.start()
    bg.step(5)
    close_scatter(scatter, mine, dh_ref, h_ref, gain_ref, out_ref, gg_ref)
    gather.finish()
    scatter.wait_all_sends()
    save.wait()
    more.wait()
    bg.step(6)
    bg.finish()


def attention_backward(
    head, docs, lengths, dh, h, gain, qgain, kgain, cosine, sine, wq, wkv, wo, n, raw, ready, o, pieces, ident, tasks=(),
    parts=PARTS,
):
    size, width = h.shape
    total, qw = 4 * size, wo.shape[0]
    kw = wkv.shape[1] // 2
    every = qw + 2 * kw
    each = width // pieces
    return hosted(
        functools.partial(attention_backward_kernel, head, docs), ident, "attention_backward",
        [lengths, dh, h, gain, qgain, kgain, cosine, sine, wq, wkv, wo, n, raw, ready, o], [INV] * 8 + [HBM] * 7,
        [
            shaped((size, width), F32), shaped((1, width), F32), shaped((1, qw), F32), shaped((1, kw), F32),
            shaped((pieces, each, every), BF), shaped((pieces, qw, each), BF),
        ],
        [INV, INV, INV, INV, HBM, HBM],
        [
            pltpu.VMEM((width, every), BF), pltpu.VMEM((qw, width), BF), pltpu.VMEM((total, width), BF),
            pltpu.VMEM((total, every), BF), pltpu.VMEM((total, every), BF), pltpu.VMEM((kw, total), BF),
            pltpu.VMEM((total, qw), BF), pltpu.VMEM((total, width), BF), pltpu.VMEM((total, qw), BF),
            pltpu.VMEM((total, qw), F32), pltpu.VMEM((kw // head, total, 2 * head), F32), pltpu.VMEM((total, every), BF),
            pltpu.VMEM((pieces, each, every), BF), pltpu.VMEM((pieces, qw, each), BF),
            pltpu.VMEM((size // parts, width), F32), pltpu.VMEM((size, width), F32),
            *gather_scratch(parts), *scatter_scratch(size, width, parts), DMA((7,)), DMA((2,)),
        ],
        tasks, 4 * total * width * (every + qw), 2**25,
    )


def tail_kernel(bg):
    g = Group(bg.others)
    g.greet()
    g.meet()
    for k in range(4):
        bg.step(k)
    bg.step(6)
    bg.finish()


def tail(ident, tasks):
    return hosted(tail_kernel, ident, "tail", [], [], [], [], [], tasks, 0, 2**22)[1]


rope_base = 1000000.0
TP = ("c", "zl")
DP = ("r", "s", "zh")


def rope_speeds(head_dim):
    half_dim = head_dim // 2
    inverse = rope_base ** (-2.0 * jnp.arange(half_dim, dtype=F32) / head_dim)
    return jnp.tile(inverse, LANES // half_dim)[None]


def swap(x):
    return lax.ppermute(x, ("c", "zh"), [(0, 0), (1, 2), (2, 1), (3, 3)])


def gather_dp(shard, axis):
    return lax.all_gather(swap(shard), DP, axis=axis, tiled=True)


def scatter_dp(partial, axis):
    return swap(lax.psum_scatter(partial, DP, scatter_dimension=axis, tiled=True)).astype(F32)


def local(
    planes, tokens, doc_lengths, grad_out, norm_gains, head_gains, conv_in, conv_kernel, conv_out,
    query_w, kv_w, out_w, gate_up, down,
):
    length = tokens.shape[0]
    head_dim = head_gains.shape[1]
    docs, count = doc_lengths.shape[1], conv_kernel.shape[0]
    conv_in = conv_in.reshape(conv_in.shape[0], -1)
    kv_w = kv_w.reshape(kv_w.shape[0], -1)
    own_w = [gate_up[l].reshape(gate_up.shape[1], -1) for l in (0, 1)]
    own_v = [down[l] for l in (0, 1)]
    pieces = 8 if planes else 1
    kv_width = kv_w.shape[1] // 2
    qgain = jnp.tile(head_gains[0:1], (1, query_w.shape[1] // head_dim))
    kgain = jnp.tile(head_gains[1:2], (1, kv_width // head_dim))
    gain = [norm_gains[i : i + 1] for i in range(4)]
    lens = jnp.pad(doc_lengths.astype(F32), ((0, 7), (0, LANES - docs)))
    taps = jnp.pad(conv_kernel, ((0, 8 - count), (0, 0)))
    rows_of = lambda got: got.reshape(-1, got.shape[-1])
    if planes:
        first = [Take(conv_in, (0, 0, 0, 2, 2), True), Take(conv_out, (0, 0, 0, 2, 2), True)]
        first += [Fetch(own_w[0], (0, 1, 1, 2, 2, 2, 4, 5, 3), 4), Fetch(own_v[0], (0, 1, 1, 2, 4, 5, 3), 2)]
        second = [Take(x, (0, 0, 0, 2, 2)) for x in (query_w, kv_w, out_w)]
        second += [Fetch(own_w[1], (0, 0, 0, 2), 1, 1), Fetch(own_v[1], (0, 0, 0, 2), 1, 1)]
    else:
        first, second, third = [], [], []
        conv_in, conv_out, query_w, kv_w, out_w = map(swap, (conv_in, conv_out, query_w, kv_w, out_w))
        w0, w1 = (gather_dp(w, 0) for w in own_w)
        v0, v1 = (gather_dp(v, 1)[None] for v in own_v)

    (h1, x_block, n0, projected, lens, taps, conv_in, conv_out), got = conv_forward(
        docs, count, lens, tokens, gain[0], taps, conv_in, conv_out, planes, 0, first
    )
    if planes:
        w0, v0 = rows_of(got[0]), got[1]
    (h2, n1, hidden0), got = ffn_forward(h1, gain[1], w0, v0, 1, second)
    if planes:
        query_w, kv_w, out_w = got[:3]
        third = [Fetch(got[3], (0, 4), 2, 2), Fetch(got[4], (0, 4), 1, 2)]
    (h3, n2, raw, ready, attended, cosine, sine), got = attention_forward(
        head_dim, docs, lens, h2, gain[2], qgain, kgain, rope_speeds(head_dim), query_w, kv_w, out_w, 2, third
    )
    if planes:
        w1, v1 = rows_of(got[0]), got[1]
    (h4, n3, hidden1), (up_full,) = ffn_forward(h3, gain[3], w1, v1, 3, [Spread(grad_out, (0, 1, 2))])

    def halves(grad, first, second, last=False):
        half = grad.shape[1] // 2
        return [Reduce(grad, 0, half, first, last), Reduce(grad, half, half, second, False)] if planes else []

    def whole(grad, at, last=False):
        return [Reduce(grad, 0, grad.shape[1], at, last)] if planes else []

    def settled(sums, at):
        return [Settle(x, at) for x in sums]

    (dh3, gain3, gw1, gv1), (output,) = ffn_backward(
        None, h3, gain[3], up_full, w1, v1, n3, hidden1, 4, [Deliver(h4, (0, 2))]
    )
    (dh2, gain2, gq, gk, gqkv, gow), sums = attention_backward(
        head_dim, docs, lens, dh3, h2, gain[2], qgain, kgain, cosine, sine, query_w, kv_w, out_w, n2, raw, ready, attended,
        pieces, 5, halves(gw1, (0, 2, 5), (0, 4, 6)),
    )
    (dh1, gain1, gw0, gv0), got = ffn_backward(
        dh2, h1, gain[1], None, w0, v0, n1, hidden0, 6,
        settled(sums, (0, 0)) + whole(gv1, (0, 1, 2)) + whole(gqkv, (0, 2, 3)) + whole(gow, (0, 2, 3)),
    )
    sums_w1, sums = got[:2], got[2:]
    (dh0, gain0, gtaps, gci, gco), got = conv_backward(
        docs, count, lens, dh1, x_block.astype(F32), gain[0], taps, conv_in, conv_out, n0, projected, pieces, 7,
        settled(sums, (0, 0)) + halves(gw0, (0, 1, 4), (0, 3, 6), True),
    )
    others, first_w0, sums = got[:3], got[3:4], got[4:]
    totals, grads, *got = tail(
        8,
        [Total([gain0, gain1, gain2, gain3, gtaps, gq, gk], (0, 1, 2, 3), count, ("zh", "s", *(("r",) if planes else ()), "zl", "c")), Deliver(dh0, (0, 0))]
        + settled(sums, (0, 0)) + whole(gv0, (0, 0, 1), True) + whole(gci, (1, 2, 3), True) + whole(gco, (1, 2, 3), True),
    )
    if planes:
        gw1 = jnp.concatenate(sums_w1, axis=0)
        gv1, gqkv, gow = others
        gw0 = jnp.concatenate([first_w0[0], got[0]], axis=0)
        gv0, gci, gco = got[1:]
    else:
        totals = lax.psum(totals, "r")
        gw0, gw1, gci, gqkv = (scatter_dp(g[0], 0) for g in (gw0, gw1, gci, gqkv))
        gv0, gv1, gco, gow = (scatter_dp(g[0], 1) for g in (gv0, gv1, gco, gow))
    heads = totals[7, : gq.shape[1] + gk.shape[1]].reshape(-1, head_dim)
    split = gq.shape[1] // head_dim
    return (
        output,
        grads.astype(F32),
        totals[:4],
        jnp.stack([jnp.sum(heads[:split], axis=0), jnp.sum(heads[split:], axis=0)]),
        gci.reshape(-1, 3, conv_kernel.shape[1]),
        totals[4 : 4 + count],
        gco,
        gqkv[:, : query_w.shape[1]],
        gqkv[:, query_w.shape[1] :].reshape(-1, 2, kv_width),
        gow,
        jnp.stack([gw0, gw1]).reshape(2, gate_up.shape[1], 2, -1),
        jnp.stack([gv0, gv1]),
    )


def solution(mesh):
    devices = mesh.devices
    dp, tp = devices.shape
    inner = Mesh(devices.reshape(dp // 4, 2, 2, 2, tp // 2), ("r", "s", "c", "zh", "zl"))
    D = ("r", "s", "c")
    T = ("zh", "zl")
    return jax.shard_map(
        functools.partial(local, dp == 8),
        mesh=inner,
        in_specs=(
            P(D, T), P(D, None), P(D, T), P(), P(), P(None, None, T), P(None, T), P(T, None),
            P(None, T), P(None, None, T), P(T, None), P(None, D, None, T), P(None, T, D),
        ),
        out_specs=(
            P(D, T), P(D, T), P(), P(), P(D, None, T), P(), P(T, D), P(D, T), P(D, None, T),
            P(T, D), P(None, D, None, T), P(None, T, D),
        ),
        check_vma=False,
    )
```

```python
import functools
import jax
import jax.numpy as jnp
from jax import lax
from jax.experimental import pallas as pl
from jax.experimental.pallas import tpu as pltpu
from jax.sharding import Mesh, PartitionSpec as P

epsilon = 1e-05
BF = jnp.bfloat16
F32 = jnp.float32
MESH = pl.DeviceIdType.MESH
DMA = pltpu.SemaphoreType.DMA
HBM = pl.BlockSpec(memory_space=pl.ANY)
INV = pl.BlockSpec(memory_space=pltpu.VMEM)
PARTS = 2
LANES = 128


class Group:
    def __init__(self, others=(), calls=True):
        c, z = lax.axis_index("c"), lax.axis_index("zl")
        self.partner, self.twin = {"c": 1 - c}, {"zl": 1 - z}
        self.mine, self.beside = 2 * c + z, 2 * (1 - c) + z
        self.across, self.far = 2 * c + (1 - z), 2 * (1 - c) + (1 - z)
        self.known = [self.partner, self.twin, *others]
        self.c, self.z = c, z
        self.barrier = pltpu.get_barrier_semaphore() if calls else None

    def greet(self):
        for other in self.known:
            pl.semaphore_signal(self.barrier, inc=1, device_id=other, device_id_type=MESH)

    def meet(self):
        pl.semaphore_wait(self.barrier, len(self.known))


def at_rows(block, size, start, count):
    return pl.ds(pl.multiple_of(block * size + start, 16), count)


def send(src, dst, sems, index, where):
    return pltpu.make_async_remote_copy(
        src_ref=src, dst_ref=dst, send_sem=sems.at[0, index], recv_sem=sems.at[1, index],
        device_id=where, device_id_type=MESH,
    )


class Gather:
    def __init__(self, group, full, size, near, over, onward):
        self.g, self.full, self.size, self.parts = group, full, size, over.shape[1]
        self.near, self.over, self.onward = near, over, onward
        self.step = size // self.parts

    def view(self, block, part):
        return self.full.at[at_rows(block, self.size, part * self.step, self.step)]

    def link(self, part, block):
        v = self.view(block, part)
        return send(v, v, self.over, part, self.g.twin)

    def close(self, part, block):
        v = self.view(block, part)
        return send(v, v, self.near, part, self.g.partner)

    def pass_on(self, part, block):
        v = self.view(block, part)
        return send(v, v, self.onward, part, self.g.partner)

    def start(self):
        for p in range(self.parts):
            self.link(p, self.g.mine).start()
            self.close(p, self.g.mine).start()

    def wait_beside(self):
        for p in range(self.parts):
            self.close(p, self.g.beside).wait_recv()

    def wait_part(self, p):
        self.link(p, self.g.across).wait_recv()
        self.pass_on(p, self.g.across).start()

    def wait_far(self, p):
        self.pass_on(p, self.g.far).wait_recv()

    def finish(self):
        for p in range(self.parts):
            self.link(p, self.g.mine).wait_send()
            self.close(p, self.g.mine).wait_send()
            self.pass_on(p, self.g.across).wait_send()


class Scatter:
    def __init__(self, group, out_near, in_near, out_over, in_over, near, over, size):
        self.g, self.size, self.parts = group, size, over.shape[1]
        self.out_near, self.in_near, self.out_over, self.in_over = out_near, in_near, out_over, in_over
        self.near, self.over = near, over
        self.step = size // self.parts

    def rows(self, part):
        return pl.ds(part * self.step, self.step)

    def close(self, which, part):
        r = self.rows(part)
        return send(self.out_near.at[which, r], self.in_near.at[which, r], self.near, which * self.parts + part, self.g.partner)

    def link(self, part):
        r = self.rows(part)
        return send(self.out_over.at[r], self.in_over.at[r], self.over, part, self.g.twin)

    def wait_all_sends(self):
        for p in range(self.parts):
            self.close(0, p).wait_send()
            self.close(1, p).wait_send()
            self.link(p).wait_send()


def scatter_scratch(size, width, parts):
    return [
        pltpu.VMEM((2, size, width), BF), pltpu.VMEM((2, size, width), BF), pltpu.VMEM((size, width), BF),
        pltpu.VMEM((size, width), BF), DMA((2, 2 * parts)), DMA((2, parts)),
    ]


def gather_scratch(parts):
    return [DMA((2, parts)), DMA((2, parts)), DMA((2, parts))]


def normalise(h, gain):
    return h * lax.rsqrt(jnp.mean(h * h, axis=-1, keepdims=True) + epsilon) * gain


def mm(a, b):
    return jnp.dot(a, b, preferred_element_type=F32)


def mm_nt(a, b):
    return lax.dot_general(a, b, (((1,), (1,)), ((), ())), preferred_element_type=F32)


def lanes(start, width):
    return pl.ds(pl.multiple_of(start, LANES), width)


def start_all(pairs, sems):
    copies = [pltpu.make_async_copy(src, dst, sems.at[i]) for i, (src, dst) in enumerate(pairs)]
    for copy in copies:
        copy.start()
    return copies


def wait_all(copies):
    for copy in copies:
        copy.wait()


def params(ident):
    return pltpu.CompilerParams(collective_id=ident, has_side_effects=True, vmem_limit_bytes=56 * 2**20)


def shaped(shape, dtype):
    return jax.ShapeDtypeStruct(shape, dtype)


END = 99


class Place:
    def __init__(self):
        self.y, self.x, self.c, self.zh = (lax.axis_index(a) for a in ("r", "s", "c", "zh"))
        self.across_x, self.across_y = {"s": 1 - self.x}, {"r": 1 - self.y}
        self.partner = {"c": 1 - self.c}
        self.plain = self.c == self.zh
        self.outer = lax.axis_index("zl") == self.zh

    def over(self, core):
        return {"c": core, "zh": 1 - self.zh}

    def swapped(self):
        return self.over(self.zh)

    PLANES = ("x", "y")
    ENDS = ("end", "swap")
    COLUMN = ("end", "swap", "z core", "z end", "z swap")

    def called(self, name):
        z = 1 - lax.axis_index("zl")
        other, far = 1 - self.c, 1 - self.zh
        return {
            "x": self.across_x, "y": self.across_y, "end": self.over(self.c), "swap": self.over(other),
            "z core": {"c": other, "zl": z}, "z end": {"zh": far, "zl": z}, "z swap": {"c": other, "zh": far, "zl": z},
        }[name]

    def piece(self, flip_y, flip_x, a):
        y = 1 - self.y if flip_y else self.y
        x = 1 - self.x if flip_x else self.x
        return 4 * y + 2 * x + a


class Fetch:
    def __init__(self, shard, at, cuts=1, stage=0, layer=None):
        rows, cols = shard.shape[-2:]
        self.layer = layer
        self.at, self.cuts, self.stage, self.step_rows = at, cuts, stage, rows // cuts
        self.ins = [shard]
        self.outs = [jax.ShapeDtypeStruct((8, rows, cols), shard.dtype)]
        self.out_specs = [HBM]
        self.in_place = stage == 2
        self.semaphores()
        if not self.in_place:
            self.scratch.append(pltpu.VMEM((rows, cols), BF))

    def semaphores(self):
        self.scratch = [DMA((9 * self.cuts,)), DMA((8 * self.cuts,)), DMA((2,))]

    def bind(self, ins, outs, scratch):
        (self.own,), (self.out,) = ins, outs
        if self.layer is not None:
            self.own = self.own.at[self.layer]
        self.sent, self.come, self.sem = scratch[:3]
        self.bounce = scratch[3] if len(scratch) > 3 else None
        self.p = Place()

    def greets(self):
        return Place.PLANES if self.stage == 2 else Place.PLANES + Place.ENDS

    def part(self, ref, q):
        return ref.at[pl.ds(q * self.step_rows, self.step_rows)]

    def given(self, q):
        return self.part(self.own, q)

    def slot(self, piece, q):
        return self.part(self.out.at[piece], q)

    def home(self, a, q):
        return self.slot(self.p.piece(0, 0, a), q)

    def copy(self, src, dst, q, sent, come, where):
        return pltpu.make_async_remote_copy(
            src_ref=src, dst_ref=dst, send_sem=self.sent.at[9 * q + sent], recv_sem=self.come.at[8 * q + come],
            device_id=where, device_id_type=MESH,
        )

    def to_plane(self, q):
        p = self.p
        return self.copy(self.given(q), self.home(p.c, q), q, 0, p.c, p.over(p.zh))

    def to_partner(self, q):
        p = self.p
        return self.copy(self.given(q), self.home(p.c, q), q, 1, p.c, p.partner)

    def arrived(self, a, q):
        self.copy(self.given(q), self.home(a, q), q, 0, a, self.p.partner).wait_recv()

    def keep(self):
        slot = self.out.at[self.p.piece(0, 0, self.p.c)]
        return [
            pltpu.make_async_copy(self.own, self.bounce, self.sem.at[0]),
            pltpu.make_async_copy(self.bounce, slot, self.sem.at[1]),
        ]

    def kept(self):
        self.keep()[0].start()

    def land(self):
        copies = self.keep()
        for i, copy in enumerate(copies):
            if i:
                copy.start()
            copy.wait()

    def to_x(self, a, q, src=None):
        dst = self.slot(self.p.piece(0, 0, a), q)
        return self.copy(dst if src is None else src, dst, q, 2 + a, 2 + a, self.p.across_x)

    def to_y(self, a, q, src=None):
        dst = self.slot(self.p.piece(0, 0, a), q)
        return self.copy(dst if src is None else src, dst, q, 4 + a, 4 + a, self.p.across_y)

    def spread(self, a, q, src):
        self.to_x(a, q, src).start()
        self.to_y(a, q, src).start()

    def on_y(self, q):
        there = self.slot(self.p.piece(0, 1, 0), q)
        return self.copy(there, there, q, 6, 6, self.p.across_y)

    def on_x(self, q):
        there = self.slot(self.p.piece(1, 0, 1), q)
        return self.copy(there, there, q, 7, 7, self.p.across_x)

    def forward(self, q):
        self.to_x(0, q).wait_recv()
        self.on_y(q).start()
        self.to_y(1, q).wait_recv()
        self.on_x(q).start()

    def plain(self, run):
        pl.when(self.p.plain)(run)

    def other(self, run):
        pl.when(jnp.logical_not(self.p.plain))(run)

    def step(self, k):
        p, every = self.p, range(self.cuts)

        def own():
            for q in every:
                self.spread(p.c, q, self.given(q))

        def partner():
            for q in every:
                self.to_partner(q).start()

        def second():
            for q in every:
                self.arrived(1 - p.c, q)
                self.spread(1 - p.c, q, self.home(1 - p.c, q))

        def planes():
            for q in every:
                for a in (0, 1):
                    self.spread(a, q, self.home(a, q))

        def there(q):
            for a in (0, 1):
                self.arrived(a, q)
                self.spread(a, q, self.home(a, q))

        if self.stage == 2:
            if k == 0:
                self.other(planes)
            elif k == 1:
                self.other(lambda: [self.forward(q) for q in every] and None)
            elif k == END:
                self.other(self.close)
        elif k == 0:
            self.plain(self.kept)
            self.other(partner)
            self.plain(own)
            self.plain(second)
        elif k == END:
            for q in every:
                self.to_plane(q).wait_send()
            if self.stage:
                self.plain(self.close)
                self.other(lambda: [self.arrived(a, q) for q in every for a in (0, 1)] and None)
            else:
                self.close()
            self.plain(self.land)
            self.other(lambda: [self.to_partner(q).wait_send() for q in every] and None)
        elif k in (1, 2):
            self.leave(k == 1)
        elif k == 3:
            self.plain(lambda: [self.forward(q) for q in every] and None)
        elif not self.stage:
            q = k - 4
            if q < self.cuts:
                self.other(functools.partial(there, q))
            if q:
                self.other(lambda: self.forward(q - 1))

    def leave(self, outer):
        @pl.when(self.p.outer if outer else jnp.logical_not(self.p.outer))
        def _():
            for q in range(self.cuts):
                self.to_plane(q).start()

    def close(self):
        for q in range(self.cuts):
            self.to_x(1, q).wait_recv()
            self.to_y(0, q).wait_recv()
            self.on_y(q).wait()
            self.on_x(q).wait()
            for a in (0, 1):
                self.to_x(a, q).wait_send()
                self.to_y(a, q).wait_send()


class Take(Fetch):
    def __init__(self, whole, at, inside=False):
        rows, cols = whole.shape
        self.at, self.each, self.cuts, self.stage = at, rows // 8, 1, 0
        self.ins = [whole]
        self.outs = [] if inside else [jax.ShapeDtypeStruct((rows, cols), whole.dtype)]
        self.out_specs = [] if inside else [HBM]
        self.in_place = False
        self.semaphores()
        if not inside:
            self.scratch.append(pltpu.VMEM((rows, cols), BF))

    def bind(self, ins, outs, scratch):
        (self.own,) = ins
        self.whole = outs[0] if outs else None
        self.sent, self.come, self.sem = scratch[:3]
        self.bounce = scratch[3] if len(scratch) > 3 else None
        self.p = Place()

    def rows(self, piece):
        return pl.ds(pl.multiple_of(piece * self.each, 16), self.each)

    def given(self, q):
        return self.own.at[self.rows(self.p.piece(0, 0, self.p.c))]

    def slot(self, piece, q):
        return self.whole.at[self.rows(piece)]

    def keep(self):
        if self.bounce is None:
            return [pltpu.make_async_copy(self.own, self.whole, self.sem.at[0])]
        return [
            pltpu.make_async_copy(self.own, self.bounce, self.sem.at[0]),
            pltpu.make_async_copy(self.bounce, self.whole, self.sem.at[1]),
        ]

    def step(self, k):
        def there():
            for a in (0, 1):
                self.arrived(a, 0)
                self.spread(a, 0, self.home(a, 0))

        def last():
            self.close()

        if k == 0:
            self.plain(self.kept)
        elif k in (1, 2):
            self.leave(k == 1)
        elif k == 3:
            self.other(there)
        elif k == 4:
            self.other(lambda: self.forward(0))
        elif k == END:
            self.to_plane(0).wait_send()
            self.plain(self.land)
            self.other(last)


class Exchange:
    def __init__(self, src, dst, there, sems, sem, index=0):
        self.p = Place()
        self.src, self.dst, self.there, self.sems, self.sem, self.index = src, dst, there, sems, sem, index

    def stay(self):
        return pltpu.make_async_copy(self.src, self.dst, self.sem.at[self.index])

    def leave(self):
        return send(self.src, self.there, self.sems, self.index, self.p.swapped())

    def come(self):
        return send(self.src, self.dst, self.sems, self.index, self.p.swapped())

    def both(self, stay, leave):
        pl.when(self.p.plain)(stay)
        pl.when(jnp.logical_not(self.p.plain))(leave)

    def start(self):
        self.both(lambda: self.stay().start(), lambda: self.leave().start())

    def arrive(self):
        self.both(lambda: self.stay().wait(), lambda: self.come().wait_recv())

    def finish(self):
        pl.when(jnp.logical_not(self.p.plain))(lambda: self.leave().wait_send())


class Spread:
    def __init__(self, block, at, parts=2):
        rows, cols = block.shape
        self.at, self.parts = at, parts
        self.ins = [block]
        self.outs = [jax.ShapeDtypeStruct((rows, 4 * cols), block.dtype)]
        self.out_specs = [HBM]
        self.scratch = [*gather_scratch(parts), DMA((2, 1)), DMA((1,))]

    def bind(self, ins, outs, scratch):
        (self.block,), (self.full,) = ins, outs
        near, over, onward, sems, sem = scratch
        self.p, self.g = Place(), Group(calls=False)
        self.gather = Columns(self.g, self.full, near, over, onward)
        cols = self.block.shape[1]
        mine, there = (self.full.at[:, lanes(b * cols, cols)] for b in (self.g.mine, self.g.beside))
        self.exchange = Exchange(self.block, mine, there, sems, sem)

    def greets(self):
        return Place.ENDS

    def step(self, k):
        if k == 0:
            self.exchange.start()
        elif k == 1:
            self.exchange.arrive()
            self.gather.start()
        elif k == 2:
            for p in range(self.parts):
                self.gather.wait_part(p)
        elif k == END:
            self.gather.wait_beside()
            for p in range(self.parts):
                self.gather.wait_far(p)
            self.gather.finish()
            self.exchange.finish()


class Deliver:
    def __init__(self, block, at):
        rows, width = block.shape
        self.at = at
        self.ins = [block]
        self.outs = [jax.ShapeDtypeStruct((4 * rows, width // 4), BF)]
        self.out_specs = [HBM]
        self.scratch = [pltpu.VMEM((rows, width), BF), DMA((4,)), DMA((4,)), DMA((2,))]
        if block.dtype != BF:
            self.scratch.append(pltpu.VMEM((rows, width), block.dtype))

    def bind(self, ins, outs, scratch):
        (self.block,), (self.out,) = ins, outs
        self.low, self.sent, self.come, self.sem = scratch[:4]
        self.wide = scratch[4] if len(scratch) > 4 else self.low
        self.p, self.g = Place(), Group(calls=False)

    def greets(self):
        return Place.COLUMN

    def load(self):
        return pltpu.make_async_copy(self.block, self.wide, self.sem.at[0])

    def parts(self):
        rows, width = self.low.shape
        cols = width // 4
        dst = self.out.at[at_rows(self.g.mine, rows, 0, rows)]
        for f in range(4):
            half, z = divmod(f, 2)
            here = (self.p.c == self.p.zh) & (self.p.zh == half) & (self.g.z == z)
            src = self.low.at[:, pl.ds(f * cols, cols)]
            where = {"c": self.p.zh, "zh": jnp.int32(half), "zl": jnp.int32(z)}
            yield here, pltpu.make_async_copy(src, dst, self.sem.at[1]), pltpu.make_async_remote_copy(
                src_ref=src, dst_ref=dst, send_sem=self.sent.at[f], recv_sem=self.come.at[self.g.mine],
                device_id=where, device_id_type=MESH,
            )

    def step(self, k):
        if k == 0:
            self.load().start()
        elif k == 1:
            self.load().wait()
            if self.wide is not self.low:
                self.low[...] = self.wide[...].astype(BF)
            for here, stay, leave in self.parts():
                pl.when(here)(lambda stay=stay: stay.start())
                pl.when(jnp.logical_not(here))(lambda leave=leave: leave.start())
        elif k == END:
            rows, width = self.low.shape
            for here, stay, leave in self.parts():
                pl.when(here)(lambda stay=stay: stay.wait())
                pl.when(jnp.logical_not(here))(lambda leave=leave: leave.wait_send())
            for b in range(4):
                core, z = divmod(b, 2)
                here = (self.p.c == self.p.zh) & (self.p.c == core) & (self.g.z == z)
                come = pltpu.make_async_remote_copy(
                    src_ref=self.low.at[:, pl.ds(0, width // 4)], dst_ref=self.out.at[pl.ds(b * rows, rows)],
                    send_sem=self.sent.at[0], recv_sem=self.come.at[b], device_id=self.p.partner, device_id_type=MESH,
                )
                pl.when(jnp.logical_not(here))(lambda come=come: come.wait_recv())


class Total:
    def __init__(self, pieces, at, count, axes):
        self.at, self.count, self.axes = at, count, axes
        self.ins = pieces
        self.in_specs = [INV] * len(pieces)
        width = pieces[0].shape[1]
        self.outs = [jax.ShapeDtypeStruct((8, width), F32)]
        self.out_specs = [INV]
        self.scratch = [
            pltpu.VMEM((len(self.axes), 8, width), F32), pltpu.VMEM((len(self.axes), 8, width), F32),
            DMA((2, len(self.axes))),
        ]

    def bind(self, ins, outs, scratch):
        self.pieces, (self.out,) = ins, outs
        self.sum, self.other, self.sems = scratch
        self.p, self.g = Place(), Group(calls=False)

    def greets(self):
        return ("x",) + Place.ENDS + (("y",) if "r" in self.axes else ())

    def hop(self, i):
        axis = self.axes[i]
        return send(self.sum.at[i], self.other.at[i], self.sems, i, {axis: 1 - lax.axis_index(axis)})

    def step(self, k):
        if k == 0:
            gains, taps, heads = self.pieces[:4], self.pieces[4], self.pieces[5:]
            self.sum[0] = jnp.zeros(self.sum.shape[1:], F32)
            for i, gain in enumerate(gains):
                self.sum[0, pl.ds(i, 1), :] = gain[...]
            cols = taps.shape[1]
            self.sum[0, pl.ds(4, self.count), lanes(self.g.mine * cols, cols)] = taps[pl.ds(0, self.count), :]
            done = 0
            for head in heads:
                self.sum[0, pl.ds(7, 1), pl.ds(done, head.shape[1])] = head[...]
                done += head.shape[1]
            self.hop(0).start()
        else:
            k = min(k, 4)
            last = len(self.axes) if k == 4 else k
            for i in range(k - 1, last):
                self.hop(i).wait()
                value = self.sum[i] + self.other[i]
                if i + 1 < len(self.axes):
                    self.sum[i + 1] = value
                    self.hop(i + 1).start()
                else:
                    self.out[...] = value


class Reduce:
    def __init__(self, grad, first, rows, at, last=True):
        self.first, self.rows, self.at, self.last = first, rows, at, last
        cols = grad.shape[2]
        self.ins = [grad]
        self.outs = [shaped((rows, cols), F32) if last else shaped((2, rows, cols), BF)]
        self.out_specs = [INV]
        self.scratch = [
            pltpu.VMEM((4, rows, cols), BF), pltpu.VMEM((4, rows, cols), BF), pltpu.VMEM((2, rows, cols), BF),
            DMA((9,)), DMA((8,)), DMA((4,)),
        ]
        if last:
            self.scratch.append(pltpu.VMEM((2, rows, cols), BF))

    def bind(self, ins, outs, scratch):
        (self.grad,), (self.out,) = ins, outs
        self.held, self.in1, self.in2, self.sent, self.come, self.sem = scratch[:6]
        self.in3 = scratch[6] if self.last else None
        self.p = Place()

    def greets(self):
        return Place.PLANES + (Place.ENDS if self.last else ())

    def fin(self, a):
        return self.held.at[2 * a]

    def piece(self, flip_y, flip_x, a):
        return self.grad.at[self.p.piece(flip_y, flip_x, a), pl.ds(self.first, self.rows)]

    def copy(self, src, dst, sent, come, where):
        return pltpu.make_async_remote_copy(
            src_ref=src, dst_ref=dst, send_sem=self.sent.at[sent], recv_sem=self.come.at[come],
            device_id=where, device_id_type=MESH,
        )

    def loads(self):
        kept = [(0, 0, 0), (0, 1, 0), (0, 0, 1), (1, 0, 1)]
        return [pltpu.make_async_copy(self.piece(*k), self.held.at[i], self.sem.at[i]) for i, k in enumerate(kept)]

    def first_hops(self):
        p = self.p
        return [
            self.copy(self.piece(1, 0, 0), self.in1.at[0], 0, 0, p.across_y),
            self.copy(self.piece(1, 1, 0), self.in1.at[1], 1, 1, p.across_y),
            self.copy(self.piece(0, 1, 1), self.in1.at[2], 2, 2, p.across_x),
            self.copy(self.piece(1, 1, 1), self.in1.at[3], 3, 3, p.across_x),
        ]

    def second_hops(self):
        return [
            self.copy(self.held.at[1], self.in2.at[0], 4, 4, self.p.across_x),
            self.copy(self.held.at[3], self.in2.at[1], 5, 5, self.p.across_y),
        ]

    def to_owner(self, a):
        return self.copy(self.fin(a), self.in3.at[0], 6 + a, 6, self.p.over(a))

    def to_partner(self):
        return self.copy(self.fin(1 - self.p.c), self.in3.at[1], 8, 7, self.p.partner)

    def add(self, i, other):
        self.held[i] = (self.held[i].astype(F32) + other.astype(F32)).astype(BF)

    def step(self, k):
        p = self.p
        if k == 0:
            for hop in [self.first_hops()[i] for i in (1, 3, 0, 2)]:
                hop.start()
            for load in self.loads():
                load.start()
        elif k == 1:
            for load in self.loads():
                load.wait()
            hops, after = self.first_hops(), self.second_hops()
            for i in (1, 3):
                hops[i].wait_recv()
                self.add(i, self.in1[i])
                after[i // 2].start()
            for i in (0, 2):
                hops[i].wait_recv()
                self.add(i, self.in1[i])
        elif k == 2:
            for i, hop in enumerate(self.second_hops()):
                hop.wait_recv()
                if self.last:
                    self.add(2 * i, self.in2[i])
                else:
                    self.out[i] = (self.held[2 * i].astype(F32) + self.in2[i].astype(F32)).astype(BF)
            if self.last:
                self.settle()
                self.settle(False)
        elif k == END:
            if self.last:
                self.close()
            for hop in self.first_hops() + self.second_hops():
                hop.wait_send()

    def settle(self, outer=True):
        if outer:

            @pl.when(self.p.plain)
            def _():
                self.to_partner().start()

        now = self.p.outer if outer else jnp.logical_not(self.p.outer)

        @pl.when(now & jnp.logical_not(self.p.plain))
        def _():
            self.to_owner(0).start()
            self.to_owner(1).start()

    def close(self):
        p = self.p
        self.to_owner(0).wait_recv()

        @pl.when(p.plain)
        def _():
            self.out[...] = self.own(p.c).astype(F32) + self.in3[0].astype(F32)
            self.to_partner().wait_send()

        @pl.when(jnp.logical_not(p.plain))
        def _():
            self.to_partner().wait_recv()
            self.out[...] = self.in3[1].astype(F32) + self.in3[0].astype(F32)
            self.to_owner(0).wait_send()
            self.to_owner(1).wait_send()

    def own(self, a):
        return self.held[2 * a]


class Settle(Reduce):
    def __init__(self, sums, at):
        _, rows, cols = sums.shape
        self.at = at
        self.ins = [sums]
        self.outs = [shaped((rows, cols), F32)]
        self.out_specs = [INV]
        self.scratch = [pltpu.VMEM((rows, cols), BF), pltpu.VMEM((2, rows, cols), BF), DMA((9,)), DMA((8,)), DMA((1,))]

    def bind(self, ins, outs, scratch):
        (self.sums,), (self.out,) = ins, outs
        self.kept, self.in3, self.sent, self.come, self.sem = scratch
        self.p = Place()

    def greets(self):
        return Place.ENDS

    def fin(self, a):
        return self.sums.at[a]

    def own(self, a):
        return self.kept[...]

    def load(self):
        return pltpu.make_async_copy(self.sums.at[self.p.c], self.kept, self.sem.at[0])

    def step(self, k):
        if k == 0:
            self.load().start()
            self.settle()
        elif k == 1:
            self.settle(False)
        elif k == END:
            self.load().wait()
            self.close()


class Background:
    def __init__(self, tasks, greets):
        self.tasks, self.done, names = tasks, [], list(greets)
        for task in tasks:
            names += [name for name in task.greets() if name not in names]
        place = Place()
        self.others = [place.called(name) for name in names]

    def step(self, k):
        for i in range(max([len(task.at) for task in self.tasks], default=0)):
            for task in self.tasks:
                if i < len(task.at) and task.at[i] == k:
                    task.step(i)

    def finish(self, tasks=None):
        for task in self.tasks if tasks is None else tasks:
            if task not in self.done:
                task.step(END)
                self.done.append(task)


def hosted(kernel, ident, name, ins, in_specs, outs, out_specs, scratch, tasks, flops, traffic, greets=()):
    groups = ([], [], [])
    for group, own in zip(groups, (ins, outs, scratch)):
        group.append(len(own))
    ins, in_specs, outs, out_specs, scratch = list(ins), list(in_specs), list(outs), list(out_specs), list(scratch)
    for task in tasks:
        for group, more in zip(groups, (task.ins, task.outs, task.scratch)):
            group.append(len(more))
        ins += task.ins
        in_specs += getattr(task, "in_specs", [HBM] * len(task.ins))
        outs += task.outs
        out_specs += task.out_specs
        scratch += task.scratch

    def split(refs, counts):
        at, found = 0, []
        for count in counts:
            found.append(refs[at : at + count])
            at += count
        return found

    def body(*refs):
        parts = [split(part, group) for part, group in zip(split(refs, [sum(g) for g in groups]), groups)]
        for task, *mine in zip(tasks, *(part[1:] for part in parts)):
            task.bind(*mine)
        kernel(*parts[0][0], *parts[1][0], *parts[2][0], Background(tasks, greets))

    aliases, at_in, at_out = {}, groups[0][0], groups[1][0]
    for task in tasks:
        if getattr(task, "in_place", False):
            aliases[at_in] = at_out
        at_in += len(task.ins)
        at_out += len(task.outs)
    results = pl.pallas_call(
        body,
        out_shape=tuple(outs),
        in_specs=in_specs,
        out_specs=tuple(out_specs),
        scratch_shapes=scratch,
        input_output_aliases=aliases,
        compiler_params=params(ident),
        cost_estimate=pl.CostEstimate(flops=flops, bytes_accessed=traffic, transcendentals=0),
        name=name,
    )(*ins)
    results = split(list(results), groups[1])
    return results[0], [r[0] for r in results[1:] if r]


def put_rows(scratch, first, value, cols=slice(None)):
    tall = scratch.shape[1]
    done = 0
    while done < value.shape[0]:
        piece, at = divmod(first + done, tall)
        count = min(tall - at, value.shape[0] - done)
        scratch[piece, pl.ds(at, count), cols] = value[done : done + count]
        done += count


def put_columns(scratch, first, value):
    wide_piece = scratch.shape[2]
    for piece in range(scratch.shape[0]):
        scratch[piece, pl.ds(first, value.shape[0]), :] = value[:, piece * wide_piece : (piece + 1) * wide_piece]


def column_loads(pieces, whole):
    each = pieces.shape[2]
    return [(pieces.at[i], whole.at[:, pl.ds(i * each, each)]) for i in range(pieces.shape[0])]


def ffn_forward_kernel(
    h_ref, gain_ref, w_hbm, v_hbm, out_ref, n_hbm, u_hbm,
    w, v, nf, u, act, tpart, mine, n_near, n_over, n_on, o_near, i_near, o_over, i_over, s_near, s_over,
    wsem, osem, bg,
):
    g = Group(bg.others)
    g.greet()
    size, width = h_ref.shape
    hidden = v.shape[0]
    loads = start_all([(w_hbm, w)] + column_loads(v_hbm, v), wsem)
    gather = Gather(g, nf, size, n_near, n_over, n_on)
    scatter = Scatter(g, o_near, i_near, o_over, i_over, s_near, s_over, size)
    parts, step = gather.parts, gather.step
    for p in range(parts):
        nf[at_rows(g.mine, size, p * step, step), :] = normalise(
            h_ref[pl.ds(p * step, step), :], gain_ref[...]
        ).astype(BF)
    g.meet()
    gather.start()
    bg.step(0)
    wait_all(loads)

    third = hidden // 3

    def rows_of(places):
        return jnp.concatenate([nf[r, :] for r, _ in places], axis=0) if len(places) > 1 else nf[places[0][0], :]

    def up(places):
        def body(t, carry):
            x = rows_of(places)
            cols, more = lanes(t * third, third), lanes(hidden + t * third, third)
            both = mm(x, jnp.concatenate([w[:, cols], w[:, more]], axis=1))
            gate, upper = both[:, :third], both[:, third:]
            a = gate * jax.nn.sigmoid(gate) * upper
            act[:, cols] = a.astype(BF)
            at = 0
            for r, count in places:
                u[r, cols] = gate[at : at + count].astype(BF)
                u[r, more] = upper[at : at + count].astype(BF)
                at += count
            return carry

        lax.fori_loop(0, 3, body, 0)

    def down(store):
        store(slice(None), mm(act[...], v[...]))

    def keep(index, r, count):
        return pltpu.make_async_copy(u.at[r], u_hbm.at[r], osem.at[index])

    whole = lambda block: at_rows(block, size, 0, size)
    up([(whole(g.mine), size)])
    keep(0, whole(g.mine), size).start()

    def put_mine(cols, value):
        mine[:, cols] = value

    down(put_mine)
    gather.wait_beside()
    up([(whole(g.beside), size)])
    keep(1, whole(g.beside), size).start()

    def put_beside(cols, value):
        o_near[1, :, cols] = value.astype(BF)

    down(put_beside)
    for p in range(parts):
        scatter.close(1, p).start()
    bg.step(1)
    for p in range(parts):
        gather.wait_part(p)
        gather.wait_far(p)
        r_across, r_far = at_rows(g.across, size, p * step, step), at_rows(g.far, size, p * step, step)
        up([(r_across, step), (r_far, step)])
        keep(2 + 2 * p, r_across, step).start()
        keep(3 + 2 * p, r_far, step).start()
        here = scatter.rows(p)

        def put(cols, value):
            tpart[:, cols] = value[:step]
            o_near[0, here, cols] = value[step:].astype(BF)

        down(put)
        scatter.close(0, p).start()
        scatter.close(0, p).wait_recv()
        o_over[here, :] = (tpart[...] + i_near[0, here, :].astype(F32)).astype(BF)
        scatter.link(p).start()
        bg.step(10 + p)
    n_out = pltpu.make_async_copy(nf, n_hbm, osem.at[2 + 2 * parts])
    n_out.start()
    bg.step(2)
    for p in range(parts):
        here = scatter.rows(p)
        scatter.close(1, p).wait_recv()
        scatter.link(p).wait_recv()
        out_ref[here, :] = (
            h_ref[here, :] + mine[here, :] + i_near[1, here, :].astype(F32) + i_over[here, :].astype(F32)
        )
    gather.finish()
    scatter.wait_all_sends()
    keep(0, whole(g.mine), size).wait()
    keep(1, whole(g.beside), size).wait()
    for p in range(parts):
        keep(2 + 2 * p, at_rows(g.across, size, p * step, step), step).wait()
        keep(3 + 2 * p, at_rows(g.far, size, p * step, step), step).wait()
    n_out.wait()
    bg.step(6)
    bg.finish()


def ffn_forward(h, gain, w, v, ident, tasks=(), parts=PARTS):
    size, width = h.shape
    hidden = v.shape[1]
    total = 4 * size
    return hosted(
        ffn_forward_kernel, ident, "ffn_forward", [h, gain, w, v], [INV, INV, HBM, HBM],
        [shaped((size, width), F32), shaped((total, width), BF), shaped((total, 2 * hidden), BF)], [INV, HBM, HBM],
        [
            pltpu.VMEM((width, 2 * hidden), BF), pltpu.VMEM((hidden, width), BF), pltpu.VMEM((total, width), BF),
            pltpu.VMEM((total, 2 * hidden), BF), pltpu.VMEM((size, hidden), BF),
            pltpu.VMEM((size // parts, width), F32), pltpu.VMEM((size, width), F32),
            *gather_scratch(parts), *scatter_scratch(size, width, parts), DMA((1 + v.shape[0],)), DMA((3 + 2 * parts,)),
        ],
        tasks, 6 * total * width * hidden, 2**24,
    )


def mm_tn(a, b):
    return lax.dot_general(a, b, (((0,), (0,)), ((), ())), preferred_element_type=F32)


def rms_back(dn, h, gain):
    inverse = lax.rsqrt(jnp.mean(h * h, axis=-1, keepdims=True) + epsilon)
    scaled = dn * gain
    inner = jnp.mean(scaled * h, axis=-1, keepdims=True)
    grad_gain = jnp.sum(dn * h * inverse, axis=0, keepdims=True)
    return inverse * scaled - h * (inverse * inverse * inverse * inner), grad_gain


def close_scatter(scatter, mine, dh_ref, h_ref, gain_ref, out_ref, gg_ref):
    gg_ref[...] = jnp.zeros_like(gg_ref)
    for p in range(scatter.parts):
        here = scatter.rows(p)
        scatter.close(1, p).wait_recv()
        scatter.link(p).wait_recv()
        dn = mine[here, :] + scatter.in_near[1, here, :].astype(F32) + scatter.in_over[here, :].astype(F32)
        term, grad_gain = rms_back(dn, h_ref[here, :], gain_ref[...])
        out_ref[here, :] = dh_ref[here, :].astype(F32) + term
        gg_ref[...] += grad_gain


def ffn_backward_kernel(
    known, dh_ref, h_ref, gain_ref, df_hbm, w_hbm, v_hbm, n_hbm, u_hbm, out_ref, gg_ref, gw_hbm, gv_hbm,
    w, v, nf, u, act, df, tpart, mine, gw, gv, n_near, n_over, n_on, o_near, i_near, o_over, i_over, s_near, s_over,
    wsem, osem, bg,
):
    g = Group(bg.others)
    g.greet()
    size, width = h_ref.shape
    hidden = v.shape[0]
    loads = column_loads(v_hbm, v) + [(u_hbm, u), (w_hbm, w), (n_hbm, nf)]
    loads = start_all(loads + [(df_hbm, df)] if known else loads, wsem)
    gather = Gather(g, df, size, n_near, n_over, n_on)
    scatter = Scatter(g, o_near, i_near, o_over, i_over, s_near, s_over, size)
    parts, step = gather.parts, gather.step
    if not known:
        df[at_rows(g.mine, size, 0, size), :] = dh_ref[...].astype(BF)
    g.meet()
    if not known:
        gather.start()
    bg.step(0)
    wait_all(loads)

    third = hidden // 3

    def cat(ref, places, cols):
        found = [ref[r, cols] for r, _ in places]
        return found[0] if len(found) == 1 else jnp.concatenate(found, axis=0)

    def first(places):
        def body(t, carry):
            cols, more = lanes(t * third, third), lanes(hidden + t * third, third)
            da = mm_nt(cat(df, places, slice(None)), v[cols, :])
            gate, upper = cat(u, places, cols).astype(F32), cat(u, places, more).astype(F32)
            s = jax.nn.sigmoid(gate)
            lit = gate * s
            dgate = (da * upper * s * (1.0 + gate * (1.0 - s))).astype(BF)
            dupper = (da * lit).astype(BF)
            a = (lit * upper).astype(BF)
            at = 0
            for r, count in places:
                u[r, cols] = dgate[at : at + count]
                u[r, more] = dupper[at : at + count]
                act[r, cols] = a[at : at + count]
                at += count
            return carry

        lax.fori_loop(0, 3, body, 0)

    def second(places, store):
        def body(t, carry):
            cols = lanes(t * 512, 512)
            store(cols, mm_nt(cat(u, places, slice(None)), w[cols, :]))
            return carry

        lax.fori_loop(0, width // 512, body, 0)

    whole = lambda block: [(at_rows(block, size, 0, size), size)]

    def put_mine(cols, value):
        mine[:, cols] = value

    def put_beside(cols, value):
        o_near[1, :, cols] = value.astype(BF)

    def own():
        first(whole(g.mine))
        second(whole(g.mine), put_mine)

    def beside():
        first(whole(g.beside))
        second(whole(g.beside), put_beside)
        for p in range(parts):
            scatter.close(1, p).start()

    if not known:
        own()
        gather.wait_beside()
        beside()
    bg.step(1)
    for p in range(parts):
        if not known:
            gather.wait_part(p)
            gather.wait_far(p)
        pair = [(at_rows(b, size, p * step, step), step) for b in (g.across, g.far)]
        first(pair)
        here = scatter.rows(p)

        def put(cols, value):
            tpart[:, cols] = value[:step]
            o_near[0, here, cols] = value[step:].astype(BF)

        second(pair, put)
        scatter.close(0, p).start()
        scatter.close(0, p).wait_recv()
        o_over[here, :] = (tpart[...] + i_near[0, here, :].astype(F32)).astype(BF)
        scatter.link(p).start()
    bg.step(2)
    if known:
        beside()
        own()
    for t in range(3):
        put_columns(gv, t * third, mm_tn(act[:, t * third : (t + 1) * third], df[...]).astype(BF))
    save = pltpu.make_async_copy(gv, gv_hbm, osem.at[2])
    save.start()
    bg.step(3)
    for t in range(width // 512):
        for k in range(2):
            cols = slice(k * hidden, (k + 1) * hidden)
            put_rows(gw, t * 512, mm_tn(nf[:, t * 512 : (t + 1) * 512], u[:, cols]).astype(BF), cols)
    more = pltpu.make_async_copy(gw, gw_hbm, osem.at[0])
    more.start()
    bg.step(4)
    close_scatter(scatter, mine, df.at[at_rows(g.mine, size, 0, size)] if known else dh_ref, h_ref, gain_ref, out_ref, gg_ref)
    if not known:
        gather.finish()
    scatter.wait_all_sends()
    more.wait()
    save.wait()
    bg.step(6)
    bg.finish()


def ffn_backward(dh, h, gain, df, w, v, n, u, ident, tasks=(), parts=PARTS):
    size, width = h.shape
    pieces, hidden = v.shape[:2]
    total = 4 * size
    known = df is not None
    if known:
        dh = gain
    else:
        df = n
    return hosted(
        functools.partial(ffn_backward_kernel, known), ident, "ffn_backward", [dh, h, gain, df, w, v, n, u],
        [INV, INV, INV] + [HBM] * 5,
        [
            shaped((size, width), F32), shaped((1, width), F32), shaped((pieces, width // pieces, 2 * hidden), BF),
            shaped((pieces, hidden, width // pieces), BF),
        ],
        [INV, INV, HBM, HBM],
        [
            pltpu.VMEM((width, 2 * hidden), BF), pltpu.VMEM((hidden, width), BF), pltpu.VMEM((total, width), BF),
            pltpu.VMEM((total, 2 * hidden), BF), pltpu.VMEM((total, hidden), BF), pltpu.VMEM((total, width), BF),
            pltpu.VMEM((size // parts, width), F32), pltpu.VMEM((size, width), F32),
            pltpu.VMEM((pieces, width // pieces, 2 * hidden), BF), pltpu.VMEM((pieces, hidden, width // pieces), BF),
            *gather_scratch(parts), *scatter_scratch(size, width, parts), DMA((4 + pieces,)), DMA((3,)),
        ],
        tasks, 12 * total * width * hidden, 2**25,
    )


MOST_DOC = 512


class Columns(Gather):
    def __init__(self, group, full, near, over, onward):
        super().__init__(group, full, full.shape[0], near, over, onward)
        self.cols = full.shape[1] // 4

    def view(self, block, part):
        return self.full.at[pl.ds(part * self.step, self.step), lanes(block * self.cols, self.cols)]


def cat_rows(ref, places, cols=slice(None)):
    found = [ref[r, cols] for r, _ in places]
    return found[0] if len(found) == 1 else jnp.concatenate(found, axis=0)


def product(src, weight, turned, tile=1024):
    def run(places, store):
        width = weight.shape[0] if turned else weight.shape[1]

        def body(t, carry):
            cols = lanes(t * tile, tile)
            x = cat_rows(src, places)
            store(cols, mm_nt(x, weight[cols, :]) if turned else mm(x, weight[:, cols]))
            return carry

        lax.fori_loop(0, width // tile, body, 0)

    return run


def scatter_all(g, scatter, run, mine, tpart):
    size, step = scatter.size, scatter.step
    for p in range(scatter.parts):
        here = scatter.rows(p)

        def put(cols, value):
            tpart[:, cols] = value[:step]
            scatter.out_near[0, here, cols] = value[step:].astype(BF)

        run([(at_rows(b, size, p * step, step), step) for b in (g.across, g.far)], put)
        scatter.close(0, p).start()
        scatter.close(0, p).wait_recv()
        scatter.out_over[here, :] = (tpart[...] + scatter.in_near[0, here, :].astype(F32)).astype(BF)
        scatter.link(p).start()

    def put_beside(cols, value):
        scatter.out_near[1, :, cols] = value.astype(BF)

    run([(at_rows(g.beside, size, 0, size), size)], put_beside)
    for p in range(scatter.parts):
        scatter.close(1, p).start()

    def put_mine(cols, value):
        mine[:, cols] = value

    run([(at_rows(g.mine, size, 0, size), size)], put_mine)


def gather_everything(gather):
    gather.wait_beside()
    for p in range(gather.parts):
        gather.wait_part(p)
    for p in range(gather.parts):
        gather.wait_far(p)


def doc_starts(docs, lengths, places):
    row = lengths[pl.ds(0, 1), :]
    end = jnp.zeros((1, 1), F32)
    start = jnp.zeros_like(places)
    for d in range(docs):
        end = end + row[:, d : d + 1]
        start = jnp.where(places >= end.astype(jnp.int32), end.astype(jnp.int32), start)
    return start


def conv_taps(gated, within, taps):
    total = gated.shape[0]
    summed = taps[0] * gated
    for j in range(1, len(taps)):
        summed = summed + taps[j] * jnp.where(within >= j, pltpu.roll(gated, j, 0), 0.0)
    return summed


def conv_forward_kernel(
    docs, count, inside, lens_ref, x_hbm, gain_ref, taps_ref, win_hbm, wout_hbm,
    out_ref, block_ref, n_hbm, p_hbm, lengths, taps_out, win_out, wout_out,
    win, wout, full, nf, proj, low, mixed, tpart, mine, n_near, n_over, n_on, o_near, i_near, o_over, i_over,
    s_near, s_over, wsem, osem, xsem, xlocal, bg,
):
    g = Group(bg.others)
    g.greet()
    size, width = out_ref.shape
    total, chans = x_hbm.shape[0], wout.shape[0]
    loads = []
    if inside:
        bg.tasks[0].whole, bg.tasks[1].whole = win, wout
    else:
        loads = start_all([(win_hbm, win), (wout_hbm, wout)], wsem)
    gather = Columns(g, full, n_near, n_over, n_on)
    scatter = Scatter(g, o_near, i_near, o_over, i_over, s_near, s_over, size)
    parts = gather.parts
    blocks = [
        Exchange(
            x_hbm.at[pl.ds(p * gather.step, gather.step)],
            *(full.at[pl.ds(p * gather.step, gather.step), lanes(b * chans, chans)] for b in (g.mine, g.beside)),
            xsem, xlocal, p,
        )
        for p in range(parts)
    ]
    small = [Exchange(lens_ref, lengths, lengths, xsem, xlocal, parts), Exchange(taps_ref, taps_out, taps_out, xsem, xlocal, parts + 1)]
    g.meet()
    for block in blocks + small:
        block.start()
    bg.step(0)
    for p in range(parts):
        blocks[p].arrive()
        gather.link(p, g.mine).start()
        gather.close(p, g.mine).start()
    bg.step(1)
    gather.wait_beside()
    for p in range(parts):
        gather.wait_part(p)
    for p in range(parts):
        gather.wait_far(p)
    for block in small:
        block.arrive()
    bg.step(2)
    if inside:
        bg.finish(bg.tasks[:2])
    wait_all(loads)

    def project(t, carry):
        rows = at_rows(t, size, 0, size)
        n = normalise(full[rows, :].astype(F32), gain_ref[...]).astype(BF)
        nf[rows, :] = n
        p = mm(n, win[...])
        proj[rows, :] = p
        low[rows, :] = p.astype(BF)
        return carry

    lax.fori_loop(0, total // size, project, 0)
    bg.step(4)
    saves = start_all([(nf, n_hbm), (low, p_hbm), (win, win_out), (wout, wout_out)], osem)
    places = lax.broadcasted_iota(jnp.int32, (total, LANES), 0)
    within = places - doc_starts(docs, lengths, places)
    for k in range(chans // LANES):
        b, c, x = (proj[:, pl.ds(i * chans + k * LANES, LANES)] for i in range(3))
        taps = [taps_out[pl.ds(j, 1), pl.ds(k * LANES, LANES)] for j in range(count)]
        mixed[:, pl.ds(k * LANES, LANES)] = (c * conv_taps(b * x, within, taps)).astype(BF)
    bg.step(5)
    scatter_all(g, scatter, product(mixed, wout, False), mine, tpart)
    bg.step(3)
    block_ref[...] = full[at_rows(g.mine, size, 0, size), :]
    for p in range(scatter.parts):
        here = scatter.rows(p)
        scatter.close(1, p).wait_recv()
        scatter.link(p).wait_recv()
        out_ref[here, :] = (
            block_ref[here, :].astype(F32) + mine[here, :] + i_near[1, here, :].astype(F32) + i_over[here, :].astype(F32)
        )
    for block in blocks + small:
        block.finish()
    gather.finish()
    scatter.wait_all_sends()
    wait_all(saves)
    bg.step(6)
    bg.finish()


def conv_forward(docs, count, lens, x, gain, taps, win, wout, inside, ident, tasks=(), parts=PARTS, cuts=4):
    total, chans = x.shape
    width = wout.shape[1]
    size = total // 4
    return hosted(
        functools.partial(conv_forward_kernel, docs, count, inside), ident, "conv_forward",
        [lens, x, gain, taps, win, wout], [INV, HBM, INV, INV, HBM, HBM],
        [
            shaped((size, width), F32), shaped((size, width), BF), shaped((total, width), BF), shaped((total, 3 * chans), BF),
            shaped(lens.shape, F32), shaped(taps.shape, F32), shaped(win.shape, BF), shaped(wout.shape, BF),
        ],
        [INV, INV, HBM, HBM, INV, INV, HBM, HBM],
        [
            pltpu.VMEM((width, 3 * chans), BF), pltpu.VMEM((chans, width), BF), pltpu.VMEM((total, width), BF),
            pltpu.VMEM((total, width), BF), pltpu.VMEM((total, 3 * chans), F32), pltpu.VMEM((total, 3 * chans), BF),
            pltpu.VMEM((total, chans), BF), pltpu.VMEM((size // parts, width), F32), pltpu.VMEM((size, width), F32),
            *gather_scratch(cuts), *scatter_scratch(size, width, parts), DMA((2,)), DMA((4,)),
            DMA((2, cuts + 2)), DMA((cuts + 2,)),
        ],
        tasks, 8 * total * width * chans, 2**24, ("swap",),
    )


def conv_backward_kernel(
    docs, count, lengths, dh_ref, h_ref, gain_ref, taps_ref, win_hbm, wout_hbm, n_hbm, p_hbm, out_ref, gg_ref, gt_ref, gin_hbm, gout_hbm,
    win, wout, nf, low, dz, dy, mixed, dproj, gin, gout, tpart, mine, n_near, n_over, n_on, o_near, i_near, o_over, i_over,
    s_near, s_over, wsem, osem, bg,
):
    g = Group(bg.others)
    g.greet()
    size, width = dh_ref.shape
    total, chans = 4 * size, wout.shape[0]
    loads = start_all([(wout_hbm, wout), (p_hbm, low), (win_hbm, win), (n_hbm, nf)], wsem)
    gather = Gather(g, dz, size, n_near, n_over, n_on)
    scatter = Scatter(g, o_near, i_near, o_over, i_over, s_near, s_over, size)
    dz[at_rows(g.mine, size, 0, size), :] = dh_ref[...].astype(BF)
    g.meet()
    gather.start()
    bg.step(0)
    wait_all(loads)
    places = lax.broadcasted_iota(jnp.int32, (total, LANES), 0)
    within = places - doc_starts(docs, lengths, places)
    gather_everything(gather)
    bg.step(1)

    def project(t, carry):
        rows = at_rows(t, size, 0, size)
        dy[rows, :] = mm_nt(dz[rows, :], wout[...])
        return carry

    lax.fori_loop(0, total // size, project, 0)
    for k in range(chans // LANES):
        b, c, x = (low[:, pl.ds(i * chans + k * LANES, LANES)].astype(F32) for i in range(3))
        here = pl.ds(k * LANES, LANES)
        taps = [taps_ref[pl.ds(j, 1), here] for j in range(count)]
        gated = b * x
        summed = conv_taps(gated, within, taps)
        d = dy[:, here]
        mixed[:, here] = (c * summed).astype(BF)
        ds = d * c
        dg = taps[0] * ds
        gt_ref[pl.ds(0, 1), here] = jnp.sum(ds * gated, axis=0, keepdims=True)
        for j in range(1, len(taps)):
            masked = jnp.where(within >= j, ds, 0.0)
            dg = dg + taps[j] * pltpu.roll(masked, total - j, 0)
            gt_ref[pl.ds(j, 1), here] = jnp.sum(masked * pltpu.roll(gated, j, 0), axis=0, keepdims=True)
        dproj[:, pl.ds(k * LANES, LANES)] = (dg * x).astype(BF)
        dproj[:, pl.ds(chans + k * LANES, LANES)] = (d * summed).astype(BF)
        dproj[:, pl.ds(2 * chans + k * LANES, LANES)] = (dg * b).astype(BF)
    bg.step(2)
    scatter_all(g, scatter, product(dproj, win, True), mine, tpart)
    bg.step(3)
    put_columns(gout, 0, mm_tn(mixed[...], dz[...]).astype(BF))
    save = pltpu.make_async_copy(gout, gout_hbm, osem.at[0])
    save.start()
    for t in range(width // 256):
        put_rows(gin, t * 256, mm_tn(nf[:, pl.ds(t * 256, 256)], dproj[...]).astype(BF))
    more = pltpu.make_async_copy(gin, gin_hbm, osem.at[1])
    more.start()
    bg.step(4)
    close_scatter(scatter, mine, dh_ref, h_ref, gain_ref, out_ref, gg_ref)
    gather.finish()
    scatter.wait_all_sends()
    save.wait()
    more.wait()
    bg.step(5)
    bg.step(6)
    bg.finish()


def conv_backward(docs, count, lengths, dh, h, gain, taps, win, wout, n, p, pieces, ident, tasks=(), parts=PARTS):
    size, width = dh.shape
    total, chans = 4 * size, wout.shape[0]
    each = width // pieces
    return hosted(
        functools.partial(conv_backward_kernel, docs, count), ident, "conv_backward",
        [lengths, dh, h, gain, taps, win, wout, n, p],
        [INV, INV, INV, INV, INV, HBM, HBM, HBM, HBM],
        [
            shaped((size, width), F32), shaped((1, width), F32), shaped(taps.shape, F32),
            shaped((pieces, each, 3 * chans), BF), shaped((pieces, chans, each), BF),
        ],
        [INV, INV, INV, HBM, HBM],
        [
            pltpu.VMEM((width, 3 * chans), BF), pltpu.VMEM((chans, width), BF), pltpu.VMEM((total, width), BF),
            pltpu.VMEM((total, 3 * chans), BF), pltpu.VMEM((total, width), BF), pltpu.VMEM((total, chans), F32),
            pltpu.VMEM((total, chans), BF), pltpu.VMEM((total, 3 * chans), BF), pltpu.VMEM((pieces, each, 3 * chans), BF),
            pltpu.VMEM((pieces, chans, each), BF), pltpu.VMEM((size // parts, width), F32), pltpu.VMEM((size, width), F32),
            *gather_scratch(parts), *scatter_scratch(size, width, parts), DMA((4,)), DMA((2,)),
        ],
        tasks, 16 * total * width * chans, 2**24,
    )


def head_sums(values, head):
    width = values.shape[1]
    a = lax.broadcasted_iota(jnp.int32, (width, width), 0) // head
    b = lax.broadcasted_iota(jnp.int32, (width, width), 1) // head
    same = jnp.where(a == b, 1.0, 0.0).astype(BF)
    high = values.astype(BF)
    low = (values - high.astype(F32)).astype(BF)
    return mm(high, same) + mm(low, same)


def turn(values, head):
    width = values.shape[1]
    lane = lax.broadcasted_iota(jnp.int32, values.shape, 1)
    return jnp.where(
        lane % head < head // 2, pltpu.roll(values, width - head // 2, 1), pltpu.roll(values, head // 2, 1)
    )


def wide(table, width):
    return jnp.concatenate([table] * (width // table.shape[1]), axis=1)


def norm_turn(raw, gain, cosine, sine, head):
    inverse = lax.rsqrt(head_sums(raw * raw, head) * (1.0 / head) + epsilon)
    v = raw * inverse * gain
    return v * wide(cosine, raw.shape[1]) + turn(v, head) * wide(sine, raw.shape[1])


def norm_turn_back(d, raw, gain, cosine, sine, head):
    d = d * wide(cosine, raw.shape[1]) - turn(d, head) * wide(sine, raw.shape[1])
    inverse = lax.rsqrt(head_sums(raw * raw, head) * (1.0 / head) + epsilon)
    scaled = d * gain
    inner = head_sums(scaled * raw, head) * (1.0 / head)
    grad_gain = jnp.sum(d * raw * inverse, axis=0, keepdims=True)
    return inverse * scaled - raw * (inverse * inverse * inverse * inner), grad_gain


def score_tile(q, k, starts, first_key, first_query, scale):
    raw = mm_nt(k, q) * scale
    key = first_key + lax.broadcasted_iota(jnp.int32, raw.shape, 0)
    query = first_query + lax.broadcasted_iota(jnp.int32, (1, starts.shape[1]), 1)
    copies = raw.shape[1] // starts.shape[1]
    allowed = (key <= wide(query, raw.shape[1])) & (key >= wide(starts, raw.shape[1]))
    return jnp.where(allowed, raw, -1e30)


def softmax_tile(scores):
    top = jnp.max(scores, axis=0, keepdims=True)
    weights = jnp.exp(scores - top)
    return weights / jnp.sum(weights, axis=0, keepdims=True)


def stack_heads(values, head):
    return jnp.concatenate([values[:, i * head : (i + 1) * head] for i in range(values.shape[1] // head)], axis=0)


def attention_tiles(total, tile):
    back = -(-MOST_DOC // tile)
    return [(i * tile, max(0, i - back) * tile, (i + 1) * tile) for i in range(total // tile)]


def attention_forward_kernel(
    head, docs, lengths, h_ref, gain_ref, qgain_ref, kgain_ref, speed_ref, wq_hbm, wkv_hbm, wo_hbm,
    out_ref, n_hbm, raw_hbm, ready_hbm, o_hbm, cos_ref, sin_ref,
    w, wo, nf, low, ready, vt, o, tpart, mine, n_near, n_over, n_on, o_near, i_near, o_over, i_over,
    s_near, s_over, wsem, osem, bg,
):
    g = Group(bg.others)
    g.greet()
    size, width = h_ref.shape
    total, qw = 4 * size, wo.shape[0]
    kw = (w.shape[1] - qw) // 2
    loads = start_all([(wq_hbm, w.at[:, pl.ds(0, qw)]), (wkv_hbm, w.at[:, pl.ds(qw, 2 * kw)]), (wo_hbm, wo)], wsem)
    gather = Gather(g, nf, size, n_near, n_over, n_on)
    scatter = Scatter(g, o_near, i_near, o_over, i_over, s_near, s_over, size)
    parts, step = gather.parts, gather.step
    nf[at_rows(g.mine, size, 0, size), :] = normalise(h_ref[...], gain_ref[...]).astype(BF)
    g.meet()
    gather.start()
    bg.step(0)
    places = lax.broadcasted_iota(jnp.int32, (total, LANES), 0)
    angles = (places - doc_starts(docs, lengths, places)).astype(F32) * speed_ref[...]
    lane = lax.broadcasted_iota(jnp.int32, (total, LANES), 1)
    sine = jnp.sin(angles)
    cos_ref[...] = jnp.cos(angles)
    sin_ref[...] = jnp.where(lane % head < head // 2, -sine, sine)
    wait_all(loads)

    def project(block):
        rows = at_rows(block, size, 0, size)
        raw = mm(nf[rows, :], w[...])
        low[rows, :] = raw.astype(BF)
        cosine, sine = cos_ref[rows, :], sin_ref[rows, :]
        ready[rows, pl.ds(0, qw)] = norm_turn(raw[:, :qw], qgain_ref[...], cosine, sine, head).astype(BF)
        ready[rows, pl.ds(qw, kw)] = norm_turn(raw[:, qw : qw + kw], kgain_ref[...], cosine, sine, head).astype(BF)
        ready[rows, pl.ds(qw + kw, kw)] = raw[:, qw + kw :].astype(BF)

    project(g.mine)
    gather.wait_beside()
    project(g.beside)
    for p in range(parts):
        gather.wait_part(p)
    for p in range(parts):
        gather.wait_far(p)

    def rest(i, carry):
        project(jnp.where(i == 0, g.across, g.far))
        return carry

    lax.fori_loop(0, 2, rest, 0)
    bg.step(1)
    saves = start_all([(nf, n_hbm), (low, raw_hbm), (ready, ready_hbm)], osem)
    vt[...] = jnp.transpose(ready[:, pl.ds(qw + kw, kw)].astype(F32)).astype(BF)
    groups = qw // kw
    tile = 256
    scale = head ** (-0.5)
    starts = doc_starts(docs, lengths, lax.broadcasted_iota(jnp.int32, (1, total), 1))
    for first, low_key, high_key in attention_tiles(total, tile):
        keys = pl.ds(low_key, high_key - low_key)
        for kv in range(kw // head):
            q = stack_heads(ready[pl.ds(first, tile), pl.ds(kv * groups * head, groups * head)], head)
            k = ready[keys, pl.ds(qw, kw)][:, kv * head : (kv + 1) * head]
            p = softmax_tile(score_tile(q, k, starts[:, first : first + tile], low_key, first, scale)).astype(BF)
            ot = mm(vt[pl.ds(kv * head, head), keys], p)
            joined = jnp.concatenate([ot[:, i * tile : (i + 1) * tile] for i in range(groups)], axis=0)
            o[pl.ds(first, tile), pl.ds(kv * groups * head, groups * head)] = jnp.transpose(joined).astype(BF)
        if first == tile:
            bg.step(2)
    bg.step(3)
    save_o = pltpu.make_async_copy(o, o_hbm, osem.at[3])
    save_o.start()
    scatter_all(g, scatter, product(o, wo, False), mine, tpart)
    bg.step(4)
    for p in range(parts):
        here = scatter.rows(p)
        scatter.close(1, p).wait_recv()
        scatter.link(p).wait_recv()
        out_ref[here, :] = (
            h_ref[here, :] + mine[here, :] + i_near[1, here, :].astype(F32) + i_over[here, :].astype(F32)
        )
    gather.finish()
    scatter.wait_all_sends()
    wait_all(saves)
    save_o.wait()
    bg.step(6)
    bg.finish()


def attention_forward(head, docs, lengths, h, gain, qgain, kgain, speed, wq, wkv, wo, ident, tasks=(), parts=PARTS):
    size, width = h.shape
    total, qw = 4 * size, wo.shape[0]
    kw = wkv.shape[1] // 2
    every = qw + 2 * kw
    return hosted(
        functools.partial(attention_forward_kernel, head, docs), ident, "attention_forward",
        [lengths, h, gain, qgain, kgain, speed, wq, wkv, wo], [INV] * 6 + [HBM] * 3,
        [
            shaped((size, width), F32), shaped((total, width), BF), shaped((total, every), BF), shaped((total, every), BF),
            shaped((total, qw), BF), shaped((total, LANES), F32), shaped((total, LANES), F32),
        ],
        [INV] + [HBM] * 4 + [INV] * 2,
        [
            pltpu.VMEM((width, every), BF), pltpu.VMEM((qw, width), BF), pltpu.VMEM((total, width), BF),
            pltpu.VMEM((total, every), BF), pltpu.VMEM((total, every), BF),
            pltpu.VMEM((kw, total), BF), pltpu.VMEM((total, qw), BF),
            pltpu.VMEM((size // parts, width), F32), pltpu.VMEM((size, width), F32),
            *gather_scratch(parts), *scatter_scratch(size, width, parts), DMA((3,)), DMA((4,)),
        ],
        tasks, 2 * total * width * (every + qw), 2**24,
    )


def attention_backward_kernel(
    head, docs, lengths, dh_ref, h_ref, gain_ref, qgain_ref, kgain_ref, cos_ref, sin_ref, wq_hbm, wkv_hbm, wo_hbm,
    n_hbm, raw_hbm, ready_hbm, o_hbm, out_ref, gg_ref, gq_ref, gk_ref, gw_hbm, gwo_hbm,
    w, wo, nf, low, ready, kt, o, dz, do, dq, dkv, dlow, gw, gwo, tpart, mine,
    n_near, n_over, n_on, o_near, i_near, o_over, i_over, s_near, s_over, wsem, osem, bg,
):
    g = Group(bg.others)
    g.greet()
    size, width = h_ref.shape
    total, qw = 4 * size, wo.shape[0]
    kw = (w.shape[1] - qw) // 2
    loads = start_all(
        [
            (ready_hbm, ready), (wo_hbm, wo), (o_hbm, o), (raw_hbm, low), (wq_hbm, w.at[:, pl.ds(0, qw)]),
            (wkv_hbm, w.at[:, pl.ds(qw, 2 * kw)]), (n_hbm, nf),
        ],
        wsem,
    )
    gather = Gather(g, dz, size, n_near, n_over, n_on)
    scatter = Scatter(g, o_near, i_near, o_over, i_over, s_near, s_over, size)
    dz[at_rows(g.mine, size, 0, size), :] = dh_ref[...].astype(BF)
    g.meet()
    gather.start()
    bg.step(0)
    wait_all(loads)
    kt[...] = jnp.transpose(ready[:, pl.ds(qw, kw)].astype(F32)).astype(BF)
    dkv[...] = jnp.zeros_like(dkv)
    gather_everything(gather)

    def project(t, carry):
        rows = at_rows(t, size, 0, size)
        do[rows, :] = mm_nt(dz[rows, :], wo[...]).astype(BF)
        return carry

    bg.step(1)

    lax.fori_loop(0, total // size, project, 0)
    groups = qw // kw
    tile = 256
    scale = head ** (-0.5)
    starts = doc_starts(docs, lengths, lax.broadcasted_iota(jnp.int32, (1, total), 1))
    for first, low_key, high_key in attention_tiles(total, tile):
        keys = pl.ds(low_key, high_key - low_key)
        for kv in range(kw // head):
            cols = pl.ds(kv * groups * head, groups * head)
            lane = slice(kv * head, (kv + 1) * head)
            q = stack_heads(ready[pl.ds(first, tile), cols], head)
            k, v = ready[keys, pl.ds(qw, kw)][:, lane], ready[keys, pl.ds(qw + kw, kw)][:, lane]
            p = softmax_tile(score_tile(q, k, starts[:, first : first + tile], low_key, first, scale))
            d = stack_heads(do[pl.ds(first, tile), cols], head)
            dp = mm_nt(v, d)
            inner = jnp.sum(p * dp, axis=0, keepdims=True)
            ds = (p * (dp - inner)).astype(BF)
            both = jnp.concatenate([mm(ds, q) * scale, mm(p.astype(BF), d)], axis=1)
            dkv[kv, keys, :] += both
            dqt = mm(kt[pl.ds(kv * head, head), keys], ds) * scale
            joined = jnp.concatenate([dqt[:, i * tile : (i + 1) * tile] for i in range(groups)], axis=0)
            dq[pl.ds(first, tile), cols] = jnp.transpose(joined)
        if first == tile:
            bg.step(2)
        if first == 2 * tile:
            bg.step(3)
    bg.step(4)
    gq_ref[...] = jnp.zeros_like(gq_ref)
    gk_ref[...] = jnp.zeros_like(gk_ref)

    def finish(t, carry):
        rows = at_rows(t, size, 0, size)
        cosine, sine = cos_ref[rows, :], sin_ref[rows, :]
        d, gq = norm_turn_back(dq[rows, :], low[rows, pl.ds(0, qw)].astype(F32), qgain_ref[...], cosine, sine, head)
        gq_ref[...] += gq
        dlow[rows, pl.ds(0, qw)] = d.astype(BF)
        pairs = [dkv[kv, rows, :] for kv in range(kw // head)]
        dk = jnp.concatenate([x[:, :head] for x in pairs], axis=1)
        dv = jnp.concatenate([x[:, head:] for x in pairs], axis=1)
        d, gk = norm_turn_back(dk, low[rows, pl.ds(qw, kw)].astype(F32), kgain_ref[...], cosine, sine, head)
        gk_ref[...] += gk
        dlow[rows, pl.ds(qw, kw)] = d.astype(BF)
        dlow[rows, pl.ds(qw + kw, kw)] = dv.astype(BF)
        return carry

    lax.fori_loop(0, total // size, finish, 0)
    scatter_all(g, scatter, product(dlow, w, True), mine, tpart)
    put_columns(gwo, 0, mm_tn(o[...], dz[...]).astype(BF))
    save = pltpu.make_async_copy(gwo, gwo_hbm, osem.at[0])
    save.start()
    for t in range(width // 256):
        put_rows(gw, t * 256, mm_tn(nf[:, pl.ds(t * 256, 256)], dlow[...]).astype(BF))
    more = pltpu.make_async_copy(gw, gw_hbm, osem.at[1])
    more.start()
    bg.step(5)
    close_scatter(scatter, mine, dh_ref, h_ref, gain_ref, out_ref, gg_ref)
    gather.finish()
    scatter.wait_all_sends()
    save.wait()
    more.wait()
    bg.step(6)
    bg.finish()


def attention_backward(
    head, docs, lengths, dh, h, gain, qgain, kgain, cosine, sine, wq, wkv, wo, n, raw, ready, o, pieces, ident, tasks=(),
    parts=PARTS,
):
    size, width = h.shape
    total, qw = 4 * size, wo.shape[0]
    kw = wkv.shape[1] // 2
    every = qw + 2 * kw
    each = width // pieces
    return hosted(
        functools.partial(attention_backward_kernel, head, docs), ident, "attention_backward",
        [lengths, dh, h, gain, qgain, kgain, cosine, sine, wq, wkv, wo, n, raw, ready, o], [INV] * 8 + [HBM] * 7,
        [
            shaped((size, width), F32), shaped((1, width), F32), shaped((1, qw), F32), shaped((1, kw), F32),
            shaped((pieces, each, every), BF), shaped((pieces, qw, each), BF),
        ],
        [INV, INV, INV, INV, HBM, HBM],
        [
            pltpu.VMEM((width, every), BF), pltpu.VMEM((qw, width), BF), pltpu.VMEM((total, width), BF),
            pltpu.VMEM((total, every), BF), pltpu.VMEM((total, every), BF), pltpu.VMEM((kw, total), BF),
            pltpu.VMEM((total, qw), BF), pltpu.VMEM((total, width), BF), pltpu.VMEM((total, qw), BF),
            pltpu.VMEM((total, qw), F32), pltpu.VMEM((kw // head, total, 2 * head), F32), pltpu.VMEM((total, every), BF),
            pltpu.VMEM((pieces, each, every), BF), pltpu.VMEM((pieces, qw, each), BF),
            pltpu.VMEM((size // parts, width), F32), pltpu.VMEM((size, width), F32),
            *gather_scratch(parts), *scatter_scratch(size, width, parts), DMA((7,)), DMA((2,)),
        ],
        tasks, 4 * total * width * (every + qw), 2**25,
    )


def tail_kernel(bg):
    g = Group(bg.others)
    g.greet()
    g.meet()
    for k in range(4):
        bg.step(k)
    bg.step(6)
    bg.finish()


def tail(ident, tasks):
    return hosted(tail_kernel, ident, "tail", [], [], [], [], [], tasks, 0, 2**22)[1]


rope_base = 1000000.0
TP = ("c", "zl")
DP = ("r", "s", "zh")


def rope_speeds(head_dim):
    half_dim = head_dim // 2
    inverse = rope_base ** (-2.0 * jnp.arange(half_dim, dtype=F32) / head_dim)
    return jnp.tile(inverse, LANES // half_dim)[None]


def swap(x):
    return lax.ppermute(x, ("c", "zh"), [(0, 0), (1, 2), (2, 1), (3, 3)])


def gather_dp(shard, axis):
    return lax.all_gather(swap(shard), DP, axis=axis, tiled=True)


def scatter_dp(partial, axis):
    return swap(lax.psum_scatter(partial, DP, scatter_dimension=axis, tiled=True)).astype(F32)


def local(
    planes, tokens, doc_lengths, grad_out, norm_gains, head_gains, conv_in, conv_kernel, conv_out,
    query_w, kv_w, out_w, gate_up, down,
):
    length = tokens.shape[0]
    head_dim = head_gains.shape[1]
    docs, count = doc_lengths.shape[1], conv_kernel.shape[0]
    conv_in = conv_in.reshape(conv_in.shape[0], -1)
    kv_w = kv_w.reshape(kv_w.shape[0], -1)
    own_w = gate_up.reshape(*gate_up.shape[:2], -1)
    pieces = 8 if planes else 1
    kv_width = kv_w.shape[1] // 2
    qgain = jnp.tile(head_gains[0:1], (1, query_w.shape[1] // head_dim))
    kgain = jnp.tile(head_gains[1:2], (1, kv_width // head_dim))
    gain = [norm_gains[i : i + 1] for i in range(4)]
    lens = jnp.pad(doc_lengths.astype(F32), ((0, 7), (0, LANES - docs)))
    taps = jnp.pad(conv_kernel, ((0, 8 - count), (0, 0)))
    rows_of = lambda got: got.reshape(-1, got.shape[-1])
    if planes:
        first = [Take(conv_in, (0, 0, 0, 2, 2), True), Take(conv_out, (0, 0, 0, 2, 2), True)]
        first += [Fetch(own_w, (0, 1, 1, 2, 2, 2, 4, 5, 3), 4, 0, 0), Fetch(down, (0, 1, 1, 2, 4, 5, 3), 2, 0, 0)]
        second = [Take(x, (0, 0, 0, 2, 2)) for x in (query_w, kv_w, out_w)]
        second += [Fetch(own_w, (0, 0, 0, 2), 1, 1, 1), Fetch(down, (0, 0, 0, 2), 1, 1, 1)]
    else:
        first, second, third = [], [], []
        conv_in, conv_out, query_w, kv_w, out_w = map(swap, (conv_in, conv_out, query_w, kv_w, out_w))
        w0, w1 = (gather_dp(w, 0) for w in own_w)
        v0, v1 = (gather_dp(v, 1)[None] for v in down)

    (h1, x_block, n0, projected, lens, taps, conv_in, conv_out), got = conv_forward(
        docs, count, lens, tokens, gain[0], taps, conv_in, conv_out, planes, 0, first
    )
    if planes:
        w0, v0 = rows_of(got[0]), got[1]
    (h2, n1, hidden0), got = ffn_forward(h1, gain[1], w0, v0, 1, second)
    if planes:
        query_w, kv_w, out_w = got[:3]
        third = [Fetch(got[3], (0, 4), 2, 2), Fetch(got[4], (0, 4), 1, 2)]
    (h3, n2, raw, ready, attended, cosine, sine), got = attention_forward(
        head_dim, docs, lens, h2, gain[2], qgain, kgain, rope_speeds(head_dim), query_w, kv_w, out_w, 2, third
    )
    if planes:
        w1, v1 = rows_of(got[0]), got[1]
    (h4, n3, hidden1), (up_full,) = ffn_forward(h3, gain[3], w1, v1, 3, [Spread(grad_out, (0, 1, 2))])

    def halves(grad, first, second, last=False):
        half = grad.shape[1] // 2
        return [Reduce(grad, 0, half, first, last), Reduce(grad, half, half, second, False)] if planes else []

    def whole(grad, at, last=False):
        return [Reduce(grad, 0, grad.shape[1], at, last)] if planes else []

    def settled(sums, at):
        return [Settle(x, at) for x in sums]

    (dh3, gain3, gw1, gv1), (output,) = ffn_backward(
        None, h3, gain[3], up_full, w1, v1, n3, hidden1, 4, [Deliver(h4, (0, 2))]
    )
    (dh2, gain2, gq, gk, gqkv, gow), sums = attention_backward(
        head_dim, docs, lens, dh3, h2, gain[2], qgain, kgain, cosine, sine, query_w, kv_w, out_w, n2, raw, ready, attended,
        pieces, 5, halves(gw1, (0, 2, 5), (0, 4, 6)),
    )
    (dh1, gain1, gw0, gv0), got = ffn_backward(
        dh2, h1, gain[1], None, w0, v0, n1, hidden0, 6,
        settled(sums, (0, 0)) + whole(gv1, (0, 1, 2)) + whole(gqkv, (0, 2, 3)) + whole(gow, (0, 2, 3)),
    )
    sums_w1, sums = got[:2], got[2:]
    (dh0, gain0, gtaps, gci, gco), got = conv_backward(
        docs, count, lens, dh1, x_block.astype(F32), gain[0], taps, conv_in, conv_out, n0, projected, pieces, 7,
        settled(sums, (0, 0)) + halves(gw0, (0, 1, 4), (0, 3, 6), True),
    )
    others, first_w0, sums = got[:3], got[3:4], got[4:]
    totals, grads, *got = tail(
        8,
        [Total([gain0, gain1, gain2, gain3, gtaps, gq, gk], (0, 1, 2, 3), count, ("zh", "s", *(("r",) if planes else ()), "zl", "c")), Deliver(dh0, (0, 0))]
        + settled(sums, (0, 0)) + whole(gv0, (0, 0, 1), True) + whole(gci, (1, 2, 3), True) + whole(gco, (1, 2, 3), True),
    )
    if planes:
        gv1, gqkv, gow = others
        gate_ups = [*first_w0, got[0], *sums_w1]
        gv0, gci, gco = got[1:]
    else:
        totals = lax.psum(totals, "r")
        gw0, gw1, gci, gqkv = (scatter_dp(g[0], 0) for g in (gw0, gw1, gci, gqkv))
        gv0, gv1, gco, gow = (scatter_dp(g[0], 1) for g in (gv0, gv1, gco, gow))
        gate_ups = [gw0, gw1]
    heads = totals[7, : gq.shape[1] + gk.shape[1]].reshape(-1, head_dim)
    split = gq.shape[1] // head_dim
    return (
        output,
        grads.astype(F32),
        totals[:4],
        jnp.stack([jnp.sum(heads[:split], axis=0), jnp.sum(heads[split:], axis=0)]),
        gci.reshape(-1, 3, conv_kernel.shape[1]),
        totals[4 : 4 + count],
        gco,
        gqkv[:, : query_w.shape[1]],
        gqkv[:, query_w.shape[1] :].reshape(-1, 2, kv_width),
        gow,
        jnp.concatenate(gate_ups, axis=0).reshape(2, gate_up.shape[1], 2, -1),
        jnp.stack([gv0, gv1]),
    )


def solution(mesh):
    devices = mesh.devices
    dp, tp = devices.shape
    inner = Mesh(devices.reshape(dp // 4, 2, 2, 2, tp // 2), ("r", "s", "c", "zh", "zl"))
    D = ("r", "s", "c")
    T = ("zh", "zl")
    return jax.shard_map(
        functools.partial(local, dp == 8),
        mesh=inner,
        in_specs=(
            P(D, T), P(D, None), P(D, T), P(), P(), P(None, None, T), P(None, T), P(T, None),
            P(None, T), P(None, None, T), P(T, None), P(None, D, None, T), P(None, T, D),
        ),
        out_specs=(
            P(D, T), P(D, T), P(), P(), P(D, None, T), P(), P(T, D), P(D, T), P(D, None, T),
            P(T, D), P(None, D, None, T), P(None, T, D),
        ),
        check_vma=False,
    )
```

```python
import functools
import jax
import jax.numpy as jnp
from jax import lax
from jax.experimental import pallas as pl
from jax.experimental.pallas import tpu as pltpu
from jax.sharding import Mesh, PartitionSpec as P

epsilon = 1e-05
BF = jnp.bfloat16
F32 = jnp.float32
MESH = pl.DeviceIdType.MESH
DMA = pltpu.SemaphoreType.DMA
HBM = pl.BlockSpec(memory_space=pl.ANY)
INV = pl.BlockSpec(memory_space=pltpu.VMEM)
PARTS = 2
LANES = 128


class Group:
    def __init__(self, others=(), calls=True):
        c, z = lax.axis_index("c"), lax.axis_index("zl")
        self.partner, self.twin = {"c": 1 - c}, {"zl": 1 - z}
        self.mine, self.beside = 2 * c + z, 2 * (1 - c) + z
        self.across, self.far = 2 * c + (1 - z), 2 * (1 - c) + (1 - z)
        self.known = [self.partner, self.twin, *others]
        self.c, self.z = c, z
        self.barrier = pltpu.get_barrier_semaphore() if calls else None

    def greet(self):
        for other in self.known:
            pl.semaphore_signal(self.barrier, inc=1, device_id=other, device_id_type=MESH)

    def meet(self):
        pl.semaphore_wait(self.barrier, len(self.known))


def at_rows(block, size, start, count):
    return pl.ds(pl.multiple_of(block * size + start, 16), count)


def send(src, dst, sems, index, where):
    return pltpu.make_async_remote_copy(
        src_ref=src, dst_ref=dst, send_sem=sems.at[0, index], recv_sem=sems.at[1, index],
        device_id=where, device_id_type=MESH,
    )


class Gather:
    def __init__(self, group, full, size, near, over, onward):
        self.g, self.full, self.size, self.parts = group, full, size, over.shape[1]
        self.near, self.over, self.onward = near, over, onward
        self.step = size // self.parts

    def view(self, block, part):
        return self.full.at[at_rows(block, self.size, part * self.step, self.step)]

    def link(self, part, block):
        v = self.view(block, part)
        return send(v, v, self.over, part, self.g.twin)

    def close(self, part, block):
        v = self.view(block, part)
        return send(v, v, self.near, part, self.g.partner)

    def pass_on(self, part, block):
        v = self.view(block, part)
        return send(v, v, self.onward, part, self.g.partner)

    def start(self):
        for p in range(self.parts):
            self.link(p, self.g.mine).start()
            self.close(p, self.g.mine).start()

    def wait_beside(self):
        for p in range(self.parts):
            self.close(p, self.g.beside).wait_recv()

    def wait_part(self, p):
        self.link(p, self.g.across).wait_recv()
        self.pass_on(p, self.g.across).start()

    def wait_far(self, p):
        self.pass_on(p, self.g.far).wait_recv()

    def finish(self):
        for p in range(self.parts):
            self.link(p, self.g.mine).wait_send()
            self.close(p, self.g.mine).wait_send()
            self.pass_on(p, self.g.across).wait_send()


class Scatter:
    def __init__(self, group, out_near, in_near, out_over, in_over, near, over, size):
        self.g, self.size, self.parts = group, size, over.shape[1]
        self.out_near, self.in_near, self.out_over, self.in_over = out_near, in_near, out_over, in_over
        self.near, self.over = near, over
        self.step = size // self.parts

    def rows(self, part):
        return pl.ds(part * self.step, self.step)

    def close(self, which, part):
        r = self.rows(part)
        return send(self.out_near.at[which, r], self.in_near.at[which, r], self.near, which * self.parts + part, self.g.partner)

    def link(self, part):
        r = self.rows(part)
        return send(self.out_over.at[r], self.in_over.at[r], self.over, part, self.g.twin)

    def wait_all_sends(self):
        for p in range(self.parts):
            self.close(0, p).wait_send()
            self.close(1, p).wait_send()
            self.link(p).wait_send()


def scatter_scratch(size, width, parts):
    return [
        pltpu.VMEM((2, size, width), BF), pltpu.VMEM((2, size, width), BF), pltpu.VMEM((size, width), BF),
        pltpu.VMEM((size, width), BF), DMA((2, 2 * parts)), DMA((2, parts)),
    ]


def gather_scratch(parts):
    return [DMA((2, parts)), DMA((2, parts)), DMA((2, parts))]


def normalise(h, gain):
    return h * lax.rsqrt(jnp.mean(h * h, axis=-1, keepdims=True) + epsilon) * gain


def mm(a, b):
    return jnp.dot(a, b, preferred_element_type=F32)


def mm_nt(a, b):
    return lax.dot_general(a, b, (((1,), (1,)), ((), ())), preferred_element_type=F32)


def lanes(start, width):
    return pl.ds(pl.multiple_of(start, LANES), width)


def start_all(pairs, sems):
    copies = [pltpu.make_async_copy(src, dst, sems.at[i]) for i, (src, dst) in enumerate(pairs)]
    for copy in copies:
        copy.start()
    return copies


def wait_all(copies):
    for copy in copies:
        copy.wait()


def params(ident):
    return pltpu.CompilerParams(collective_id=ident, has_side_effects=True, vmem_limit_bytes=56 * 2**20)


def shaped(shape, dtype):
    return jax.ShapeDtypeStruct(shape, dtype)


END = 99


class Place:
    def __init__(self):
        self.y, self.x, self.c, self.zh = (lax.axis_index(a) for a in ("r", "s", "c", "zh"))
        self.across_x, self.across_y = {"s": 1 - self.x}, {"r": 1 - self.y}
        self.partner = {"c": 1 - self.c}
        self.plain = self.c == self.zh
        self.outer = lax.axis_index("zl") == self.zh

    def over(self, core):
        return {"c": core, "zh": 1 - self.zh}

    def swapped(self):
        return self.over(self.zh)

    PLANES = ("x", "y")
    ENDS = ("end", "swap")
    COLUMN = ("end", "swap", "z core", "z end", "z swap")

    def called(self, name):
        z = 1 - lax.axis_index("zl")
        other, far = 1 - self.c, 1 - self.zh
        return {
            "x": self.across_x, "y": self.across_y, "end": self.over(self.c), "swap": self.over(other),
            "z core": {"c": other, "zl": z}, "z end": {"zh": far, "zl": z}, "z swap": {"c": other, "zh": far, "zl": z},
        }[name]

    def piece(self, flip_y, flip_x, a):
        y = 1 - self.y if flip_y else self.y
        x = 1 - self.x if flip_x else self.x
        return 4 * y + 2 * x + a


class Fetch:
    def __init__(self, shard, at, cuts=1, stage=0, layer=None):
        rows, cols = shard.shape[-2:]
        self.layer = layer
        self.at, self.cuts, self.stage, self.step_rows = at, cuts, stage, rows // cuts
        self.ins = [shard]
        self.outs = [jax.ShapeDtypeStruct((8, rows, cols), shard.dtype)]
        self.out_specs = [HBM]
        self.in_place = stage == 2
        self.semaphores()
        if not self.in_place:
            self.scratch.append(pltpu.VMEM((rows, cols), BF))

    def semaphores(self):
        self.scratch = [DMA((9 * self.cuts,)), DMA((8 * self.cuts,)), DMA((2,))]

    def bind(self, ins, outs, scratch):
        (self.own,), (self.out,) = ins, outs
        if self.layer is not None:
            self.own = self.own.at[self.layer]
        self.sent, self.come, self.sem = scratch[:3]
        self.bounce = scratch[3] if len(scratch) > 3 else None
        self.p = Place()

    def greets(self):
        return Place.PLANES if self.stage == 2 else Place.PLANES + Place.ENDS

    def part(self, ref, q):
        return ref.at[pl.ds(q * self.step_rows, self.step_rows)]

    def given(self, q):
        return self.part(self.own, q)

    def slot(self, piece, q):
        return self.part(self.out.at[piece], q)

    def home(self, a, q):
        return self.slot(self.p.piece(0, 0, a), q)

    def copy(self, src, dst, q, sent, come, where):
        return pltpu.make_async_remote_copy(
            src_ref=src, dst_ref=dst, send_sem=self.sent.at[9 * q + sent], recv_sem=self.come.at[8 * q + come],
            device_id=where, device_id_type=MESH,
        )

    def to_plane(self, q):
        p = self.p
        return self.copy(self.given(q), self.home(p.c, q), q, 0, p.c, p.over(p.zh))

    def to_partner(self, q):
        p = self.p
        return self.copy(self.given(q), self.home(p.c, q), q, 1, p.c, p.partner)

    def arrived(self, a, q):
        self.copy(self.given(q), self.home(a, q), q, 0, a, self.p.partner).wait_recv()

    def keep(self):
        slot = self.out.at[self.p.piece(0, 0, self.p.c)]
        return [
            pltpu.make_async_copy(self.own, self.bounce, self.sem.at[0]),
            pltpu.make_async_copy(self.bounce, slot, self.sem.at[1]),
        ]

    def kept(self):
        self.keep()[0].start()

    def land(self):
        copies = self.keep()
        for i, copy in enumerate(copies):
            if i:
                copy.start()
            copy.wait()

    def to_x(self, a, q, src=None):
        dst = self.slot(self.p.piece(0, 0, a), q)
        return self.copy(dst if src is None else src, dst, q, 2 + a, 2 + a, self.p.across_x)

    def to_y(self, a, q, src=None):
        dst = self.slot(self.p.piece(0, 0, a), q)
        return self.copy(dst if src is None else src, dst, q, 4 + a, 4 + a, self.p.across_y)

    def spread(self, a, q, src):
        self.to_x(a, q, src).start()
        self.to_y(a, q, src).start()

    def on_y(self, q):
        there = self.slot(self.p.piece(0, 1, 0), q)
        return self.copy(there, there, q, 6, 6, self.p.across_y)

    def on_x(self, q):
        there = self.slot(self.p.piece(1, 0, 1), q)
        return self.copy(there, there, q, 7, 7, self.p.across_x)

    def forward(self, q):
        self.to_x(0, q).wait_recv()
        self.on_y(q).start()
        self.to_y(1, q).wait_recv()
        self.on_x(q).start()

    def plain(self, run):
        pl.when(self.p.plain)(run)

    def other(self, run):
        pl.when(jnp.logical_not(self.p.plain))(run)

    def step(self, k):
        p, every = self.p, range(self.cuts)

        def own():
            for q in every:
                self.spread(p.c, q, self.given(q))

        def partner():
            for q in every:
                self.to_partner(q).start()

        def second():
            for q in every:
                self.arrived(1 - p.c, q)
                self.spread(1 - p.c, q, self.home(1 - p.c, q))

        def planes():
            for q in every:
                for a in (0, 1):
                    self.spread(a, q, self.home(a, q))

        def there(q):
            for a in (0, 1):
                self.arrived(a, q)
                self.spread(a, q, self.home(a, q))

        if self.stage == 2:
            if k == 0:
                self.other(planes)
            elif k == 1:
                self.other(lambda: [self.forward(q) for q in every] and None)
            elif k == END:
                self.other(self.close)
        elif k == 0:
            self.plain(self.kept)
            self.other(partner)
            self.plain(own)
            self.plain(second)
        elif k == END:
            for q in every:
                self.to_plane(q).wait_send()
            if self.stage:
                self.plain(self.close)
                self.other(lambda: [self.arrived(a, q) for q in every for a in (0, 1)] and None)
            else:
                self.close()
            self.plain(self.land)
            self.other(lambda: [self.to_partner(q).wait_send() for q in every] and None)
        elif k in (1, 2):
            self.leave(k == 1)
        elif k == 3:
            self.plain(lambda: [self.forward(q) for q in every] and None)
        elif not self.stage:
            q = k - 4
            if q < self.cuts:
                self.other(functools.partial(there, q))
            if q:
                self.other(lambda: self.forward(q - 1))

    def leave(self, outer):
        @pl.when(self.p.outer if outer else jnp.logical_not(self.p.outer))
        def _():
            for q in range(self.cuts):
                self.to_plane(q).start()

    def close(self):
        for q in range(self.cuts):
            self.to_x(1, q).wait_recv()
            self.to_y(0, q).wait_recv()
            self.on_y(q).wait()
            self.on_x(q).wait()
            for a in (0, 1):
                self.to_x(a, q).wait_send()
                self.to_y(a, q).wait_send()


class Take(Fetch):
    def __init__(self, whole, at, inside=False):
        rows, cols = whole.shape
        self.at, self.each, self.cuts, self.stage = at, rows // 8, 1, 0
        self.ins = [whole]
        self.outs = [] if inside else [jax.ShapeDtypeStruct((rows, cols), whole.dtype)]
        self.out_specs = [] if inside else [HBM]
        self.in_place = False
        self.semaphores()
        if not inside:
            self.scratch.append(pltpu.VMEM((rows, cols), BF))

    def bind(self, ins, outs, scratch):
        (self.own,) = ins
        self.whole = outs[0] if outs else None
        self.sent, self.come, self.sem = scratch[:3]
        self.bounce = scratch[3] if len(scratch) > 3 else None
        self.p = Place()

    def rows(self, piece):
        return pl.ds(pl.multiple_of(piece * self.each, 16), self.each)

    def given(self, q):
        return self.own.at[self.rows(self.p.piece(0, 0, self.p.c))]

    def slot(self, piece, q):
        return self.whole.at[self.rows(piece)]

    def keep(self):
        if self.bounce is None:
            return [pltpu.make_async_copy(self.own, self.whole, self.sem.at[0])]
        return [
            pltpu.make_async_copy(self.own, self.bounce, self.sem.at[0]),
            pltpu.make_async_copy(self.bounce, self.whole, self.sem.at[1]),
        ]

    def step(self, k):
        def there():
            for a in (0, 1):
                self.arrived(a, 0)
                self.spread(a, 0, self.home(a, 0))

        def last():
            self.close()

        if k == 0:
            self.plain(self.kept)
        elif k in (1, 2):
            self.leave(k == 1)
        elif k == 3:
            self.other(there)
        elif k == 4:
            self.other(lambda: self.forward(0))
        elif k == END:
            self.to_plane(0).wait_send()
            self.plain(self.land)
            self.other(last)


class Exchange:
    def __init__(self, src, dst, there, sems, sem, index=0):
        self.p = Place()
        self.src, self.dst, self.there, self.sems, self.sem, self.index = src, dst, there, sems, sem, index

    def stay(self):
        return pltpu.make_async_copy(self.src, self.dst, self.sem.at[self.index])

    def leave(self):
        return send(self.src, self.there, self.sems, self.index, self.p.swapped())

    def come(self):
        return send(self.src, self.dst, self.sems, self.index, self.p.swapped())

    def both(self, stay, leave):
        pl.when(self.p.plain)(stay)
        pl.when(jnp.logical_not(self.p.plain))(leave)

    def start(self):
        self.both(lambda: self.stay().start(), lambda: self.leave().start())

    def arrive(self):
        self.both(lambda: self.stay().wait(), lambda: self.come().wait_recv())

    def finish(self):
        pl.when(jnp.logical_not(self.p.plain))(lambda: self.leave().wait_send())


class Spread:
    def __init__(self, block, at, parts=2):
        rows, cols = block.shape
        self.at, self.parts = at, parts
        self.ins = [block]
        self.outs = [jax.ShapeDtypeStruct((rows, 4 * cols), block.dtype)]
        self.out_specs = [HBM]
        self.scratch = [*gather_scratch(parts), DMA((2, parts)), DMA((parts,))]

    def bind(self, ins, outs, scratch):
        (self.block,), (self.full,) = ins, outs
        near, over, onward, sems, sem = scratch
        self.p, self.g = Place(), Group(calls=False)
        self.gather = Columns(self.g, self.full, near, over, onward)
        cols = self.block.shape[1]
        self.exchanges = []
        for p in range(self.parts):
            rows = pl.ds(p * self.gather.step, self.gather.step)
            mine, there = (self.full.at[rows, lanes(b * cols, cols)] for b in (self.g.mine, self.g.beside))
            self.exchanges.append(Exchange(self.block.at[rows], mine, there, sems, sem, p))

    def greets(self):
        return Place.ENDS

    def step(self, k):
        if k == 0:
            for exchange in self.exchanges:
                exchange.start()
        elif k == 1:
            for p, exchange in enumerate(self.exchanges):
                exchange.arrive()
                self.gather.link(p, self.g.mine).start()
                self.gather.close(p, self.g.mine).start()
        elif k == 2:
            for p in range(self.parts):
                self.gather.wait_part(p)
        elif k == END:
            self.gather.wait_beside()
            for p in range(self.parts):
                self.gather.wait_far(p)
            self.gather.finish()
            for exchange in self.exchanges:
                exchange.finish()


class Deliver:
    def __init__(self, block, at):
        rows, width = block.shape
        self.at = at
        self.ins = [block]
        self.outs = [jax.ShapeDtypeStruct((4 * rows, width // 4), BF)]
        self.out_specs = [HBM]
        self.scratch = [pltpu.VMEM((rows, width), BF), DMA((4,)), DMA((4,)), DMA((2,))]
        if block.dtype != BF:
            self.scratch.append(pltpu.VMEM((rows, width), block.dtype))

    def bind(self, ins, outs, scratch):
        (self.block,), (self.out,) = ins, outs
        self.low, self.sent, self.come, self.sem = scratch[:4]
        self.wide = scratch[4] if len(scratch) > 4 else self.low
        self.p, self.g = Place(), Group(calls=False)

    def greets(self):
        return Place.COLUMN

    def load(self):
        return pltpu.make_async_copy(self.block, self.wide, self.sem.at[0])

    def parts(self):
        rows, width = self.low.shape
        cols = width // 4
        dst = self.out.at[at_rows(self.g.mine, rows, 0, rows)]
        for f in range(4):
            half, z = divmod(f, 2)
            here = (self.p.c == self.p.zh) & (self.p.zh == half) & (self.g.z == z)
            src = self.low.at[:, pl.ds(f * cols, cols)]
            where = {"c": self.p.zh, "zh": jnp.int32(half), "zl": jnp.int32(z)}
            yield here, pltpu.make_async_copy(src, dst, self.sem.at[1]), pltpu.make_async_remote_copy(
                src_ref=src, dst_ref=dst, send_sem=self.sent.at[f], recv_sem=self.come.at[self.g.mine],
                device_id=where, device_id_type=MESH,
            )

    def step(self, k):
        if k == 0:
            self.load().start()
        elif k == 1:
            self.load().wait()
            if self.wide is not self.low:
                self.low[...] = self.wide[...].astype(BF)
            for here, stay, leave in self.parts():
                pl.when(here)(lambda stay=stay: stay.start())
                pl.when(jnp.logical_not(here))(lambda leave=leave: leave.start())
        elif k == END:
            rows, width = self.low.shape
            for here, stay, leave in self.parts():
                pl.when(here)(lambda stay=stay: stay.wait())
                pl.when(jnp.logical_not(here))(lambda leave=leave: leave.wait_send())
            for b in range(4):
                core, z = divmod(b, 2)
                here = (self.p.c == self.p.zh) & (self.p.c == core) & (self.g.z == z)
                come = pltpu.make_async_remote_copy(
                    src_ref=self.low.at[:, pl.ds(0, width // 4)], dst_ref=self.out.at[pl.ds(b * rows, rows)],
                    send_sem=self.sent.at[0], recv_sem=self.come.at[b], device_id=self.p.partner, device_id_type=MESH,
                )
                pl.when(jnp.logical_not(here))(lambda come=come: come.wait_recv())


class Total:
    def __init__(self, pieces, at, count, axes):
        self.at, self.count, self.axes = at, count, axes
        self.ins = pieces
        self.in_specs = [INV] * len(pieces)
        width = pieces[0].shape[1]
        self.outs = [jax.ShapeDtypeStruct((8, width), F32)]
        self.out_specs = [INV]
        self.scratch = [
            pltpu.VMEM((len(self.axes), 8, width), F32), pltpu.VMEM((len(self.axes), 8, width), F32),
            DMA((2, len(self.axes))),
        ]

    def bind(self, ins, outs, scratch):
        self.pieces, (self.out,) = ins, outs
        self.sum, self.other, self.sems = scratch
        self.p, self.g = Place(), Group(calls=False)

    def greets(self):
        return ("x",) + Place.ENDS + (("y",) if "r" in self.axes else ())

    def hop(self, i):
        axis = self.axes[i]
        return send(self.sum.at[i], self.other.at[i], self.sems, i, {axis: 1 - lax.axis_index(axis)})

    def step(self, k):
        if k == 0:
            gains, taps, heads = self.pieces[:4], self.pieces[4], self.pieces[5:]
            self.sum[0] = jnp.zeros(self.sum.shape[1:], F32)
            for i, gain in enumerate(gains):
                self.sum[0, pl.ds(i, 1), :] = gain[...]
            cols = taps.shape[1]
            self.sum[0, pl.ds(4, self.count), lanes(self.g.mine * cols, cols)] = taps[pl.ds(0, self.count), :]
            done = 0
            for head in heads:
                self.sum[0, pl.ds(7, 1), pl.ds(done, head.shape[1])] = head[...]
                done += head.shape[1]
            self.hop(0).start()
        else:
            k = min(k, 4)
            last = len(self.axes) if k == 4 else k
            for i in range(k - 1, last):
                self.hop(i).wait()
                value = self.sum[i] + self.other[i]
                if i + 1 < len(self.axes):
                    self.sum[i + 1] = value
                    self.hop(i + 1).start()
                else:
                    self.out[...] = value


class Reduce:
    def __init__(self, grad, first, rows, at, last=True):
        self.first, self.rows, self.at, self.last = first, rows, at, last
        cols = grad.shape[2]
        self.ins = [grad]
        self.outs = [shaped((rows, cols), F32) if last else shaped((2, rows, cols), BF)]
        self.out_specs = [INV]
        self.scratch = [
            pltpu.VMEM((4, rows, cols), BF), pltpu.VMEM((4, rows, cols), BF), pltpu.VMEM((2, rows, cols), BF),
            DMA((9,)), DMA((8,)), DMA((4,)),
        ]
        if last:
            self.scratch.append(pltpu.VMEM((2, rows, cols), BF))

    def bind(self, ins, outs, scratch):
        (self.grad,), (self.out,) = ins, outs
        self.held, self.in1, self.in2, self.sent, self.come, self.sem = scratch[:6]
        self.in3 = scratch[6] if self.last else None
        self.p = Place()

    def greets(self):
        return Place.PLANES + (Place.ENDS if self.last else ())

    def fin(self, a):
        return self.held.at[2 * a]

    def piece(self, flip_y, flip_x, a):
        return self.grad.at[self.p.piece(flip_y, flip_x, a), pl.ds(self.first, self.rows)]

    def copy(self, src, dst, sent, come, where):
        return pltpu.make_async_remote_copy(
            src_ref=src, dst_ref=dst, send_sem=self.sent.at[sent], recv_sem=self.come.at[come],
            device_id=where, device_id_type=MESH,
        )

    def loads(self):
        kept = [(0, 0, 0), (0, 1, 0), (0, 0, 1), (1, 0, 1)]
        return [pltpu.make_async_copy(self.piece(*k), self.held.at[i], self.sem.at[i]) for i, k in enumerate(kept)]

    def first_hops(self):
        p = self.p
        return [
            self.copy(self.piece(1, 0, 0), self.in1.at[0], 0, 0, p.across_y),
            self.copy(self.piece(1, 1, 0), self.in1.at[1], 1, 1, p.across_y),
            self.copy(self.piece(0, 1, 1), self.in1.at[2], 2, 2, p.across_x),
            self.copy(self.piece(1, 1, 1), self.in1.at[3], 3, 3, p.across_x),
        ]

    def second_hops(self):
        return [
            self.copy(self.held.at[1], self.in2.at[0], 4, 4, self.p.across_x),
            self.copy(self.held.at[3], self.in2.at[1], 5, 5, self.p.across_y),
        ]

    def to_owner(self, a):
        return self.copy(self.fin(a), self.in3.at[0], 6 + a, 6, self.p.over(a))

    def to_partner(self):
        return self.copy(self.fin(1 - self.p.c), self.in3.at[1], 8, 7, self.p.partner)

    def add(self, i, other):
        self.held[i] = (self.held[i].astype(F32) + other.astype(F32)).astype(BF)

    def step(self, k):
        p = self.p
        if k == 0:
            for hop in [self.first_hops()[i] for i in (1, 3, 0, 2)]:
                hop.start()
            for load in self.loads():
                load.start()
        elif k == 1:
            for load in self.loads():
                load.wait()
            hops, after = self.first_hops(), self.second_hops()
            for i in (1, 3):
                hops[i].wait_recv()
                self.add(i, self.in1[i])
                after[i // 2].start()
            for i in (0, 2):
                hops[i].wait_recv()
                self.add(i, self.in1[i])
        elif k == 2:
            for i, hop in enumerate(self.second_hops()):
                hop.wait_recv()
                if self.last:
                    self.add(2 * i, self.in2[i])
                else:
                    self.out[i] = (self.held[2 * i].astype(F32) + self.in2[i].astype(F32)).astype(BF)
            if self.last:
                self.settle()
                self.settle(False)
        elif k == END:
            if self.last:
                self.close()
            for hop in self.first_hops() + self.second_hops():
                hop.wait_send()

    def settle(self, outer=True):
        if outer:

            @pl.when(self.p.plain)
            def _():
                self.to_partner().start()

        now = self.p.outer if outer else jnp.logical_not(self.p.outer)

        @pl.when(now & jnp.logical_not(self.p.plain))
        def _():
            self.to_owner(0).start()
            self.to_owner(1).start()

    def close(self):
        p = self.p
        self.to_owner(0).wait_recv()

        @pl.when(p.plain)
        def _():
            self.out[...] = self.own(p.c).astype(F32) + self.in3[0].astype(F32)
            self.to_partner().wait_send()

        @pl.when(jnp.logical_not(p.plain))
        def _():
            self.to_partner().wait_recv()
            self.out[...] = self.in3[1].astype(F32) + self.in3[0].astype(F32)
            self.to_owner(0).wait_send()
            self.to_owner(1).wait_send()

    def own(self, a):
        return self.held[2 * a]


class Settle(Reduce):
    def __init__(self, sums, at):
        _, rows, cols = sums.shape
        self.at = at
        self.ins = [sums]
        self.outs = [shaped((rows, cols), F32)]
        self.out_specs = [INV]
        self.scratch = [pltpu.VMEM((rows, cols), BF), pltpu.VMEM((2, rows, cols), BF), DMA((9,)), DMA((8,)), DMA((1,))]

    def bind(self, ins, outs, scratch):
        (self.sums,), (self.out,) = ins, outs
        self.kept, self.in3, self.sent, self.come, self.sem = scratch
        self.p = Place()

    def greets(self):
        return Place.ENDS

    def fin(self, a):
        return self.sums.at[a]

    def own(self, a):
        return self.kept[...]

    def load(self):
        return pltpu.make_async_copy(self.sums.at[self.p.c], self.kept, self.sem.at[0])

    def step(self, k):
        if k == 0:
            self.load().start()
            self.settle()
        elif k == 1:
            self.settle(False)
        elif k == END:
            self.load().wait()
            self.close()


class Background:
    def __init__(self, tasks, greets):
        self.tasks, self.done, names = tasks, [], list(greets)
        for task in tasks:
            names += [name for name in task.greets() if name not in names]
        place = Place()
        self.others = [place.called(name) for name in names]

    def step(self, k):
        for i in range(max([len(task.at) for task in self.tasks], default=0)):
            for task in self.tasks:
                if i < len(task.at) and task.at[i] == k:
                    task.step(i)

    def finish(self, tasks=None):
        for task in self.tasks if tasks is None else tasks:
            if task not in self.done:
                task.step(END)
                self.done.append(task)


def hosted(kernel, ident, name, ins, in_specs, outs, out_specs, scratch, tasks, flops, traffic, greets=()):
    groups = ([], [], [])
    for group, own in zip(groups, (ins, outs, scratch)):
        group.append(len(own))
    ins, in_specs, outs, out_specs, scratch = list(ins), list(in_specs), list(outs), list(out_specs), list(scratch)
    for task in tasks:
        for group, more in zip(groups, (task.ins, task.outs, task.scratch)):
            group.append(len(more))
        ins += task.ins
        in_specs += getattr(task, "in_specs", [HBM] * len(task.ins))
        outs += task.outs
        out_specs += task.out_specs
        scratch += task.scratch

    def split(refs, counts):
        at, found = 0, []
        for count in counts:
            found.append(refs[at : at + count])
            at += count
        return found

    def body(*refs):
        parts = [split(part, group) for part, group in zip(split(refs, [sum(g) for g in groups]), groups)]
        for task, *mine in zip(tasks, *(part[1:] for part in parts)):
            task.bind(*mine)
        kernel(*parts[0][0], *parts[1][0], *parts[2][0], Background(tasks, greets))

    aliases, at_in, at_out = {}, groups[0][0], groups[1][0]
    for task in tasks:
        if getattr(task, "in_place", False):
            aliases[at_in] = at_out
        at_in += len(task.ins)
        at_out += len(task.outs)
    results = pl.pallas_call(
        body,
        out_shape=tuple(outs),
        in_specs=in_specs,
        out_specs=tuple(out_specs),
        scratch_shapes=scratch,
        input_output_aliases=aliases,
        compiler_params=params(ident),
        cost_estimate=pl.CostEstimate(flops=flops, bytes_accessed=traffic, transcendentals=0),
        name=name,
    )(*ins)
    results = split(list(results), groups[1])
    return results[0], [r[0] for r in results[1:] if r]


def put_rows(scratch, first, value, cols=slice(None)):
    tall = scratch.shape[1]
    done = 0
    while done < value.shape[0]:
        piece, at = divmod(first + done, tall)
        count = min(tall - at, value.shape[0] - done)
        scratch[piece, pl.ds(at, count), cols] = value[done : done + count]
        done += count


def put_columns(scratch, first, value):
    wide_piece = scratch.shape[2]
    for piece in range(scratch.shape[0]):
        scratch[piece, pl.ds(first, value.shape[0]), :] = value[:, piece * wide_piece : (piece + 1) * wide_piece]


def column_loads(pieces, whole):
    each = pieces.shape[2]
    return [(pieces.at[i], whole.at[:, pl.ds(i * each, each)]) for i in range(pieces.shape[0])]


def ffn_forward_kernel(
    h_ref, gain_ref, w_hbm, v_hbm, out_ref, n_hbm, u_hbm,
    w, v, nf, u, act, tpart, mine, n_near, n_over, n_on, o_near, i_near, o_over, i_over, s_near, s_over,
    wsem, osem, bg,
):
    g = Group(bg.others)
    g.greet()
    size, width = h_ref.shape
    hidden = v.shape[0]
    loads = start_all([(w_hbm, w)] + column_loads(v_hbm, v), wsem)
    gather = Gather(g, nf, size, n_near, n_over, n_on)
    scatter = Scatter(g, o_near, i_near, o_over, i_over, s_near, s_over, size)
    parts, step = gather.parts, gather.step
    for p in range(parts):
        nf[at_rows(g.mine, size, p * step, step), :] = normalise(
            h_ref[pl.ds(p * step, step), :], gain_ref[...]
        ).astype(BF)
    g.meet()
    gather.start()
    bg.step(0)
    wait_all(loads)

    third = hidden // 3

    def rows_of(places):
        return jnp.concatenate([nf[r, :] for r, _ in places], axis=0) if len(places) > 1 else nf[places[0][0], :]

    def up(places):
        def body(t, carry):
            x = rows_of(places)
            cols, more = lanes(t * third, third), lanes(hidden + t * third, third)
            both = mm(x, jnp.concatenate([w[:, cols], w[:, more]], axis=1))
            gate, upper = both[:, :third], both[:, third:]
            a = gate * jax.nn.sigmoid(gate) * upper
            act[:, cols] = a.astype(BF)
            at = 0
            for r, count in places:
                u[r, cols] = gate[at : at + count].astype(BF)
                u[r, more] = upper[at : at + count].astype(BF)
                at += count
            return carry

        lax.fori_loop(0, 3, body, 0)

    def down(store):
        store(slice(None), mm(act[...], v[...]))

    def keep(index, r, count):
        return pltpu.make_async_copy(u.at[r], u_hbm.at[r], osem.at[index])

    whole = lambda block: at_rows(block, size, 0, size)
    up([(whole(g.mine), size)])
    keep(0, whole(g.mine), size).start()

    def put_mine(cols, value):
        mine[:, cols] = value

    down(put_mine)
    gather.wait_beside()
    up([(whole(g.beside), size)])
    keep(1, whole(g.beside), size).start()

    def put_beside(cols, value):
        o_near[1, :, cols] = value.astype(BF)

    down(put_beside)
    for p in range(parts):
        scatter.close(1, p).start()
    bg.step(1)
    for p in range(parts):
        gather.wait_part(p)
        gather.wait_far(p)
        r_across, r_far = at_rows(g.across, size, p * step, step), at_rows(g.far, size, p * step, step)
        up([(r_across, step), (r_far, step)])
        keep(2 + 2 * p, r_across, step).start()
        keep(3 + 2 * p, r_far, step).start()
        here = scatter.rows(p)

        def put(cols, value):
            tpart[:, cols] = value[:step]
            o_near[0, here, cols] = value[step:].astype(BF)

        down(put)
        scatter.close(0, p).start()
        scatter.close(0, p).wait_recv()
        o_over[here, :] = (tpart[...] + i_near[0, here, :].astype(F32)).astype(BF)
        scatter.link(p).start()
        bg.step(10 + p)
    n_out = pltpu.make_async_copy(nf, n_hbm, osem.at[2 + 2 * parts])
    n_out.start()
    bg.step(2)
    for p in range(parts):
        here = scatter.rows(p)
        scatter.close(1, p).wait_recv()
        scatter.link(p).wait_recv()
        out_ref[here, :] = (
            h_ref[here, :] + mine[here, :] + i_near[1, here, :].astype(F32) + i_over[here, :].astype(F32)
        )
    gather.finish()
    scatter.wait_all_sends()
    keep(0, whole(g.mine), size).wait()
    keep(1, whole(g.beside), size).wait()
    for p in range(parts):
        keep(2 + 2 * p, at_rows(g.across, size, p * step, step), step).wait()
        keep(3 + 2 * p, at_rows(g.far, size, p * step, step), step).wait()
    n_out.wait()
    bg.step(6)
    bg.finish()


def ffn_forward(h, gain, w, v, ident, tasks=(), parts=PARTS):
    size, width = h.shape
    hidden = v.shape[1]
    total = 4 * size
    return hosted(
        ffn_forward_kernel, ident, "ffn_forward", [h, gain, w, v], [INV, INV, HBM, HBM],
        [shaped((size, width), F32), shaped((total, width), BF), shaped((total, 2 * hidden), BF)], [INV, HBM, HBM],
        [
            pltpu.VMEM((width, 2 * hidden), BF), pltpu.VMEM((hidden, width), BF), pltpu.VMEM((total, width), BF),
            pltpu.VMEM((total, 2 * hidden), BF), pltpu.VMEM((size, hidden), BF),
            pltpu.VMEM((size // parts, width), F32), pltpu.VMEM((size, width), F32),
            *gather_scratch(parts), *scatter_scratch(size, width, parts), DMA((1 + v.shape[0],)), DMA((3 + 2 * parts,)),
        ],
        tasks, 6 * total * width * hidden, 2**24,
    )


def mm_tn(a, b):
    return lax.dot_general(a, b, (((0,), (0,)), ((), ())), preferred_element_type=F32)


def rms_back(dn, h, gain):
    inverse = lax.rsqrt(jnp.mean(h * h, axis=-1, keepdims=True) + epsilon)
    scaled = dn * gain
    inner = jnp.mean(scaled * h, axis=-1, keepdims=True)
    grad_gain = jnp.sum(dn * h * inverse, axis=0, keepdims=True)
    return inverse * scaled - h * (inverse * inverse * inverse * inner), grad_gain


def close_scatter(scatter, mine, dh_ref, h_ref, gain_ref, out_ref, gg_ref):
    gg_ref[...] = jnp.zeros_like(gg_ref)
    for p in range(scatter.parts):
        here = scatter.rows(p)
        scatter.close(1, p).wait_recv()
        scatter.link(p).wait_recv()
        dn = mine[here, :] + scatter.in_near[1, here, :].astype(F32) + scatter.in_over[here, :].astype(F32)
        term, grad_gain = rms_back(dn, h_ref[here, :], gain_ref[...])
        out_ref[here, :] = dh_ref[here, :].astype(F32) + term
        gg_ref[...] += grad_gain


def ffn_backward_kernel(
    known, dh_ref, h_ref, gain_ref, df_hbm, w_hbm, v_hbm, n_hbm, u_hbm, out_ref, gg_ref, gw_hbm, gv_hbm,
    w, v, nf, u, act, df, tpart, mine, gw, gv, n_near, n_over, n_on, o_near, i_near, o_over, i_over, s_near, s_over,
    wsem, osem, bg,
):
    g = Group(bg.others)
    g.greet()
    size, width = h_ref.shape
    hidden = v.shape[0]
    loads = column_loads(v_hbm, v) + [(u_hbm, u), (w_hbm, w), (n_hbm, nf)]
    loads = start_all(loads + [(df_hbm, df)] if known else loads, wsem)
    gather = Gather(g, df, size, n_near, n_over, n_on)
    scatter = Scatter(g, o_near, i_near, o_over, i_over, s_near, s_over, size)
    parts, step = gather.parts, gather.step
    if not known:
        df[at_rows(g.mine, size, 0, size), :] = dh_ref[...].astype(BF)
    g.meet()
    if not known:
        gather.start()
    bg.step(0)
    wait_all(loads)

    third = hidden // 3

    def cat(ref, places, cols):
        found = [ref[r, cols] for r, _ in places]
        return found[0] if len(found) == 1 else jnp.concatenate(found, axis=0)

    def first(places):
        def body(t, carry):
            cols, more = lanes(t * third, third), lanes(hidden + t * third, third)
            da = mm_nt(cat(df, places, slice(None)), v[cols, :])
            gate, upper = cat(u, places, cols).astype(F32), cat(u, places, more).astype(F32)
            s = jax.nn.sigmoid(gate)
            lit = gate * s
            dgate = (da * upper * s * (1.0 + gate * (1.0 - s))).astype(BF)
            dupper = (da * lit).astype(BF)
            a = (lit * upper).astype(BF)
            at = 0
            for r, count in places:
                u[r, cols] = dgate[at : at + count]
                u[r, more] = dupper[at : at + count]
                act[r, cols] = a[at : at + count]
                at += count
            return carry

        lax.fori_loop(0, 3, body, 0)

    def second(places, store):
        def body(t, carry):
            cols = lanes(t * 512, 512)
            store(cols, mm_nt(cat(u, places, slice(None)), w[cols, :]))
            return carry

        lax.fori_loop(0, width // 512, body, 0)

    whole = lambda block: [(at_rows(block, size, 0, size), size)]

    def put_mine(cols, value):
        mine[:, cols] = value

    def put_beside(cols, value):
        o_near[1, :, cols] = value.astype(BF)

    def own():
        first(whole(g.mine))
        second(whole(g.mine), put_mine)

    def beside():
        first(whole(g.beside))
        second(whole(g.beside), put_beside)
        for p in range(parts):
            scatter.close(1, p).start()

    if not known:
        own()
        gather.wait_beside()
        beside()
    bg.step(1)
    for p in range(parts):
        if not known:
            gather.wait_part(p)
            gather.wait_far(p)
        pair = [(at_rows(b, size, p * step, step), step) for b in (g.across, g.far)]
        first(pair)
        here = scatter.rows(p)

        def put(cols, value):
            tpart[:, cols] = value[:step]
            o_near[0, here, cols] = value[step:].astype(BF)

        second(pair, put)
        scatter.close(0, p).start()
        scatter.close(0, p).wait_recv()
        o_over[here, :] = (tpart[...] + i_near[0, here, :].astype(F32)).astype(BF)
        scatter.link(p).start()
    bg.step(2)
    if known:
        beside()
        own()
    for t in range(3):
        put_columns(gv, t * third, mm_tn(act[:, t * third : (t + 1) * third], df[...]).astype(BF))
    save = pltpu.make_async_copy(gv, gv_hbm, osem.at[2])
    save.start()
    bg.step(3)
    for t in range(width // 512):
        for k in range(2):
            cols = slice(k * hidden, (k + 1) * hidden)
            put_rows(gw, t * 512, mm_tn(nf[:, t * 512 : (t + 1) * 512], u[:, cols]).astype(BF), cols)
    more = pltpu.make_async_copy(gw, gw_hbm, osem.at[0])
    more.start()
    bg.step(4)
    close_scatter(scatter, mine, df.at[at_rows(g.mine, size, 0, size)] if known else dh_ref, h_ref, gain_ref, out_ref, gg_ref)
    if not known:
        gather.finish()
    scatter.wait_all_sends()
    more.wait()
    save.wait()
    bg.step(6)
    bg.finish()


def ffn_backward(dh, h, gain, df, w, v, n, u, ident, tasks=(), parts=PARTS):
    size, width = h.shape
    pieces, hidden = v.shape[:2]
    total = 4 * size
    known = df is not None
    if known:
        dh = gain
    else:
        df = n
    return hosted(
        functools.partial(ffn_backward_kernel, known), ident, "ffn_backward", [dh, h, gain, df, w, v, n, u],
        [INV, INV, INV] + [HBM] * 5,
        [
            shaped((size, width), F32), shaped((1, width), F32), shaped((pieces, width // pieces, 2 * hidden), BF),
            shaped((pieces, hidden, width // pieces), BF),
        ],
        [INV, INV, HBM, HBM],
        [
            pltpu.VMEM((width, 2 * hidden), BF), pltpu.VMEM((hidden, width), BF), pltpu.VMEM((total, width), BF),
            pltpu.VMEM((total, 2 * hidden), BF), pltpu.VMEM((total, hidden), BF), pltpu.VMEM((total, width), BF),
            pltpu.VMEM((size // parts, width), F32), pltpu.VMEM((size, width), F32),
            pltpu.VMEM((pieces, width // pieces, 2 * hidden), BF), pltpu.VMEM((pieces, hidden, width // pieces), BF),
            *gather_scratch(parts), *scatter_scratch(size, width, parts), DMA((4 + pieces,)), DMA((3,)),
        ],
        tasks, 12 * total * width * hidden, 2**25,
    )


MOST_DOC = 512


class Columns(Gather):
    def __init__(self, group, full, near, over, onward):
        super().__init__(group, full, full.shape[0], near, over, onward)
        self.cols = full.shape[1] // 4

    def view(self, block, part):
        return self.full.at[pl.ds(part * self.step, self.step), lanes(block * self.cols, self.cols)]


def cat_rows(ref, places, cols=slice(None)):
    found = [ref[r, cols] for r, _ in places]
    return found[0] if len(found) == 1 else jnp.concatenate(found, axis=0)


def product(src, weight, turned, tile=1024):
    def run(places, store):
        width = weight.shape[0] if turned else weight.shape[1]

        def body(t, carry):
            cols = lanes(t * tile, tile)
            x = cat_rows(src, places)
            store(cols, mm_nt(x, weight[cols, :]) if turned else mm(x, weight[:, cols]))
            return carry

        lax.fori_loop(0, width // tile, body, 0)

    return run


def scatter_all(g, scatter, run, mine, tpart):
    size, step = scatter.size, scatter.step
    for p in range(scatter.parts):
        here = scatter.rows(p)

        def put(cols, value):
            tpart[:, cols] = value[:step]
            scatter.out_near[0, here, cols] = value[step:].astype(BF)

        run([(at_rows(b, size, p * step, step), step) for b in (g.across, g.far)], put)
        scatter.close(0, p).start()
        scatter.close(0, p).wait_recv()
        scatter.out_over[here, :] = (tpart[...] + scatter.in_near[0, here, :].astype(F32)).astype(BF)
        scatter.link(p).start()

    def put_beside(cols, value):
        scatter.out_near[1, :, cols] = value.astype(BF)

    run([(at_rows(g.beside, size, 0, size), size)], put_beside)
    for p in range(scatter.parts):
        scatter.close(1, p).start()

    def put_mine(cols, value):
        mine[:, cols] = value

    run([(at_rows(g.mine, size, 0, size), size)], put_mine)


def gather_everything(gather):
    gather.wait_beside()
    for p in range(gather.parts):
        gather.wait_part(p)
    for p in range(gather.parts):
        gather.wait_far(p)


def doc_starts(docs, lengths, places):
    row = lengths[pl.ds(0, 1), :]
    end = jnp.zeros((1, 1), F32)
    start = jnp.zeros_like(places)
    for d in range(docs):
        end = end + row[:, d : d + 1]
        start = jnp.where(places >= end.astype(jnp.int32), end.astype(jnp.int32), start)
    return start


def conv_taps(gated, within, taps):
    total = gated.shape[0]
    summed = taps[0] * gated
    for j in range(1, len(taps)):
        summed = summed + taps[j] * jnp.where(within >= j, pltpu.roll(gated, j, 0), 0.0)
    return summed


def conv_forward_kernel(
    docs, count, inside, lens_ref, x_hbm, gain_ref, taps_ref, win_hbm, wout_hbm,
    out_ref, block_ref, n_hbm, p_hbm, lengths, taps_out, win_out, wout_out,
    win, wout, full, nf, proj, low, mixed, tpart, mine, n_near, n_over, n_on, o_near, i_near, o_over, i_over,
    s_near, s_over, wsem, osem, xsem, xlocal, bg,
):
    g = Group(bg.others)
    g.greet()
    size, width = out_ref.shape
    total, chans = x_hbm.shape[0], wout.shape[0]
    loads = []
    if inside:
        bg.tasks[0].whole, bg.tasks[1].whole = win, wout
    else:
        loads = start_all([(win_hbm, win), (wout_hbm, wout)], wsem)
    gather = Columns(g, full, n_near, n_over, n_on)
    scatter = Scatter(g, o_near, i_near, o_over, i_over, s_near, s_over, size)
    parts = gather.parts
    blocks = [
        Exchange(
            x_hbm.at[pl.ds(p * gather.step, gather.step)],
            *(full.at[pl.ds(p * gather.step, gather.step), lanes(b * chans, chans)] for b in (g.mine, g.beside)),
            xsem, xlocal, p,
        )
        for p in range(parts)
    ]
    small = [Exchange(lens_ref, lengths, lengths, xsem, xlocal, parts), Exchange(taps_ref, taps_out, taps_out, xsem, xlocal, parts + 1)]
    g.meet()
    for block in blocks + small:
        block.start()
    bg.step(0)
    for p in range(parts):
        blocks[p].arrive()
        gather.link(p, g.mine).start()
        gather.close(p, g.mine).start()
    bg.step(1)
    gather.wait_beside()
    for p in range(parts):
        gather.wait_part(p)
    for p in range(parts):
        gather.wait_far(p)
    for block in small:
        block.arrive()
    bg.step(2)
    if inside:
        bg.finish(bg.tasks[:2])
    wait_all(loads)

    def project(t, carry):
        rows = at_rows(t, size, 0, size)
        n = normalise(full[rows, :].astype(F32), gain_ref[...]).astype(BF)
        nf[rows, :] = n
        p = mm(n, win[...])
        proj[rows, :] = p
        low[rows, :] = p.astype(BF)
        return carry

    lax.fori_loop(0, total // size, project, 0)
    bg.step(4)
    saves = start_all([(nf, n_hbm), (low, p_hbm), (win, win_out), (wout, wout_out)], osem)
    places = lax.broadcasted_iota(jnp.int32, (total, LANES), 0)
    within = places - doc_starts(docs, lengths, places)
    for k in range(chans // LANES):
        b, c, x = (proj[:, pl.ds(i * chans + k * LANES, LANES)] for i in range(3))
        taps = [taps_out[pl.ds(j, 1), pl.ds(k * LANES, LANES)] for j in range(count)]
        mixed[:, pl.ds(k * LANES, LANES)] = (c * conv_taps(b * x, within, taps)).astype(BF)
    bg.step(5)
    scatter_all(g, scatter, product(mixed, wout, False), mine, tpart)
    bg.step(3)
    block_ref[...] = full[at_rows(g.mine, size, 0, size), :]
    for p in range(scatter.parts):
        here = scatter.rows(p)
        scatter.close(1, p).wait_recv()
        scatter.link(p).wait_recv()
        out_ref[here, :] = (
            block_ref[here, :].astype(F32) + mine[here, :] + i_near[1, here, :].astype(F32) + i_over[here, :].astype(F32)
        )
    for block in blocks + small:
        block.finish()
    gather.finish()
    scatter.wait_all_sends()
    wait_all(saves)
    bg.step(6)
    bg.finish()


def conv_forward(docs, count, lens, x, gain, taps, win, wout, inside, ident, tasks=(), parts=PARTS, cuts=4):
    total, chans = x.shape
    width = wout.shape[1]
    size = total // 4
    return hosted(
        functools.partial(conv_forward_kernel, docs, count, inside), ident, "conv_forward",
        [lens, x, gain, taps, win, wout], [INV, HBM, INV, INV, HBM, HBM],
        [
            shaped((size, width), F32), shaped((size, width), BF), shaped((total, width), BF), shaped((total, 3 * chans), BF),
            shaped(lens.shape, F32), shaped(taps.shape, F32), shaped(win.shape, BF), shaped(wout.shape, BF),
        ],
        [INV, INV, HBM, HBM, INV, INV, HBM, HBM],
        [
            pltpu.VMEM((width, 3 * chans), BF), pltpu.VMEM((chans, width), BF), pltpu.VMEM((total, width), BF),
            pltpu.VMEM((total, width), BF), pltpu.VMEM((total, 3 * chans), F32), pltpu.VMEM((total, 3 * chans), BF),
            pltpu.VMEM((total, chans), BF), pltpu.VMEM((size // parts, width), F32), pltpu.VMEM((size, width), F32),
            *gather_scratch(cuts), *scatter_scratch(size, width, parts), DMA((2,)), DMA((4,)),
            DMA((2, cuts + 2)), DMA((cuts + 2,)),
        ],
        tasks, 8 * total * width * chans, 2**24, ("swap",),
    )


def conv_backward_kernel(
    docs, count, lengths, dh_ref, h_ref, gain_ref, taps_ref, win_hbm, wout_hbm, n_hbm, p_hbm, out_ref, gg_ref, gt_ref, gin_hbm, gout_hbm,
    win, wout, nf, low, dz, dy, mixed, dproj, gin, gout, tpart, mine, n_near, n_over, n_on, o_near, i_near, o_over, i_over,
    s_near, s_over, wsem, osem, bg,
):
    g = Group(bg.others)
    g.greet()
    size, width = dh_ref.shape
    total, chans = 4 * size, wout.shape[0]
    loads = start_all([(wout_hbm, wout), (p_hbm, low), (win_hbm, win), (n_hbm, nf)], wsem)
    gather = Gather(g, dz, size, n_near, n_over, n_on)
    scatter = Scatter(g, o_near, i_near, o_over, i_over, s_near, s_over, size)
    dz[at_rows(g.mine, size, 0, size), :] = dh_ref[...].astype(BF)
    g.meet()
    gather.start()
    bg.step(0)
    wait_all(loads)
    places = lax.broadcasted_iota(jnp.int32, (total, LANES), 0)
    within = places - doc_starts(docs, lengths, places)
    gather_everything(gather)
    bg.step(1)

    def project(t, carry):
        rows = at_rows(t, size, 0, size)
        dy[rows, :] = mm_nt(dz[rows, :], wout[...])
        return carry

    lax.fori_loop(0, total // size, project, 0)
    for k in range(chans // LANES):
        b, c, x = (low[:, pl.ds(i * chans + k * LANES, LANES)].astype(F32) for i in range(3))
        here = pl.ds(k * LANES, LANES)
        taps = [taps_ref[pl.ds(j, 1), here] for j in range(count)]
        gated = b * x
        summed = conv_taps(gated, within, taps)
        d = dy[:, here]
        mixed[:, here] = (c * summed).astype(BF)
        ds = d * c
        dg = taps[0] * ds
        gt_ref[pl.ds(0, 1), here] = jnp.sum(ds * gated, axis=0, keepdims=True)
        for j in range(1, len(taps)):
            masked = jnp.where(within >= j, ds, 0.0)
            dg = dg + taps[j] * pltpu.roll(masked, total - j, 0)
            gt_ref[pl.ds(j, 1), here] = jnp.sum(masked * pltpu.roll(gated, j, 0), axis=0, keepdims=True)
        dproj[:, pl.ds(k * LANES, LANES)] = (dg * x).astype(BF)
        dproj[:, pl.ds(chans + k * LANES, LANES)] = (d * summed).astype(BF)
        dproj[:, pl.ds(2 * chans + k * LANES, LANES)] = (dg * b).astype(BF)
    bg.step(2)
    scatter_all(g, scatter, product(dproj, win, True), mine, tpart)
    bg.step(3)
    put_columns(gout, 0, mm_tn(mixed[...], dz[...]).astype(BF))
    save = pltpu.make_async_copy(gout, gout_hbm, osem.at[0])
    save.start()
    for t in range(width // 256):
        put_rows(gin, t * 256, mm_tn(nf[:, pl.ds(t * 256, 256)], dproj[...]).astype(BF))
    more = pltpu.make_async_copy(gin, gin_hbm, osem.at[1])
    more.start()
    bg.step(4)
    close_scatter(scatter, mine, dh_ref, h_ref, gain_ref, out_ref, gg_ref)
    gather.finish()
    scatter.wait_all_sends()
    save.wait()
    more.wait()
    bg.step(5)
    bg.step(6)
    bg.finish()


def conv_backward(docs, count, lengths, dh, h, gain, taps, win, wout, n, p, pieces, ident, tasks=(), parts=PARTS):
    size, width = dh.shape
    total, chans = 4 * size, wout.shape[0]
    each = width // pieces
    return hosted(
        functools.partial(conv_backward_kernel, docs, count), ident, "conv_backward",
        [lengths, dh, h, gain, taps, win, wout, n, p],
        [INV, INV, INV, INV, INV, HBM, HBM, HBM, HBM],
        [
            shaped((size, width), F32), shaped((1, width), F32), shaped(taps.shape, F32),
            shaped((pieces, each, 3 * chans), BF), shaped((pieces, chans, each), BF),
        ],
        [INV, INV, INV, HBM, HBM],
        [
            pltpu.VMEM((width, 3 * chans), BF), pltpu.VMEM((chans, width), BF), pltpu.VMEM((total, width), BF),
            pltpu.VMEM((total, 3 * chans), BF), pltpu.VMEM((total, width), BF), pltpu.VMEM((total, chans), F32),
            pltpu.VMEM((total, chans), BF), pltpu.VMEM((total, 3 * chans), BF), pltpu.VMEM((pieces, each, 3 * chans), BF),
            pltpu.VMEM((pieces, chans, each), BF), pltpu.VMEM((size // parts, width), F32), pltpu.VMEM((size, width), F32),
            *gather_scratch(parts), *scatter_scratch(size, width, parts), DMA((4,)), DMA((2,)),
        ],
        tasks, 16 * total * width * chans, 2**24,
    )


def head_sums(values, head):
    width = values.shape[1]
    a = lax.broadcasted_iota(jnp.int32, (width, width), 0) // head
    b = lax.broadcasted_iota(jnp.int32, (width, width), 1) // head
    same = jnp.where(a == b, 1.0, 0.0).astype(BF)
    high = values.astype(BF)
    low = (values - high.astype(F32)).astype(BF)
    return mm(high, same) + mm(low, same)


def turn(values, head):
    width = values.shape[1]
    lane = lax.broadcasted_iota(jnp.int32, values.shape, 1)
    return jnp.where(
        lane % head < head // 2, pltpu.roll(values, width - head // 2, 1), pltpu.roll(values, head // 2, 1)
    )


def wide(table, width):
    return jnp.concatenate([table] * (width // table.shape[1]), axis=1)


def norm_turn(raw, gain, cosine, sine, head):
    inverse = lax.rsqrt(head_sums(raw * raw, head) * (1.0 / head) + epsilon)
    v = raw * inverse * gain
    return v * wide(cosine, raw.shape[1]) + turn(v, head) * wide(sine, raw.shape[1])


def norm_turn_back(d, raw, gain, cosine, sine, head):
    d = d * wide(cosine, raw.shape[1]) - turn(d, head) * wide(sine, raw.shape[1])
    inverse = lax.rsqrt(head_sums(raw * raw, head) * (1.0 / head) + epsilon)
    scaled = d * gain
    inner = head_sums(scaled * raw, head) * (1.0 / head)
    grad_gain = jnp.sum(d * raw * inverse, axis=0, keepdims=True)
    return inverse * scaled - raw * (inverse * inverse * inverse * inner), grad_gain


def score_tile(q, k, starts, first_key, first_query, scale):
    raw = mm_nt(k, q) * scale
    key = first_key + lax.broadcasted_iota(jnp.int32, raw.shape, 0)
    query = first_query + lax.broadcasted_iota(jnp.int32, (1, starts.shape[1]), 1)
    copies = raw.shape[1] // starts.shape[1]
    allowed = (key <= wide(query, raw.shape[1])) & (key >= wide(starts, raw.shape[1]))
    return jnp.where(allowed, raw, -1e30)


def softmax_tile(scores):
    top = jnp.max(scores, axis=0, keepdims=True)
    weights = jnp.exp(scores - top)
    return weights / jnp.sum(weights, axis=0, keepdims=True)


def stack_heads(values, head):
    return jnp.concatenate([values[:, i * head : (i + 1) * head] for i in range(values.shape[1] // head)], axis=0)


def attention_tiles(total, tile):
    back = -(-MOST_DOC // tile)
    return [(i * tile, max(0, i - back) * tile, (i + 1) * tile) for i in range(total // tile)]


def attention_forward_kernel(
    head, docs, lengths, h_ref, gain_ref, qgain_ref, kgain_ref, speed_ref, wq_hbm, wkv_hbm, wo_hbm,
    out_ref, n_hbm, raw_hbm, ready_hbm, o_hbm, cos_ref, sin_ref,
    w, wo, nf, low, ready, vt, o, tpart, mine, n_near, n_over, n_on, o_near, i_near, o_over, i_over,
    s_near, s_over, wsem, osem, bg,
):
    g = Group(bg.others)
    g.greet()
    size, width = h_ref.shape
    total, qw = 4 * size, wo.shape[0]
    kw = (w.shape[1] - qw) // 2
    loads = start_all([(wq_hbm, w.at[:, pl.ds(0, qw)]), (wkv_hbm, w.at[:, pl.ds(qw, 2 * kw)]), (wo_hbm, wo)], wsem)
    gather = Gather(g, nf, size, n_near, n_over, n_on)
    scatter = Scatter(g, o_near, i_near, o_over, i_over, s_near, s_over, size)
    parts, step = gather.parts, gather.step
    nf[at_rows(g.mine, size, 0, size), :] = normalise(h_ref[...], gain_ref[...]).astype(BF)
    g.meet()
    gather.start()
    bg.step(0)
    places = lax.broadcasted_iota(jnp.int32, (total, LANES), 0)
    angles = (places - doc_starts(docs, lengths, places)).astype(F32) * speed_ref[...]
    lane = lax.broadcasted_iota(jnp.int32, (total, LANES), 1)
    sine = jnp.sin(angles)
    cos_ref[...] = jnp.cos(angles)
    sin_ref[...] = jnp.where(lane % head < head // 2, -sine, sine)
    wait_all(loads)

    def project(block):
        rows = at_rows(block, size, 0, size)
        raw = mm(nf[rows, :], w[...])
        low[rows, :] = raw.astype(BF)
        cosine, sine = cos_ref[rows, :], sin_ref[rows, :]
        ready[rows, pl.ds(0, qw)] = norm_turn(raw[:, :qw], qgain_ref[...], cosine, sine, head).astype(BF)
        ready[rows, pl.ds(qw, kw)] = norm_turn(raw[:, qw : qw + kw], kgain_ref[...], cosine, sine, head).astype(BF)
        ready[rows, pl.ds(qw + kw, kw)] = raw[:, qw + kw :].astype(BF)

    project(g.mine)
    gather.wait_beside()
    project(g.beside)
    for p in range(parts):
        gather.wait_part(p)
    for p in range(parts):
        gather.wait_far(p)

    def rest(i, carry):
        project(jnp.where(i == 0, g.across, g.far))
        return carry

    lax.fori_loop(0, 2, rest, 0)
    bg.step(1)
    saves = start_all([(nf, n_hbm), (low, raw_hbm), (ready, ready_hbm)], osem)
    vt[...] = jnp.transpose(ready[:, pl.ds(qw + kw, kw)].astype(F32)).astype(BF)
    groups = qw // kw
    tile = 256
    scale = head ** (-0.5)
    starts = doc_starts(docs, lengths, lax.broadcasted_iota(jnp.int32, (1, total), 1))
    for first, low_key, high_key in attention_tiles(total, tile):
        keys = pl.ds(low_key, high_key - low_key)
        for kv in range(kw // head):
            q = stack_heads(ready[pl.ds(first, tile), pl.ds(kv * groups * head, groups * head)], head)
            k = ready[keys, pl.ds(qw, kw)][:, kv * head : (kv + 1) * head]
            p = softmax_tile(score_tile(q, k, starts[:, first : first + tile], low_key, first, scale)).astype(BF)
            ot = mm(vt[pl.ds(kv * head, head), keys], p)
            joined = jnp.concatenate([ot[:, i * tile : (i + 1) * tile] for i in range(groups)], axis=0)
            o[pl.ds(first, tile), pl.ds(kv * groups * head, groups * head)] = jnp.transpose(joined).astype(BF)
        if first == tile:
            bg.step(2)
    bg.step(3)
    save_o = pltpu.make_async_copy(o, o_hbm, osem.at[3])
    save_o.start()
    scatter_all(g, scatter, product(o, wo, False), mine, tpart)
    bg.step(4)
    for p in range(parts):
        here = scatter.rows(p)
        scatter.close(1, p).wait_recv()
        scatter.link(p).wait_recv()
        out_ref[here, :] = (
            h_ref[here, :] + mine[here, :] + i_near[1, here, :].astype(F32) + i_over[here, :].astype(F32)
        )
    gather.finish()
    scatter.wait_all_sends()
    wait_all(saves)
    save_o.wait()
    bg.step(6)
    bg.finish()


def attention_forward(head, docs, lengths, h, gain, qgain, kgain, speed, wq, wkv, wo, ident, tasks=(), parts=PARTS):
    size, width = h.shape
    total, qw = 4 * size, wo.shape[0]
    kw = wkv.shape[1] // 2
    every = qw + 2 * kw
    return hosted(
        functools.partial(attention_forward_kernel, head, docs), ident, "attention_forward",
        [lengths, h, gain, qgain, kgain, speed, wq, wkv, wo], [INV] * 6 + [HBM] * 3,
        [
            shaped((size, width), F32), shaped((total, width), BF), shaped((total, every), BF), shaped((total, every), BF),
            shaped((total, qw), BF), shaped((total, LANES), F32), shaped((total, LANES), F32),
        ],
        [INV] + [HBM] * 4 + [INV] * 2,
        [
            pltpu.VMEM((width, every), BF), pltpu.VMEM((qw, width), BF), pltpu.VMEM((total, width), BF),
            pltpu.VMEM((total, every), BF), pltpu.VMEM((total, every), BF),
            pltpu.VMEM((kw, total), BF), pltpu.VMEM((total, qw), BF),
            pltpu.VMEM((size // parts, width), F32), pltpu.VMEM((size, width), F32),
            *gather_scratch(parts), *scatter_scratch(size, width, parts), DMA((3,)), DMA((4,)),
        ],
        tasks, 2 * total * width * (every + qw), 2**24,
    )


def attention_backward_kernel(
    head, docs, lengths, dh_ref, h_ref, gain_ref, qgain_ref, kgain_ref, cos_ref, sin_ref, wq_hbm, wkv_hbm, wo_hbm,
    n_hbm, raw_hbm, ready_hbm, o_hbm, out_ref, gg_ref, gq_ref, gk_ref, gw_hbm, gwo_hbm,
    w, wo, nf, low, ready, kt, o, dz, do, dq, dkv, dlow, gw, gwo, tpart, mine,
    n_near, n_over, n_on, o_near, i_near, o_over, i_over, s_near, s_over, wsem, osem, bg,
):
    g = Group(bg.others)
    g.greet()
    size, width = h_ref.shape
    total, qw = 4 * size, wo.shape[0]
    kw = (w.shape[1] - qw) // 2
    loads = start_all(
        [
            (ready_hbm, ready), (wo_hbm, wo), (o_hbm, o), (raw_hbm, low), (wq_hbm, w.at[:, pl.ds(0, qw)]),
            (wkv_hbm, w.at[:, pl.ds(qw, 2 * kw)]), (n_hbm, nf),
        ],
        wsem,
    )
    gather = Gather(g, dz, size, n_near, n_over, n_on)
    scatter = Scatter(g, o_near, i_near, o_over, i_over, s_near, s_over, size)
    dz[at_rows(g.mine, size, 0, size), :] = dh_ref[...].astype(BF)
    g.meet()
    gather.start()
    bg.step(0)
    wait_all(loads)
    kt[...] = jnp.transpose(ready[:, pl.ds(qw, kw)].astype(F32)).astype(BF)
    dkv[...] = jnp.zeros_like(dkv)
    gather_everything(gather)

    def project(t, carry):
        rows = at_rows(t, size, 0, size)
        do[rows, :] = mm_nt(dz[rows, :], wo[...]).astype(BF)
        return carry

    bg.step(1)

    lax.fori_loop(0, total // size, project, 0)
    groups = qw // kw
    tile = 256
    scale = head ** (-0.5)
    starts = doc_starts(docs, lengths, lax.broadcasted_iota(jnp.int32, (1, total), 1))
    for first, low_key, high_key in attention_tiles(total, tile):
        keys = pl.ds(low_key, high_key - low_key)
        for kv in range(kw // head):
            cols = pl.ds(kv * groups * head, groups * head)
            lane = slice(kv * head, (kv + 1) * head)
            q = stack_heads(ready[pl.ds(first, tile), cols], head)
            k, v = ready[keys, pl.ds(qw, kw)][:, lane], ready[keys, pl.ds(qw + kw, kw)][:, lane]
            p = softmax_tile(score_tile(q, k, starts[:, first : first + tile], low_key, first, scale))
            d = stack_heads(do[pl.ds(first, tile), cols], head)
            dp = mm_nt(v, d)
            inner = jnp.sum(p * dp, axis=0, keepdims=True)
            ds = (p * (dp - inner)).astype(BF)
            both = jnp.concatenate([mm(ds, q) * scale, mm(p.astype(BF), d)], axis=1)
            dkv[kv, keys, :] += both
            dqt = mm(kt[pl.ds(kv * head, head), keys], ds) * scale
            joined = jnp.concatenate([dqt[:, i * tile : (i + 1) * tile] for i in range(groups)], axis=0)
            dq[pl.ds(first, tile), cols] = jnp.transpose(joined)
        if first == tile:
            bg.step(2)
        if first == 2 * tile:
            bg.step(3)
    bg.step(4)
    gq_ref[...] = jnp.zeros_like(gq_ref)
    gk_ref[...] = jnp.zeros_like(gk_ref)

    def finish(t, carry):
        rows = at_rows(t, size, 0, size)
        cosine, sine = cos_ref[rows, :], sin_ref[rows, :]
        d, gq = norm_turn_back(dq[rows, :], low[rows, pl.ds(0, qw)].astype(F32), qgain_ref[...], cosine, sine, head)
        gq_ref[...] += gq
        dlow[rows, pl.ds(0, qw)] = d.astype(BF)
        pairs = [dkv[kv, rows, :] for kv in range(kw // head)]
        dk = jnp.concatenate([x[:, :head] for x in pairs], axis=1)
        dv = jnp.concatenate([x[:, head:] for x in pairs], axis=1)
        d, gk = norm_turn_back(dk, low[rows, pl.ds(qw, kw)].astype(F32), kgain_ref[...], cosine, sine, head)
        gk_ref[...] += gk
        dlow[rows, pl.ds(qw, kw)] = d.astype(BF)
        dlow[rows, pl.ds(qw + kw, kw)] = dv.astype(BF)
        return carry

    lax.fori_loop(0, total // size, finish, 0)
    scatter_all(g, scatter, product(dlow, w, True), mine, tpart)
    put_columns(gwo, 0, mm_tn(o[...], dz[...]).astype(BF))
    save = pltpu.make_async_copy(gwo, gwo_hbm, osem.at[0])
    save.start()
    for t in range(width // 256):
        put_rows(gw, t * 256, mm_tn(nf[:, pl.ds(t * 256, 256)], dlow[...]).astype(BF))
    more = pltpu.make_async_copy(gw, gw_hbm, osem.at[1])
    more.start()
    bg.step(5)
    close_scatter(scatter, mine, dh_ref, h_ref, gain_ref, out_ref, gg_ref)
    gather.finish()
    scatter.wait_all_sends()
    save.wait()
    more.wait()
    bg.step(6)
    bg.finish()


def attention_backward(
    head, docs, lengths, dh, h, gain, qgain, kgain, cosine, sine, wq, wkv, wo, n, raw, ready, o, pieces, ident, tasks=(),
    parts=PARTS,
):
    size, width = h.shape
    total, qw = 4 * size, wo.shape[0]
    kw = wkv.shape[1] // 2
    every = qw + 2 * kw
    each = width // pieces
    return hosted(
        functools.partial(attention_backward_kernel, head, docs), ident, "attention_backward",
        [lengths, dh, h, gain, qgain, kgain, cosine, sine, wq, wkv, wo, n, raw, ready, o], [INV] * 8 + [HBM] * 7,
        [
            shaped((size, width), F32), shaped((1, width), F32), shaped((1, qw), F32), shaped((1, kw), F32),
            shaped((pieces, each, every), BF), shaped((pieces, qw, each), BF),
        ],
        [INV, INV, INV, INV, HBM, HBM],
        [
            pltpu.VMEM((width, every), BF), pltpu.VMEM((qw, width), BF), pltpu.VMEM((total, width), BF),
            pltpu.VMEM((total, every), BF), pltpu.VMEM((total, every), BF), pltpu.VMEM((kw, total), BF),
            pltpu.VMEM((total, qw), BF), pltpu.VMEM((total, width), BF), pltpu.VMEM((total, qw), BF),
            pltpu.VMEM((total, qw), F32), pltpu.VMEM((kw // head, total, 2 * head), F32), pltpu.VMEM((total, every), BF),
            pltpu.VMEM((pieces, each, every), BF), pltpu.VMEM((pieces, qw, each), BF),
            pltpu.VMEM((size // parts, width), F32), pltpu.VMEM((size, width), F32),
            *gather_scratch(parts), *scatter_scratch(size, width, parts), DMA((7,)), DMA((2,)),
        ],
        tasks, 4 * total * width * (every + qw), 2**25,
    )


def tail_kernel(bg):
    g = Group(bg.others)
    g.greet()
    g.meet()
    for k in range(4):
        bg.step(k)
    bg.step(6)
    bg.finish()


def tail(ident, tasks):
    return hosted(tail_kernel, ident, "tail", [], [], [], [], [], tasks, 0, 2**22)[1]


rope_base = 1000000.0
TP = ("c", "zl")
DP = ("r", "s", "zh")


def rope_speeds(head_dim):
    half_dim = head_dim // 2
    inverse = rope_base ** (-2.0 * jnp.arange(half_dim, dtype=F32) / head_dim)
    return jnp.tile(inverse, LANES // half_dim)[None]


def swap(x):
    return lax.ppermute(x, ("c", "zh"), [(0, 0), (1, 2), (2, 1), (3, 3)])


def gather_dp(shard, axis):
    return lax.all_gather(swap(shard), DP, axis=axis, tiled=True)


def scatter_dp(partial, axis):
    return swap(lax.psum_scatter(partial, DP, scatter_dimension=axis, tiled=True)).astype(F32)


def local(
    planes, tokens, doc_lengths, grad_out, norm_gains, head_gains, conv_in, conv_kernel, conv_out,
    query_w, kv_w, out_w, gate_up, down,
):
    length = tokens.shape[0]
    head_dim = head_gains.shape[1]
    docs, count = doc_lengths.shape[1], conv_kernel.shape[0]
    conv_in = conv_in.reshape(conv_in.shape[0], -1)
    kv_w = kv_w.reshape(kv_w.shape[0], -1)
    own_w = gate_up.reshape(*gate_up.shape[:2], -1)
    pieces = 8 if planes else 1
    kv_width = kv_w.shape[1] // 2
    qgain = jnp.tile(head_gains[0:1], (1, query_w.shape[1] // head_dim))
    kgain = jnp.tile(head_gains[1:2], (1, kv_width // head_dim))
    gain = [norm_gains[i : i + 1] for i in range(4)]
    lens = jnp.pad(doc_lengths.astype(F32), ((0, 7), (0, LANES - docs)))
    taps = jnp.pad(conv_kernel, ((0, 8 - count), (0, 0)))
    rows_of = lambda got: got.reshape(-1, got.shape[-1])
    if planes:
        first = [Take(conv_in, (0, 0, 0, 2, 2), True), Take(conv_out, (0, 0, 0, 2, 2), True)]
        first += [Fetch(own_w, (0, 1, 1, 2, 2, 4, 5), 2, 0, 0), Fetch(down, (0, 1, 1, 2, 5, 3), 1, 0, 0)]
        second = [Take(x, (0, 0, 0, 2, 2)) for x in (query_w, kv_w, out_w)]
        second += [Fetch(own_w, (0, 0, 0, 2), 1, 1, 1), Fetch(down, (0, 0, 0, 2), 1, 1, 1)]
    else:
        first, second, third = [], [], []
        conv_in, conv_out, query_w, kv_w, out_w = map(swap, (conv_in, conv_out, query_w, kv_w, out_w))
        w0, w1 = (gather_dp(w, 0) for w in own_w)
        v0, v1 = (gather_dp(v, 1)[None] for v in down)

    (h1, x_block, n0, projected, lens, taps, conv_in, conv_out), got = conv_forward(
        docs, count, lens, tokens, gain[0], taps, conv_in, conv_out, planes, 0, first
    )
    if planes:
        w0, v0 = rows_of(got[0]), got[1]
    (h2, n1, hidden0), got = ffn_forward(h1, gain[1], w0, v0, 1, second)
    if planes:
        query_w, kv_w, out_w = got[:3]
        third = [Fetch(got[3], (0, 4), 2, 2), Fetch(got[4], (0, 4), 1, 2)]
    (h3, n2, raw, ready, attended, cosine, sine), got = attention_forward(
        head_dim, docs, lens, h2, gain[2], qgain, kgain, rope_speeds(head_dim), query_w, kv_w, out_w, 2, third
    )
    if planes:
        w1, v1 = rows_of(got[0]), got[1]
    (h4, n3, hidden1), (up_full,) = ffn_forward(h3, gain[3], w1, v1, 3, [Spread(grad_out, (0, 1, 2))])

    def halves(grad, first, second, last=False):
        half = grad.shape[1] // 2
        return [Reduce(grad, 0, half, first, last), Reduce(grad, half, half, second, False)] if planes else []

    def whole(grad, at, last=False):
        return [Reduce(grad, 0, grad.shape[1], at, last)] if planes else []

    def settled(sums, at):
        return [Settle(x, at) for x in sums]

    (dh3, gain3, gw1, gv1), (output,) = ffn_backward(
        None, h3, gain[3], up_full, w1, v1, n3, hidden1, 4, [Deliver(h4, (0, 2))]
    )
    (dh2, gain2, gq, gk, gqkv, gow), sums = attention_backward(
        head_dim, docs, lens, dh3, h2, gain[2], qgain, kgain, cosine, sine, query_w, kv_w, out_w, n2, raw, ready, attended,
        pieces, 5, halves(gw1, (0, 2, 5), (0, 4, 6)),
    )
    (dh1, gain1, gw0, gv0), got = ffn_backward(
        dh2, h1, gain[1], None, w0, v0, n1, hidden0, 6,
        settled(sums, (0, 0)) + whole(gv1, (0, 1, 2)) + whole(gqkv, (0, 2, 3)) + whole(gow, (0, 2, 3)),
    )
    sums_w1, sums = got[:2], got[2:]
    (dh0, gain0, gtaps, gci, gco), got = conv_backward(
        docs, count, lens, dh1, x_block.astype(F32), gain[0], taps, conv_in, conv_out, n0, projected, pieces, 7,
        settled(sums, (0, 0)) + halves(gw0, (0, 1, 4), (0, 3, 6), True),
    )
    others, first_w0, sums = got[:3], got[3:4], got[4:]
    totals, grads, *got = tail(
        8,
        [Total([gain0, gain1, gain2, gain3, gtaps, gq, gk], (0, 1, 2, 3), count, ("zh", "s", *(("r",) if planes else ()), "zl", "c")), Deliver(dh0, (0, 0))]
        + settled(sums, (0, 0)) + whole(gv0, (0, 0, 1), True) + whole(gci, (1, 2, 3), True) + whole(gco, (1, 2, 3), True),
    )
    if planes:
        gv1, gqkv, gow = others
        gate_ups = [*first_w0, got[0], *sums_w1]
        gv0, gci, gco = got[1:]
    else:
        totals = lax.psum(totals, "r")
        gw0, gw1, gci, gqkv = (scatter_dp(g[0], 0) for g in (gw0, gw1, gci, gqkv))
        gv0, gv1, gco, gow = (scatter_dp(g[0], 1) for g in (gv0, gv1, gco, gow))
        gate_ups = [gw0, gw1]
    heads = totals[7, : gq.shape[1] + gk.shape[1]].reshape(-1, head_dim)
    split = gq.shape[1] // head_dim
    return (
        output,
        grads.astype(F32),
        totals[:4],
        jnp.stack([jnp.sum(heads[:split], axis=0), jnp.sum(heads[split:], axis=0)]),
        gci.reshape(-1, 3, conv_kernel.shape[1]),
        totals[4 : 4 + count],
        gco,
        gqkv[:, : query_w.shape[1]],
        gqkv[:, query_w.shape[1] :].reshape(-1, 2, kv_width),
        gow,
        jnp.concatenate(gate_ups, axis=0).reshape(2, gate_up.shape[1], 2, -1),
        jnp.stack([gv0, gv1]),
    )


def solution(mesh):
    devices = mesh.devices
    dp, tp = devices.shape
    inner = Mesh(devices.reshape(dp // 4, 2, 2, 2, tp // 2), ("r", "s", "c", "zh", "zl"))
    D = ("r", "s", "c")
    T = ("zh", "zl")
    return jax.shard_map(
        functools.partial(local, dp == 8),
        mesh=inner,
        in_specs=(
            P(D, T), P(D, None), P(D, T), P(), P(), P(None, None, T), P(None, T), P(T, None),
            P(None, T), P(None, None, T), P(T, None), P(None, D, None, T), P(None, T, D),
        ),
        out_specs=(
            P(D, T), P(D, T), P(), P(), P(D, None, T), P(), P(T, D), P(D, T), P(D, None, T),
            P(T, D), P(None, D, None, T), P(None, T, D),
        ),
        check_vma=False,
    )
```

```python
import functools
import jax
import jax.numpy as jnp
from jax import lax
from jax.experimental import pallas as pl
from jax.experimental.pallas import tpu as pltpu
from jax.sharding import Mesh, PartitionSpec as P

epsilon = 1e-05
BF = jnp.bfloat16
F32 = jnp.float32
MESH = pl.DeviceIdType.MESH
DMA = pltpu.SemaphoreType.DMA
HBM = pl.BlockSpec(memory_space=pl.ANY)
INV = pl.BlockSpec(memory_space=pltpu.VMEM)
PARTS = 2
LANES = 128


class Group:
    def __init__(self, others=(), calls=True):
        c, z = lax.axis_index("c"), lax.axis_index("zl")
        self.partner, self.twin = {"c": 1 - c}, {"zl": 1 - z}
        self.mine, self.beside = 2 * c + z, 2 * (1 - c) + z
        self.across, self.far = 2 * c + (1 - z), 2 * (1 - c) + (1 - z)
        self.known = [self.partner, self.twin, *others]
        self.c, self.z = c, z
        self.barrier = pltpu.get_barrier_semaphore() if calls else None

    def greet(self):
        for other in self.known:
            pl.semaphore_signal(self.barrier, inc=1, device_id=other, device_id_type=MESH)

    def meet(self):
        pl.semaphore_wait(self.barrier, len(self.known))


def at_rows(block, size, start, count):
    return pl.ds(pl.multiple_of(block * size + start, 16), count)


def send(src, dst, sems, index, where):
    return pltpu.make_async_remote_copy(
        src_ref=src, dst_ref=dst, send_sem=sems.at[0, index], recv_sem=sems.at[1, index],
        device_id=where, device_id_type=MESH,
    )


class Gather:
    def __init__(self, group, full, size, near, over, onward):
        self.g, self.full, self.size, self.parts = group, full, size, over.shape[1]
        self.near, self.over, self.onward = near, over, onward
        self.step = size // self.parts

    def view(self, block, part):
        return self.full.at[at_rows(block, self.size, part * self.step, self.step)]

    def link(self, part, block):
        v = self.view(block, part)
        return send(v, v, self.over, part, self.g.twin)

    def close(self, part, block):
        v = self.view(block, part)
        return send(v, v, self.near, part, self.g.partner)

    def pass_on(self, part, block):
        v = self.view(block, part)
        return send(v, v, self.onward, part, self.g.partner)

    def start(self):
        for p in range(self.parts):
            self.link(p, self.g.mine).start()
            self.close(p, self.g.mine).start()

    def wait_beside(self):
        for p in range(self.parts):
            self.close(p, self.g.beside).wait_recv()

    def wait_part(self, p):
        self.link(p, self.g.across).wait_recv()
        self.pass_on(p, self.g.across).start()

    def wait_far(self, p):
        self.pass_on(p, self.g.far).wait_recv()

    def finish(self):
        for p in range(self.parts):
            self.link(p, self.g.mine).wait_send()
            self.close(p, self.g.mine).wait_send()
            self.pass_on(p, self.g.across).wait_send()


class Scatter:
    def __init__(self, group, out_near, in_near, out_over, in_over, near, over, size):
        self.g, self.size, self.parts = group, size, over.shape[1]
        self.out_near, self.in_near, self.out_over, self.in_over = out_near, in_near, out_over, in_over
        self.near, self.over = near, over
        self.step = size // self.parts

    def rows(self, part):
        return pl.ds(part * self.step, self.step)

    def close(self, which, part):
        r = self.rows(part)
        return send(self.out_near.at[which, r], self.in_near.at[which, r], self.near, which * self.parts + part, self.g.partner)

    def link(self, part):
        r = self.rows(part)
        return send(self.out_over.at[r], self.in_over.at[r], self.over, part, self.g.twin)

    def wait_all_sends(self):
        for p in range(self.parts):
            self.close(0, p).wait_send()
            self.close(1, p).wait_send()
            self.link(p).wait_send()


def scatter_scratch(size, width, parts):
    return [
        pltpu.VMEM((2, size, width), BF), pltpu.VMEM((2, size, width), BF), pltpu.VMEM((size, width), BF),
        pltpu.VMEM((size, width), BF), DMA((2, 2 * parts)), DMA((2, parts)),
    ]


def gather_scratch(parts):
    return [DMA((2, parts)), DMA((2, parts)), DMA((2, parts))]


def normalise(h, gain):
    return h * lax.rsqrt(jnp.mean(h * h, axis=-1, keepdims=True) + epsilon) * gain


def mm(a, b):
    return jnp.dot(a, b, preferred_element_type=F32)


def mm_nt(a, b):
    return lax.dot_general(a, b, (((1,), (1,)), ((), ())), preferred_element_type=F32)


def lanes(start, width):
    return pl.ds(pl.multiple_of(start, LANES), width)


def start_all(pairs, sems):
    copies = [pltpu.make_async_copy(src, dst, sems.at[i]) for i, (src, dst) in enumerate(pairs)]
    for copy in copies:
        copy.start()
    return copies


def wait_all(copies):
    for copy in copies:
        copy.wait()


def params(ident):
    return pltpu.CompilerParams(collective_id=ident, has_side_effects=True, vmem_limit_bytes=56 * 2**20)


def shaped(shape, dtype):
    return jax.ShapeDtypeStruct(shape, dtype)


END = 99


class Place:
    def __init__(self):
        self.y, self.x, self.c, self.zh = (lax.axis_index(a) for a in ("r", "s", "c", "zh"))
        self.across_x, self.across_y = {"s": 1 - self.x}, {"r": 1 - self.y}
        self.partner = {"c": 1 - self.c}
        self.plain = self.c == self.zh
        self.outer = lax.axis_index("zl") == self.zh

    def over(self, core):
        return {"c": core, "zh": 1 - self.zh}

    def swapped(self):
        return self.over(self.zh)

    PLANES = ("x", "y")
    ENDS = ("end", "swap")
    COLUMN = ("end", "swap", "z core", "z end", "z swap")

    def called(self, name):
        z = 1 - lax.axis_index("zl")
        other, far = 1 - self.c, 1 - self.zh
        return {
            "x": self.across_x, "y": self.across_y, "end": self.over(self.c), "swap": self.over(other),
            "z core": {"c": other, "zl": z}, "z end": {"zh": far, "zl": z}, "z swap": {"c": other, "zh": far, "zl": z},
        }[name]

    def piece(self, flip_y, flip_x, a):
        y = 1 - self.y if flip_y else self.y
        x = 1 - self.x if flip_x else self.x
        return 4 * y + 2 * x + a


class Fetch:
    def __init__(self, shard, at, cuts=1, stage=0, layer=None):
        rows, cols = shard.shape[-2:]
        self.layer = layer
        self.at, self.cuts, self.stage, self.step_rows = at, cuts, stage, rows // cuts
        self.ins = [shard]
        self.outs = [jax.ShapeDtypeStruct((8, rows, cols), shard.dtype)]
        self.out_specs = [HBM]
        self.in_place = stage == 2
        self.semaphores()
        if not self.in_place:
            self.scratch.append(pltpu.VMEM((rows, cols), BF))

    def semaphores(self):
        self.scratch = [DMA((9 * self.cuts,)), DMA((8 * self.cuts,)), DMA((2,))]

    def bind(self, ins, outs, scratch):
        (self.own,), (self.out,) = ins, outs
        if self.layer is not None:
            self.own = self.own.at[self.layer]
        self.sent, self.come, self.sem = scratch[:3]
        self.bounce = scratch[3] if len(scratch) > 3 else None
        self.p = Place()

    def greets(self):
        return Place.PLANES if self.stage == 2 else Place.PLANES + Place.ENDS

    def part(self, ref, q):
        return ref.at[pl.ds(q * self.step_rows, self.step_rows)]

    def given(self, q):
        return self.part(self.own, q)

    def slot(self, piece, q):
        return self.part(self.out.at[piece], q)

    def home(self, a, q):
        return self.slot(self.p.piece(0, 0, a), q)

    def copy(self, src, dst, q, sent, come, where):
        return pltpu.make_async_remote_copy(
            src_ref=src, dst_ref=dst, send_sem=self.sent.at[9 * q + sent], recv_sem=self.come.at[8 * q + come],
            device_id=where, device_id_type=MESH,
        )

    def to_plane(self, q):
        p = self.p
        return self.copy(self.given(q), self.home(p.c, q), q, 0, p.c, p.over(p.zh))

    def to_partner(self, q):
        p = self.p
        return self.copy(self.given(q), self.home(p.c, q), q, 1, p.c, p.partner)

    def arrived(self, a, q):
        self.copy(self.given(q), self.home(a, q), q, 0, a, self.p.partner).wait_recv()

    def keep(self):
        slot = self.out.at[self.p.piece(0, 0, self.p.c)]
        return [
            pltpu.make_async_copy(self.own, self.bounce, self.sem.at[0]),
            pltpu.make_async_copy(self.bounce, slot, self.sem.at[1]),
        ]

    def kept(self):
        self.keep()[0].start()

    def land(self):
        copies = self.keep()
        for i, copy in enumerate(copies):
            if i:
                copy.start()
            copy.wait()

    def to_x(self, a, q, src=None):
        dst = self.slot(self.p.piece(0, 0, a), q)
        return self.copy(dst if src is None else src, dst, q, 2 + a, 2 + a, self.p.across_x)

    def to_y(self, a, q, src=None):
        dst = self.slot(self.p.piece(0, 0, a), q)
        return self.copy(dst if src is None else src, dst, q, 4 + a, 4 + a, self.p.across_y)

    def spread(self, a, q, src):
        self.to_x(a, q, src).start()
        self.to_y(a, q, src).start()

    def on_y(self, q):
        there = self.slot(self.p.piece(0, 1, 0), q)
        return self.copy(there, there, q, 6, 6, self.p.across_y)

    def on_x(self, q):
        there = self.slot(self.p.piece(1, 0, 1), q)
        return self.copy(there, there, q, 7, 7, self.p.across_x)

    def forward(self, q):
        self.to_x(0, q).wait_recv()
        self.on_y(q).start()
        self.to_y(1, q).wait_recv()
        self.on_x(q).start()

    def plain(self, run):
        pl.when(self.p.plain)(run)

    def other(self, run):
        pl.when(jnp.logical_not(self.p.plain))(run)

    def step(self, k):
        p, every = self.p, range(self.cuts)

        def own():
            for q in every:
                self.spread(p.c, q, self.given(q))

        def partner():
            for q in every:
                self.to_partner(q).start()

        def second():
            for q in every:
                self.arrived(1 - p.c, q)
                self.spread(1 - p.c, q, self.home(1 - p.c, q))

        def planes():
            for q in every:
                for a in (0, 1):
                    self.spread(a, q, self.home(a, q))

        def there(q):
            for a in (0, 1):
                self.arrived(a, q)
                self.spread(a, q, self.home(a, q))

        if self.stage == 2:
            if k == 0:
                self.other(planes)
            elif k == 1:
                self.other(lambda: [self.forward(q) for q in every] and None)
            elif k == END:
                self.other(self.close)
        elif k == 0:
            self.plain(self.kept)
            self.other(partner)
            self.plain(own)
            self.plain(second)
        elif k == END:
            for q in every:
                self.to_plane(q).wait_send()
            if self.stage:
                self.plain(self.close)
                self.other(lambda: [self.arrived(a, q) for q in every for a in (0, 1)] and None)
            else:
                self.close()
            self.plain(self.land)
            self.other(lambda: [self.to_partner(q).wait_send() for q in every] and None)
        elif k in (1, 2):
            self.leave(k == 1)
        elif k == 3:
            self.plain(lambda: [self.forward(q) for q in every] and None)
        elif not self.stage:
            q = k - 4
            if q < self.cuts:
                self.other(functools.partial(there, q))
            if q:
                self.other(lambda: self.forward(q - 1))

    def leave(self, outer):
        @pl.when(self.p.outer if outer else jnp.logical_not(self.p.outer))
        def _():
            for q in range(self.cuts):
                self.to_plane(q).start()

    def close(self):
        for q in range(self.cuts):
            self.to_x(1, q).wait_recv()
            self.to_y(0, q).wait_recv()
            self.on_y(q).wait()
            self.on_x(q).wait()
            for a in (0, 1):
                self.to_x(a, q).wait_send()
                self.to_y(a, q).wait_send()


class Take(Fetch):
    def __init__(self, whole, at, inside=False):
        rows, cols = whole.shape
        self.at, self.each, self.cuts, self.stage = at, rows // 8, 1, 0
        self.ins = [whole]
        self.outs = [] if inside else [jax.ShapeDtypeStruct((rows, cols), whole.dtype)]
        self.out_specs = [] if inside else [HBM]
        self.in_place = False
        self.semaphores()
        if not inside:
            self.scratch.append(pltpu.VMEM((rows, cols), BF))

    def bind(self, ins, outs, scratch):
        (self.own,) = ins
        self.whole = outs[0] if outs else None
        self.sent, self.come, self.sem = scratch[:3]
        self.bounce = scratch[3] if len(scratch) > 3 else None
        self.p = Place()

    def rows(self, piece):
        return pl.ds(pl.multiple_of(piece * self.each, 16), self.each)

    def given(self, q):
        return self.own.at[self.rows(self.p.piece(0, 0, self.p.c))]

    def slot(self, piece, q):
        return self.whole.at[self.rows(piece)]

    def keep(self):
        if self.bounce is None:
            return [pltpu.make_async_copy(self.own, self.whole, self.sem.at[0])]
        return [
            pltpu.make_async_copy(self.own, self.bounce, self.sem.at[0]),
            pltpu.make_async_copy(self.bounce, self.whole, self.sem.at[1]),
        ]

    def step(self, k):
        def there():
            for a in (0, 1):
                self.arrived(a, 0)
                self.spread(a, 0, self.home(a, 0))

        def last():
            self.close()

        if k == 0:
            self.plain(self.kept)
        elif k in (1, 2):
            self.leave(k == 1)
        elif k == 3:
            self.other(there)
        elif k == 4:
            self.other(lambda: self.forward(0))
        elif k == END:
            self.to_plane(0).wait_send()
            self.plain(self.land)
            self.other(last)


class Exchange:
    def __init__(self, src, dst, there, sems, sem, index=0):
        self.p = Place()
        self.src, self.dst, self.there, self.sems, self.sem, self.index = src, dst, there, sems, sem, index

    def stay(self):
        return pltpu.make_async_copy(self.src, self.dst, self.sem.at[self.index])

    def leave(self):
        return send(self.src, self.there, self.sems, self.index, self.p.swapped())

    def come(self):
        return send(self.src, self.dst, self.sems, self.index, self.p.swapped())

    def both(self, stay, leave):
        pl.when(self.p.plain)(stay)
        pl.when(jnp.logical_not(self.p.plain))(leave)

    def start(self):
        self.both(lambda: self.stay().start(), lambda: self.leave().start())

    def arrive(self):
        self.both(lambda: self.stay().wait(), lambda: self.come().wait_recv())

    def finish(self):
        pl.when(jnp.logical_not(self.p.plain))(lambda: self.leave().wait_send())


class Spread:
    def __init__(self, block, at, parts=2):
        rows, cols = block.shape
        self.at, self.parts = at, parts
        self.ins = [block]
        self.outs = [jax.ShapeDtypeStruct((rows, 4 * cols), block.dtype)]
        self.out_specs = [HBM]
        self.scratch = [*gather_scratch(parts), DMA((2, parts)), DMA((parts,))]

    def bind(self, ins, outs, scratch):
        (self.block,), (self.full,) = ins, outs
        near, over, onward, sems, sem = scratch
        self.p, self.g = Place(), Group(calls=False)
        self.gather = Columns(self.g, self.full, near, over, onward)
        cols = self.block.shape[1]
        self.exchanges = []
        for p in range(self.parts):
            rows = pl.ds(p * self.gather.step, self.gather.step)
            mine, there = (self.full.at[rows, lanes(b * cols, cols)] for b in (self.g.mine, self.g.beside))
            self.exchanges.append(Exchange(self.block.at[rows], mine, there, sems, sem, p))

    def greets(self):
        return Place.ENDS

    def step(self, k):
        if k == 0:
            for exchange in self.exchanges:
                exchange.start()
        elif k == 1:
            for p, exchange in enumerate(self.exchanges):
                exchange.arrive()
                self.gather.link(p, self.g.mine).start()
                self.gather.close(p, self.g.mine).start()
        elif k == 2:
            for p in range(self.parts):
                self.gather.wait_part(p)
        elif k == END:
            self.gather.wait_beside()
            for p in range(self.parts):
                self.gather.wait_far(p)
            self.gather.finish()
            for exchange in self.exchanges:
                exchange.finish()


class Deliver:
    def __init__(self, block, at):
        rows, width = block.shape
        self.at = at
        self.ins = [block]
        self.outs = [jax.ShapeDtypeStruct((4 * rows, width // 4), BF)]
        self.out_specs = [HBM]
        self.scratch = [pltpu.VMEM((rows, width), BF), DMA((4,)), DMA((4,)), DMA((2,))]
        if block.dtype != BF:
            self.scratch.append(pltpu.VMEM((rows, width), block.dtype))

    def bind(self, ins, outs, scratch):
        (self.block,), (self.out,) = ins, outs
        self.low, self.sent, self.come, self.sem = scratch[:4]
        self.wide = scratch[4] if len(scratch) > 4 else self.low
        self.p, self.g = Place(), Group(calls=False)

    def greets(self):
        return Place.COLUMN

    def load(self):
        return pltpu.make_async_copy(self.block, self.wide, self.sem.at[0])

    def parts(self):
        rows, width = self.low.shape
        cols = width // 4
        dst = self.out.at[at_rows(self.g.mine, rows, 0, rows)]
        for f in range(4):
            half, z = divmod(f, 2)
            here = (self.p.c == self.p.zh) & (self.p.zh == half) & (self.g.z == z)
            src = self.low.at[:, pl.ds(f * cols, cols)]
            where = {"c": self.p.zh, "zh": jnp.int32(half), "zl": jnp.int32(z)}
            yield here, pltpu.make_async_copy(src, dst, self.sem.at[1]), pltpu.make_async_remote_copy(
                src_ref=src, dst_ref=dst, send_sem=self.sent.at[f], recv_sem=self.come.at[self.g.mine],
                device_id=where, device_id_type=MESH,
            )

    def step(self, k):
        if k == 0:
            self.load().start()
        elif k == 1:
            self.load().wait()
            if self.wide is not self.low:
                self.low[...] = self.wide[...].astype(BF)
            for here, stay, leave in self.parts():
                pl.when(here)(lambda stay=stay: stay.start())
                pl.when(jnp.logical_not(here))(lambda leave=leave: leave.start())
        elif k == END:
            rows, width = self.low.shape
            for here, stay, leave in self.parts():
                pl.when(here)(lambda stay=stay: stay.wait())
                pl.when(jnp.logical_not(here))(lambda leave=leave: leave.wait_send())
            for b in range(4):
                core, z = divmod(b, 2)
                here = (self.p.c == self.p.zh) & (self.p.c == core) & (self.g.z == z)
                come = pltpu.make_async_remote_copy(
                    src_ref=self.low.at[:, pl.ds(0, width // 4)], dst_ref=self.out.at[pl.ds(b * rows, rows)],
                    send_sem=self.sent.at[0], recv_sem=self.come.at[b], device_id=self.p.partner, device_id_type=MESH,
                )
                pl.when(jnp.logical_not(here))(lambda come=come: come.wait_recv())


class Total:
    def __init__(self, pieces, at, count, axes):
        self.at, self.count, self.axes = at, count, axes
        self.ins = pieces
        self.in_specs = [INV] * len(pieces)
        width = pieces[0].shape[1]
        self.outs = [jax.ShapeDtypeStruct((8, width), F32)]
        self.out_specs = [INV]
        self.scratch = [
            pltpu.VMEM((len(self.axes), 8, width), F32), pltpu.VMEM((len(self.axes), 8, width), F32),
            DMA((2, len(self.axes))),
        ]

    def bind(self, ins, outs, scratch):
        self.pieces, (self.out,) = ins, outs
        self.sum, self.other, self.sems = scratch
        self.p, self.g = Place(), Group(calls=False)

    def greets(self):
        return ("x",) + Place.ENDS + (("y",) if "r" in self.axes else ())

    def hop(self, i):
        axis = self.axes[i]
        return send(self.sum.at[i], self.other.at[i], self.sems, i, {axis: 1 - lax.axis_index(axis)})

    def step(self, k):
        if k == 0:
            gains, taps, heads = self.pieces[:4], self.pieces[4], self.pieces[5:]
            self.sum[0] = jnp.zeros(self.sum.shape[1:], F32)
            for i, gain in enumerate(gains):
                self.sum[0, pl.ds(i, 1), :] = gain[...]
            cols = taps.shape[1]
            self.sum[0, pl.ds(4, self.count), lanes(self.g.mine * cols, cols)] = taps[pl.ds(0, self.count), :]
            done = 0
            for head in heads:
                self.sum[0, pl.ds(7, 1), pl.ds(done, head.shape[1])] = head[...]
                done += head.shape[1]
            self.hop(0).start()
        else:
            k = min(k, 4)
            last = len(self.axes) if k == 4 else k
            for i in range(k - 1, last):
                self.hop(i).wait()
                value = self.sum[i] + self.other[i]
                if i + 1 < len(self.axes):
                    self.sum[i + 1] = value
                    self.hop(i + 1).start()
                else:
                    self.out[...] = value


class Reduce:
    def __init__(self, grad, first, rows, at, last=True):
        self.first, self.rows, self.at, self.last = first, rows, at, last
        cols = grad.shape[2]
        self.ins = [grad]
        self.outs = [shaped((rows, cols), F32) if last else shaped((2, rows, cols), BF)]
        self.out_specs = [INV]
        self.scratch = [
            pltpu.VMEM((4, rows, cols), BF), pltpu.VMEM((4, rows, cols), BF), pltpu.VMEM((2, rows, cols), BF),
            DMA((9,)), DMA((8,)), DMA((4,)),
        ]
        if last:
            self.scratch.append(pltpu.VMEM((2, rows, cols), BF))

    def bind(self, ins, outs, scratch):
        (self.grad,), (self.out,) = ins, outs
        self.held, self.in1, self.in2, self.sent, self.come, self.sem = scratch[:6]
        self.in3 = scratch[6] if self.last else None
        self.p = Place()

    def greets(self):
        return Place.PLANES + (Place.ENDS if self.last else ())

    def fin(self, a):
        return self.held.at[2 * a]

    def piece(self, flip_y, flip_x, a):
        return self.grad.at[self.p.piece(flip_y, flip_x, a), pl.ds(self.first, self.rows)]

    def copy(self, src, dst, sent, come, where):
        return pltpu.make_async_remote_copy(
            src_ref=src, dst_ref=dst, send_sem=self.sent.at[sent], recv_sem=self.come.at[come],
            device_id=where, device_id_type=MESH,
        )

    def loads(self):
        kept = [(0, 0, 0), (0, 1, 0), (0, 0, 1), (1, 0, 1)]
        return [pltpu.make_async_copy(self.piece(*k), self.held.at[i], self.sem.at[i]) for i, k in enumerate(kept)]

    def first_hops(self):
        p = self.p
        return [
            self.copy(self.piece(1, 0, 0), self.in1.at[0], 0, 0, p.across_y),
            self.copy(self.piece(1, 1, 0), self.in1.at[1], 1, 1, p.across_y),
            self.copy(self.piece(0, 1, 1), self.in1.at[2], 2, 2, p.across_x),
            self.copy(self.piece(1, 1, 1), self.in1.at[3], 3, 3, p.across_x),
        ]

    def second_hops(self):
        return [
            self.copy(self.held.at[1], self.in2.at[0], 4, 4, self.p.across_x),
            self.copy(self.held.at[3], self.in2.at[1], 5, 5, self.p.across_y),
        ]

    def to_owner(self, a):
        return self.copy(self.fin(a), self.in3.at[0], 6 + a, 6, self.p.over(a))

    def to_partner(self):
        return self.copy(self.fin(1 - self.p.c), self.in3.at[1], 8, 7, self.p.partner)

    def add(self, i, other):
        self.held[i] = (self.held[i].astype(F32) + other.astype(F32)).astype(BF)

    def step(self, k):
        p = self.p
        if k == 0:
            for hop in [self.first_hops()[i] for i in (1, 3, 0, 2)]:
                hop.start()
            for load in self.loads():
                load.start()
        elif k == 1:
            for load in self.loads():
                load.wait()
            hops, after = self.first_hops(), self.second_hops()
            for i in (1, 3):
                hops[i].wait_recv()
                self.add(i, self.in1[i])
                after[i // 2].start()
            for i in (0, 2):
                hops[i].wait_recv()
                self.add(i, self.in1[i])
        elif k == 2:
            for i, hop in enumerate(self.second_hops()):
                hop.wait_recv()
                if self.last:
                    self.add(2 * i, self.in2[i])
                else:
                    self.out[i] = (self.held[2 * i].astype(F32) + self.in2[i].astype(F32)).astype(BF)
            if self.last:
                self.settle()
                self.settle(False)
        elif k == END:
            if self.last:
                self.close()
            for hop in self.first_hops() + self.second_hops():
                hop.wait_send()

    def settle(self, outer=True):
        if outer:

            @pl.when(self.p.plain)
            def _():
                self.to_partner().start()

        now = self.p.outer if outer else jnp.logical_not(self.p.outer)

        @pl.when(now & jnp.logical_not(self.p.plain))
        def _():
            self.to_owner(0).start()
            self.to_owner(1).start()

    def close(self):
        p = self.p
        self.to_owner(0).wait_recv()

        @pl.when(p.plain)
        def _():
            self.out[...] = self.own(p.c).astype(F32) + self.in3[0].astype(F32)
            self.to_partner().wait_send()

        @pl.when(jnp.logical_not(p.plain))
        def _():
            self.to_partner().wait_recv()
            self.out[...] = self.in3[1].astype(F32) + self.in3[0].astype(F32)
            self.to_owner(0).wait_send()
            self.to_owner(1).wait_send()

    def own(self, a):
        return self.held[2 * a]


class Settle(Reduce):
    def __init__(self, sums, at):
        _, rows, cols = sums.shape
        self.at = at
        self.ins = [sums]
        self.outs = [shaped((rows, cols), F32)]
        self.out_specs = [INV]
        self.scratch = [pltpu.VMEM((rows, cols), BF), pltpu.VMEM((2, rows, cols), BF), DMA((9,)), DMA((8,)), DMA((1,))]

    def bind(self, ins, outs, scratch):
        (self.sums,), (self.out,) = ins, outs
        self.kept, self.in3, self.sent, self.come, self.sem = scratch
        self.p = Place()

    def greets(self):
        return Place.ENDS

    def fin(self, a):
        return self.sums.at[a]

    def own(self, a):
        return self.kept[...]

    def load(self):
        return pltpu.make_async_copy(self.sums.at[self.p.c], self.kept, self.sem.at[0])

    def step(self, k):
        if k == 0:
            self.load().start()
            self.settle()
        elif k == 1:
            self.settle(False)
        elif k == END:
            self.load().wait()
            self.close()


class Background:
    def __init__(self, tasks, greets):
        self.tasks, self.done, names = tasks, [], list(greets)
        for task in tasks:
            names += [name for name in task.greets() if name not in names]
        place = Place()
        self.others = [place.called(name) for name in names]

    def step(self, k):
        for i in range(max([len(task.at) for task in self.tasks], default=0)):
            for task in self.tasks:
                if i < len(task.at) and task.at[i] == k:
                    task.step(i)

    def finish(self, tasks=None):
        for task in self.tasks if tasks is None else tasks:
            if task not in self.done:
                task.step(END)
                self.done.append(task)


def hosted(kernel, ident, name, ins, in_specs, outs, out_specs, scratch, tasks, flops, traffic, greets=()):
    groups = ([], [], [])
    for group, own in zip(groups, (ins, outs, scratch)):
        group.append(len(own))
    ins, in_specs, outs, out_specs, scratch = list(ins), list(in_specs), list(outs), list(out_specs), list(scratch)
    for task in tasks:
        for group, more in zip(groups, (task.ins, task.outs, task.scratch)):
            group.append(len(more))
        ins += task.ins
        in_specs += getattr(task, "in_specs", [HBM] * len(task.ins))
        outs += task.outs
        out_specs += task.out_specs
        scratch += task.scratch

    def split(refs, counts):
        at, found = 0, []
        for count in counts:
            found.append(refs[at : at + count])
            at += count
        return found

    def body(*refs):
        parts = [split(part, group) for part, group in zip(split(refs, [sum(g) for g in groups]), groups)]
        for task, *mine in zip(tasks, *(part[1:] for part in parts)):
            task.bind(*mine)
        kernel(*parts[0][0], *parts[1][0], *parts[2][0], Background(tasks, greets))

    aliases, at_in, at_out = {}, groups[0][0], groups[1][0]
    for task in tasks:
        if getattr(task, "in_place", False):
            aliases[at_in] = at_out
        at_in += len(task.ins)
        at_out += len(task.outs)
    results = pl.pallas_call(
        body,
        out_shape=tuple(outs),
        in_specs=in_specs,
        out_specs=tuple(out_specs),
        scratch_shapes=scratch,
        input_output_aliases=aliases,
        compiler_params=params(ident),
        cost_estimate=pl.CostEstimate(flops=flops, bytes_accessed=traffic, transcendentals=0),
        name=name,
    )(*ins)
    results = split(list(results), groups[1])
    return results[0], [r[0] for r in results[1:] if r]


def put_rows(scratch, first, value, cols=slice(None)):
    tall = scratch.shape[1]
    done = 0
    while done < value.shape[0]:
        piece, at = divmod(first + done, tall)
        count = min(tall - at, value.shape[0] - done)
        scratch[piece, pl.ds(at, count), cols] = value[done : done + count]
        done += count


def put_columns(scratch, first, value):
    wide_piece = scratch.shape[2]
    for piece in range(scratch.shape[0]):
        scratch[piece, pl.ds(first, value.shape[0]), :] = value[:, piece * wide_piece : (piece + 1) * wide_piece]


def column_loads(pieces, whole):
    each = pieces.shape[2]
    return [(pieces.at[i], whole.at[:, pl.ds(i * each, each)]) for i in range(pieces.shape[0])]


def ffn_forward_kernel(
    h_ref, gain_ref, w_hbm, v_hbm, out_ref, n_hbm, u_hbm,
    w, v, nf, u, act, tpart, mine, n_near, n_over, n_on, o_near, i_near, o_over, i_over, s_near, s_over,
    wsem, osem, bg,
):
    g = Group(bg.others)
    g.greet()
    size, width = h_ref.shape
    hidden = v.shape[0]
    loads = start_all([(w_hbm, w)] + column_loads(v_hbm, v), wsem)
    gather = Gather(g, nf, size, n_near, n_over, n_on)
    scatter = Scatter(g, o_near, i_near, o_over, i_over, s_near, s_over, size)
    parts, step = gather.parts, gather.step
    for p in range(parts):
        nf[at_rows(g.mine, size, p * step, step), :] = normalise(
            h_ref[pl.ds(p * step, step), :], gain_ref[...]
        ).astype(BF)
    g.meet()
    gather.start()
    bg.step(0)
    wait_all(loads)

    third = hidden // 3

    def rows_of(places):
        return jnp.concatenate([nf[r, :] for r, _ in places], axis=0) if len(places) > 1 else nf[places[0][0], :]

    def up(places):
        def body(t, carry):
            x = rows_of(places)
            cols, more = lanes(t * third, third), lanes(hidden + t * third, third)
            both = mm(x, jnp.concatenate([w[:, cols], w[:, more]], axis=1))
            gate, upper = both[:, :third], both[:, third:]
            a = gate * jax.nn.sigmoid(gate) * upper
            act[:, cols] = a.astype(BF)
            at = 0
            for r, count in places:
                u[r, cols] = gate[at : at + count].astype(BF)
                u[r, more] = upper[at : at + count].astype(BF)
                at += count
            return carry

        lax.fori_loop(0, 3, body, 0)

    def down(store):
        store(slice(None), mm(act[...], v[...]))

    def keep(index, r, count):
        return pltpu.make_async_copy(u.at[r], u_hbm.at[r], osem.at[index])

    whole = lambda block: at_rows(block, size, 0, size)
    up([(whole(g.mine), size)])
    keep(0, whole(g.mine), size).start()

    def put_mine(cols, value):
        mine[:, cols] = value

    down(put_mine)
    gather.wait_beside()
    up([(whole(g.beside), size)])
    keep(1, whole(g.beside), size).start()

    def put_beside(cols, value):
        o_near[1, :, cols] = value.astype(BF)

    down(put_beside)
    for p in range(parts):
        scatter.close(1, p).start()
    bg.step(1)
    for p in range(parts):
        gather.wait_part(p)
        gather.wait_far(p)
        r_across, r_far = at_rows(g.across, size, p * step, step), at_rows(g.far, size, p * step, step)
        up([(r_across, step), (r_far, step)])
        keep(2 + 2 * p, r_across, step).start()
        keep(3 + 2 * p, r_far, step).start()
        here = scatter.rows(p)

        def put(cols, value):
            tpart[:, cols] = value[:step]
            o_near[0, here, cols] = value[step:].astype(BF)

        down(put)
        scatter.close(0, p).start()
        scatter.close(0, p).wait_recv()
        o_over[here, :] = (tpart[...] + i_near[0, here, :].astype(F32)).astype(BF)
        scatter.link(p).start()
        bg.step(10 + p)
    n_out = pltpu.make_async_copy(nf, n_hbm, osem.at[2 + 2 * parts])
    n_out.start()
    bg.step(2)
    for p in range(parts):
        here = scatter.rows(p)
        scatter.close(1, p).wait_recv()
        scatter.link(p).wait_recv()
        out_ref[here, :] = (
            h_ref[here, :] + mine[here, :] + i_near[1, here, :].astype(F32) + i_over[here, :].astype(F32)
        )
    gather.finish()
    scatter.wait_all_sends()
    keep(0, whole(g.mine), size).wait()
    keep(1, whole(g.beside), size).wait()
    for p in range(parts):
        keep(2 + 2 * p, at_rows(g.across, size, p * step, step), step).wait()
        keep(3 + 2 * p, at_rows(g.far, size, p * step, step), step).wait()
    n_out.wait()
    bg.step(6)
    bg.finish()


def ffn_forward(h, gain, w, v, ident, tasks=(), parts=PARTS):
    size, width = h.shape
    hidden = v.shape[1]
    total = 4 * size
    return hosted(
        ffn_forward_kernel, ident, "ffn_forward", [h, gain, w, v], [INV, INV, HBM, HBM],
        [shaped((size, width), F32), shaped((total, width), BF), shaped((total, 2 * hidden), BF)], [INV, HBM, HBM],
        [
            pltpu.VMEM((width, 2 * hidden), BF), pltpu.VMEM((hidden, width), BF), pltpu.VMEM((total, width), BF),
            pltpu.VMEM((total, 2 * hidden), BF), pltpu.VMEM((size, hidden), BF),
            pltpu.VMEM((size // parts, width), F32), pltpu.VMEM((size, width), F32),
            *gather_scratch(parts), *scatter_scratch(size, width, parts), DMA((1 + v.shape[0],)), DMA((3 + 2 * parts,)),
        ],
        tasks, 6 * total * width * hidden, 2**24,
    )


def mm_tn(a, b):
    return lax.dot_general(a, b, (((0,), (0,)), ((), ())), preferred_element_type=F32)


def rms_back(dn, h, gain):
    inverse = lax.rsqrt(jnp.mean(h * h, axis=-1, keepdims=True) + epsilon)
    scaled = dn * gain
    inner = jnp.mean(scaled * h, axis=-1, keepdims=True)
    grad_gain = jnp.sum(dn * h * inverse, axis=0, keepdims=True)
    return inverse * scaled - h * (inverse * inverse * inverse * inner), grad_gain


def close_scatter(scatter, mine, dh_ref, h_ref, gain_ref, out_ref, gg_ref):
    gg_ref[...] = jnp.zeros_like(gg_ref)
    for p in range(scatter.parts):
        here = scatter.rows(p)
        scatter.close(1, p).wait_recv()
        scatter.link(p).wait_recv()
        dn = mine[here, :] + scatter.in_near[1, here, :].astype(F32) + scatter.in_over[here, :].astype(F32)
        term, grad_gain = rms_back(dn, h_ref[here, :], gain_ref[...])
        out_ref[here, :] = dh_ref[here, :].astype(F32) + term
        gg_ref[...] += grad_gain


def ffn_backward_kernel(
    known, dh_ref, h_ref, gain_ref, df_hbm, w_hbm, v_hbm, n_hbm, u_hbm, out_ref, gg_ref, gw_hbm, gv_hbm,
    w, v, nf, u, act, df, tpart, mine, gw, gv, n_near, n_over, n_on, o_near, i_near, o_over, i_over, s_near, s_over,
    wsem, osem, bg,
):
    g = Group(bg.others)
    g.greet()
    size, width = h_ref.shape
    hidden = v.shape[0]
    loads = column_loads(v_hbm, v) + [(u_hbm, u), (w_hbm, w), (n_hbm, nf)]
    loads = start_all(loads + [(df_hbm, df)] if known else loads, wsem)
    gather = Gather(g, df, size, n_near, n_over, n_on)
    scatter = Scatter(g, o_near, i_near, o_over, i_over, s_near, s_over, size)
    parts, step = gather.parts, gather.step
    if not known:
        df[at_rows(g.mine, size, 0, size), :] = dh_ref[...].astype(BF)
    g.meet()
    if not known:
        gather.start()
    bg.step(0)
    wait_all(loads)

    third = hidden // 3

    def cat(ref, places, cols):
        found = [ref[r, cols] for r, _ in places]
        return found[0] if len(found) == 1 else jnp.concatenate(found, axis=0)

    def first(places):
        def body(t, carry):
            cols, more = lanes(t * third, third), lanes(hidden + t * third, third)
            da = mm_nt(cat(df, places, slice(None)), v[cols, :])
            gate, upper = cat(u, places, cols).astype(F32), cat(u, places, more).astype(F32)
            s = jax.nn.sigmoid(gate)
            lit = gate * s
            dgate = (da * upper * s * (1.0 + gate * (1.0 - s))).astype(BF)
            dupper = (da * lit).astype(BF)
            a = (lit * upper).astype(BF)
            at = 0
            for r, count in places:
                u[r, cols] = dgate[at : at + count]
                u[r, more] = dupper[at : at + count]
                act[r, cols] = a[at : at + count]
                at += count
            return carry

        lax.fori_loop(0, 3, body, 0)

    def second(places, store):
        def body(t, carry):
            cols = lanes(t * 512, 512)
            store(cols, mm_nt(cat(u, places, slice(None)), w[cols, :]))
            return carry

        lax.fori_loop(0, width // 512, body, 0)

    whole = lambda block: [(at_rows(block, size, 0, size), size)]

    def put_mine(cols, value):
        mine[:, cols] = value

    def put_beside(cols, value):
        o_near[1, :, cols] = value.astype(BF)

    def own():
        first(whole(g.mine))
        second(whole(g.mine), put_mine)

    def beside():
        first(whole(g.beside))
        second(whole(g.beside), put_beside)
        for p in range(parts):
            scatter.close(1, p).start()

    if not known:
        own()
        gather.wait_beside()
        beside()
    bg.step(1)
    for p in range(parts):
        if not known:
            gather.wait_part(p)
            gather.wait_far(p)
        pair = [(at_rows(b, size, p * step, step), step) for b in (g.across, g.far)]
        first(pair)
        here = scatter.rows(p)

        def put(cols, value):
            tpart[:, cols] = value[:step]
            o_near[0, here, cols] = value[step:].astype(BF)

        second(pair, put)
        scatter.close(0, p).start()
        scatter.close(0, p).wait_recv()
        o_over[here, :] = (tpart[...] + i_near[0, here, :].astype(F32)).astype(BF)
        scatter.link(p).start()
    bg.step(2)
    if known:
        beside()
        own()
    for t in range(3):
        put_columns(gv, t * third, mm_tn(act[:, t * third : (t + 1) * third], df[...]).astype(BF))
    save = pltpu.make_async_copy(gv, gv_hbm, osem.at[2])
    save.start()
    bg.step(3)
    for t in range(width // 512):
        for k in range(2):
            cols = slice(k * hidden, (k + 1) * hidden)
            put_rows(gw, t * 512, mm_tn(nf[:, t * 512 : (t + 1) * 512], u[:, cols]).astype(BF), cols)
    more = pltpu.make_async_copy(gw, gw_hbm, osem.at[0])
    more.start()
    bg.step(4)
    close_scatter(scatter, mine, df.at[at_rows(g.mine, size, 0, size)] if known else dh_ref, h_ref, gain_ref, out_ref, gg_ref)
    if not known:
        gather.finish()
    scatter.wait_all_sends()
    more.wait()
    save.wait()
    bg.step(6)
    bg.finish()


def ffn_backward(dh, h, gain, df, w, v, n, u, ident, tasks=(), parts=PARTS):
    size, width = h.shape
    pieces, hidden = v.shape[:2]
    total = 4 * size
    known = df is not None
    if known:
        dh = gain
    else:
        df = n
    return hosted(
        functools.partial(ffn_backward_kernel, known), ident, "ffn_backward", [dh, h, gain, df, w, v, n, u],
        [INV, INV, INV] + [HBM] * 5,
        [
            shaped((size, width), F32), shaped((1, width), F32), shaped((pieces, width // pieces, 2 * hidden), BF),
            shaped((pieces, hidden, width // pieces), BF),
        ],
        [INV, INV, HBM, HBM],
        [
            pltpu.VMEM((width, 2 * hidden), BF), pltpu.VMEM((hidden, width), BF), pltpu.VMEM((total, width), BF),
            pltpu.VMEM((total, 2 * hidden), BF), pltpu.VMEM((total, hidden), BF), pltpu.VMEM((total, width), BF),
            pltpu.VMEM((size // parts, width), F32), pltpu.VMEM((size, width), F32),
            pltpu.VMEM((pieces, width // pieces, 2 * hidden), BF), pltpu.VMEM((pieces, hidden, width // pieces), BF),
            *gather_scratch(parts), *scatter_scratch(size, width, parts), DMA((4 + pieces,)), DMA((3,)),
        ],
        tasks, 12 * total * width * hidden, 2**25,
    )


MOST_DOC = 512


class Columns(Gather):
    def __init__(self, group, full, near, over, onward):
        super().__init__(group, full, full.shape[0], near, over, onward)
        self.cols = full.shape[1] // 4

    def view(self, block, part):
        return self.full.at[pl.ds(part * self.step, self.step), lanes(block * self.cols, self.cols)]


def cat_rows(ref, places, cols=slice(None)):
    found = [ref[r, cols] for r, _ in places]
    return found[0] if len(found) == 1 else jnp.concatenate(found, axis=0)


def product(src, weight, turned, tile=1024):
    def run(places, store):
        width = weight.shape[0] if turned else weight.shape[1]

        def body(t, carry):
            cols = lanes(t * tile, tile)
            x = cat_rows(src, places)
            store(cols, mm_nt(x, weight[cols, :]) if turned else mm(x, weight[:, cols]))
            return carry

        lax.fori_loop(0, width // tile, body, 0)

    return run


def scatter_all(g, scatter, run, mine, tpart):
    size, step = scatter.size, scatter.step
    for p in range(scatter.parts):
        here = scatter.rows(p)

        def put(cols, value):
            tpart[:, cols] = value[:step]
            scatter.out_near[0, here, cols] = value[step:].astype(BF)

        run([(at_rows(b, size, p * step, step), step) for b in (g.across, g.far)], put)
        scatter.close(0, p).start()
        scatter.close(0, p).wait_recv()
        scatter.out_over[here, :] = (tpart[...] + scatter.in_near[0, here, :].astype(F32)).astype(BF)
        scatter.link(p).start()

    def put_beside(cols, value):
        scatter.out_near[1, :, cols] = value.astype(BF)

    run([(at_rows(g.beside, size, 0, size), size)], put_beside)
    for p in range(scatter.parts):
        scatter.close(1, p).start()

    def put_mine(cols, value):
        mine[:, cols] = value

    run([(at_rows(g.mine, size, 0, size), size)], put_mine)


def gather_everything(gather):
    gather.wait_beside()
    for p in range(gather.parts):
        gather.wait_part(p)
    for p in range(gather.parts):
        gather.wait_far(p)


def doc_starts(docs, lengths, places):
    row = lengths[pl.ds(0, 1), :]
    end = jnp.zeros((1, 1), F32)
    start = jnp.zeros_like(places)
    for d in range(docs):
        end = end + row[:, d : d + 1]
        start = jnp.where(places >= end.astype(jnp.int32), end.astype(jnp.int32), start)
    return start


def conv_taps(gated, within, taps):
    total = gated.shape[0]
    summed = taps[0] * gated
    for j in range(1, len(taps)):
        summed = summed + taps[j] * jnp.where(within >= j, pltpu.roll(gated, j, 0), 0.0)
    return summed


def conv_forward_kernel(
    docs, count, inside, lens_ref, x_hbm, gain_ref, taps_ref, win_hbm, wout_hbm,
    out_ref, block_ref, n_hbm, p_hbm, lengths, taps_out, win_out, wout_out,
    win, wout, full, nf, proj, low, mixed, tpart, mine, n_near, n_over, n_on, o_near, i_near, o_over, i_over,
    s_near, s_over, wsem, osem, xsem, xlocal, bg,
):
    g = Group(bg.others)
    g.greet()
    size, width = out_ref.shape
    total, chans = x_hbm.shape[0], wout.shape[0]
    loads = []
    if inside:
        bg.tasks[0].whole, bg.tasks[1].whole = win, wout
    else:
        loads = start_all([(win_hbm, win), (wout_hbm, wout)], wsem)
    gather = Columns(g, full, n_near, n_over, n_on)
    scatter = Scatter(g, o_near, i_near, o_over, i_over, s_near, s_over, size)
    parts = gather.parts
    blocks = [
        Exchange(
            x_hbm.at[pl.ds(p * gather.step, gather.step)],
            *(full.at[pl.ds(p * gather.step, gather.step), lanes(b * chans, chans)] for b in (g.mine, g.beside)),
            xsem, xlocal, p,
        )
        for p in range(parts)
    ]
    small = [Exchange(lens_ref, lengths, lengths, xsem, xlocal, parts), Exchange(taps_ref, taps_out, taps_out, xsem, xlocal, parts + 1)]
    g.meet()
    for block in blocks + small:
        block.start()
    bg.step(0)
    for p in range(parts):
        blocks[p].arrive()
        gather.link(p, g.mine).start()
        gather.close(p, g.mine).start()
    bg.step(1)
    gather.wait_beside()
    for p in range(parts):
        gather.wait_part(p)
    for p in range(parts):
        gather.wait_far(p)
    for block in small:
        block.arrive()
    bg.step(2)
    if inside:
        bg.finish(bg.tasks[:2])
    wait_all(loads)

    def project(t, carry):
        rows = at_rows(t, size, 0, size)
        n = normalise(full[rows, :].astype(F32), gain_ref[...]).astype(BF)
        nf[rows, :] = n
        p = mm(n, win[...])
        proj[rows, :] = p
        low[rows, :] = p.astype(BF)
        return carry

    lax.fori_loop(0, total // size, project, 0)
    bg.step(4)
    saves = start_all([(nf, n_hbm), (low, p_hbm), (win, win_out), (wout, wout_out)], osem)
    places = lax.broadcasted_iota(jnp.int32, (total, LANES), 0)
    within = places - doc_starts(docs, lengths, places)
    for k in range(chans // LANES):
        b, c, x = (proj[:, pl.ds(i * chans + k * LANES, LANES)] for i in range(3))
        taps = [taps_out[pl.ds(j, 1), pl.ds(k * LANES, LANES)] for j in range(count)]
        mixed[:, pl.ds(k * LANES, LANES)] = (c * conv_taps(b * x, within, taps)).astype(BF)
    bg.step(5)
    scatter_all(g, scatter, product(mixed, wout, False), mine, tpart)
    bg.step(3)
    block_ref[...] = full[at_rows(g.mine, size, 0, size), :]
    for p in range(scatter.parts):
        here = scatter.rows(p)
        scatter.close(1, p).wait_recv()
        scatter.link(p).wait_recv()
        out_ref[here, :] = (
            block_ref[here, :].astype(F32) + mine[here, :] + i_near[1, here, :].astype(F32) + i_over[here, :].astype(F32)
        )
    for block in blocks + small:
        block.finish()
    gather.finish()
    scatter.wait_all_sends()
    wait_all(saves)
    bg.step(6)
    bg.finish()


def conv_forward(docs, count, lens, x, gain, taps, win, wout, inside, ident, tasks=(), parts=PARTS, cuts=4):
    total, chans = x.shape
    width = wout.shape[1]
    size = total // 4
    return hosted(
        functools.partial(conv_forward_kernel, docs, count, inside), ident, "conv_forward",
        [lens, x, gain, taps, win, wout], [INV, HBM, INV, INV, HBM, HBM],
        [
            shaped((size, width), F32), shaped((size, width), BF), shaped((total, width), BF), shaped((total, 3 * chans), BF),
            shaped(lens.shape, F32), shaped(taps.shape, F32), shaped(win.shape, BF), shaped(wout.shape, BF),
        ],
        [INV, INV, HBM, HBM, INV, INV, HBM, HBM],
        [
            pltpu.VMEM((width, 3 * chans), BF), pltpu.VMEM((chans, width), BF), pltpu.VMEM((total, width), BF),
            pltpu.VMEM((total, width), BF), pltpu.VMEM((total, 3 * chans), F32), pltpu.VMEM((total, 3 * chans), BF),
            pltpu.VMEM((total, chans), BF), pltpu.VMEM((size // parts, width), F32), pltpu.VMEM((size, width), F32),
            *gather_scratch(cuts), *scatter_scratch(size, width, parts), DMA((2,)), DMA((4,)),
            DMA((2, cuts + 2)), DMA((cuts + 2,)),
        ],
        tasks, 8 * total * width * chans, 2**24, ("swap",),
    )


def conv_backward_kernel(
    docs, count, lengths, dh_ref, h_ref, gain_ref, taps_ref, win_hbm, wout_hbm, n_hbm, p_hbm, out_ref, gg_ref, gt_ref, gin_hbm, gout_hbm,
    win, wout, nf, low, dz, dy, mixed, dproj, gin, gout, tpart, mine, n_near, n_over, n_on, o_near, i_near, o_over, i_over,
    s_near, s_over, wsem, osem, bg,
):
    g = Group(bg.others)
    g.greet()
    size, width = dh_ref.shape
    total, chans = 4 * size, wout.shape[0]
    loads = start_all([(wout_hbm, wout), (p_hbm, low), (win_hbm, win), (n_hbm, nf)], wsem)
    gather = Gather(g, dz, size, n_near, n_over, n_on)
    scatter = Scatter(g, o_near, i_near, o_over, i_over, s_near, s_over, size)
    dz[at_rows(g.mine, size, 0, size), :] = dh_ref[...].astype(BF)
    g.meet()
    gather.start()
    bg.step(0)
    wait_all(loads)
    places = lax.broadcasted_iota(jnp.int32, (total, LANES), 0)
    within = places - doc_starts(docs, lengths, places)
    gather_everything(gather)
    bg.step(1)

    def project(t, carry):
        rows = at_rows(t, size, 0, size)
        dy[rows, :] = mm_nt(dz[rows, :], wout[...])
        return carry

    lax.fori_loop(0, total // size, project, 0)
    for k in range(chans // LANES):
        b, c, x = (low[:, pl.ds(i * chans + k * LANES, LANES)].astype(F32) for i in range(3))
        here = pl.ds(k * LANES, LANES)
        taps = [taps_ref[pl.ds(j, 1), here] for j in range(count)]
        gated = b * x
        summed = conv_taps(gated, within, taps)
        d = dy[:, here]
        mixed[:, here] = (c * summed).astype(BF)
        ds = d * c
        dg = taps[0] * ds
        gt_ref[pl.ds(0, 1), here] = jnp.sum(ds * gated, axis=0, keepdims=True)
        for j in range(1, len(taps)):
            masked = jnp.where(within >= j, ds, 0.0)
            dg = dg + taps[j] * pltpu.roll(masked, total - j, 0)
            gt_ref[pl.ds(j, 1), here] = jnp.sum(masked * pltpu.roll(gated, j, 0), axis=0, keepdims=True)
        dproj[:, pl.ds(k * LANES, LANES)] = (dg * x).astype(BF)
        dproj[:, pl.ds(chans + k * LANES, LANES)] = (d * summed).astype(BF)
        dproj[:, pl.ds(2 * chans + k * LANES, LANES)] = (dg * b).astype(BF)
    bg.step(2)
    scatter_all(g, scatter, product(dproj, win, True), mine, tpart)
    bg.step(3)
    put_columns(gout, 0, mm_tn(mixed[...], dz[...]).astype(BF))
    save = pltpu.make_async_copy(gout, gout_hbm, osem.at[0])
    save.start()
    for t in range(width // 256):
        put_rows(gin, t * 256, mm_tn(nf[:, pl.ds(t * 256, 256)], dproj[...]).astype(BF))
    more = pltpu.make_async_copy(gin, gin_hbm, osem.at[1])
    more.start()
    bg.step(4)
    close_scatter(scatter, mine, dh_ref, h_ref, gain_ref, out_ref, gg_ref)
    gather.finish()
    scatter.wait_all_sends()
    save.wait()
    more.wait()
    bg.step(5)
    bg.step(6)
    bg.finish()


def conv_backward(docs, count, lengths, dh, h, gain, taps, win, wout, n, p, pieces, ident, tasks=(), parts=PARTS):
    size, width = dh.shape
    total, chans = 4 * size, wout.shape[0]
    each = width // pieces
    return hosted(
        functools.partial(conv_backward_kernel, docs, count), ident, "conv_backward",
        [lengths, dh, h, gain, taps, win, wout, n, p],
        [INV, INV, INV, INV, INV, HBM, HBM, HBM, HBM],
        [
            shaped((size, width), F32), shaped((1, width), F32), shaped(taps.shape, F32),
            shaped((pieces, each, 3 * chans), BF), shaped((pieces, chans, each), BF),
        ],
        [INV, INV, INV, HBM, HBM],
        [
            pltpu.VMEM((width, 3 * chans), BF), pltpu.VMEM((chans, width), BF), pltpu.VMEM((total, width), BF),
            pltpu.VMEM((total, 3 * chans), BF), pltpu.VMEM((total, width), BF), pltpu.VMEM((total, chans), F32),
            pltpu.VMEM((total, chans), BF), pltpu.VMEM((total, 3 * chans), BF), pltpu.VMEM((pieces, each, 3 * chans), BF),
            pltpu.VMEM((pieces, chans, each), BF), pltpu.VMEM((size // parts, width), F32), pltpu.VMEM((size, width), F32),
            *gather_scratch(parts), *scatter_scratch(size, width, parts), DMA((4,)), DMA((2,)),
        ],
        tasks, 16 * total * width * chans, 2**24,
    )


def head_sums(values, head):
    width = values.shape[1]
    a = lax.broadcasted_iota(jnp.int32, (width, width), 0) // head
    b = lax.broadcasted_iota(jnp.int32, (width, width), 1) // head
    same = jnp.where(a == b, 1.0, 0.0).astype(BF)
    high = values.astype(BF)
    low = (values - high.astype(F32)).astype(BF)
    return mm(high, same) + mm(low, same)


def turn(values, head):
    width = values.shape[1]
    lane = lax.broadcasted_iota(jnp.int32, values.shape, 1)
    return jnp.where(
        lane % head < head // 2, pltpu.roll(values, width - head // 2, 1), pltpu.roll(values, head // 2, 1)
    )


def wide(table, width):
    return jnp.concatenate([table] * (width // table.shape[1]), axis=1)


def norm_turn(raw, gain, cosine, sine, head):
    inverse = lax.rsqrt(head_sums(raw * raw, head) * (1.0 / head) + epsilon)
    v = raw * inverse * gain
    return v * wide(cosine, raw.shape[1]) + turn(v, head) * wide(sine, raw.shape[1])


def norm_turn_back(d, raw, gain, cosine, sine, head):
    d = d * wide(cosine, raw.shape[1]) - turn(d, head) * wide(sine, raw.shape[1])
    inverse = lax.rsqrt(head_sums(raw * raw, head) * (1.0 / head) + epsilon)
    scaled = d * gain
    inner = head_sums(scaled * raw, head) * (1.0 / head)
    grad_gain = jnp.sum(d * raw * inverse, axis=0, keepdims=True)
    return inverse * scaled - raw * (inverse * inverse * inverse * inner), grad_gain


def score_tile(q, k, starts, first_key, first_query, scale):
    raw = mm_nt(k, q) * scale
    key = first_key + lax.broadcasted_iota(jnp.int32, raw.shape, 0)
    query = first_query + lax.broadcasted_iota(jnp.int32, (1, starts.shape[1]), 1)
    copies = raw.shape[1] // starts.shape[1]
    allowed = (key <= wide(query, raw.shape[1])) & (key >= wide(starts, raw.shape[1]))
    return jnp.where(allowed, raw, -1e30)


def softmax_tile(scores):
    top = jnp.max(scores, axis=0, keepdims=True)
    weights = jnp.exp(scores - top)
    return weights / jnp.sum(weights, axis=0, keepdims=True)


def stack_heads(values, head):
    return jnp.concatenate([values[:, i * head : (i + 1) * head] for i in range(values.shape[1] // head)], axis=0)


def attention_tiles(total, tile):
    back = -(-MOST_DOC // tile)
    return [(i * tile, max(0, i - back) * tile, (i + 1) * tile) for i in range(total // tile)]


def attention_forward_kernel(
    head, docs, lengths, h_ref, gain_ref, qgain_ref, kgain_ref, speed_ref, wq_hbm, wkv_hbm, wo_hbm,
    out_ref, n_hbm, raw_hbm, ready_hbm, o_hbm, cos_ref, sin_ref,
    w, wo, nf, low, ready, vt, o, tpart, mine, n_near, n_over, n_on, o_near, i_near, o_over, i_over,
    s_near, s_over, wsem, osem, bg,
):
    g = Group(bg.others)
    g.greet()
    size, width = h_ref.shape
    total, qw = 4 * size, wo.shape[0]
    kw = (w.shape[1] - qw) // 2
    loads = start_all([(wq_hbm, w.at[:, pl.ds(0, qw)]), (wkv_hbm, w.at[:, pl.ds(qw, 2 * kw)]), (wo_hbm, wo)], wsem)
    gather = Gather(g, nf, size, n_near, n_over, n_on)
    scatter = Scatter(g, o_near, i_near, o_over, i_over, s_near, s_over, size)
    parts, step = gather.parts, gather.step
    nf[at_rows(g.mine, size, 0, size), :] = normalise(h_ref[...], gain_ref[...]).astype(BF)
    g.meet()
    gather.start()
    bg.step(0)
    places = lax.broadcasted_iota(jnp.int32, (total, LANES), 0)
    angles = (places - doc_starts(docs, lengths, places)).astype(F32) * speed_ref[...]
    lane = lax.broadcasted_iota(jnp.int32, (total, LANES), 1)
    sine = jnp.sin(angles)
    cos_ref[...] = jnp.cos(angles)
    sin_ref[...] = jnp.where(lane % head < head // 2, -sine, sine)
    wait_all(loads)

    def project(block):
        rows = at_rows(block, size, 0, size)
        raw = mm(nf[rows, :], w[...])
        low[rows, :] = raw.astype(BF)
        cosine, sine = cos_ref[rows, :], sin_ref[rows, :]
        ready[rows, pl.ds(0, qw)] = norm_turn(raw[:, :qw], qgain_ref[...], cosine, sine, head).astype(BF)
        ready[rows, pl.ds(qw, kw)] = norm_turn(raw[:, qw : qw + kw], kgain_ref[...], cosine, sine, head).astype(BF)
        ready[rows, pl.ds(qw + kw, kw)] = raw[:, qw + kw :].astype(BF)

    project(g.mine)
    gather.wait_beside()
    project(g.beside)
    for p in range(parts):
        gather.wait_part(p)
    for p in range(parts):
        gather.wait_far(p)

    def rest(i, carry):
        project(jnp.where(i == 0, g.across, g.far))
        return carry

    lax.fori_loop(0, 2, rest, 0)
    bg.step(1)
    saves = start_all([(nf, n_hbm), (low, raw_hbm), (ready, ready_hbm)], osem)
    vt[...] = jnp.transpose(ready[:, pl.ds(qw + kw, kw)].astype(F32)).astype(BF)
    groups = qw // kw
    tile = 256
    scale = head ** (-0.5)
    starts = doc_starts(docs, lengths, lax.broadcasted_iota(jnp.int32, (1, total), 1))
    for first, low_key, high_key in attention_tiles(total, tile):
        keys = pl.ds(low_key, high_key - low_key)
        for kv in range(kw // head):
            q = stack_heads(ready[pl.ds(first, tile), pl.ds(kv * groups * head, groups * head)], head)
            k = ready[keys, pl.ds(qw, kw)][:, kv * head : (kv + 1) * head]
            p = softmax_tile(score_tile(q, k, starts[:, first : first + tile], low_key, first, scale)).astype(BF)
            ot = mm(vt[pl.ds(kv * head, head), keys], p)
            joined = jnp.concatenate([ot[:, i * tile : (i + 1) * tile] for i in range(groups)], axis=0)
            o[pl.ds(first, tile), pl.ds(kv * groups * head, groups * head)] = jnp.transpose(joined).astype(BF)
        if first == tile:
            bg.step(2)
    bg.step(3)
    save_o = pltpu.make_async_copy(o, o_hbm, osem.at[3])
    save_o.start()
    scatter_all(g, scatter, product(o, wo, False), mine, tpart)
    bg.step(4)
    for p in range(parts):
        here = scatter.rows(p)
        scatter.close(1, p).wait_recv()
        scatter.link(p).wait_recv()
        out_ref[here, :] = (
            h_ref[here, :] + mine[here, :] + i_near[1, here, :].astype(F32) + i_over[here, :].astype(F32)
        )
    gather.finish()
    scatter.wait_all_sends()
    wait_all(saves)
    save_o.wait()
    bg.step(6)
    bg.finish()


def attention_forward(head, docs, lengths, h, gain, qgain, kgain, speed, wq, wkv, wo, ident, tasks=(), parts=PARTS):
    size, width = h.shape
    total, qw = 4 * size, wo.shape[0]
    kw = wkv.shape[1] // 2
    every = qw + 2 * kw
    return hosted(
        functools.partial(attention_forward_kernel, head, docs), ident, "attention_forward",
        [lengths, h, gain, qgain, kgain, speed, wq, wkv, wo], [INV] * 6 + [HBM] * 3,
        [
            shaped((size, width), F32), shaped((total, width), BF), shaped((total, every), BF), shaped((total, every), BF),
            shaped((total, qw), BF), shaped((total, LANES), F32), shaped((total, LANES), F32),
        ],
        [INV] + [HBM] * 4 + [INV] * 2,
        [
            pltpu.VMEM((width, every), BF), pltpu.VMEM((qw, width), BF), pltpu.VMEM((total, width), BF),
            pltpu.VMEM((total, every), BF), pltpu.VMEM((total, every), BF),
            pltpu.VMEM((kw, total), BF), pltpu.VMEM((total, qw), BF),
            pltpu.VMEM((size // parts, width), F32), pltpu.VMEM((size, width), F32),
            *gather_scratch(parts), *scatter_scratch(size, width, parts), DMA((3,)), DMA((4,)),
        ],
        tasks, 2 * total * width * (every + qw), 2**24,
    )


def attention_backward_kernel(
    head, docs, lengths, dh_ref, h_ref, gain_ref, qgain_ref, kgain_ref, cos_ref, sin_ref, wq_hbm, wkv_hbm, wo_hbm,
    n_hbm, raw_hbm, ready_hbm, o_hbm, out_ref, gg_ref, gq_ref, gk_ref, gw_hbm, gwo_hbm,
    w, wo, nf, low, ready, kt, o, dz, do, dq, dkv, dlow, gw, gwo, tpart, mine,
    n_near, n_over, n_on, o_near, i_near, o_over, i_over, s_near, s_over, wsem, osem, bg,
):
    g = Group(bg.others)
    g.greet()
    size, width = h_ref.shape
    total, qw = 4 * size, wo.shape[0]
    kw = (w.shape[1] - qw) // 2
    loads = start_all(
        [
            (ready_hbm, ready), (wo_hbm, wo), (o_hbm, o), (raw_hbm, low), (wq_hbm, w.at[:, pl.ds(0, qw)]),
            (wkv_hbm, w.at[:, pl.ds(qw, 2 * kw)]), (n_hbm, nf),
        ],
        wsem,
    )
    gather = Gather(g, dz, size, n_near, n_over, n_on)
    scatter = Scatter(g, o_near, i_near, o_over, i_over, s_near, s_over, size)
    dz[at_rows(g.mine, size, 0, size), :] = dh_ref[...].astype(BF)
    g.meet()
    gather.start()
    bg.step(0)
    wait_all(loads)
    kt[...] = jnp.transpose(ready[:, pl.ds(qw, kw)].astype(F32)).astype(BF)
    dkv[...] = jnp.zeros_like(dkv)
    gather_everything(gather)

    def project(t, carry):
        rows = at_rows(t, size, 0, size)
        do[rows, :] = mm_nt(dz[rows, :], wo[...]).astype(BF)
        return carry

    bg.step(1)

    lax.fori_loop(0, total // size, project, 0)
    groups = qw // kw
    tile = 256
    scale = head ** (-0.5)
    starts = doc_starts(docs, lengths, lax.broadcasted_iota(jnp.int32, (1, total), 1))
    for first, low_key, high_key in attention_tiles(total, tile):
        keys = pl.ds(low_key, high_key - low_key)
        for kv in range(kw // head):
            cols = pl.ds(kv * groups * head, groups * head)
            lane = slice(kv * head, (kv + 1) * head)
            q = stack_heads(ready[pl.ds(first, tile), cols], head)
            k, v = ready[keys, pl.ds(qw, kw)][:, lane], ready[keys, pl.ds(qw + kw, kw)][:, lane]
            p = softmax_tile(score_tile(q, k, starts[:, first : first + tile], low_key, first, scale))
            d = stack_heads(do[pl.ds(first, tile), cols], head)
            dp = mm_nt(v, d)
            inner = jnp.sum(p * dp, axis=0, keepdims=True)
            ds = (p * (dp - inner)).astype(BF)
            both = jnp.concatenate([mm(ds, q) * scale, mm(p.astype(BF), d)], axis=1)
            dkv[kv, keys, :] += both
            dqt = mm(kt[pl.ds(kv * head, head), keys], ds) * scale
            joined = jnp.concatenate([dqt[:, i * tile : (i + 1) * tile] for i in range(groups)], axis=0)
            dq[pl.ds(first, tile), cols] = jnp.transpose(joined)
        if first == tile:
            bg.step(2)
        if first == 2 * tile:
            bg.step(3)
    bg.step(4)
    gq_ref[...] = jnp.zeros_like(gq_ref)
    gk_ref[...] = jnp.zeros_like(gk_ref)

    def finish(t, carry):
        rows = at_rows(t, size, 0, size)
        cosine, sine = cos_ref[rows, :], sin_ref[rows, :]
        d, gq = norm_turn_back(dq[rows, :], low[rows, pl.ds(0, qw)].astype(F32), qgain_ref[...], cosine, sine, head)
        gq_ref[...] += gq
        dlow[rows, pl.ds(0, qw)] = d.astype(BF)
        pairs = [dkv[kv, rows, :] for kv in range(kw // head)]
        dk = jnp.concatenate([x[:, :head] for x in pairs], axis=1)
        dv = jnp.concatenate([x[:, head:] for x in pairs], axis=1)
        d, gk = norm_turn_back(dk, low[rows, pl.ds(qw, kw)].astype(F32), kgain_ref[...], cosine, sine, head)
        gk_ref[...] += gk
        dlow[rows, pl.ds(qw, kw)] = d.astype(BF)
        dlow[rows, pl.ds(qw + kw, kw)] = dv.astype(BF)
        return carry

    lax.fori_loop(0, total // size, finish, 0)
    scatter_all(g, scatter, product(dlow, w, True), mine, tpart)
    put_columns(gwo, 0, mm_tn(o[...], dz[...]).astype(BF))
    save = pltpu.make_async_copy(gwo, gwo_hbm, osem.at[0])
    save.start()
    for t in range(width // 256):
        put_rows(gw, t * 256, mm_tn(nf[:, pl.ds(t * 256, 256)], dlow[...]).astype(BF))
    more = pltpu.make_async_copy(gw, gw_hbm, osem.at[1])
    more.start()
    bg.step(5)
    close_scatter(scatter, mine, dh_ref, h_ref, gain_ref, out_ref, gg_ref)
    gather.finish()
    scatter.wait_all_sends()
    save.wait()
    more.wait()
    bg.step(6)
    bg.finish()


def attention_backward(
    head, docs, lengths, dh, h, gain, qgain, kgain, cosine, sine, wq, wkv, wo, n, raw, ready, o, pieces, ident, tasks=(),
    parts=PARTS,
):
    size, width = h.shape
    total, qw = 4 * size, wo.shape[0]
    kw = wkv.shape[1] // 2
    every = qw + 2 * kw
    each = width // pieces
    return hosted(
        functools.partial(attention_backward_kernel, head, docs), ident, "attention_backward",
        [lengths, dh, h, gain, qgain, kgain, cosine, sine, wq, wkv, wo, n, raw, ready, o], [INV] * 8 + [HBM] * 7,
        [
            shaped((size, width), F32), shaped((1, width), F32), shaped((1, qw), F32), shaped((1, kw), F32),
            shaped((pieces, each, every), BF), shaped((pieces, qw, each), BF),
        ],
        [INV, INV, INV, INV, HBM, HBM],
        [
            pltpu.VMEM((width, every), BF), pltpu.VMEM((qw, width), BF), pltpu.VMEM((total, width), BF),
            pltpu.VMEM((total, every), BF), pltpu.VMEM((total, every), BF), pltpu.VMEM((kw, total), BF),
            pltpu.VMEM((total, qw), BF), pltpu.VMEM((total, width), BF), pltpu.VMEM((total, qw), BF),
            pltpu.VMEM((total, qw), F32), pltpu.VMEM((kw // head, total, 2 * head), F32), pltpu.VMEM((total, every), BF),
            pltpu.VMEM((pieces, each, every), BF), pltpu.VMEM((pieces, qw, each), BF),
            pltpu.VMEM((size // parts, width), F32), pltpu.VMEM((size, width), F32),
            *gather_scratch(parts), *scatter_scratch(size, width, parts), DMA((7,)), DMA((2,)),
        ],
        tasks, 4 * total * width * (every + qw), 2**25,
    )


def tail_kernel(bg):
    g = Group(bg.others)
    g.greet()
    g.meet()
    for k in range(4):
        bg.step(k)
    bg.step(6)
    bg.finish()


def tail(ident, tasks):
    return hosted(tail_kernel, ident, "tail", [], [], [], [], [], tasks, 0, 2**22)[1]


rope_base = 1000000.0
TP = ("c", "zl")
DP = ("r", "s", "zh")


def rope_speeds(head_dim):
    half_dim = head_dim // 2
    inverse = rope_base ** (-2.0 * jnp.arange(half_dim, dtype=F32) / head_dim)
    return jnp.tile(inverse, LANES // half_dim)[None]


def swap(x):
    return lax.ppermute(x, ("c", "zh"), [(0, 0), (1, 2), (2, 1), (3, 3)])


def gather_dp(shard, axis):
    return lax.all_gather(swap(shard), DP, axis=axis, tiled=True)


def scatter_dp(partial, axis):
    return swap(lax.psum_scatter(partial, DP, scatter_dimension=axis, tiled=True)).astype(F32)


def local(
    planes, tokens, doc_lengths, grad_out, norm_gains, head_gains, conv_in, conv_kernel, conv_out,
    query_w, kv_w, out_w, gate_up, down,
):
    length = tokens.shape[0]
    head_dim = head_gains.shape[1]
    docs, count = doc_lengths.shape[1], conv_kernel.shape[0]
    conv_in = conv_in.reshape(conv_in.shape[0], -1)
    kv_w = kv_w.reshape(kv_w.shape[0], -1)
    own_w = gate_up.reshape(*gate_up.shape[:2], -1)
    pieces = 8 if planes else 1
    kv_width = kv_w.shape[1] // 2
    qgain = jnp.tile(head_gains[0:1], (1, query_w.shape[1] // head_dim))
    kgain = jnp.tile(head_gains[1:2], (1, kv_width // head_dim))
    gain = [norm_gains[i : i + 1] for i in range(4)]
    lens = jnp.pad(doc_lengths.astype(F32), ((0, 7), (0, LANES - docs)))
    taps = jnp.pad(conv_kernel, ((0, 8 - count), (0, 0)))
    rows_of = lambda got: got.reshape(-1, got.shape[-1])
    if planes:
        first = [Take(conv_in, (0, 0, 0, 2, 2), True), Take(conv_out, (0, 0, 0, 2, 2), True)]
        first += [Fetch(own_w, (0, 1, 1, 2, 2, 4, 5), 2, 0, 0), Fetch(down, (0, 1, 1, 2, 5, 3), 1, 0, 0)]
        second = [Take(x, (0, 0, 0, 2, 2)) for x in (query_w, kv_w, out_w)]
        second += [Fetch(own_w, (0, 0, 0, 2), 1, 1, 1), Fetch(down, (0, 0, 0, 2), 1, 1, 1)]
    else:
        first, second, third = [], [], []
        conv_in, conv_out, query_w, kv_w, out_w = map(swap, (conv_in, conv_out, query_w, kv_w, out_w))
        w0, w1 = (gather_dp(w, 0) for w in own_w)
        v0, v1 = (gather_dp(v, 1)[None] for v in down)

    (h1, x_block, n0, projected, lens, taps, conv_in, conv_out), got = conv_forward(
        docs, count, lens, tokens, gain[0], taps, conv_in, conv_out, planes, 0, first
    )
    if planes:
        w0, v0 = rows_of(got[0]), got[1]
    (h2, n1, hidden0), got = ffn_forward(h1, gain[1], w0, v0, 1, second)
    if planes:
        query_w, kv_w, out_w = got[:3]
        third = [Fetch(got[3], (0, 4), 2, 2), Fetch(got[4], (0, 4), 1, 2)]
    (h3, n2, raw, ready, attended, cosine, sine), got = attention_forward(
        head_dim, docs, lens, h2, gain[2], qgain, kgain, rope_speeds(head_dim), query_w, kv_w, out_w, 2, third
    )
    if planes:
        w1, v1 = rows_of(got[0]), got[1]
    (h4, n3, hidden1), (up_full,) = ffn_forward(h3, gain[3], w1, v1, 3, [Spread(grad_out, (0, 1, 2))])

    def halves(grad, first, second, last=False):
        half = grad.shape[1] // 2
        return [Reduce(grad, 0, half, first, last), Reduce(grad, half, half, second, False)] if planes else []

    def whole(grad, at, last=False):
        return [Reduce(grad, 0, grad.shape[1], at, last)] if planes else []

    def settled(sums, at):
        return [Settle(x, at) for x in sums]

    (dh3, gain3, gw1, gv1), (output,) = ffn_backward(
        None, h3, gain[3], up_full, w1, v1, n3, hidden1, 4, [Deliver(h4, (0, 2))]
    )
    (dh2, gain2, gq, gk, gqkv, gow), sums = attention_backward(
        head_dim, docs, lens, dh3, h2, gain[2], qgain, kgain, cosine, sine, query_w, kv_w, out_w, n2, raw, ready, attended,
        pieces, 5, halves(gw1, (0, 2, 5), (0, 4, 6)),
    )
    (dh1, gain1, gw0, gv0), got = ffn_backward(
        dh2, h1, gain[1], None, w0, v0, n1, hidden0, 6,
        settled(sums, (0, 0)) + whole(gv1, (0, 2, 4)) + whole(gqkv, (0, 2, 4)) + whole(gow, (0, 2, 4)),
    )
    sums_w1, sums = got[:2], got[2:]
    (dh0, gain0, gtaps, gci, gco), got = conv_backward(
        docs, count, lens, dh1, x_block.astype(F32), gain[0], taps, conv_in, conv_out, n0, projected, pieces, 7,
        settled(sums, (0, 0)) + halves(gw0, (0, 1, 4), (0, 3, 6), True),
    )
    others, first_w0, sums = got[:3], got[3:4], got[4:]
    totals, grads, *got = tail(
        8,
        [Total([gain0, gain1, gain2, gain3, gtaps, gq, gk], (0, 1, 2, 3), count, ("zh", "s", *(("r",) if planes else ()), "zl", "c")), Deliver(dh0, (0, 0))]
        + settled(sums, (0, 0)) + whole(gv0, (0, 0, 1), True) + whole(gci, (1, 2, 3), True) + whole(gco, (1, 2, 3), True),
    )
    if planes:
        gv1, gqkv, gow = others
        gate_ups = [*first_w0, got[0], *sums_w1]
        gv0, gci, gco = got[1:]
    else:
        totals = lax.psum(totals, "r")
        gw0, gw1, gci, gqkv = (scatter_dp(g[0], 0) for g in (gw0, gw1, gci, gqkv))
        gv0, gv1, gco, gow = (scatter_dp(g[0], 1) for g in (gv0, gv1, gco, gow))
        gate_ups = [gw0, gw1]
    heads = totals[7, : gq.shape[1] + gk.shape[1]].reshape(-1, head_dim)
    split = gq.shape[1] // head_dim
    return (
        output,
        grads.astype(F32),
        totals[:4],
        jnp.stack([jnp.sum(heads[:split], axis=0), jnp.sum(heads[split:], axis=0)]),
        gci.reshape(-1, 3, conv_kernel.shape[1]),
        totals[4 : 4 + count],
        gco,
        gqkv[:, : query_w.shape[1]],
        gqkv[:, query_w.shape[1] :].reshape(-1, 2, kv_width),
        gow,
        jnp.concatenate(gate_ups, axis=0).reshape(2, gate_up.shape[1], 2, -1),
        jnp.stack([gv0, gv1]),
    )


def solution(mesh):
    devices = mesh.devices
    dp, tp = devices.shape
    inner = Mesh(devices.reshape(dp // 4, 2, 2, 2, tp // 2), ("r", "s", "c", "zh", "zl"))
    D = ("r", "s", "c")
    T = ("zh", "zl")
    return jax.shard_map(
        functools.partial(local, dp == 8),
        mesh=inner,
        in_specs=(
            P(D, T), P(D, None), P(D, T), P(), P(), P(None, None, T), P(None, T), P(T, None),
            P(None, T), P(None, None, T), P(T, None), P(None, D, None, T), P(None, T, D),
        ),
        out_specs=(
            P(D, T), P(D, T), P(), P(), P(D, None, T), P(), P(T, D), P(D, T), P(D, None, T),
            P(T, D), P(None, D, None, T), P(None, T, D),
        ),
        check_vma=False,
    )
```
